32 devices in a mesh: dp: 4 (over y, x), ctx: 8 (over z, core).
Axes of the slice: x: 2, y: 2, z: 4, core: 2. Of those that a mesh axis runs over, the one named last changes fastest.
Arguments:
- tokens: bfloat16 [8, 2048, 1024], P('dp', 'ctx'), may hold values from -6 to 6
- cotangent: bfloat16 [8, 2048, 1024], P('dp', 'ctx'), may hold values from -6 to 6
- starts: int32 [8, 4], P('dp'), may hold values from 0 to 1792, as said below
- w_query: bfloat16 [1024, 2048], P(('dp', 'ctx')), may hold values from -0.1875 to 0.1875
- key_matrix: bfloat16 [1024, 1024], P(('dp', 'ctx')), may hold values from -0.1875 to 0.1875
- value_matrix: bfloat16 [1024, 1024], P(('dp', 'ctx')), may hold values from -0.1875 to 0.1875
- w_out: bfloat16 [2048, 1024], P(('dp', 'ctx')), may hold values from -3 to 3
- w_gate: bfloat16 [1024, 3072], P(('dp', 'ctx')), may hold values from -0.1875 to 0.1875
- w_up: bfloat16 [1024, 3072], P(('dp', 'ctx')), may hold values from -0.1875 to 0.1875
- w_down: bfloat16 [3072, 1024], P(('dp', 'ctx')), may hold values from -0.109375 to 0.109375
- gains: bfloat16 [2304], P(('dp', 'ctx')), may hold values from 0.5 to 1.5
Outputs:
- output: bfloat16 [8, 2048, 1024], P('dp', 'ctx')
- grad_tokens: float32 [8, 2048, 1024], P('dp', 'ctx')
- grad_query: float32 [1024, 2048], P(('dp', 'ctx'))
- grad_key: float32 [1024, 1024], P(('dp', 'ctx'))
- grad_value: float32 [1024, 1024], P(('dp', 'ctx'))
- grad_out: float32 [2048, 1024], P(('dp', 'ctx'))
- grad_gate: float32 [1024, 3072], P(('dp', 'ctx'))
- grad_up: float32 [1024, 3072], P(('dp', 'ctx'))
- grad_down: float32 [3072, 1024], P(('dp', 'ctx'))
- grad_gains: float32 [2304], P(('dp', 'ctx'))
The draws below stay inside these ranges and needn't reach their ends.
Inputs may be any that keep to these rules, and one draw needn't show every extreme that they name: `starts`: each row holds 4 distinct multiples of 256 in increasing order, so pieces never intersect.
All inputs are finite; a program needn't handle non-finite values.
Results may differ from the reference program's by a relative error of at most 0.017.
Values may be sent and summed in bfloat16 or wider, within the bound.
A program may use at most 320 MiB of HBM per device.

```python
import math
import jax
import jax.numpy as jnp
from jax import lax

MODEL_DIM = 1024
QUERY_HEADS = 16
KEY_VALUE_HEADS = 8
HEAD_DIM = 128
FF = 3072
SEQUENCE_TOKENS = 2048
PIECE = 256
NPIECE = 4
NSEQ = 8
GAINS = 2304


def draw_starts(key, part):
    slot_count = SEQUENCE_TOKENS // PIECE
    key_list = jax.random.split(key, NSEQ + 1)

    def select(one_key):
        return jnp.sort(jax.random.permutation(one_key, slot_count)[:NPIECE])
    chosen = jax.vmap(select)(key_list[1:]).astype(jnp.int32)
    middle = jnp.sort(jax.random.permutation(key_list[0], slot_count - 2)[:NPIECE - 2] + 1)
    leading = jnp.concatenate([jnp.zeros((1,), jnp.int32), middle.astype(jnp.int32), jnp.full((1,), slot_count - 1, jnp.int32)])
    chosen = chosen.at[0].set(leading)
    return (chosen * PIECE).astype(jnp.int32)


def block_scale(own_key, extent, shards, low, high):
    def one(axis_at, blocks):
        steps = jax.random.uniform(jax.random.fold_in(jax.random.fold_in(own_key, 6), axis_at), (blocks,), jnp.float32, low / len(shards), high / len(shards))
        return jnp.repeat(jnp.exp(steps), extent[axis_at] // blocks).reshape((-1,) + (1,) * (len(extent) - axis_at - 1))

    gain = one(*shards[0])
    for cut in shards[1:]:
        gain = gain * one(*cut)
    return gain


def centred(own_key, shape, spread, bound, cuts=(), kind=jnp.bfloat16):
    drawn = jax.random.normal(own_key, shape, jnp.float32) * spread
    if len(cuts) > 0:
        drawn = block_scale(own_key, shape, cuts, -0.22, 0.18) * drawn
    return jnp.clip(drawn, min=-bound, max=bound).astype(kind)


def setup_inputs(seed: int = 0) -> dict:
    seeds = jax.random.split(jax.random.key(seed), 12)
    tokens = centred(seeds[0], (NSEQ, SEQUENCE_TOKENS, MODEL_DIM), 1.0, 6.0, ((0, 4), (1, 8)))
    cotangent = centred(seeds[1], (NSEQ, SEQUENCE_TOKENS, MODEL_DIM), 1.0, 6.0, ((0, 4), (1, 8)))
    starts = draw_starts(jax.random.fold_in(seeds[11], 71), 0)
    w_query = centred(seeds[3], (MODEL_DIM, QUERY_HEADS * HEAD_DIM), MODEL_DIM ** -0.5, 0.1875, ((0, 32),))
    key_matrix = centred(seeds[4], (MODEL_DIM, KEY_VALUE_HEADS * HEAD_DIM), MODEL_DIM ** -0.5, 0.1875, ((0, 32),))
    value_matrix = centred(seeds[5], (MODEL_DIM, KEY_VALUE_HEADS * HEAD_DIM), MODEL_DIM ** -0.5, 0.1875, ((0, 32),))
    w_out = centred(seeds[6], (QUERY_HEADS * HEAD_DIM, MODEL_DIM), (max(QUERY_HEADS * HEAD_DIM // 512, 1)) ** -0.5, 3.0, ((0, 32),))
    w_gate = centred(seeds[7], (MODEL_DIM, FF), MODEL_DIM ** -0.5, 0.1875, ((0, 32),))
    w_up = centred(seeds[8], (MODEL_DIM, FF), MODEL_DIM ** -0.5, 0.1875, ((0, 32),))
    w_down = centred(seeds[9], (FF, MODEL_DIM), FF ** -0.5, 0.109375, ((0, 32),))
    gains = jnp.clip(1.0 + 0.1 * jax.random.normal(seeds[10], (GAINS,), jnp.float32), 0.5, 1.5).astype(jnp.bfloat16)
    return dict(tokens=tokens, cotangent=cotangent, starts=starts, w_query=w_query, key_matrix=key_matrix, value_matrix=value_matrix, w_out=w_out, w_gate=w_gate, w_up=w_up, w_down=w_down, gains=gains)


EPS = 1e-06
THETA = 1000000.0
NEG = -1e+30
HIGH = lax.Precision.HIGHEST

@jax.custom_vjp
def reduced_precision(v):
    return lax.optimization_barrier(v.astype(jnp.bfloat16)).astype(jnp.float32)

@jax.custom_vjp
def low_back(v):
    return v

def low_keep(v):
    return (reduced_precision(v), None)

def low_pass(kept, grad):
    return (grad,)

def back_keep(v):
    return (v, None)

def back_low(kept, grad):
    return (reduced_precision(grad),)
reduced_precision.defvjp(low_keep, low_pass)
low_back.defvjp(back_keep, back_low)

def rms_norm(incoming_values, gain_vector):
    return incoming_values * lax.rsqrt(lax.optimization_barrier(jnp.mean(incoming_values * incoming_values, axis=-1, keepdims=True)) + EPS) * gain_vector

def rope_tables(positions):
    half_steps = jnp.arange(HEAD_DIM // 2, dtype=jnp.float32)
    inverse = THETA ** (-2.0 * half_steps / HEAD_DIM)
    angles = positions.astype(jnp.float32)[:, None] * inverse[None, :]
    angles = jnp.concatenate([angles, angles], axis=-1)
    return (jnp.cos(angles), jnp.sin(angles))

def rotate(incoming_values, cosine_table, sine_table):
    half_dim = HEAD_DIM // 2
    turned = jnp.concatenate([-incoming_values[..., half_dim:], incoming_values[..., :half_dim]], axis=-1)
    return incoming_values * cosine_table[:, None, :] + turned * sine_table[:, None, :]

def per_head_route(unrotated_projection, gain_vector, cosine_table, sine_table, head_count):
    shaped = unrotated_projection.reshape(unrotated_projection.shape[:-1] + (head_count, HEAD_DIM))
    return rotate(rms_norm(shaped, gain_vector), cosine_table, sine_table).reshape(unrotated_projection.shape)

def piece_ids(positions, piece_starts):
    inside = (positions[:, None] >= piece_starts[None, :]) & (positions[:, None] < piece_starts[None, :] + PIECE)
    number = jnp.arange(1, NPIECE + 1, dtype=jnp.int32)
    return lax.optimization_barrier(jnp.sum(jnp.where(inside, number[None, :], 0), axis=1)).astype(jnp.int32) - 1

def visible(query_pos, query_id, key_pos, key_id):
    causal = key_pos[None, :] <= query_pos[:, None]
    same_piece = (query_id[:, None] == key_id[None, :]) & (query_id[:, None] >= 0)
    return causal | same_piece

def block_layer(sequence, piece_starts, params):
    w_query, key_matrix, value_matrix, w_out, w_gate, w_up, w_down, gains = params
    g_attn = gains[:MODEL_DIM]
    g_mlp = gains[MODEL_DIM:2 * MODEL_DIM]
    g_query = gains[2 * MODEL_DIM:2 * MODEL_DIM + HEAD_DIM]
    key_grad_total = gains[2 * MODEL_DIM + HEAD_DIM:]
    query_group_factor = QUERY_HEADS // KEY_VALUE_HEADS
    scaling = 1.0 / math.sqrt(HEAD_DIM)
    positions = jnp.arange(SEQUENCE_TOKENS, dtype=jnp.int32)
    cosine_table, sine_table = rope_tables(positions)
    id_all = piece_ids(positions, piece_starts)
    normed = reduced_precision(rms_norm(sequence, g_attn))
    query_raw = low_back(jnp.dot(normed, w_query, precision=HIGH))
    key_unrotated = low_back(jnp.dot(normed, key_matrix, precision=HIGH))
    value_reduced = reduced_precision(low_back(jnp.dot(normed, value_matrix, precision=HIGH)))
    query_reduced = reduced_precision(per_head_route(query_raw, g_query, cosine_table, sine_table, QUERY_HEADS))
    key_reduced = reduced_precision(per_head_route(key_unrotated, key_grad_total, cosine_table, sine_table, KEY_VALUE_HEADS))
    rows_per_block = min(SEQUENCE_TOKENS, 512)
    number_of_blocks = SEQUENCE_TOKENS // rows_per_block
    key_head_rows = key_reduced.reshape(SEQUENCE_TOKENS, KEY_VALUE_HEADS, HEAD_DIM)
    value_head_rows = value_reduced.reshape(SEQUENCE_TOKENS, KEY_VALUE_HEADS, HEAD_DIM)
    query_block_list = query_reduced.reshape(number_of_blocks, rows_per_block, KEY_VALUE_HEADS, query_group_factor, HEAD_DIM)
    pos_blocks = positions.reshape(number_of_blocks, rows_per_block)
    id_blocks = id_all.reshape(number_of_blocks, rows_per_block)

    def attend(packed):
        query_block, pos_block, id_block = packed
        scores = low_back(jnp.einsum('tagd,kad->agtk', query_block, key_head_rows, precision=HIGH) * scaling)
        allowed = visible(pos_block, id_block, positions, id_all)
        scores = jnp.where(allowed[None, None], scores, NEG)
        row_max = lax.optimization_barrier(jnp.max(scores, axis=-1, keepdims=True))
        exp_scores = jnp.exp(scores - row_max)
        prob_all = exp_scores / lax.optimization_barrier(jnp.sum(exp_scores, axis=-1, keepdims=True))
        mixed_out = jnp.einsum('agtk,kad->tagd', reduced_precision(prob_all), value_head_rows, precision=HIGH)
        return mixed_out.reshape(rows_per_block, QUERY_HEADS * HEAD_DIM)
    mixed_all = lax.map(jax.checkpoint(attend), (query_block_list, pos_blocks, id_blocks)).reshape(SEQUENCE_TOKENS, QUERY_HEADS * HEAD_DIM)
    attn_out = reduced_precision(low_back(mixed_all))
    residual = sequence + low_back(jnp.dot(attn_out, w_out, precision=HIGH))
    mlp_in = reduced_precision(rms_norm(residual, g_mlp))
    gate_proj = low_back(jnp.dot(mlp_in, w_gate, precision=HIGH))
    up_proj = low_back(jnp.dot(mlp_in, w_up, precision=HIGH))
    hidden = reduced_precision(jax.nn.silu(gate_proj) * up_proj)
    return residual + low_back(jnp.dot(hidden, w_down, precision=HIGH))

def reference(tokens, cotangent, starts, w_query, key_matrix, value_matrix, w_out, w_gate, w_up, w_down, gains):
    params = (w_query.astype(jnp.float32), key_matrix.astype(jnp.float32), value_matrix.astype(jnp.float32), w_out.astype(jnp.float32), w_gate.astype(jnp.float32), w_up.astype(jnp.float32), w_down.astype(jnp.float32), gains.astype(jnp.float32))

    def forward(inputs, weights):

        def one_seq(packed):
            return block_layer(packed[0], packed[1], weights)
        return lax.map(jax.checkpoint(one_seq), (inputs, starts))
    result, pullback = jax.vjp(forward, tokens.astype(jnp.float32), params)
    grad_tokens, grad_params = pullback(cotangent.astype(jnp.float32))
    return (result.astype(jnp.bfloat16), grad_tokens, grad_params[0], grad_params[1], grad_params[2], grad_params[3], grad_params[4], grad_params[5], grad_params[6], grad_params[7])
```

```python
import functools
import math

import jax
import jax.numpy as jnp
from jax import lax
from jax.experimental import pallas as pl
from jax.experimental.pallas import tpu as pltpu
from jax.sharding import Mesh
from jax.sharding import PartitionSpec as P

MODEL_DIM = 1024
QUERY_HEADS = 16
KEY_VALUE_HEADS = 8
HEAD_DIM = 128
SEQUENCE_TOKENS = 2048
PIECE = 256
NPIECE = 4


EPS = 1e-06
THETA = 1000000.0
NEG = -1e30


def rms_norm(incoming_values, gain_vector):
    return (
        incoming_values
        * lax.rsqrt(jnp.mean(incoming_values * incoming_values, axis=-1, keepdims=True) + EPS)
        * gain_vector
    )


def rope_tables(positions):
    half_steps = jnp.arange(HEAD_DIM // 2, dtype=jnp.float32)
    inverse = THETA ** (-2.0 * half_steps / HEAD_DIM)
    angles = positions.astype(jnp.float32)[:, None] * inverse[None, :]
    angles = jnp.concatenate([angles, angles], axis=-1)
    return (jnp.cos(angles), jnp.sin(angles))


def rotate(incoming_values, cosine_table, sine_table):
    half_dim = HEAD_DIM // 2
    turned = jnp.concatenate(
        [-incoming_values[..., half_dim:], incoming_values[..., :half_dim]], axis=-1
    )
    return incoming_values * cosine_table[:, None, :] + turned * sine_table[:, None, :]


def per_head_route(unrotated_projection, gain_vector, cosine_table, sine_table, head_count):
    shaped = unrotated_projection.reshape(unrotated_projection.shape[:-1] + (head_count, HEAD_DIM))
    return rotate(rms_norm(shaped, gain_vector), cosine_table, sine_table).reshape(
        unrotated_projection.shape
    )


def piece_ids(positions, piece_starts):
    inside = (positions[:, None] >= piece_starts[None, :]) & (
        positions[:, None] < piece_starts[None, :] + PIECE
    )
    number = jnp.arange(1, NPIECE + 1, dtype=jnp.int32)
    return jnp.sum(jnp.where(inside, number[None, :], 0), axis=1) - 1


def visible(query_pos, query_id, key_pos, key_id):
    causal = key_pos[None, :] <= query_pos[:, None]
    same_piece = (query_id[:, None] == key_id[None, :]) & (query_id[:, None] >= 0)
    return causal | same_piece


def swiglu(gate_proj, up_proj):
    return jax.nn.silu(gate_proj) * up_proj


def block_extent(kv_count, per_head):
    target = max(1, 512 // per_head)
    chosen = 1
    for candidate in range(1, kv_count + 1):
        if kv_count % candidate == 0 and candidate <= target:
            chosen = candidate
    return chosen


def attend_forward(incoming_query, incoming_keys, incoming_values, allowed, head_group_block):
    sequence_rows = incoming_query.shape[0]
    query_group_factor = QUERY_HEADS // KEY_VALUE_HEADS
    scaling = 1.0 / math.sqrt(HEAD_DIM)
    query_per_head = incoming_query.reshape(
        sequence_rows, KEY_VALUE_HEADS, query_group_factor, HEAD_DIM
    )
    key_per_head = incoming_keys.reshape(incoming_keys.shape[0], KEY_VALUE_HEADS, HEAD_DIM)
    value_per_head = incoming_values.reshape(incoming_values.shape[0], KEY_VALUE_HEADS, HEAD_DIM)
    mixed_parts = []
    total_parts = []
    for head_offset in range(0, KEY_VALUE_HEADS, head_group_block):
        q_part = query_per_head[:, head_offset : head_offset + head_group_block]
        k_part = key_per_head[:, head_offset : head_offset + head_group_block]
        v_part = value_per_head[:, head_offset : head_offset + head_group_block]
        scores = (
            jnp.einsum("tagd,kad->agtk", q_part, k_part, preferred_element_type=jnp.float32)
            * scaling
        )
        scores = jnp.where(allowed[None, None], scores, NEG)
        row_max = jnp.max(scores, axis=-1, keepdims=True)
        exp_scores = jnp.exp(scores - row_max)
        summed = jnp.sum(exp_scores, axis=-1, keepdims=True)
        prob_low = (exp_scores / summed).astype(jnp.bfloat16)
        mixed_parts.append(
            jnp.einsum("agtk,kad->tagd", prob_low, v_part, preferred_element_type=jnp.float32)
        )
        total_parts.append(row_max + jnp.log(summed))
    mixed_out = jnp.concatenate(mixed_parts, axis=1).reshape(sequence_rows, QUERY_HEADS * HEAD_DIM)
    return (mixed_out, jnp.concatenate(total_parts, axis=0))


def attend_backward(
    incoming_query,
    incoming_keys,
    incoming_values,
    allowed,
    log_total,
    mixed_gradient,
    head_group_block,
):
    sequence_rows = incoming_query.shape[0]
    key_row_matrix = incoming_keys.shape[0]
    query_group_factor = QUERY_HEADS // KEY_VALUE_HEADS
    scaling = 1.0 / math.sqrt(HEAD_DIM)
    query_per_head = incoming_query.reshape(
        sequence_rows, KEY_VALUE_HEADS, query_group_factor, HEAD_DIM
    )
    gradient_per_head = mixed_gradient.reshape(
        sequence_rows, KEY_VALUE_HEADS, query_group_factor, HEAD_DIM
    )
    key_per_head = incoming_keys.reshape(key_row_matrix, KEY_VALUE_HEADS, HEAD_DIM)
    value_per_head = incoming_values.reshape(key_row_matrix, KEY_VALUE_HEADS, HEAD_DIM)
    dq_parts = []
    key_gradient_pieces = []
    value_gradient_pieces = []
    for head_offset in range(0, KEY_VALUE_HEADS, head_group_block):
        q_part = query_per_head[:, head_offset : head_offset + head_group_block]
        g_part = gradient_per_head[:, head_offset : head_offset + head_group_block]
        k_part = key_per_head[:, head_offset : head_offset + head_group_block]
        v_part = value_per_head[:, head_offset : head_offset + head_group_block]
        scores = (
            jnp.einsum("tagd,kad->agtk", q_part, k_part, preferred_element_type=jnp.float32)
            * scaling
        )
        scores = jnp.where(allowed[None, None], scores, NEG)
        prob_all = jnp.exp(scores - log_total[head_offset : head_offset + head_group_block])
        prob_low = prob_all.astype(jnp.bfloat16)
        d_probs = jnp.einsum("tagd,kad->agtk", g_part, v_part, preferred_element_type=jnp.float32)
        row_dot = jnp.sum(prob_all * d_probs, axis=-1, keepdims=True)
        d_scores = (prob_all * (d_probs - row_dot)).astype(jnp.bfloat16)
        dq_parts.append(
            jnp.einsum("agtk,kad->tagd", d_scores, k_part, preferred_element_type=jnp.float32)
            * scaling
        )
        key_gradient_pieces.append(
            jnp.einsum("agtk,tagd->kad", d_scores, q_part, preferred_element_type=jnp.float32)
            * scaling
        )
        value_gradient_pieces.append(
            jnp.einsum("agtk,tagd->kad", prob_low, g_part, preferred_element_type=jnp.float32)
        )
    d_query = jnp.concatenate(dq_parts, axis=1).reshape(sequence_rows, QUERY_HEADS * HEAD_DIM)
    key_gradient = jnp.concatenate(key_gradient_pieces, axis=1).reshape(
        key_row_matrix, KEY_VALUE_HEADS * HEAD_DIM
    )
    value_gradient = jnp.concatenate(value_gradient_pieces, axis=1).reshape(
        key_row_matrix, KEY_VALUE_HEADS * HEAD_DIM
    )
    return (d_query, key_gradient, value_gradient)


def generic_device(
    tokens, cotangent, starts, w_query, key_matrix, value_matrix, w_out, w_gate, w_up, w_down, gains
):
    sequence_count, sequence_rows, model_width = tokens.shape
    number_of_rows = sequence_count * sequence_rows
    head_group_block = block_extent(KEY_VALUE_HEADS, QUERY_HEADS // KEY_VALUE_HEADS * sequence_rows)
    attn_set = (
        lax.all_gather(w_query, ("dp", "ctx"), axis=0, tiled=True),
        lax.all_gather(key_matrix, ("dp", "ctx"), axis=0, tiled=True),
        lax.all_gather(value_matrix, ("dp", "ctx"), axis=0, tiled=True),
        lax.all_gather(w_out, ("dp", "ctx"), axis=0, tiled=True),
        lax.all_gather(gains, ("dp", "ctx"), axis=0, tiled=True),
    )
    mlp_set = (
        lax.all_gather(w_gate, ("dp", "ctx"), axis=0, tiled=True),
        lax.all_gather(w_up, ("dp", "ctx"), axis=0, tiled=True),
        lax.all_gather(w_down, ("dp", "ctx"), axis=0, tiled=True),
    )
    gain_all = attn_set[4].astype(jnp.float32)
    g_attn = gain_all[:MODEL_DIM]
    g_mlp = gain_all[MODEL_DIM : 2 * MODEL_DIM]
    g_query = gain_all[2 * MODEL_DIM : 2 * MODEL_DIM + HEAD_DIM]
    key_grad_total = gain_all[2 * MODEL_DIM + HEAD_DIM :]
    positions = lax.axis_index("ctx") * sequence_rows + jnp.arange(sequence_rows, dtype=jnp.int32)
    key_places = jnp.arange(SEQUENCE_TOKENS, dtype=jnp.int32)
    cosine_table, sine_table = rope_tables(positions)

    def query_map(unrotated_projection, gain_vector):
        return per_head_route(
            unrotated_projection, gain_vector, cosine_table, sine_table, QUERY_HEADS
        )

    def key_map(unrotated_projection, gain_vector):
        return per_head_route(
            unrotated_projection, gain_vector, cosine_table, sine_table, KEY_VALUE_HEADS
        )

    flat_in = tokens.reshape(number_of_rows, model_width).astype(jnp.float32)
    normed = rms_norm(flat_in, g_attn).astype(jnp.bfloat16)
    query_raw = jnp.dot(normed, attn_set[0], preferred_element_type=jnp.float32).reshape(
        sequence_count, sequence_rows, QUERY_HEADS * HEAD_DIM
    )
    key_unrotated = jnp.dot(normed, attn_set[1], preferred_element_type=jnp.float32).reshape(
        sequence_count, sequence_rows, KEY_VALUE_HEADS * HEAD_DIM
    )
    value_reduced = jnp.dot(normed, attn_set[2], preferred_element_type=jnp.float32).astype(
        jnp.bfloat16
    )
    value_reduced = value_reduced.reshape(sequence_count, sequence_rows, KEY_VALUE_HEADS * HEAD_DIM)
    query_reduced = query_map(query_raw, g_query).astype(jnp.bfloat16)
    key_reduced = key_map(key_unrotated, key_grad_total).astype(jnp.bfloat16)
    mask_list = []
    mixed_list = []
    total_list = []
    for seq_index in range(sequence_count):
        query_ids = piece_ids(positions, starts[seq_index])
        key_ids = piece_ids(key_places, starts[seq_index])
        allowed = visible(positions, query_ids, key_places, key_ids)
        key_full, value_full = (
            lax.all_gather(key_reduced[seq_index], "ctx", axis=0, tiled=True),
            lax.all_gather(value_reduced[seq_index], "ctx", axis=0, tiled=True),
        )
        mixed_out, log_total = attend_forward(
            query_reduced[seq_index], key_full, value_full, allowed, head_group_block
        )
        mask_list.append(allowed)
        mixed_list.append(mixed_out)
        total_list.append(log_total)
    attn_low = (
        jnp.stack(mixed_list).reshape(number_of_rows, QUERY_HEADS * HEAD_DIM).astype(jnp.bfloat16)
    )
    residual = flat_in + jnp.dot(attn_low, attn_set[3], preferred_element_type=jnp.float32)
    mlp_in = rms_norm(residual, g_mlp).astype(jnp.bfloat16)
    gate_proj = jnp.dot(mlp_in, mlp_set[0], preferred_element_type=jnp.float32)
    up_proj = jnp.dot(mlp_in, mlp_set[1], preferred_element_type=jnp.float32)
    hidden = swiglu(gate_proj, up_proj).astype(jnp.bfloat16)
    result = residual + jnp.dot(hidden, mlp_set[2], preferred_element_type=jnp.float32)
    output = result.astype(jnp.bfloat16).reshape(tokens.shape)
    mlp_back = (
        lax.all_gather(w_gate, ("dp", "ctx"), axis=0, tiled=True),
        lax.all_gather(w_up, ("dp", "ctx"), axis=0, tiled=True),
        lax.all_gather(w_down, ("dp", "ctx"), axis=0, tiled=True),
    )
    grad_flat = cotangent.reshape(number_of_rows, model_width)
    grad_down = jnp.dot(hidden.T, grad_flat, preferred_element_type=jnp.float32)
    d_hidden = jnp.dot(grad_flat, mlp_back[2].T, preferred_element_type=jnp.float32)
    swiglu_pull = jax.vjp(swiglu, gate_proj, up_proj)[1]
    d_gate, d_up = swiglu_pull(d_hidden)
    d_gate = d_gate.astype(jnp.bfloat16)
    d_up = d_up.astype(jnp.bfloat16)
    grad_gate = jnp.dot(mlp_in.T, d_gate, preferred_element_type=jnp.float32)
    grad_up = jnp.dot(mlp_in.T, d_up, preferred_element_type=jnp.float32)
    mlp_grads = (
        lax.psum_scatter(grad_gate, ("dp", "ctx"), scatter_dimension=0, tiled=True),
        lax.psum_scatter(grad_up, ("dp", "ctx"), scatter_dimension=0, tiled=True),
        lax.psum_scatter(grad_down, ("dp", "ctx"), scatter_dimension=0, tiled=True),
    )
    d_mlp_in = jnp.dot(d_gate, mlp_back[0].T, preferred_element_type=jnp.float32)
    d_mlp_in = d_mlp_in + jnp.dot(d_up, mlp_back[1].T, preferred_element_type=jnp.float32)
    mlp_norm_pull = jax.vjp(rms_norm, residual, g_mlp)[1]
    d_resid_norm, d_g_mlp = mlp_norm_pull(d_mlp_in)
    d_resid = grad_flat.astype(jnp.float32) + d_resid_norm
    attn_back = (
        lax.all_gather(w_query, ("dp", "ctx"), axis=0, tiled=True),
        lax.all_gather(key_matrix, ("dp", "ctx"), axis=0, tiled=True),
        lax.all_gather(value_matrix, ("dp", "ctx"), axis=0, tiled=True),
        lax.all_gather(w_out, ("dp", "ctx"), axis=0, tiled=True),
        lax.all_gather(gains, ("dp", "ctx"), axis=0, tiled=True),
    )
    d_branch = d_resid.astype(jnp.bfloat16)
    grad_out = jnp.dot(attn_low.T, d_branch, preferred_element_type=jnp.float32)
    d_attn = jnp.dot(d_branch, attn_back[3].T, preferred_element_type=jnp.float32).astype(
        jnp.bfloat16
    )
    d_attn = d_attn.reshape(sequence_count, sequence_rows, QUERY_HEADS * HEAD_DIM)
    dq_list = []
    dk_list = []
    value_gradient_list = []
    for seq_index in range(sequence_count):
        key_full, value_full = (
            lax.all_gather(key_reduced[seq_index], "ctx", axis=0, tiled=True),
            lax.all_gather(value_reduced[seq_index], "ctx", axis=0, tiled=True),
        )
        d_query_seq, d_key_full, d_value_full = attend_backward(
            query_reduced[seq_index],
            key_full,
            value_full,
            mask_list[seq_index],
            total_list[seq_index],
            d_attn[seq_index],
            head_group_block,
        )
        d_key_seq, d_value_seq = (
            lax.psum_scatter(
                d_key_full.astype(jnp.bfloat16), "ctx", scatter_dimension=0, tiled=True
            ).astype(jnp.float32),
            lax.psum_scatter(
                d_value_full.astype(jnp.bfloat16), "ctx", scatter_dimension=0, tiled=True
            ).astype(jnp.float32),
        )
        dq_list.append(d_query_seq)
        dk_list.append(d_key_seq)
        value_gradient_list.append(d_value_seq)
    d_query = jnp.stack(dq_list)
    key_gradient = jnp.stack(dk_list)
    value_gradient_reduced = (
        jnp.stack(value_gradient_list)
        .reshape(number_of_rows, KEY_VALUE_HEADS * HEAD_DIM)
        .astype(jnp.bfloat16)
    )
    query_pull = jax.vjp(query_map, query_raw, g_query)[1]
    d_query_raw, d_g_query = query_pull(d_query)
    key_pull = jax.vjp(key_map, key_unrotated, key_grad_total)[1]
    key_gradient_unrotated, d_g_key = key_pull(key_gradient)
    d_query_low = d_query_raw.reshape(number_of_rows, QUERY_HEADS * HEAD_DIM).astype(jnp.bfloat16)
    key_gradient_reduced = key_gradient_unrotated.reshape(
        number_of_rows, KEY_VALUE_HEADS * HEAD_DIM
    ).astype(jnp.bfloat16)
    grad_query = jnp.dot(normed.T, d_query_low, preferred_element_type=jnp.float32)
    grad_key = jnp.dot(normed.T, key_gradient_reduced, preferred_element_type=jnp.float32)
    grad_value = jnp.dot(normed.T, value_gradient_reduced, preferred_element_type=jnp.float32)
    d_normed = jnp.dot(d_query_low, attn_back[0].T, preferred_element_type=jnp.float32)
    d_normed = d_normed + jnp.dot(
        key_gradient_reduced, attn_back[1].T, preferred_element_type=jnp.float32
    )
    d_normed = d_normed + jnp.dot(
        value_gradient_reduced, attn_back[2].T, preferred_element_type=jnp.float32
    )
    input_pull = jax.vjp(rms_norm, flat_in, g_attn)[1]
    d_input_norm, d_g_attn = input_pull(d_normed)
    grad_tokens = (d_resid + d_input_norm).reshape(tokens.shape)
    grad_gains = jnp.concatenate([d_g_attn, d_g_mlp, d_g_query, d_g_key])
    attn_grads = (
        lax.psum_scatter(grad_query, ("dp", "ctx"), scatter_dimension=0, tiled=True),
        lax.psum_scatter(grad_key, ("dp", "ctx"), scatter_dimension=0, tiled=True),
        lax.psum_scatter(grad_value, ("dp", "ctx"), scatter_dimension=0, tiled=True),
        lax.psum_scatter(grad_out, ("dp", "ctx"), scatter_dimension=0, tiled=True),
        lax.psum_scatter(grad_gains, ("dp", "ctx"), scatter_dimension=0, tiled=True),
    )
    return (
        output,
        grad_tokens,
        attn_grads[0],
        attn_grads[1],
        attn_grads[2],
        attn_grads[3],
        mlp_grads[0],
        mlp_grads[1],
        mlp_grads[2],
        attn_grads[4],
    )


def generic_solution(mesh):
    return jax.shard_map(
        generic_device,
        mesh=mesh,
        in_specs=(
            P("dp", "ctx", None),
            P("dp", "ctx", None),
            P("dp", None),
            P(("dp", "ctx"), None),
            P(("dp", "ctx"), None),
            P(("dp", "ctx"), None),
            P(("dp", "ctx"), None),
            P(("dp", "ctx"), None),
            P(("dp", "ctx"), None),
            P(("dp", "ctx"), None),
            P(("dp", "ctx")),
        ),
        out_specs=(
            P("dp", "ctx", None),
            P("dp", "ctx", None),
            P(("dp", "ctx"), None),
            P(("dp", "ctx"), None),
            P(("dp", "ctx"), None),
            P(("dp", "ctx"), None),
            P(("dp", "ctx"), None),
            P(("dp", "ctx"), None),
            P(("dp", "ctx"), None),
            P(("dp", "ctx")),
        ),
        check_vma=False,
    )


AXES = ("y", "x", "p", "l", "c")
FF = 3072
HALF_FF = FF // 2
ROWS = 256
SEQ_ROWS = SEQUENCE_TOKENS
OWN = SEQ_ROWS // 4
BLK = 512
NBLK = SEQ_ROWS // BLK
QH = 4
KH = 2
MESH = pl.DeviceIdType.MESH
SCALE = 1.0 / math.sqrt(HEAD_DIM)
LOG2E = 1.4426950408889634
NT = (((1,), (1,)), ((), ()))
TN = (((0,), (0,)), ((), ()))


def dot(a, b, dims=None):
    if dims is None:
        dims = (((1,), (0,)), ((), ()))
    return lax.dot_general(a, b, dims, preferred_element_type=jnp.float32)


def greet(peers):
    barrier = pltpu.get_barrier_semaphore()
    for peer in peers:
        pl.semaphore_signal(barrier, inc=1, device_id=peer, device_id_type=MESH)
    pl.semaphore_wait(barrier, len(peers))


class Net:
    def __init__(self, send_sem, recv_sem):
        self.send_sem = send_sem
        self.recv_sem = recv_sem
        self.count = 0
        self.started = []

    def send(self, peer, *pairs):
        copies = []
        for src, dst in pairs:
            copy = pltpu.make_async_remote_copy(
                src_ref=src,
                dst_ref=dst,
                send_sem=self.send_sem.at[self.count],
                recv_sem=self.recv_sem.at[self.count],
                device_id=peer,
                device_id_type=MESH,
            )
            self.count += 1
            copy.start()
            copies.append(copy)
        self.started += copies
        return copies

    def finish(self):
        for copy in self.started:
            copy.wait_send()


def arrived(copies):
    for copy in copies:
        copy.wait_recv()


def place():
    return tuple(lax.axis_index(name) for name in AXES)


def front_kernel(tok, wa, gn, xs, wf, gf, send_sem, recv_sem, local_sem):
    y, x, p, l, c = place()
    net = Net(send_sem, recv_sem)
    peer_c, peer_l, peer_p = {"c": 1 - c}, {"l": 1 - l}, {"p": 1 - p}
    peer_d = {"l": 1 - l, "c": 1 - c}
    peer_x, peer_y = {"x": 1 - x}, {"y": 1 - y}
    block = 4 * p + 2 * l + c
    group = (y * 2 + x) * 8
    me = group + block
    greet((peer_c, peer_l, peer_d, peer_p, peer_x, peer_y))
    first = []
    for peer, quarter in ((peer_l, 2 * (1 - l) + c), (peer_d, 2 * (1 - l) + 1 - c), (peer_c, 2 * l + 1 - c)):
        first += net.send(peer, (wa.at[quarter], wf.at[me]), (gn, gf.at[me]))
    near = net.send(peer_l, (tok.at[p], xs.at[block]))
    far = net.send(peer_p, (tok.at[1 - p], xs.at[block]))
    near_c = net.send(peer_c, (tok.at[p], xs.at[block]))
    own = (
        pltpu.make_async_copy(wa.at[2 * l + c], wf.at[me], local_sem.at[0]),
        pltpu.make_async_copy(gn, gf.at[me], local_sem.at[1]),
        pltpu.make_async_copy(tok.at[p], xs.at[block], local_sem.at[2]),
    )
    for copy in own:
        copy.start()

    def span(base, count):
        ref = pl.ds(base, count)
        return (wf.at[ref], wf.at[ref]), (gf.at[ref], gf.at[ref])

    for copy in own:
        copy.wait()
    arrived(first)
    mine, other = group + 4 * p, group + 4 * (1 - p)
    across = net.send(peer_p, *span(mine, 4))
    own_x = net.send(peer_x, *span(mine, 4))
    arrived(near)
    relay = net.send(peer_c, (xs.at[block ^ 2], xs.at[block ^ 2]))
    arrived(own_x)
    own_y = net.send(peer_y, *span(mine, 4), *span((y * 2 + 1 - x) * 8 + 4 * p, 4))
    arrived(across)
    other_y = net.send(peer_y, *span(other, 4))
    arrived(far)
    far_l = net.send(peer_l, (xs.at[block ^ 4], xs.at[block ^ 4]))
    relay += net.send(peer_c, (xs.at[block ^ 4], xs.at[block ^ 4]))
    arrived(other_y)
    other_x = net.send(peer_x, *span(other, 4), *span(((1 - y) * 2 + x) * 8 + 4 * (1 - p), 4))
    arrived(far_l)
    relay += net.send(peer_c, (xs.at[block ^ 6], xs.at[block ^ 6]))
    arrived(near_c)
    arrived(relay)
    arrived(own_y)
    arrived(other_x)
    net.finish()


def front(tok, wa, gn):
    any_spec = pl.BlockSpec(memory_space=pl.ANY)
    copies = 30
    return pl.pallas_call(
        front_kernel,
        out_shape=(
            jax.ShapeDtypeStruct((8, ROWS, MODEL_DIM), jnp.bfloat16),
            jax.ShapeDtypeStruct((32, 48, 1024), jnp.bfloat16),
            jax.ShapeDtypeStruct((32, 8, 128), jnp.float32),
        ),
        in_specs=[any_spec] * 3,
        out_specs=[any_spec] * 3,
        scratch_shapes=[
            pltpu.SemaphoreType.DMA((copies,)),
            pltpu.SemaphoreType.DMA((copies,)),
            pltpu.SemaphoreType.DMA((3,)),
        ],
        compiler_params=pltpu.CompilerParams(collective_id=0, has_side_effects=True),
        name="front_gather",
    )(tok, wa, gn)


def back_kernel(
    part, gpart, out, gout, work, gwork, ry, rx, ox, oy, rp, rq, gry, grx, gox, goy, grp, grq, send_sem, recv_sem
):
    y, x, p, l, c = place()
    net = Net(send_sem, recv_sem)
    peer_c, peer_l, peer_p = {"c": 1 - c}, {"l": 1 - l}, {"p": 1 - p}
    peer_d = {"l": 1 - l, "c": 1 - c}
    peer_x, peer_y = {"x": 1 - x}, {"y": 1 - y}
    greet((peer_c, peer_l, peer_d, peer_p, peer_x, peer_y))

    def slots(yy, xx, pp):
        return pl.ds(((yy * 2 + xx) * 2 + pp) * 4, 4)

    def pairs(from_refs, spans, to_refs):
        found = []
        for index, span in enumerate(spans):
            for src, dst in zip(from_refs, to_refs):
                found.append((src.at[span], dst.at[pl.ds(4 * index, 4)]))
        return found

    source = (part, gpart)
    own_y = net.send(peer_y, *pairs(source, (slots(1 - y, 0, p), slots(1 - y, 1, p)), (ry, gry)))
    other_x = net.send(peer_x, *pairs(source, (slots(0, 1 - x, 1 - p), slots(1, 1 - x, 1 - p)), (ox, gox)))

    def add(targets, span, left, right, place_at):
        for target, a, b in zip(targets, left, right):
            total = a.astype(jnp.float32) + b[pl.ds(4 * place_at, 4)].astype(jnp.float32)
            target[span] = total.astype(target.dtype)

    working = (work, gwork)
    arrived(own_y)
    for xx in (0, 1):
        span = slots(y, xx, p)
        add(working, span, (part[span], gpart[span]), (ry, gry), xx)
    own_x = net.send(peer_x, *pairs(working, (slots(y, 1 - x, p),), (rx, grx)))
    arrived(other_x)
    for yy in (0, 1):
        span = slots(yy, x, 1 - p)
        add(working, span, (part[span], gpart[span]), (ox, gox), yy)
    other_y = net.send(peer_y, *pairs(working, (slots(1 - y, x, 1 - p),), (oy, goy)))
    arrived(other_y)
    span = slots(y, x, 1 - p)
    add(working, span, (work[span], gwork[span]), (oy, goy), 0)
    across = net.send(peer_p, *pairs(working, (span,), (rp, grp)))
    arrived(own_x)
    span = slots(y, x, p)
    add(working, span, (work[span], gwork[span]), (rx, grx), 0)
    arrived(across)
    add(working, span, (work[span], gwork[span]), (rp, grp), 0)
    base = ((y * 2 + x) * 2 + p) * 4
    me = 2 * l + c
    last = []
    for peer, quarter in ((peer_l, 2 * (1 - l) + c), (peer_d, 2 * (1 - l) + 1 - c), (peer_c, 2 * l + 1 - c)):
        last += net.send(peer, (work.at[base + quarter], rq.at[me]), (gwork.at[base + quarter], grq.at[me]))
    rq[me] = work[base + me]
    grq[me] = gwork[base + me]
    arrived(last)
    out[...] = rq[...].astype(jnp.float32)
    gout[...] = grq[0] + grq[1] + grq[2] + grq[3]
    net.finish()


def back(part, gpart):
    def both(*lead):
        return pltpu.VMEM(lead + (48, 1024), jnp.bfloat16), pltpu.VMEM(lead + (8, 128), jnp.float32)

    sizes = (8, 4, 8, 4, 4, 4)
    grads = [both(size)[0] for size in sizes]
    gains = [both(size)[1] for size in sizes]
    vmem = pl.BlockSpec(memory_space=pltpu.VMEM)
    copies = 24
    return pl.pallas_call(
        back_kernel,
        out_shape=(
            jax.ShapeDtypeStruct((4, 48, 1024), jnp.float32),
            jax.ShapeDtypeStruct((8, 128), jnp.float32),
        ),
        in_specs=[vmem] * 2,
        out_specs=[vmem] * 2,
        scratch_shapes=[*both(32)] + grads + gains + [pltpu.SemaphoreType.DMA((copies,))] * 2,
        compiler_params=pltpu.CompilerParams(
            collective_id=1, has_side_effects=True, vmem_limit_bytes=48 * 1024 * 1024
        ),
        name="back_reduce",
    )(part, gpart)


def turn(value):
    return pltpu.roll(value, HEAD_DIM // 2, 1)


def qkv_kernel(x_ref, w_ref, ga_ref, gq_ref, gk_ref, cos_ref, sin_ref, n_ref, q_ref, k_ref, v_ref, qr_ref, kr_ref):
    x = x_ref[...].astype(jnp.float32)
    r = lax.rsqrt(jnp.mean(x * x, axis=-1, keepdims=True) + EPS)
    normed = (x * r * ga_ref[...]).astype(jnp.bfloat16)
    n_ref[...] = normed
    full = dot(normed, w_ref[...])
    cosine, sine = cos_ref[...], sin_ref[...]
    for h in range(QH + KH):
        u = full[:, h * HEAD_DIM : (h + 1) * HEAD_DIM]
        raw_ref, out_ref, g_ref, at = (qr_ref, q_ref, gq_ref, h) if h < QH else (kr_ref, k_ref, gk_ref, h - QH)
        raw_ref[at] = u
        n = u * lax.rsqrt(jnp.mean(u * u, axis=-1, keepdims=True) + EPS) * g_ref[...]
        out_ref[at] = (n * cosine + turn(n) * sine).astype(jnp.bfloat16)
    for h in range(KH):
        at = (QH + KH + h) * HEAD_DIM
        v_ref[h] = full[:, at : at + HEAD_DIM].astype(jnp.bfloat16)


def qkv(x, w, ga, gq, gk, cosine, sine):
    rows = 256

    def row(width):
        return pl.BlockSpec((rows, width), lambda i: (i, 0))

    def whole(a):
        return pl.BlockSpec(a.shape, lambda i: (0, 0))

    def heads(n):
        return pl.BlockSpec((n, rows, HEAD_DIM), lambda i: (0, i, 0))

    def shape(n, dtype):
        return jax.ShapeDtypeStruct((n, SEQ_ROWS, HEAD_DIM), dtype)

    return pl.pallas_call(
        qkv_kernel,
        grid=(SEQ_ROWS // rows,),
        out_shape=(
            jax.ShapeDtypeStruct((SEQ_ROWS, MODEL_DIM), jnp.bfloat16),
            shape(QH, jnp.bfloat16),
            shape(KH, jnp.bfloat16),
            shape(KH, jnp.bfloat16),
            shape(QH, jnp.float32),
            shape(KH, jnp.float32),
        ),
        in_specs=[row(MODEL_DIM), whole(w), whole(ga), whole(gq), whole(gk), row(HEAD_DIM), row(HEAD_DIM)],
        out_specs=[row(MODEL_DIM), heads(QH), heads(KH), heads(KH), heads(QH), heads(KH)],
        compiler_params=pltpu.CompilerParams(vmem_limit_bytes=48 * 1024 * 1024),
        cost_estimate=pl.CostEstimate(flops=2 * SEQ_ROWS * 1024 * 1024, bytes_accessed=24 << 20, transcendentals=0),
        name="project",
    )(x, w, ga, gq, gk, cosine, sine)


def block_mask(key_dim, flags, index):
    shape = (BLK, BLK)
    key = lax.broadcasted_iota(jnp.int32, shape, key_dim)
    query = lax.broadcasted_iota(jnp.int32, shape, 1 - key_dim)
    upper = query // PIECE
    piece = jnp.where(upper == 0, flags[2 * index], flags[2 * index + 1])
    return (key <= query) | ((key // PIECE == upper) & (piece > 0))


def attend_kernel(flags, q_ref, k_ref, v_ref, o_ref, lse_ref):
    i = pl.program_id(1)
    ones = jnp.ones((BLK, HEAD_DIM), jnp.bfloat16)
    mask = block_mask(1, flags, i)

    def values(j):
        return jnp.concatenate([v_ref[0, pl.ds(j * BLK, BLK), :], ones], axis=1)

    for h in range(2):
        q = q_ref[h]

        def scores(j):
            return dot(q, k_ref[0, pl.ds(j * BLK, BLK), :], NT) * (SCALE * LOG2E)

        def step(j, acc):
            return acc + dot(jnp.exp2(scores(j)).astype(jnp.bfloat16), values(j))

        acc = lax.fori_loop(0, i, step, jnp.zeros((BLK, 2 * HEAD_DIM), jnp.float32))
        probs = jnp.where(mask, jnp.exp2(scores(i)), 0.0).astype(jnp.bfloat16)
        acc = acc + dot(probs, values(i))
        total = acc[:, HEAD_DIM:]
        o_ref[:, h * HEAD_DIM : (h + 1) * HEAD_DIM] = (acc[:, :HEAD_DIM] / total).astype(jnp.bfloat16)
        lse_ref[h] = jnp.log2(total).T[0:8, :]


def attend(flags, q, k, v):
    whole = pl.BlockSpec((1, SEQ_ROWS, HEAD_DIM), lambda g, i, f: (g, 0, 0))
    return pl.pallas_call(
        attend_kernel,
        out_shape=(
            jax.ShapeDtypeStruct((SEQ_ROWS, QH * HEAD_DIM), jnp.bfloat16),
            jax.ShapeDtypeStruct((QH, 8, SEQ_ROWS), jnp.float32),
        ),
        grid_spec=pltpu.PrefetchScalarGridSpec(
            num_scalar_prefetch=1,
            grid=(KH, NBLK),
            in_specs=[pl.BlockSpec((2, BLK, HEAD_DIM), lambda g, i, f: (g, i, 0)), whole, whole],
            out_specs=[
                pl.BlockSpec((BLK, 2 * HEAD_DIM), lambda g, i, f: (i, g)),
                pl.BlockSpec((2, 8, BLK), lambda g, i, f: (g, 0, i)),
            ],
        ),
        compiler_params=pltpu.CompilerParams(vmem_limit_bytes=48 * 1024 * 1024),
        cost_estimate=pl.CostEstimate(
            flops=4 * QH * SEQ_ROWS * SEQ_ROWS * HEAD_DIM, bytes_accessed=8 << 20, transcendentals=QH * SEQ_ROWS * SEQ_ROWS
        ),
        name="attend",
    )(flags, q, k, v)


def attend_back_kernel(flags, q_ref, k_ref, v_ref, o_ref, do_ref, lse_ref, dq_ref, dk_ref, dv_ref, delta, dk_acc, dv_acc):
    j = pl.program_id(1)

    @pl.when(j == 0)
    def _():
        dq_ref[...] = jnp.zeros_like(dq_ref)
        for h in range(2):
            cols = slice(h * HEAD_DIM, (h + 1) * HEAD_DIM)
            for i in range(NBLK):
                rows = slice(i * BLK, (i + 1) * BLK)
                prod = do_ref[rows, cols].astype(jnp.float32) * o_ref[rows, cols].astype(jnp.float32)
                delta[h, :, rows] = jnp.broadcast_to(jnp.sum(prod.T, axis=0, keepdims=True), (8, BLK))

    k = k_ref[0]
    v = v_ref[0]
    dk_acc[...] = jnp.zeros_like(dk_acc)
    dv_acc[...] = jnp.zeros_like(dv_acc)
    for h in range(2):

        def step(i, mask=None):
            rows = pl.ds(pl.multiple_of(i * BLK, BLK), BLK)
            q = q_ref[h, rows, :]
            do = do_ref[rows, h * HEAD_DIM : (h + 1) * HEAD_DIM]
            probs = jnp.exp2(dot(k, q, NT) * (SCALE * LOG2E) - lse_ref[h, 0:1, rows])
            if mask is not None:
                probs = jnp.where(mask, probs, 0.0)
            d_scores = (probs * (dot(v, do, NT) - delta[h, 0:1, rows])).astype(jnp.bfloat16)
            dv_acc[...] += dot(probs.astype(jnp.bfloat16), do)
            dk_acc[...] += dot(d_scores, q)
            dq_ref[h, rows, :] += dot(d_scores, k, TN)

        def loop(i, carry):
            step(i)
            return carry

        step(j, block_mask(0, flags, j))
        lax.fori_loop(j + 1, NBLK, loop, 0)
    dk_ref[0] = dk_acc[...]
    dv_ref[0] = dv_acc[...].astype(jnp.bfloat16)


def attend_back(flags, q, k, v, o, do, lse):
    both = pl.BlockSpec((2, SEQ_ROWS, HEAD_DIM), lambda g, j, f: (g, 0, 0))
    wide = pl.BlockSpec((SEQ_ROWS, 2 * HEAD_DIM), lambda g, j, f: (0, g))
    part = pl.BlockSpec((1, BLK, HEAD_DIM), lambda g, j, f: (g, j, 0))
    return pl.pallas_call(
        attend_back_kernel,
        out_shape=(
            jax.ShapeDtypeStruct((QH, SEQ_ROWS, HEAD_DIM), jnp.float32),
            jax.ShapeDtypeStruct((KH, SEQ_ROWS, HEAD_DIM), jnp.float32),
            jax.ShapeDtypeStruct((KH, SEQ_ROWS, HEAD_DIM), jnp.bfloat16),
        ),
        grid_spec=pltpu.PrefetchScalarGridSpec(
            num_scalar_prefetch=1,
            grid=(KH, NBLK),
            in_specs=[both, part, part, wide, wide, pl.BlockSpec((2, 8, SEQ_ROWS), lambda g, j, f: (g, 0, 0))],
            out_specs=[both, part, part],
            scratch_shapes=[
                pltpu.VMEM((2, 8, SEQ_ROWS), jnp.float32),
                pltpu.VMEM((BLK, HEAD_DIM), jnp.float32),
                pltpu.VMEM((BLK, HEAD_DIM), jnp.float32),
            ],
        ),
        compiler_params=pltpu.CompilerParams(vmem_limit_bytes=48 * 1024 * 1024),
        cost_estimate=pl.CostEstimate(
            flops=10 * QH * SEQ_ROWS * SEQ_ROWS * HEAD_DIM, bytes_accessed=16 << 20, transcendentals=QH * SEQ_ROWS * SEQ_ROWS
        ),
        name="attend_back",
    )(flags, q, k, v, o, do, lse)


def unrope_kernel(dq_ref, dk_ref, dv_ref, qr_ref, kr_ref, gq_ref, gk_ref, cos_ref, sin_ref, d_ref, dg_ref):
    @pl.when(pl.program_id(0) == 0)
    def _():
        dg_ref[...] = jnp.zeros_like(dg_ref)

    cosine, sine = cos_ref[...], sin_ref[...]
    sums = [jnp.zeros((8, HEAD_DIM), jnp.float32)] * 2
    for h in range(QH + KH):
        at = h if h < QH else h - QH
        grad_ref, raw_ref, g_ref, kind = (dq_ref, qr_ref, gq_ref, 0) if h < QH else (dk_ref, kr_ref, gk_ref, 1)
        grad = grad_ref[at] * SCALE
        u = raw_ref[at]
        e = grad * cosine + turn(grad * sine)
        r = lax.rsqrt(jnp.mean(u * u, axis=-1, keepdims=True) + EPS)
        ur = u * r
        sums[kind] += jnp.sum((e * ur).reshape(-1, 8, HEAD_DIM), axis=0)
        ge = e * g_ref[...]
        d = r * (ge - ur * jnp.mean(ur * ge, axis=-1, keepdims=True))
        d_ref[:, h * HEAD_DIM : (h + 1) * HEAD_DIM] = d.astype(jnp.bfloat16)
    for h in range(KH):
        at = (QH + KH + h) * HEAD_DIM
        d_ref[:, at : at + HEAD_DIM] = dv_ref[h]
    for kind in range(2):
        dg_ref[kind] += sums[kind]


def unrope(dq, dk, dv, qr, kr, gq, gk, cosine, sine):
    rows = 256

    def row(width):
        return pl.BlockSpec((rows, width), lambda i: (i, 0))

    def whole(a):
        return pl.BlockSpec(a.shape, lambda i: (0, 0))

    def heads(n):
        return pl.BlockSpec((n, rows, HEAD_DIM), lambda i: (0, i, 0))

    return pl.pallas_call(
        unrope_kernel,
        grid=(SEQ_ROWS // rows,),
        out_shape=(
            jax.ShapeDtypeStruct((SEQ_ROWS, 1024), jnp.bfloat16),
            jax.ShapeDtypeStruct((2, 8, HEAD_DIM), jnp.float32),
        ),
        in_specs=[heads(QH), heads(KH), heads(KH), heads(QH), heads(KH), whole(gq), whole(gk), row(HEAD_DIM), row(HEAD_DIM)],
        out_specs=[row(1024), pl.BlockSpec((2, 8, HEAD_DIM), lambda i: (0, 0, 0))],
        compiler_params=pltpu.CompilerParams(vmem_limit_bytes=48 * 1024 * 1024),
        cost_estimate=pl.CostEstimate(flops=SEQ_ROWS * 1024 * 20, bytes_accessed=24 << 20, transcendentals=0),
        name="unrope",
    )(dq, dk, dv, qr, kr, gq, gk, cosine, sine)


def swap(value, name):
    return lax.ppermute(value, name, [(0, 1), (1, 0)])


def pick(value, index):
    return lax.dynamic_index_in_dim(value, index, 0, keepdims=False)


def in_order(index, own, other):
    return jnp.where(index == 0, jnp.stack([own, other]), jnp.stack([other, own]))


def spread_pairs(which):
    found = []
    for p in range(2):
        for l in range(2):
            for c in range(2):
                s = c if which == 0 else 1 - c
                found.append((4 * p + 2 * l + c, 4 * s + 2 * p + l))
    return found


def to_owner(value, p, c):
    first = lax.ppermute(pick(value, c), ("p", "l", "c"), spread_pairs(0))
    second = lax.ppermute(pick(value, 1 - c), ("p", "l", "c"), spread_pairs(1))
    return in_order(p, first, second).reshape(2 * ROWS, value.shape[-1])


def from_owner(value, p, c):
    rows = value.reshape(2, ROWS, value.shape[-1])
    back = [[(b, a) for a, b in spread_pairs(which)] for which in range(2)]
    first = lax.ppermute(pick(rows, p), ("p", "l", "c"), back[0])
    second = lax.ppermute(pick(rows, 1 - p), ("p", "l", "c"), back[1])
    return in_order(c, first, second)


def sum_rows(value, l, c):
    value = value.reshape(2, 2, OWN, value.shape[-1])
    mine = lax.dynamic_index_in_dim(value, c, 1, keepdims=False)
    theirs = lax.dynamic_index_in_dim(value, 1 - c, 1, keepdims=False)
    chip = mine + swap(theirs.astype(jnp.bfloat16), "c").astype(jnp.float32)
    return pick(chip, l) + swap(pick(chip, 1 - l).astype(jnp.bfloat16), "l").astype(jnp.float32)


def norm_scale(value):
    return lax.rsqrt(jnp.mean(value * value, axis=-1, keepdims=True) + EPS)


def norm_back(value, r, gain, grad):
    scaled = value * r
    gained = grad * gain
    return r * (gained - scaled * jnp.mean(scaled * gained, axis=-1, keepdims=True)), jnp.sum(grad * scaled, axis=0)


def quarters(value, width):
    return value.reshape(value.shape[0], 4, width).transpose(1, 0, 2)


def fast_device(tokens, cotangent, starts, w_query, key_matrix, value_matrix, w_out, w_gate, w_up, w_down, gains):
    y, x, p, l, c = place()
    t = 2 * l + c
    group = ("y", "x", "p", "l")
    halves = jnp.stack(
        [
            jnp.concatenate(
                [
                    w_gate[:, h * HALF_FF : (h + 1) * HALF_FF],
                    w_up[:, h * HALF_FF : (h + 1) * HALF_FF],
                    w_down[:, h * 512 : (h + 1) * 512].reshape(32, HALF_FF),
                ],
                axis=0,
            )
            for h in range(2)
        ]
    )
    chip_half = in_order(c, pick(halves, c), swap(pick(halves, 1 - c), "c")).reshape(192, HALF_FF)
    mlp = lax.all_gather(chip_half, group, axis=0, tiled=True).reshape(32, 3, 32, HALF_FF)
    wa = jnp.concatenate(
        [
            jnp.concatenate([quarters(w_query, 512), quarters(key_matrix, 256), quarters(value_matrix, 256)], axis=2),
            quarters(w_out, 256).reshape(4, 16, 1024),
        ],
        axis=1,
    )
    gn = jnp.pad(gains.astype(jnp.float32), (0, 952)).reshape(8, 128)
    xs, wf, gf = front(tokens, wa, gn)
    xs = xs.reshape(SEQ_ROWS, MODEL_DIM)
    gain_all = gf.reshape(32, 1024)[:, :72].reshape(2304)
    g_attn = gain_all[None, :1024]
    g_mlp = gain_all[None, 1024:2048]
    g_q = gain_all[None, 2048:2176]
    g_k = gain_all[None, 2176:]
    w_qkv = wf[:, :32].reshape(1024, 1024)
    cosine, sine = rope_tables(jnp.arange(SEQ_ROWS, dtype=jnp.int32))
    sine = jnp.concatenate([-sine[:, :64], sine[:, 64:]], axis=1)
    own_starts = pick(starts, p)
    block_at = jnp.arange(SEQ_ROWS // PIECE, dtype=jnp.int32) * PIECE
    flags = jnp.any(own_starts[None, :] == block_at[:, None], axis=1).astype(jnp.int32)
    normed, q, k, v, q_raw, k_raw = qkv(xs, w_qkv, g_attn, g_q, g_k, cosine, sine)
    attn, lse = attend(flags, q, k, v)
    wo_cols = wf[:, 32:].reshape(4, 512, 256)
    wo_l = swap(pick(wo_cols, 2 * (1 - l) + c), "l")
    wo_d = swap(swap(pick(wo_cols, 2 * (1 - l) + 1 - c), "l"), "c")
    wo_c = swap(pick(wo_cols, 2 * l + 1 - c), "c")
    wo_own = pick(wo_cols, t)
    upper = jnp.where(c == 0, jnp.concatenate([wo_own, wo_c], 1), jnp.concatenate([wo_c, wo_own], 1))
    lower = jnp.where(c == 0, jnp.concatenate([wo_l, wo_d], 1), jnp.concatenate([wo_d, wo_l], 1))
    wo = jnp.where(l == 0, jnp.concatenate([upper, lower], 1), jnp.concatenate([lower, upper], 1))
    branch = sum_rows(dot(attn, wo), l, c)
    x_own = pick(xs.reshape(4, OWN, MODEL_DIM), t).astype(jnp.float32)
    resid = x_own + branch
    r_mlp = norm_scale(resid)
    mlp_own = (resid * r_mlp * g_mlp).astype(jnp.bfloat16)
    mlp_in = in_order(c, mlp_own, swap(mlp_own, "c")).reshape(1024, MODEL_DIM)
    dy_own = to_owner(cotangent, p, c)
    dy = in_order(c, dy_own, swap(dy_own, "c")).reshape(1024, MODEL_DIM)
    wg = mlp[:, 0].reshape(1024, HALF_FF)
    wu = mlp[:, 1].reshape(1024, HALF_FF)
    wd_cols = mlp[:, 2].reshape(2, HALF_FF, 512)
    wd_pair = in_order(c, pick(wd_cols, c), swap(pick(wd_cols, 1 - c), "c"))
    wd = jnp.concatenate([wd_pair[0], wd_pair[1]], axis=1)
    gate = dot(mlp_in, wg)
    up = dot(mlp_in, wu)
    s = jax.nn.sigmoid(gate)
    silu = gate * s
    hidden = (silu * up).astype(jnp.bfloat16)
    d_hidden = dot(dy, wd, NT)
    d_up = (d_hidden * silu).astype(jnp.bfloat16)
    d_gate = (d_hidden * up * s * (1.0 + gate * (1.0 - s))).astype(jnp.bfloat16)
    d_in = (dot(d_gate, wg, NT) + dot(d_up, wu, NT)).reshape(2, OWN, MODEL_DIM)
    d_mlp_in = pick(d_in, c) + swap(pick(d_in, 1 - c), "c")
    d_norm, d_g_mlp = norm_back(resid, r_mlp, g_mlp, d_mlp_in)
    d_resid = dy_own.astype(jnp.float32) + d_norm
    d_branch = d_resid.astype(jnp.bfloat16)
    grad_gate = dot(mlp_in, d_gate, TN).astype(jnp.bfloat16)
    grad_up = dot(mlp_in, d_up, TN).astype(jnp.bfloat16)
    grad_down = dot(hidden, dy, TN).astype(jnp.bfloat16)
    down_cols = jnp.stack([grad_down[:, :512], grad_down[:, 512:]])
    down_half = in_order(c, pick(down_cols, c), swap(pick(down_cols, 1 - c), "c"))
    packed = jnp.stack(
        [grad_gate.reshape(32, 32, HALF_FF), grad_up.reshape(32, 32, HALF_FF), down_half.reshape(32, 32, HALF_FF)], axis=1
    ).reshape(16 * 192, HALF_FF)
    mlp_sum = lax.psum_scatter(packed, group, scatter_dimension=0, tiled=True).reshape(2, 96, HALF_FF)
    mlp_other = swap(pick(mlp_sum, 1 - c), "c")
    mlp_out = in_order(c, pick(mlp_sum, c), mlp_other).astype(jnp.float32)
    out_gate = jnp.concatenate([mlp_out[0, :32], mlp_out[1, :32]], axis=1)
    out_up = jnp.concatenate([mlp_out[0, 32:64], mlp_out[1, 32:64]], axis=1)
    out_down = jnp.concatenate([mlp_out[0, 64:].reshape(96, 512), mlp_out[1, 64:].reshape(96, 512)], axis=1)
    down = dot(hidden, wd).reshape(2, OWN, MODEL_DIM)
    result = resid + pick(down, c) + swap(pick(down, 1 - c).astype(jnp.bfloat16), "c").astype(jnp.float32)
    output = from_owner(result.astype(jnp.bfloat16), p, c)
    near = in_order(c, d_branch, swap(d_branch, "c"))
    far = swap(d_branch, "l")
    far_pair = in_order(c, far, swap(far, "c"))
    d_all = in_order(l, near, far_pair).reshape(SEQ_ROWS, MODEL_DIM)
    d_attn = dot(d_all, wo, NT).astype(jnp.bfloat16)
    grad_out = dot(attn, d_all, TN).astype(jnp.bfloat16)
    dq, dk, dv = attend_back(flags, q, k, v, attn, d_attn, lse)
    d_qkv, d_g_heads = unrope(dq, dk, dv, q_raw, k_raw, g_q, g_k, cosine, sine)
    grad_qkv = dot(normed, d_qkv, TN).astype(jnp.bfloat16)
    d_normed = sum_rows(dot(d_qkv, w_qkv, NT), l, c)
    d_in_norm, d_g_attn = norm_back(x_own, norm_scale(x_own), g_attn, d_normed)
    grad_tokens = from_owner((d_resid + d_in_norm).astype(jnp.bfloat16), p, c).astype(jnp.float32)
    go = grad_out.reshape(512, 4, 256).transpose(1, 0, 2)
    go_own = pick(go, t)
    go_l = swap(pick(go, 2 * (1 - l) + c), "l")
    go_d = swap(swap(pick(go, 2 * (1 - l) + 1 - c), "l"), "c")
    go_c = swap(pick(go, 2 * l + 1 - c), "c")
    go_all = in_order(l, in_order(c, go_own, go_c), in_order(c, go_l, go_d))
    part = jnp.concatenate([grad_qkv.reshape(32, 32, 1024), go_all.reshape(32, 16, 1024)], axis=1)
    d_gains = jnp.concatenate([d_g_attn, d_g_mlp, jnp.sum(d_g_heads, axis=1).reshape(256)])
    g_part = jnp.pad(d_gains.reshape(32, 72), ((0, 0), (0, 952))).reshape(32, 8, 128)
    sums, g_sum = back(part, g_part)
    top = sums[:, :32]
    out_query = top[:, :, :512].transpose(1, 0, 2).reshape(32, 2048)
    out_key = top[:, :, 512:768].transpose(1, 0, 2).reshape(32, 1024)
    out_value = top[:, :, 768:].transpose(1, 0, 2).reshape(32, 1024)
    out_out = sums[:, 32:].reshape(4, 64, 256).transpose(1, 0, 2).reshape(64, 1024)
    out_gains = g_sum.reshape(1024)[:72]
    return (output, grad_tokens, out_query, out_key, out_value, out_out, out_gate, out_up, out_down, out_gains)


def fast_solution(mesh):
    wide = Mesh(mesh.devices.reshape(2, 2, 2, 2, 2), AXES)
    rows = ("y", "x")
    places = ("p", "l", "c")
    weight = P(AXES, None)
    return jax.shard_map(
        fast_device,
        mesh=wide,
        in_specs=(P(rows, places, None), P(rows, places, None), P(rows, None)) + (weight,) * 7 + (P(AXES),),
        out_specs=(P(rows, places, None), P(rows, places, None)) + (weight,) * 7 + (P(AXES),),
        check_vma=False,
    )


def solution(mesh):
    if dict(mesh.shape) == {"dp": 4, "ctx": 8}:
        return fast_solution(mesh)
    return generic_solution(mesh)
```

```python
import functools
import math

import jax
import jax.numpy as jnp
from jax import lax
from jax.experimental import pallas as pl
from jax.experimental.pallas import tpu as pltpu
from jax.sharding import Mesh
from jax.sharding import PartitionSpec as P

MODEL_DIM = 1024
QUERY_HEADS = 16
KEY_VALUE_HEADS = 8
HEAD_DIM = 128
SEQUENCE_TOKENS = 2048
PIECE = 256
NPIECE = 4


EPS = 1e-06
THETA = 1000000.0
NEG = -1e30


def rms_norm(incoming_values, gain_vector):
    return (
        incoming_values
        * lax.rsqrt(jnp.mean(incoming_values * incoming_values, axis=-1, keepdims=True) + EPS)
        * gain_vector
    )


def rope_tables(positions):
    half_steps = jnp.arange(HEAD_DIM // 2, dtype=jnp.float32)
    inverse = THETA ** (-2.0 * half_steps / HEAD_DIM)
    angles = positions.astype(jnp.float32)[:, None] * inverse[None, :]
    angles = jnp.concatenate([angles, angles], axis=-1)
    return (jnp.cos(angles), jnp.sin(angles))


def rotate(incoming_values, cosine_table, sine_table):
    half_dim = HEAD_DIM // 2
    turned = jnp.concatenate(
        [-incoming_values[..., half_dim:], incoming_values[..., :half_dim]], axis=-1
    )
    return incoming_values * cosine_table[:, None, :] + turned * sine_table[:, None, :]


def per_head_route(unrotated_projection, gain_vector, cosine_table, sine_table, head_count):
    shaped = unrotated_projection.reshape(unrotated_projection.shape[:-1] + (head_count, HEAD_DIM))
    return rotate(rms_norm(shaped, gain_vector), cosine_table, sine_table).reshape(
        unrotated_projection.shape
    )


def piece_ids(positions, piece_starts):
    inside = (positions[:, None] >= piece_starts[None, :]) & (
        positions[:, None] < piece_starts[None, :] + PIECE
    )
    number = jnp.arange(1, NPIECE + 1, dtype=jnp.int32)
    return jnp.sum(jnp.where(inside, number[None, :], 0), axis=1) - 1


def visible(query_pos, query_id, key_pos, key_id):
    causal = key_pos[None, :] <= query_pos[:, None]
    same_piece = (query_id[:, None] == key_id[None, :]) & (query_id[:, None] >= 0)
    return causal | same_piece


def swiglu(gate_proj, up_proj):
    return jax.nn.silu(gate_proj) * up_proj


def block_extent(kv_count, per_head):
    target = max(1, 512 // per_head)
    chosen = 1
    for candidate in range(1, kv_count + 1):
        if kv_count % candidate == 0 and candidate <= target:
            chosen = candidate
    return chosen


def attend_forward(incoming_query, incoming_keys, incoming_values, allowed, head_group_block):
    sequence_rows = incoming_query.shape[0]
    query_group_factor = QUERY_HEADS // KEY_VALUE_HEADS
    scaling = 1.0 / math.sqrt(HEAD_DIM)
    query_per_head = incoming_query.reshape(
        sequence_rows, KEY_VALUE_HEADS, query_group_factor, HEAD_DIM
    )
    key_per_head = incoming_keys.reshape(incoming_keys.shape[0], KEY_VALUE_HEADS, HEAD_DIM)
    value_per_head = incoming_values.reshape(incoming_values.shape[0], KEY_VALUE_HEADS, HEAD_DIM)
    mixed_parts = []
    total_parts = []
    for head_offset in range(0, KEY_VALUE_HEADS, head_group_block):
        q_part = query_per_head[:, head_offset : head_offset + head_group_block]
        k_part = key_per_head[:, head_offset : head_offset + head_group_block]
        v_part = value_per_head[:, head_offset : head_offset + head_group_block]
        scores = (
            jnp.einsum("tagd,kad->agtk", q_part, k_part, preferred_element_type=jnp.float32)
            * scaling
        )
        scores = jnp.where(allowed[None, None], scores, NEG)
        row_max = jnp.max(scores, axis=-1, keepdims=True)
        exp_scores = jnp.exp(scores - row_max)
        summed = jnp.sum(exp_scores, axis=-1, keepdims=True)
        prob_low = (exp_scores / summed).astype(jnp.bfloat16)
        mixed_parts.append(
            jnp.einsum("agtk,kad->tagd", prob_low, v_part, preferred_element_type=jnp.float32)
        )
        total_parts.append(row_max + jnp.log(summed))
    mixed_out = jnp.concatenate(mixed_parts, axis=1).reshape(sequence_rows, QUERY_HEADS * HEAD_DIM)
    return (mixed_out, jnp.concatenate(total_parts, axis=0))


def attend_backward(
    incoming_query,
    incoming_keys,
    incoming_values,
    allowed,
    log_total,
    mixed_gradient,
    head_group_block,
):
    sequence_rows = incoming_query.shape[0]
    key_row_matrix = incoming_keys.shape[0]
    query_group_factor = QUERY_HEADS // KEY_VALUE_HEADS
    scaling = 1.0 / math.sqrt(HEAD_DIM)
    query_per_head = incoming_query.reshape(
        sequence_rows, KEY_VALUE_HEADS, query_group_factor, HEAD_DIM
    )
    gradient_per_head = mixed_gradient.reshape(
        sequence_rows, KEY_VALUE_HEADS, query_group_factor, HEAD_DIM
    )
    key_per_head = incoming_keys.reshape(key_row_matrix, KEY_VALUE_HEADS, HEAD_DIM)
    value_per_head = incoming_values.reshape(key_row_matrix, KEY_VALUE_HEADS, HEAD_DIM)
    dq_parts = []
    key_gradient_pieces = []
    value_gradient_pieces = []
    for head_offset in range(0, KEY_VALUE_HEADS, head_group_block):
        q_part = query_per_head[:, head_offset : head_offset + head_group_block]
        g_part = gradient_per_head[:, head_offset : head_offset + head_group_block]
        k_part = key_per_head[:, head_offset : head_offset + head_group_block]
        v_part = value_per_head[:, head_offset : head_offset + head_group_block]
        scores = (
            jnp.einsum("tagd,kad->agtk", q_part, k_part, preferred_element_type=jnp.float32)
            * scaling
        )
        scores = jnp.where(allowed[None, None], scores, NEG)
        prob_all = jnp.exp(scores - log_total[head_offset : head_offset + head_group_block])
        prob_low = prob_all.astype(jnp.bfloat16)
        d_probs = jnp.einsum("tagd,kad->agtk", g_part, v_part, preferred_element_type=jnp.float32)
        row_dot = jnp.sum(prob_all * d_probs, axis=-1, keepdims=True)
        d_scores = (prob_all * (d_probs - row_dot)).astype(jnp.bfloat16)
        dq_parts.append(
            jnp.einsum("agtk,kad->tagd", d_scores, k_part, preferred_element_type=jnp.float32)
            * scaling
        )
        key_gradient_pieces.append(
            jnp.einsum("agtk,tagd->kad", d_scores, q_part, preferred_element_type=jnp.float32)
            * scaling
        )
        value_gradient_pieces.append(
            jnp.einsum("agtk,tagd->kad", prob_low, g_part, preferred_element_type=jnp.float32)
        )
    d_query = jnp.concatenate(dq_parts, axis=1).reshape(sequence_rows, QUERY_HEADS * HEAD_DIM)
    key_gradient = jnp.concatenate(key_gradient_pieces, axis=1).reshape(
        key_row_matrix, KEY_VALUE_HEADS * HEAD_DIM
    )
    value_gradient = jnp.concatenate(value_gradient_pieces, axis=1).reshape(
        key_row_matrix, KEY_VALUE_HEADS * HEAD_DIM
    )
    return (d_query, key_gradient, value_gradient)


def generic_device(
    tokens, cotangent, starts, w_query, key_matrix, value_matrix, w_out, w_gate, w_up, w_down, gains
):
    sequence_count, sequence_rows, model_width = tokens.shape
    number_of_rows = sequence_count * sequence_rows
    head_group_block = block_extent(KEY_VALUE_HEADS, QUERY_HEADS // KEY_VALUE_HEADS * sequence_rows)
    attn_set = (
        lax.all_gather(w_query, ("dp", "ctx"), axis=0, tiled=True),
        lax.all_gather(key_matrix, ("dp", "ctx"), axis=0, tiled=True),
        lax.all_gather(value_matrix, ("dp", "ctx"), axis=0, tiled=True),
        lax.all_gather(w_out, ("dp", "ctx"), axis=0, tiled=True),
        lax.all_gather(gains, ("dp", "ctx"), axis=0, tiled=True),
    )
    mlp_set = (
        lax.all_gather(w_gate, ("dp", "ctx"), axis=0, tiled=True),
        lax.all_gather(w_up, ("dp", "ctx"), axis=0, tiled=True),
        lax.all_gather(w_down, ("dp", "ctx"), axis=0, tiled=True),
    )
    gain_all = attn_set[4].astype(jnp.float32)
    g_attn = gain_all[:MODEL_DIM]
    g_mlp = gain_all[MODEL_DIM : 2 * MODEL_DIM]
    g_query = gain_all[2 * MODEL_DIM : 2 * MODEL_DIM + HEAD_DIM]
    key_grad_total = gain_all[2 * MODEL_DIM + HEAD_DIM :]
    positions = lax.axis_index("ctx") * sequence_rows + jnp.arange(sequence_rows, dtype=jnp.int32)
    key_places = jnp.arange(SEQUENCE_TOKENS, dtype=jnp.int32)
    cosine_table, sine_table = rope_tables(positions)

    def query_map(unrotated_projection, gain_vector):
        return per_head_route(
            unrotated_projection, gain_vector, cosine_table, sine_table, QUERY_HEADS
        )

    def key_map(unrotated_projection, gain_vector):
        return per_head_route(
            unrotated_projection, gain_vector, cosine_table, sine_table, KEY_VALUE_HEADS
        )

    flat_in = tokens.reshape(number_of_rows, model_width).astype(jnp.float32)
    normed = rms_norm(flat_in, g_attn).astype(jnp.bfloat16)
    query_raw = jnp.dot(normed, attn_set[0], preferred_element_type=jnp.float32).reshape(
        sequence_count, sequence_rows, QUERY_HEADS * HEAD_DIM
    )
    key_unrotated = jnp.dot(normed, attn_set[1], preferred_element_type=jnp.float32).reshape(
        sequence_count, sequence_rows, KEY_VALUE_HEADS * HEAD_DIM
    )
    value_reduced = jnp.dot(normed, attn_set[2], preferred_element_type=jnp.float32).astype(
        jnp.bfloat16
    )
    value_reduced = value_reduced.reshape(sequence_count, sequence_rows, KEY_VALUE_HEADS * HEAD_DIM)
    query_reduced = query_map(query_raw, g_query).astype(jnp.bfloat16)
    key_reduced = key_map(key_unrotated, key_grad_total).astype(jnp.bfloat16)
    mask_list = []
    mixed_list = []
    total_list = []
    for seq_index in range(sequence_count):
        query_ids = piece_ids(positions, starts[seq_index])
        key_ids = piece_ids(key_places, starts[seq_index])
        allowed = visible(positions, query_ids, key_places, key_ids)
        key_full, value_full = (
            lax.all_gather(key_reduced[seq_index], "ctx", axis=0, tiled=True),
            lax.all_gather(value_reduced[seq_index], "ctx", axis=0, tiled=True),
        )
        mixed_out, log_total = attend_forward(
            query_reduced[seq_index], key_full, value_full, allowed, head_group_block
        )
        mask_list.append(allowed)
        mixed_list.append(mixed_out)
        total_list.append(log_total)
    attn_low = (
        jnp.stack(mixed_list).reshape(number_of_rows, QUERY_HEADS * HEAD_DIM).astype(jnp.bfloat16)
    )
    residual = flat_in + jnp.dot(attn_low, attn_set[3], preferred_element_type=jnp.float32)
    mlp_in = rms_norm(residual, g_mlp).astype(jnp.bfloat16)
    gate_proj = jnp.dot(mlp_in, mlp_set[0], preferred_element_type=jnp.float32)
    up_proj = jnp.dot(mlp_in, mlp_set[1], preferred_element_type=jnp.float32)
    hidden = swiglu(gate_proj, up_proj).astype(jnp.bfloat16)
    result = residual + jnp.dot(hidden, mlp_set[2], preferred_element_type=jnp.float32)
    output = result.astype(jnp.bfloat16).reshape(tokens.shape)
    mlp_back = (
        lax.all_gather(w_gate, ("dp", "ctx"), axis=0, tiled=True),
        lax.all_gather(w_up, ("dp", "ctx"), axis=0, tiled=True),
        lax.all_gather(w_down, ("dp", "ctx"), axis=0, tiled=True),
    )
    grad_flat = cotangent.reshape(number_of_rows, model_width)
    grad_down = jnp.dot(hidden.T, grad_flat, preferred_element_type=jnp.float32)
    d_hidden = jnp.dot(grad_flat, mlp_back[2].T, preferred_element_type=jnp.float32)
    swiglu_pull = jax.vjp(swiglu, gate_proj, up_proj)[1]
    d_gate, d_up = swiglu_pull(d_hidden)
    d_gate = d_gate.astype(jnp.bfloat16)
    d_up = d_up.astype(jnp.bfloat16)
    grad_gate = jnp.dot(mlp_in.T, d_gate, preferred_element_type=jnp.float32)
    grad_up = jnp.dot(mlp_in.T, d_up, preferred_element_type=jnp.float32)
    mlp_grads = (
        lax.psum_scatter(grad_gate, ("dp", "ctx"), scatter_dimension=0, tiled=True),
        lax.psum_scatter(grad_up, ("dp", "ctx"), scatter_dimension=0, tiled=True),
        lax.psum_scatter(grad_down, ("dp", "ctx"), scatter_dimension=0, tiled=True),
    )
    d_mlp_in = jnp.dot(d_gate, mlp_back[0].T, preferred_element_type=jnp.float32)
    d_mlp_in = d_mlp_in + jnp.dot(d_up, mlp_back[1].T, preferred_element_type=jnp.float32)
    mlp_norm_pull = jax.vjp(rms_norm, residual, g_mlp)[1]
    d_resid_norm, d_g_mlp = mlp_norm_pull(d_mlp_in)
    d_resid = grad_flat.astype(jnp.float32) + d_resid_norm
    attn_back = (
        lax.all_gather(w_query, ("dp", "ctx"), axis=0, tiled=True),
        lax.all_gather(key_matrix, ("dp", "ctx"), axis=0, tiled=True),
        lax.all_gather(value_matrix, ("dp", "ctx"), axis=0, tiled=True),
        lax.all_gather(w_out, ("dp", "ctx"), axis=0, tiled=True),
        lax.all_gather(gains, ("dp", "ctx"), axis=0, tiled=True),
    )
    d_branch = d_resid.astype(jnp.bfloat16)
    grad_out = jnp.dot(attn_low.T, d_branch, preferred_element_type=jnp.float32)
    d_attn = jnp.dot(d_branch, attn_back[3].T, preferred_element_type=jnp.float32).astype(
        jnp.bfloat16
    )
    d_attn = d_attn.reshape(sequence_count, sequence_rows, QUERY_HEADS * HEAD_DIM)
    dq_list = []
    dk_list = []
    value_gradient_list = []
    for seq_index in range(sequence_count):
        key_full, value_full = (
            lax.all_gather(key_reduced[seq_index], "ctx", axis=0, tiled=True),
            lax.all_gather(value_reduced[seq_index], "ctx", axis=0, tiled=True),
        )
        d_query_seq, d_key_full, d_value_full = attend_backward(
            query_reduced[seq_index],
            key_full,
            value_full,
            mask_list[seq_index],
            total_list[seq_index],
            d_attn[seq_index],
            head_group_block,
        )
        d_key_seq, d_value_seq = (
            lax.psum_scatter(
                d_key_full.astype(jnp.bfloat16), "ctx", scatter_dimension=0, tiled=True
            ).astype(jnp.float32),
            lax.psum_scatter(
                d_value_full.astype(jnp.bfloat16), "ctx", scatter_dimension=0, tiled=True
            ).astype(jnp.float32),
        )
        dq_list.append(d_query_seq)
        dk_list.append(d_key_seq)
        value_gradient_list.append(d_value_seq)
    d_query = jnp.stack(dq_list)
    key_gradient = jnp.stack(dk_list)
    value_gradient_reduced = (
        jnp.stack(value_gradient_list)
        .reshape(number_of_rows, KEY_VALUE_HEADS * HEAD_DIM)
        .astype(jnp.bfloat16)
    )
    query_pull = jax.vjp(query_map, query_raw, g_query)[1]
    d_query_raw, d_g_query = query_pull(d_query)
    key_pull = jax.vjp(key_map, key_unrotated, key_grad_total)[1]
    key_gradient_unrotated, d_g_key = key_pull(key_gradient)
    d_query_low = d_query_raw.reshape(number_of_rows, QUERY_HEADS * HEAD_DIM).astype(jnp.bfloat16)
    key_gradient_reduced = key_gradient_unrotated.reshape(
        number_of_rows, KEY_VALUE_HEADS * HEAD_DIM
    ).astype(jnp.bfloat16)
    grad_query = jnp.dot(normed.T, d_query_low, preferred_element_type=jnp.float32)
    grad_key = jnp.dot(normed.T, key_gradient_reduced, preferred_element_type=jnp.float32)
    grad_value = jnp.dot(normed.T, value_gradient_reduced, preferred_element_type=jnp.float32)
    d_normed = jnp.dot(d_query_low, attn_back[0].T, preferred_element_type=jnp.float32)
    d_normed = d_normed + jnp.dot(
        key_gradient_reduced, attn_back[1].T, preferred_element_type=jnp.float32
    )
    d_normed = d_normed + jnp.dot(
        value_gradient_reduced, attn_back[2].T, preferred_element_type=jnp.float32
    )
    input_pull = jax.vjp(rms_norm, flat_in, g_attn)[1]
    d_input_norm, d_g_attn = input_pull(d_normed)
    grad_tokens = (d_resid + d_input_norm).reshape(tokens.shape)
    grad_gains = jnp.concatenate([d_g_attn, d_g_mlp, d_g_query, d_g_key])
    attn_grads = (
        lax.psum_scatter(grad_query, ("dp", "ctx"), scatter_dimension=0, tiled=True),
        lax.psum_scatter(grad_key, ("dp", "ctx"), scatter_dimension=0, tiled=True),
        lax.psum_scatter(grad_value, ("dp", "ctx"), scatter_dimension=0, tiled=True),
        lax.psum_scatter(grad_out, ("dp", "ctx"), scatter_dimension=0, tiled=True),
        lax.psum_scatter(grad_gains, ("dp", "ctx"), scatter_dimension=0, tiled=True),
    )
    return (
        output,
        grad_tokens,
        attn_grads[0],
        attn_grads[1],
        attn_grads[2],
        attn_grads[3],
        mlp_grads[0],
        mlp_grads[1],
        mlp_grads[2],
        attn_grads[4],
    )


def generic_solution(mesh):
    return jax.shard_map(
        generic_device,
        mesh=mesh,
        in_specs=(
            P("dp", "ctx", None),
            P("dp", "ctx", None),
            P("dp", None),
            P(("dp", "ctx"), None),
            P(("dp", "ctx"), None),
            P(("dp", "ctx"), None),
            P(("dp", "ctx"), None),
            P(("dp", "ctx"), None),
            P(("dp", "ctx"), None),
            P(("dp", "ctx"), None),
            P(("dp", "ctx")),
        ),
        out_specs=(
            P("dp", "ctx", None),
            P("dp", "ctx", None),
            P(("dp", "ctx"), None),
            P(("dp", "ctx"), None),
            P(("dp", "ctx"), None),
            P(("dp", "ctx"), None),
            P(("dp", "ctx"), None),
            P(("dp", "ctx"), None),
            P(("dp", "ctx"), None),
            P(("dp", "ctx")),
        ),
        check_vma=False,
    )


AXES = ("y", "x", "p", "l", "c")
FF = 3072
HALF_FF = FF // 2
ROWS = 256
SEQ_ROWS = SEQUENCE_TOKENS
OWN = SEQ_ROWS // 4
BLK = 512
NBLK = SEQ_ROWS // BLK
QH = 4
KH = 2
MESH = pl.DeviceIdType.MESH
SCALE = 1.0 / math.sqrt(HEAD_DIM)
LOG2E = 1.4426950408889634
NT = (((1,), (1,)), ((), ()))
TN = (((0,), (0,)), ((), ()))


def dot(a, b, dims=None):
    if dims is None:
        dims = (((1,), (0,)), ((), ()))
    return lax.dot_general(a, b, dims, preferred_element_type=jnp.float32)


def greet(peers):
    barrier = pltpu.get_barrier_semaphore()
    for peer in peers:
        pl.semaphore_signal(barrier, inc=1, device_id=peer, device_id_type=MESH)
    pl.semaphore_wait(barrier, len(peers))


class Plan:
    def __init__(self, send_sem, recv_sem):
        self.send_sem = send_sem
        self.recv_sem = recv_sem
        self.count = 0
        self.entries = []

    def add(self, peer, pairs):
        self.entries.append((peer, pairs, self.count))
        self.count += len(pairs)
        return len(self.entries) - 1

    def copies(self, name):
        peer, pairs, at = self.entries[name]
        return [
            pltpu.make_async_remote_copy(
                src_ref=src,
                dst_ref=dst,
                send_sem=self.send_sem.at[at + k],
                recv_sem=self.recv_sem.at[at + k],
                device_id=peer,
                device_id_type=MESH,
            )
            for k, (src, dst) in enumerate(pairs)
        ]

    def start(self, *names):
        for name in names:
            for copy in self.copies(name):
                copy.start()

    def arrived(self, *names):
        for name in names:
            for copy in self.copies(name):
                copy.wait_recv()

    def sent(self):
        for name in range(len(self.entries)):
            for copy in self.copies(name):
                copy.wait_send()


def place():
    return tuple(lax.axis_index(name) for name in AXES)


def peers_of(x, y, p, l, c):
    return {
        "c": {"c": 1 - c},
        "l": {"l": 1 - l},
        "d": {"l": 1 - l, "c": 1 - c},
        "p": {"p": 1 - p},
        "x": {"x": 1 - x},
        "y": {"y": 1 - y},
    }


def rows_at(index, size, count=1):
    return pl.ds(pl.multiple_of(index * size, size), size * count)


def in_place(*refs):
    return [(ref, ref) for ref in refs]


def front_kernel(tok, wq, wk, wv, wo, gn, wg, wu, wd, inverse, xs, wa, woq, gf, wgu, wdn, cosine, sine, send_sem, recv_sem, local_sem):
    y, x, p, l, c = place()
    peer = peers_of(x, y, p, l, c)
    block = 4 * p + 2 * l + c
    group = (y * 2 + x) * 8
    me = group + block
    t = 2 * l + c
    net = Plan(send_sem, recv_sem)

    def quarter(q):
        return [
            (wq.at[:, rows_at(q, 512)], wa.at[rows_at(me, 32), pl.ds(0, 512)]),
            (wk.at[:, rows_at(q, 256)], wa.at[rows_at(me, 32), pl.ds(512, 256)]),
            (wv.at[:, rows_at(q, 256)], wa.at[rows_at(me, 32), pl.ds(768, 256)]),
            (wo.at[:, rows_at(q, 256)], woq.at[rows_at(me, 64)]),
            (gn, gf.at[me]),
        ]

    def half(h):
        return [
            (wg.at[:, rows_at(h, HALF_FF)], wgu.at[0, rows_at(me, 32)]),
            (wu.at[:, rows_at(h, HALF_FF)], wgu.at[1, rows_at(me, 32)]),
            (wd.at[:, rows_at(h, 512)], wdn.at[rows_at(me, 96)]),
        ]

    def span(base):
        return in_place(wa.at[rows_at(base // 4, 128)], woq.at[rows_at(base // 4, 256)], gf.at[pl.ds(base, 4)])

    def chip(yy, xx, pp, ll):
        slot = (yy * 2 + xx) * 4 + 2 * pp + ll
        return in_place(wgu.at[:, rows_at(slot, 64)], wdn.at[rows_at(slot, 192)])

    mine, other = group + 4 * p, group + 4 * (1 - p)
    go_first_l = net.add(peer["l"], quarter(2 * (1 - l) + c))
    go_first_d = net.add(peer["d"], quarter(2 * (1 - l) + 1 - c))
    go_first_c = net.add(peer["c"], quarter(2 * l + 1 - c))
    go_near = net.add(peer["l"], [(tok.at[p], xs.at[block])])
    upper, lower = pl.ds(0, ROWS // 2), pl.ds(ROWS // 2, ROWS // 2)
    go_far_0 = net.add(peer["p"], [(tok.at[1 - p, upper], xs.at[block, upper])])
    go_far_1 = net.add(peer["p"], [(tok.at[1 - p, lower], xs.at[block, lower])])
    go_near_c = net.add(peer["c"], [(tok.at[p], xs.at[block])])
    go_across = net.add(peer["p"], span(mine))
    go_own_x = net.add(peer["x"], span(mine))
    go_near_relay = net.add(peer["c"], in_place(xs.at[block ^ 2]))
    go_own_y = net.add(peer["y"], span(mine) + span((y * 2 + 1 - x) * 8 + 4 * p))
    go_other_y = net.add(peer["y"], span(other))
    go_far_l0 = net.add(peer["l"], in_place(xs.at[block ^ 4, upper]))
    go_far_l1 = net.add(peer["l"], in_place(xs.at[block ^ 4, lower]))
    go_far_relay = net.add(peer["c"], in_place(xs.at[block ^ 4]))
    go_other_x = net.add(peer["x"], span(other) + span(((1 - y) * 2 + x) * 8 + 4 * (1 - p)))
    go_far_l_relay = net.add(peer["c"], in_place(xs.at[block ^ 6]))
    go_mlp_c = net.add(peer["c"], half(1 - c))
    go_mlp_near = net.add(peer["l"], chip(y, x, p, l))
    go_mlp_x = net.add(peer["x"], chip(y, x, p, l))
    go_mlp_y = net.add(peer["y"], chip(y, x, p, 1 - l))
    greet(list(peer.values()))
    net.start(go_first_l, go_first_d, go_first_c, go_near_c, go_mlp_c)
    own = [
        pltpu.make_async_copy(src, dst, local_sem.at[k])
        for k, (src, dst) in enumerate(quarter(t) + half(c) + [(tok.at[p], xs.at[block])])
    ]
    for copy in own:
        copy.start()

    def table(first, last):
        def chunk(k, carry):
            rows = rows_at(k, 64)
            position = (lax.broadcasted_iota(jnp.int32, (64, HEAD_DIM), 0) + k * 64).astype(jnp.float32)
            lane = lax.broadcasted_iota(jnp.int32, (64, HEAD_DIM), 1)
            angle = position * inverse[0:1, :]
            cosine[rows, :] = jnp.cos(angle)
            sine[rows, :] = jnp.where(lane < HEAD_DIM // 2, -1.0, 1.0) * jnp.sin(angle)
            return carry

        lax.fori_loop(first, last, chunk, 0)

    for copy in own:
        copy.wait()
    net.arrived(go_first_l, go_first_d, go_first_c)
    net.start(go_across, go_own_x, go_near)
    table(0, 16)
    net.arrived(go_own_x)
    net.start(go_own_y)
    net.arrived(go_mlp_c)
    net.start(go_mlp_x)
    net.arrived(go_across)
    net.start(go_other_y, go_far_0, go_far_1)
    net.arrived(go_near)
    net.start(go_near_relay, go_mlp_near)
    table(16, 32)
    net.arrived(go_other_y)
    net.start(go_other_x)
    net.arrived(go_far_0)
    net.start(go_far_l0)
    net.arrived(go_mlp_near)
    net.start(go_mlp_y)
    net.arrived(go_far_1)
    net.start(go_far_l1, go_far_relay)
    net.arrived(go_far_l0, go_far_l1)
    net.start(go_far_l_relay)
    net.arrived(go_near_c, go_near_relay, go_far_relay, go_far_l_relay, go_own_y, go_other_x, go_mlp_x, go_mlp_y)
    net.sent()


def front(tok, wq, wk, wv, wo, gn, wg, wu, wd, inverse):
    any_spec = pl.BlockSpec(memory_space=pl.ANY)
    copies = 64
    bf16 = jnp.bfloat16
    return pl.pallas_call(
        front_kernel,
        out_shape=(
            jax.ShapeDtypeStruct((8, ROWS, MODEL_DIM), bf16),
            jax.ShapeDtypeStruct((1024, 1024), bf16),
            jax.ShapeDtypeStruct((2048, 256), bf16),
            jax.ShapeDtypeStruct((32, 8, 128), jnp.float32),
            jax.ShapeDtypeStruct((2, MODEL_DIM, HALF_FF), bf16),
            jax.ShapeDtypeStruct((FF, 512), bf16),
            jax.ShapeDtypeStruct((SEQ_ROWS, HEAD_DIM), jnp.float32),
            jax.ShapeDtypeStruct((SEQ_ROWS, HEAD_DIM), jnp.float32),
        ),
        in_specs=[any_spec] * 9 + [pl.BlockSpec(memory_space=pltpu.VMEM)],
        out_specs=[any_spec] * 6 + [pl.BlockSpec(memory_space=pltpu.VMEM)] * 2,
        scratch_shapes=[
            pltpu.SemaphoreType.DMA((copies,)),
            pltpu.SemaphoreType.DMA((copies,)),
            pltpu.SemaphoreType.DMA((9,)),
        ],
        compiler_params=pltpu.CompilerParams(collective_id=0, has_side_effects=True),
        name="front_gather",
    )(tok, wq, wk, wv, wo, gn, wg, wu, wd, inverse)


def line_peers(p, l, c):
    return [
        {"p": (p + a) % 2, "l": (l + b) % 2, "c": (c + d) % 2}
        for a in range(2)
        for b in range(2)
        for d in range(2)
        if a + b + d > 0
    ]


class Return:
    def __init__(self, where, src, dst, send_sem, recv_sem):
        self.where = where[2:]
        self.src, self.dst, self.send_sem, self.recv_sem = src, dst, send_sem, recv_sem

    def stays(self, first, second, third, fourth):
        return (first == second) & (second == third) & (third == fourth)

    def local(self, c0):
        p, l, c = self.where
        return pltpu.make_async_copy(self.src.at[pl.ds(c0 * ROWS, ROWS)], self.dst.at[p], self.send_sem.at[c0])

    def remote(self, c0):
        p, l, c = self.where
        return pltpu.make_async_remote_copy(
            src_ref=self.src.at[pl.ds(c0 * ROWS, ROWS)],
            dst_ref=self.dst.at[p],
            send_sem=self.send_sem.at[c0],
            recv_sem=self.recv_sem.at[p],
            device_id={"p": l, "l": c, "c": c0},
            device_id_type=MESH,
        )

    def start(self):
        p, l, c = self.where
        for c0 in range(2):
            here = self.stays(p, l, c, c0)

            @pl.when(here)
            def _():
                self.local(c0).start()

            @pl.when(jnp.logical_not(here))
            def _():
                self.remote(c0).start()

    def wait(self):
        p, l, c = self.where
        for c0 in range(2):
            here = self.stays(p, l, c, c0)

            @pl.when(here)
            def _():
                self.local(c0).wait()

            @pl.when(jnp.logical_not(here))
            def _():
                self.remote(c0).wait_send()

        for seq in range(2):

            @pl.when(jnp.logical_not(self.stays(seq, p, l, c)))
            def _():
                pltpu.make_async_remote_copy(
                    src_ref=self.src.at[pl.ds(0, ROWS)],
                    dst_ref=self.dst.at[seq],
                    send_sem=self.send_sem.at[0],
                    recv_sem=self.recv_sem.at[seq],
                    device_id={"p": l, "l": c, "c": 1 - c},
                    device_id_type=MESH,
                ).wait_recv()


class Spread:
    def __init__(self, where, src, dst, send_sem, recv_sem):
        self.where = where[2:]
        self.src, self.dst, self.send_sem, self.recv_sem = src, dst, send_sem, recv_sem

    def here(self, first):
        p, l, c = self.where
        return (first == p) & (p == l) & (l == c)

    def local(self, seq):
        p, l, c = self.where
        return pltpu.make_async_copy(self.src.at[seq], self.dst.at[l, c], self.send_sem.at[seq])

    def remote(self, seq):
        p, l, c = self.where
        return pltpu.make_async_remote_copy(
            src_ref=self.src.at[seq],
            dst_ref=self.dst.at[l, c],
            send_sem=self.send_sem.at[seq],
            recv_sem=self.recv_sem.at[c],
            device_id={"p": seq, "l": p, "c": l},
            device_id_type=MESH,
        )

    def start(self):
        for seq in range(2):

            @pl.when(self.here(seq))
            def _():
                self.local(seq).start()

            @pl.when(jnp.logical_not(self.here(seq)))
            def _():
                self.remote(seq).start()

    def wait(self):
        p, l, c = self.where
        for seq in range(2):

            @pl.when(self.here(seq))
            def _():
                self.local(seq).wait()

            @pl.when(jnp.logical_not(self.here(seq)))
            def _():
                self.remote(seq).wait_send()

        for block in range(2):

            @pl.when(jnp.logical_not((l == p) & (c == l) & (block == c)))
            def _():
                pltpu.make_async_remote_copy(
                    src_ref=self.src.at[0],
                    dst_ref=self.dst.at[c, block],
                    send_sem=self.send_sem.at[0],
                    recv_sem=self.recv_sem.at[block],
                    device_id={"p": l, "l": c, "c": 1 - c},
                    device_id_type=MESH,
                ).wait_recv()


def turn(value):
    return pltpu.roll(value, HEAD_DIM // 2, 1)


def block_mask(key_dim, flags, index):
    shape = (BLK, BLK)
    key = lax.broadcasted_iota(jnp.int32, shape, key_dim)
    query = lax.broadcasted_iota(jnp.int32, shape, 1 - key_dim)
    upper = query // PIECE
    piece = jnp.where(upper == 0, flags[2 * index], flags[2 * index + 1])
    return (key <= query) | ((key // PIECE == upper) & (piece > 0))


PROJECT = 8


def attend_kernel(
    flags, x_ref, w_ref, ga_ref, gq_ref, gk_ref, cos_ref, sin_ref, woq, wgu_in, wdn_in,
    n_ref, q_ref, k_ref, v_ref, qr_ref, kr_ref, o_ref, lse_ref, wo, wgu, wdn,
    send_sem, recv_sem, local_sem,
):
    y, x, p, l, c = place()
    peer = peers_of(x, y, p, l, c)
    t = 2 * l + c
    net = Plan(send_sem, recv_sem)

    def chip(yy, xx, pp, ll):
        slot = (yy * 2 + xx) * 4 + 2 * pp + ll
        return in_place(wgu.at[:, rows_at(slot, 64)], wdn.at[rows_at(slot, 192)])

    def rows_of(q):
        return woq.at[rows_at(q, 512)], wo.at[:, rows_at(t, 256)]

    go_mlp_y = net.add(peer["y"], chip(y, x, p, l) + chip(y, 1 - x, p, l))
    go_mlp_x = net.add(peer["x"], chip(y, x, p, 1 - l) + chip(1 - y, x, p, 1 - l))
    go_far = net.add(peer["p"], chip(y, x, p, l))
    go_far_l = net.add(peer["l"], chip(y, x, 1 - p, l))
    go_wo_l = net.add(peer["l"], [rows_of(2 * (1 - l) + c)])
    go_wo_d = net.add(peer["d"], [rows_of(2 * (1 - l) + 1 - c)])
    go_wo_c = net.add(peer["c"], [rows_of(2 * l + 1 - c)])
    step = pl.program_id(0)

    @pl.when(step == 0)
    def _():
        greet(list(peer.values()))
        net.start(go_far, go_mlp_y, go_mlp_x, go_wo_l, go_wo_d, go_wo_c)
        copy = pltpu.make_async_copy(*rows_of(t), local_sem.at[0])
        copy.start()
        copy.wait()

    @pl.when(step < PROJECT)
    def _():
        value = x_ref[...].astype(jnp.float32)
        r = lax.rsqrt(jnp.mean(value * value, axis=-1, keepdims=True) + EPS)
        normed = (value * r * ga_ref[...]).astype(jnp.bfloat16)
        n_ref[...] = normed
        full = dot(normed, w_ref[...])
        cosine, sine = cos_ref[...], sin_ref[...]
        rows = rows_at(jnp.minimum(step, PROJECT - 1), 256)
        for h in range(QH + KH):
            u = full[:, h * HEAD_DIM : (h + 1) * HEAD_DIM]
            raw_ref, out_ref, g_ref, at = (qr_ref, q_ref, gq_ref, h) if h < QH else (kr_ref, k_ref, gk_ref, h - QH)
            raw_ref[at] = u
            n = u * lax.rsqrt(jnp.mean(u * u, axis=-1, keepdims=True) + EPS) * g_ref[...]
            out_ref[at, rows, :] = (n * cosine + turn(n) * sine).astype(jnp.bfloat16)
        for h in range(KH):
            at = (QH + KH + h) * HEAD_DIM
            v_ref[h, rows, :] = full[:, at : at + HEAD_DIM].astype(jnp.bfloat16)

    @pl.when(step == PROJECT + 4)
    def _():
        net.arrived(go_far)
        net.start(go_far_l)

    @pl.when(step >= PROJECT)
    def _():
        order = jnp.maximum(step - PROJECT, 0)
        g, i = order // NBLK, order % NBLK
        ones = jnp.ones((BLK, HEAD_DIM), jnp.bfloat16)
        mask = block_mask(1, flags, i)

        def values(j):
            return jnp.concatenate([v_ref[g, rows_at(j, BLK), :], ones], axis=1)

        queries = [q_ref[2 * g + h, rows_at(i, BLK), :] for h in range(2)]

        def part(j, masked):
            keys, both = k_ref[g, rows_at(j, BLK), :], values(j)
            found = []
            for q in queries:
                probs = jnp.exp2(dot(q, keys, NT) * (SCALE * LOG2E))
                if masked:
                    probs = jnp.where(mask, probs, 0.0)
                found.append(dot(probs.astype(jnp.bfloat16), both))
            return found

        def one(j, accs):
            return tuple(acc + more for acc, more in zip(accs, part(j, False)))

        accs = lax.fori_loop(0, i, one, tuple(part(i, True)))
        for h, acc in enumerate(accs):
            total = acc[:, HEAD_DIM:]
            o_ref[:, h * HEAD_DIM : (h + 1) * HEAD_DIM] = (acc[:, :HEAD_DIM] / total).astype(jnp.bfloat16)
            lse_ref[h] = jnp.log2(total).T[0:8, :]

    @pl.when(step == PROJECT + 2 * NBLK - 1)
    def _():
        net.arrived(go_mlp_y, go_mlp_x, go_far_l, go_wo_l, go_wo_d, go_wo_c)
        net.sent()


def attend(flags, x, w, ga, gq, gk, cosine, sine, woq, wgu, wdn):
    bf16, f32 = jnp.bfloat16, jnp.float32

    def early(s):
        return jnp.minimum(s, PROJECT - 1)

    def late(s):
        return jnp.maximum(s - PROJECT, 0)

    def row(width):
        return pl.BlockSpec((256, width), lambda s, f: (early(s), 0))

    def whole(shape):
        return pl.BlockSpec(shape, lambda s, f: (0,) * len(shape))

    def heads(n):
        return pl.BlockSpec((n, 256, HEAD_DIM), lambda s, f: (0, early(s), 0))

    def shape(n, dtype):
        return jax.ShapeDtypeStruct((n, SEQ_ROWS, HEAD_DIM), dtype)

    any_spec = pl.BlockSpec(memory_space=pl.ANY)
    copies = 20
    return pl.pallas_call(
        attend_kernel,
        out_shape=(
            jax.ShapeDtypeStruct((SEQ_ROWS, MODEL_DIM), bf16),
            shape(QH, bf16),
            shape(KH, bf16),
            shape(KH, bf16),
            shape(QH, f32),
            shape(KH, f32),
            jax.ShapeDtypeStruct((SEQ_ROWS, QH * HEAD_DIM), bf16),
            jax.ShapeDtypeStruct((QH, 8, SEQ_ROWS), f32),
            jax.ShapeDtypeStruct((512, MODEL_DIM), bf16),
            jax.ShapeDtypeStruct(wgu.shape, bf16),
            jax.ShapeDtypeStruct(wdn.shape, bf16),
        ),
        grid_spec=pltpu.PrefetchScalarGridSpec(
            num_scalar_prefetch=1,
            grid=(PROJECT + KH * NBLK,),
            in_specs=[row(MODEL_DIM), whole(w.shape), whole(ga.shape), whole(gq.shape), whole(gk.shape), row(HEAD_DIM), row(HEAD_DIM)]
            + [any_spec] * 3,
            out_specs=[
                row(MODEL_DIM),
                whole((QH, SEQ_ROWS, HEAD_DIM)),
                whole((KH, SEQ_ROWS, HEAD_DIM)),
                whole((KH, SEQ_ROWS, HEAD_DIM)),
                heads(QH),
                heads(KH),
                pl.BlockSpec((BLK, 2 * HEAD_DIM), lambda s, f: (late(s) % NBLK, late(s) // NBLK)),
                pl.BlockSpec((2, 8, BLK), lambda s, f: (late(s) // NBLK, 0, late(s) % NBLK)),
            ]
            + [any_spec] * 3,
            scratch_shapes=[pltpu.SemaphoreType.DMA((copies,))] * 2 + [pltpu.SemaphoreType.DMA((1,))],
        ),
        input_output_aliases={9: 9, 10: 10},
        compiler_params=pltpu.CompilerParams(
            collective_id=2, has_side_effects=True, vmem_limit_bytes=48 * 1024 * 1024
        ),
        cost_estimate=pl.CostEstimate(
            flops=4 * QH * SEQ_ROWS * SEQ_ROWS * HEAD_DIM, bytes_accessed=24 << 20, transcendentals=QH * SEQ_ROWS * SEQ_ROWS
        ),
        name="attend",
    )(flags, x, w, ga, gq, gk, cosine, sine, woq, wgu, wdn)


def resid_kernel(
    attn, wo, g_mlp, xs, cot, wgu_in, wdn_in,
    resid, mlp_in, wgu, wdn, wdx, wdo, dy,
    send_c, recv_c, send_l, recv_l, keep, x_own, send_sem, recv_sem, local_sem, dy_send, dy_recv,
):
    where = place()
    y, x, p, l, c = where
    peer = peers_of(x, y, p, l, c)
    net = Plan(send_sem, recv_sem)

    def chip(yy, xx, pp, ll):
        slot = (yy * 2 + xx) * 4 + 2 * pp + ll
        return in_place(wgu.at[:, rows_at(slot, 64)], wdn.at[rows_at(slot, 192)])

    def down(pp, ll):
        found = []
        for xx in range(2):
            slot = xx * 4 + 2 * pp + ll
            found.append((wdn.at[rows_at((1 - c) * 8 + slot, 192)], wdx.at[rows_at(slot, 192)]))
        return found

    go_far_x = net.add(peer["x"], chip(y, x, 1 - p, l))
    go_far_y = net.add(peer["y"], chip(y, x, 1 - p, l) + chip(y, 1 - x, 1 - p, l))
    go_fal_y = net.add(peer["y"], chip(y, x, 1 - p, 1 - l))
    go_fal_x = net.add(peer["x"], chip(y, x, 1 - p, 1 - l) + chip(1 - y, x, 1 - p, 1 - l))
    go_down_me = net.add(peer["c"], down(p, l))
    go_down_near = net.add(peer["c"], down(p, 1 - l))
    go_down_far = net.add(peer["c"], down(1 - p, l))
    go_down_fal = net.add(peer["c"], down(1 - p, 1 - l))
    go_give_0 = net.add(peer["c"], [(send_c.at[0], recv_c.at[0])])
    go_give_1 = net.add(peer["c"], [(send_c.at[1], recv_c.at[1])])
    go_cross = net.add(peer["l"], [(send_l, recv_l)])
    go_share = net.add(peer["c"], in_place(mlp_in.at[c]))
    go_dy_c = net.add(peer["c"], in_place(dy.at[c]))
    spread = Spread(where, cot, dy, dy_send, dy_recv)
    greet(line_peers(p, l, c) + [peer["x"], peer["y"]])
    net.start(go_far_x, go_fal_y, go_down_me, go_down_near)
    fetch = pltpu.make_async_copy(xs.at[rows_at(2 * l + c, OWN)], x_own, local_sem.at[0])
    fetch.start()
    own_down = pltpu.make_async_copy(wdn.at[rows_at(c, HALF_FF)], wdo, local_sem.at[1])

    def project(ll, cc, write):
        part = attn[rows_at(2 * ll + cc, OWN), :]

        def chunk(k, carry):
            cols = rows_at(k, 256)
            write(cols, dot(part, wo[:, cols]))
            return carry

        lax.fori_loop(0, 4, chunk, 0)

    def give(k):
        def write(cols, value):
            send_c[k, :, cols] = value.astype(jnp.bfloat16)

        return write

    def hold(k):
        def write(cols, value):
            keep[k, :, cols] = value

        return write

    project(1 - l, 1 - c, give(0))
    net.start(go_give_0)
    project(1 - l, c, hold(0))
    net.arrived(go_give_0)
    send_l[...] = (keep[0] + recv_c[0].astype(jnp.float32)).astype(jnp.bfloat16)
    net.start(go_cross)
    spread.start()
    project(l, 1 - c, give(1))
    net.start(go_give_1)
    project(l, c, hold(1))
    fetch.wait()
    net.arrived(go_far_x)
    net.start(go_far_y)
    net.arrived(go_fal_y)
    net.start(go_fal_x)
    net.arrived(go_give_1)
    keep[1] += recv_c[1].astype(jnp.float32) + x_own[...].astype(jnp.float32)
    net.arrived(go_cross)
    total = keep[1] + recv_l[...].astype(jnp.float32)
    resid[...] = total
    r = lax.rsqrt(jnp.mean(total * total, axis=-1, keepdims=True) + EPS)
    mlp_in[c] = (total * r * g_mlp[...]).astype(jnp.bfloat16)
    net.start(go_share)
    net.arrived(go_far_y)
    net.start(go_down_far)
    spread.wait()
    net.start(go_dy_c)
    net.arrived(go_fal_x)
    net.start(go_down_fal)
    own_down.start()
    net.arrived(go_down_me, go_down_near, go_down_far, go_down_fal, go_share, go_dy_c)
    own_down.wait()
    net.sent()


def finish_resid(attn, wo, g_mlp, xs, cot, wgu, wdn):
    bf16, f32 = jnp.bfloat16, jnp.float32
    any_spec = pl.BlockSpec(memory_space=pl.ANY)
    vmem = pl.BlockSpec(memory_space=pltpu.VMEM)
    copies = 32
    return pl.pallas_call(
        resid_kernel,
        out_shape=(
            jax.ShapeDtypeStruct((OWN, MODEL_DIM), f32),
            jax.ShapeDtypeStruct((2, OWN, MODEL_DIM), bf16),
            jax.ShapeDtypeStruct(wgu.shape, bf16),
            jax.ShapeDtypeStruct(wdn.shape, bf16),
            jax.ShapeDtypeStruct((HALF_FF, 512), bf16),
            jax.ShapeDtypeStruct((HALF_FF, 512), bf16),
            jax.ShapeDtypeStruct((2, 2, ROWS, MODEL_DIM), bf16),
        ),
        in_specs=[vmem] * 3 + [any_spec] * 4,
        out_specs=[vmem] * 2 + [any_spec] * 5,
        scratch_shapes=[
            pltpu.VMEM((2, OWN, MODEL_DIM), bf16),
            pltpu.VMEM((2, OWN, MODEL_DIM), bf16),
            pltpu.VMEM((OWN, MODEL_DIM), bf16),
            pltpu.VMEM((OWN, MODEL_DIM), bf16),
            pltpu.VMEM((2, OWN, MODEL_DIM), f32),
            pltpu.VMEM((OWN, MODEL_DIM), bf16),
            pltpu.SemaphoreType.DMA((copies,)),
            pltpu.SemaphoreType.DMA((copies,)),
            pltpu.SemaphoreType.DMA((2,)),
            pltpu.SemaphoreType.DMA((2,)),
            pltpu.SemaphoreType.DMA((2,)),
        ],
        input_output_aliases={5: 2, 6: 3},
        compiler_params=pltpu.CompilerParams(
            collective_id=3, has_side_effects=True, vmem_limit_bytes=48 * 1024 * 1024
        ),
        name="residual",
    )(attn, wo, g_mlp, xs, cot, wgu, wdn)


CHUNK = 512


def forward_kernel(
    m_ref, dy_ref, w_ref, wo_ref, wx_ref, resid, g_mlp,
    gg, gu, gd, d_resid, db, res, dg,
    mt, dyt, hid, dgt, dup, d_in, down, give, take, send_sem, recv_sem,
):
    y, x, p, l, c = place()
    peer = {"c": 1 - c}
    net = Plan(send_sem, recv_sem)
    go_d_in = net.add(peer, [(give.at[0], take.at[0])])
    go_down = net.add(peer, [(give.at[1], take.at[1])])
    step = pl.program_id(0)

    @pl.when(step == 0)
    def _():
        greet([peer])

        def flip(k, carry):
            rows = rows_at(k, 256)
            mt[:, rows] = m_ref[rows, :].T
            dyt[:, rows] = dy_ref[rows, :].T
            return carry

        lax.fori_loop(0, 4, flip, 0)
        d_in[...] = jnp.zeros_like(d_in)
        down[...] = jnp.zeros_like(down)

    own_cols, other_cols = rows_at(c, 512), rows_at(1 - c, 512)

    def part(r, carry):
        rows = rows_at(r, 256)
        value, grad = m_ref[rows, :], dy_ref
        gate, up = dot(value, w_ref[0]), dot(value, w_ref[1])
        d_hidden = dot(grad[rows, own_cols], wo_ref[...], NT) + dot(grad[rows, other_cols], wx_ref[...], NT)
        s = 1.0 / (1.0 + jnp.exp(-gate))
        silu = gate * s
        hidden = (silu * up).astype(jnp.bfloat16)
        d_up = (d_hidden * silu).astype(jnp.bfloat16)
        d_gate = (d_hidden * up * (s * (1.0 + gate * (1.0 - s)))).astype(jnp.bfloat16)
        hid[rows, :] = hidden
        dup[rows, :] = d_up
        dgt[rows, :] = d_gate
        d_in[rows, :] += dot(d_gate, w_ref[0], NT) + dot(d_up, w_ref[1], NT)
        down[rows, own_cols] += dot(hidden, wo_ref[...])
        down[rows, other_cols] += dot(hidden, wx_ref[...])
        return carry

    lax.fori_loop(0, 4, part, 0)

    @pl.when(step == pl.num_programs(0) - 1)
    def _():
        give[0] = d_in[rows_at(1 - c, OWN), :].astype(jnp.bfloat16)
        give[1] = down[rows_at(1 - c, OWN), :].astype(jnp.bfloat16)
        net.start(go_d_in, go_down)

    def weights(k, carry):
        rows = rows_at(k, 256)
        gg[rows, :] = dot(mt[rows, :], dgt[...]).astype(jnp.bfloat16)
        gu[rows, :] = dot(mt[rows, :], dup[...]).astype(jnp.bfloat16)
        gd[:, rows] = dot(dyt[rows, :], hid[...]).T.astype(jnp.bfloat16)
        return carry

    lax.fori_loop(0, 4, weights, 0)

    @pl.when(step == pl.num_programs(0) - 1)
    def _():
        net.arrived(go_d_in, go_down)
        dg[...] = jnp.zeros_like(dg)

        def finish(k, carry):
            rows = rows_at(k, 64)
            here = pl.ds(pl.multiple_of(c * OWN + k * 64, 64), 64)
            value = resid[rows, :]
            grad = d_in[here, :] + take[0, rows, :].astype(jnp.float32)
            r = lax.rsqrt(jnp.mean(value * value, axis=-1, keepdims=True) + EPS)
            scaled = value * r
            gained = grad * g_mlp[...]
            total = dy_ref[here, :].astype(jnp.float32) + r * (gained - scaled * jnp.mean(scaled * gained, axis=-1, keepdims=True))
            d_resid[rows, :] = total
            db[rows, :] = total.astype(jnp.bfloat16)
            dg[...] += jnp.sum((grad * scaled).reshape(-1, 8, MODEL_DIM), axis=0)
            res[rows, :] = (value + down[here, :] + take[1, rows, :].astype(jnp.float32)).astype(jnp.bfloat16)
            return carry

        lax.fori_loop(0, 8, finish, 0)
        net.sent()


def feed_forward(mlp_in, dy, wgu, wdo, wdx, resid, g_mlp):
    bf16, f32 = jnp.bfloat16, jnp.float32

    def whole(shape):
        return pl.BlockSpec(shape, lambda f: (0,) * len(shape), pipeline_mode=pl.Buffered(1))

    down = pl.BlockSpec((CHUNK, 512), lambda f: (f, 0))
    wide = pl.BlockSpec((MODEL_DIM, CHUNK), lambda f: (0, f))
    rows = (1024, MODEL_DIM)
    own = (OWN, MODEL_DIM)
    return pl.pallas_call(
        forward_kernel,
        grid=(HALF_FF // CHUNK,),
        out_shape=(
            jax.ShapeDtypeStruct((MODEL_DIM, HALF_FF), bf16),
            jax.ShapeDtypeStruct((MODEL_DIM, HALF_FF), bf16),
            jax.ShapeDtypeStruct((HALF_FF, MODEL_DIM), bf16),
            jax.ShapeDtypeStruct(own, f32),
            jax.ShapeDtypeStruct(own, bf16),
            jax.ShapeDtypeStruct(own, bf16),
            jax.ShapeDtypeStruct((8, MODEL_DIM), f32),
        ),
        in_specs=[whole(rows), whole(rows), pl.BlockSpec((2, MODEL_DIM, CHUNK), lambda f: (0, 0, f)), down, down]
        + [whole(own), whole((1, MODEL_DIM))],
        out_specs=[wide, wide, pl.BlockSpec((CHUNK, MODEL_DIM), lambda f: (f, 0))]
        + [whole(own), whole(own), whole(own), whole((8, MODEL_DIM))],
        scratch_shapes=[
            pltpu.VMEM(rows, bf16),
            pltpu.VMEM(rows, bf16),
            pltpu.VMEM((1024, CHUNK), bf16),
            pltpu.VMEM((1024, CHUNK), bf16),
            pltpu.VMEM((1024, CHUNK), bf16),
            pltpu.VMEM(rows, f32),
            pltpu.VMEM(rows, f32),
            pltpu.VMEM((2,) + own, bf16),
            pltpu.VMEM((2,) + own, bf16),
            pltpu.SemaphoreType.DMA((2,)),
            pltpu.SemaphoreType.DMA((2,)),
        ],
        compiler_params=pltpu.CompilerParams(
            collective_id=6, has_side_effects=True, vmem_limit_bytes=56 * 1024 * 1024
        ),
        name="feed_forward",
    )(mlp_in, dy, wgu, wdo, wdx, resid, g_mlp)


KINDS = ME, NEAR, FAR, FAL = range(4)


def chip_slot(yy, xx, pp, ll):
    return (yy * 2 + xx) * 4 + 2 * pp + ll


class Reduction:
    def __init__(self, where):
        y, x, p, l, c = where
        self.z = ((p, l), (p, 1 - l), (1 - p, l), (1 - p, 1 - l))
        self.y, self.x = y, x

    def y_first(self, kind):
        return kind in (ME, FAR)

    def first_peer(self, kind):
        return "y" if self.y_first(kind) else "x"

    def second_peer(self, kind):
        return "x" if self.y_first(kind) else "y"

    def place(self, kind, index, given):
        if self.y_first(kind):
            return (1 - self.y if given else self.y), index
        return index, (1 - self.x if given else self.x)

    def kept(self, kind):
        return self.x if self.y_first(kind) else self.y


def attend_back_kernel(
    flags, q_in, k_in, v_in, o_in, db_in, wo_in, lse_in, qr_in, kr_in, cos_in, sin_in, gg, gu, gd, res, gq_ref, gk_ref,
    d_out, goq, fw_out, fd_out, od_out, out, dg_ref,
    q_ref, k_ref, v_ref, o_ref, dall, wo, lse_ref, qr_ref, kr_ref, cos_ref, sin_ref,
    da, delta, dbuf, dq_acc, dk_acc, dv_acc, og, gdb, od, rb, rbd, rc, rcd, rz, rzd, go,
    send_sem, recv_sem, load_sem, own_sem, out_sem, back_send, back_recv,
):
    where = place()
    y, x, p, l, c = where
    peer = peers_of(x, y, p, l, c)
    red = Reduction(where)
    net = Plan(send_sem, recv_sem)
    wide_of, deep_of, second_of = {}, {}, {}
    t = 2 * l + c

    def block(index):
        return dall.at[rows_at(index, OWN)]

    go_db_l = net.add(peer["l"], [(db_in, block(t))])
    go_db_c = net.add(peer["c"], [(db_in, block(t))])
    go_db_r = net.add(peer["c"], in_place(block(2 * (1 - l) + c)))
    go_gd_c = net.add(peer["c"], [(gd.at[:, rows_at(1 - c, 512)], gdb.at[c])])
    go_fal = net.add(peer["l"], [(og.at[1, red.kept(FAL)], rz), (od.at[3, red.kept(FAL)], rzd)])
    for n, kind in enumerate(KINDS):
        wide, deep = [], []
        for k in range(2):
            yy, xx = red.place(kind, k, True)
            slot = chip_slot(yy, xx, *red.z[kind])
            if n >= 2:
                wide.append((gg.at[rows_at(slot, 64)], rb.at[n - 2, k, 0]))
                wide.append((gu.at[rows_at(slot, 64)], rb.at[n - 2, k, 1]))
            deep.append((gdb.at[yy, rows_at(xx * 4 + 2 * red.z[kind][0] + red.z[kind][1], 192)], rbd.at[n, k]))
        deep_of[kind] = net.add(peer[red.first_peer(kind)], deep)
        if n >= 2:
            wide_of[kind] = net.add(peer[red.first_peer(kind)], wide)
            away = 1 - red.kept(kind)
            second_of[kind] = net.add(peer[red.second_peer(kind)], [(og.at[n - 2, away], rc.at[n - 2]), (od.at[n, away], rcd.at[n - 2])])
    home = Return(where, res, out, back_send, back_recv)

    def columns(q):
        return [(go.at[:, rows_at(q, 256)], goq.at[rows_at(t, 512)])]

    go_go_l = net.add(peer["l"], columns(2 * (1 - l) + c))
    go_go_d = net.add(peer["d"], columns(2 * (1 - l) + 1 - c))
    go_go_c = net.add(peer["c"], columns(2 * l + 1 - c))
    own_go = pltpu.make_async_copy(*columns(t)[0], out_sem.at[1])
    loads = [
        pltpu.make_async_copy(src, dst, load_sem.at[k])
        for k, (src, dst) in enumerate(
            [
                (db_in, block(t)), (wo_in, wo), (o_in, o_ref), (q_in, q_ref), (k_in, k_ref), (v_in, v_ref), (lse_in, lse_ref),
                (cos_in, cos_ref), (sin_in, sin_ref), (qr_in, qr_ref), (kr_in, kr_ref),
                (gd.at[:, rows_at(c, 512)], gdb.at[c]),
            ]
        )
    ]
    own = []
    for n, kind in enumerate(KINDS[2:]):
        for k in range(2):
            slot = chip_slot(*red.place(kind, k, False), *red.z[kind])
            for m, ref in enumerate((gg, gu)):
                own.append(pltpu.make_async_copy(ref.at[rows_at(slot, 64)], og.at[n, k, m], own_sem.at[len(own)]))

    def wide_sum(kind):
        n = KINDS.index(kind) - 2
        for k in range(2):

            def wide(r, carry):
                rows = rows_at(r, 16)
                for m in range(2):
                    total = og[n, k, m, rows, :].astype(jnp.float32) + rb[n, k, m, rows, :].astype(jnp.float32)
                    og[n, k, m, rows, :] = total.astype(jnp.bfloat16)
                return carry

            lax.fori_loop(0, 4, wide, 0)

    def deep_sum(kind):
        n = KINDS.index(kind)
        for k in range(2):
            yy, xx = red.place(kind, k, False)
            at = (xx * 4 + 2 * red.z[kind][0] + red.z[kind][1]) * 192

            def deep(r, carry):
                rows = rows_at(r, 32)
                mine = gdb[yy, pl.ds(pl.multiple_of(at + r * 32, 32), 32), :]
                od[n, k, rows, :] = (mine.astype(jnp.float32) + rbd[n, k, rows, :].astype(jnp.float32)).astype(jnp.bfloat16)
                return carry

            lax.fori_loop(0, 6, deep, 0)

    def more(kind, wide, deep):
        n, u = KINDS.index(kind), red.kept(kind)
        og[n - 2, u] = (og[n - 2, u].astype(jnp.float32) + wide.astype(jnp.float32)).astype(jnp.bfloat16)
        od[n, u] = (od[n, u].astype(jnp.float32) + deep.astype(jnp.float32)).astype(jnp.bfloat16)

    def branch(index):
        rows = rows_at(index, OWN)
        value = dot(dall[rows, :], wo[...], NT).astype(jnp.bfloat16)
        da[rows, :] = value
        for h in range(QH):
            cols = slice(h * HEAD_DIM, (h + 1) * HEAD_DIM)
            prod = value[:, cols].astype(jnp.float32) * o_ref[rows, cols].astype(jnp.float32)
            delta[h, :, rows] = jnp.broadcast_to(jnp.sum(prod.T, axis=0, keepdims=True), (8, BLK))

    def unrope(grad, u, gain, rows):
        grad = grad * SCALE
        e = grad * cos_ref[rows, :] + turn(grad * sin_ref[rows, :])
        r = lax.rsqrt(jnp.mean(u * u, axis=-1, keepdims=True) + EPS)
        ur = u * r
        ge = e * gain
        d = r * (ge - ur * jnp.mean(ur * ge, axis=-1, keepdims=True))
        return d.astype(jnp.bfloat16), jnp.sum((e * ur).reshape(-1, 8, HEAD_DIM), axis=0)

    step = pl.program_id(0)
    b, g = step // KH, step % KH
    i = 2 * ((l + b // 2) % 2) + b % 2

    @pl.when(step == 0)
    def _():
        for copy in loads:
            copy.start()
        greet(line_peers(p, l, c) + [peer["x"], peer["y"]])
        net.start(go_db_l, go_db_c, go_gd_c, wide_of[FAR], wide_of[FAL])
        home.start()
        for copy in own:
            copy.start()
        dk_acc[...] = jnp.zeros_like(dk_acc)
        dv_acc[...] = jnp.zeros_like(dv_acc)
        dg_ref[...] = jnp.zeros_like(dg_ref)
        for copy in loads[:3]:
            copy.wait()
        branch(t)
        loads[-1].wait()
        net.arrived(go_gd_c)
        net.start(deep_of[FAR], deep_of[FAL])
        net.arrived(go_db_c)
        branch(2 * l + 1 - c)
        for copy in loads[3:-1]:
            copy.wait()

    @pl.when(step == 2 * KH)
    def _():
        net.arrived(go_db_l)
        net.start(go_db_r)
        branch(2 * (1 - l) + c)
        for copy in own:
            copy.wait()
        for kind in (FAR, FAL):
            net.arrived(wide_of[kind], deep_of[kind])
            wide_sum(kind)
            deep_sum(kind)
            net.start(second_of[kind])
        net.arrived(go_db_r)
        branch(2 * (1 - l) + 1 - c)

    @pl.when(step == 3 * KH)
    def _():
        net.arrived(second_of[FAL])
        more(FAL, rc[1], rcd[1])
        net.start(go_fal)
        net.arrived(second_of[FAR])
        more(FAR, rc[0], rcd[0])
        net.start(deep_of[ME], deep_of[NEAR])

        def grad_out(k, carry):
            cols = rows_at(k, 256)
            go[cols, :] = dot(o_ref[:, cols], dall[...], TN).astype(jnp.bfloat16)
            return carry

        lax.fori_loop(0, 2, grad_out, 0)
        net.start(go_go_l, go_go_d, go_go_c)
        own_go.start()

    dq_acc[...] = jnp.zeros_like(dq_acc)
    rows = rows_at(i, BLK)
    heads = [2 * g + n for n in range(2)]
    spans = [rows_at(h, HEAD_DIM) for h in heads]
    queries = [q_ref[h, rows, :] for h in heads]
    grads = [da[rows, span] for span in spans]

    def tile(j, mask=None):
        keys = rows_at(j, BLK)
        k, v = k_ref[g, keys, :], v_ref[g, keys, :]
        dv, dk = None, None
        for n, h in enumerate(heads):
            probs = jnp.exp2(dot(k, queries[n], NT) * (SCALE * LOG2E) - lse_ref[h, 0:1, rows])
            if mask is not None:
                probs = jnp.where(mask, probs, 0.0)
            d_scores = (probs * (dot(v, grads[n], NT) - delta[h, 0:1, rows])).astype(jnp.bfloat16)
            dv_more, dk_more = dot(probs.astype(jnp.bfloat16), grads[n]), dot(d_scores, queries[n])
            dv, dk = (dv_more, dk_more) if dv is None else (dv + dv_more, dk + dk_more)
            dq_acc[n] += dot(d_scores, k, TN)
        dv_acc[g, keys, :] += dv
        dk_acc[g, keys, :] += dk

    def loop(j, carry):
        tile(j)
        return carry

    tile(i, block_mask(0, flags, i))
    lax.fori_loop(0, i, loop, 0)
    for n, h in enumerate(heads):
        low, total = unrope(dq_acc[n], qr_ref[h, rows, :], gq_ref[...], rows)
        dbuf[rows, spans[n]] = low
        dg_ref[0] += total

    @pl.when(step == 4 * KH - 1)
    def _():
        for gg_at in range(KH):

            def finish(r, carry):
                rows = rows_at(r, 256)
                low, total = unrope(dk_acc[gg_at, rows, :], kr_ref[gg_at, rows, :], gk_ref[...], rows)
                dbuf[rows, pl.ds((QH + gg_at) * HEAD_DIM, HEAD_DIM)] = low
                dbuf[rows, pl.ds((QH + KH + gg_at) * HEAD_DIM, HEAD_DIM)] = dv_acc[gg_at, rows, :].astype(jnp.bfloat16)
                dg_ref[1] += total
                return carry

            lax.fori_loop(0, 8, finish, 0)
        outs = [pltpu.make_async_copy(dbuf, d_out, out_sem.at[0])]
        outs[0].start()
        for kind in (ME, NEAR):
            net.arrived(deep_of[kind])
            deep_sum(kind)
        net.arrived(go_fal)
        more(FAR, rz[...], rzd[...])
        u = red.kept(FAR)
        outs += [
            pltpu.make_async_copy(og.at[0, u], fw_out, out_sem.at[2]),
            pltpu.make_async_copy(od.at[2, u], fd_out, out_sem.at[3]),
            pltpu.make_async_copy(od.at[pl.ds(0, 2)], od_out, out_sem.at[4]),
        ]
        for copy in outs[1:]:
            copy.start()
        net.arrived(go_go_l, go_go_d, go_go_c)
        own_go.wait()
        net.sent()
        home.wait()
        for copy in outs:
            copy.wait()


def attend_back(flags, q, k, v, o, db, wo, lse, qr, kr, cosine, sine, gg, gu, gd, res, gq, gk):
    bf16, f32 = jnp.bfloat16, jnp.float32
    any_spec = pl.BlockSpec(memory_space=pl.ANY)
    gain = pl.BlockSpec((1, HEAD_DIM), lambda s, f: (0, 0))
    copies = 40

    def vm(a):
        return pltpu.VMEM(a.shape, a.dtype)

    return pl.pallas_call(
        attend_back_kernel,
        out_shape=(
            jax.ShapeDtypeStruct((SEQ_ROWS, 1024), bf16),
            jax.ShapeDtypeStruct((2048, 256), bf16),
            jax.ShapeDtypeStruct((2, 64, HALF_FF), bf16),
            jax.ShapeDtypeStruct((192, 512), bf16),
            jax.ShapeDtypeStruct((2, 2, 192, 512), bf16),
            jax.ShapeDtypeStruct((2, ROWS, MODEL_DIM), bf16),
            jax.ShapeDtypeStruct((2, 8, HEAD_DIM), f32),
        ),
        grid_spec=pltpu.PrefetchScalarGridSpec(
            num_scalar_prefetch=1,
            grid=(4 * KH,),
            in_specs=[any_spec] * 15 + [gain] * 2,
            out_specs=[any_spec] * 6 + [pl.BlockSpec((2, 8, HEAD_DIM), lambda s, f: (0, 0, 0))],
            scratch_shapes=[vm(q), vm(k), vm(v), vm(o), pltpu.VMEM((SEQ_ROWS, MODEL_DIM), bf16), vm(wo), vm(lse), vm(qr), vm(kr)]
            + [vm(cosine), vm(sine)]
            + [
                pltpu.VMEM((SEQ_ROWS, QH * HEAD_DIM), bf16),
                pltpu.VMEM((QH, 8, SEQ_ROWS), f32),
                pltpu.VMEM((SEQ_ROWS, 1024), bf16),
                pltpu.VMEM((2, BLK, HEAD_DIM), f32),
                pltpu.VMEM((KH, SEQ_ROWS, HEAD_DIM), f32),
                pltpu.VMEM((KH, SEQ_ROWS, HEAD_DIM), f32),
                pltpu.VMEM((2, 2, 2, 64, HALF_FF), bf16),
                pltpu.VMEM((2, HALF_FF, 512), bf16),
                pltpu.VMEM((4, 2, 192, 512), bf16),
                pltpu.VMEM((2, 2, 2, 64, HALF_FF), bf16),
                pltpu.VMEM((4, 2, 192, 512), bf16),
                pltpu.VMEM((2, 2, 64, HALF_FF), bf16),
                pltpu.VMEM((2, 192, 512), bf16),
                pltpu.VMEM((2, 64, HALF_FF), bf16),
                pltpu.VMEM((192, 512), bf16),
                pltpu.VMEM((512, MODEL_DIM), bf16),
                pltpu.SemaphoreType.DMA((copies,)),
                pltpu.SemaphoreType.DMA((copies,)),
                pltpu.SemaphoreType.DMA((12,)),
                pltpu.SemaphoreType.DMA((8,)),
                pltpu.SemaphoreType.DMA((5,)),
                pltpu.SemaphoreType.DMA((2,)),
                pltpu.SemaphoreType.DMA((2,)),
            ],
        ),
        compiler_params=pltpu.CompilerParams(
            collective_id=4, has_side_effects=True, vmem_limit_bytes=58 * 1024 * 1024
        ),
        cost_estimate=pl.CostEstimate(
            flops=10 * QH * SEQ_ROWS * SEQ_ROWS * HEAD_DIM, bytes_accessed=40 << 20, transcendentals=QH * SEQ_ROWS * SEQ_ROWS
        ),
        name="attend_back",
    )(flags, q, k, v, o, db, wo, lse, qr, kr, cosine, sine, gg, gu, gd, res, gq, gk)


def normed_kernel(
    d_in, w_in, n_in, xs, gg, gu, fw_in, fd_in, od_in, dr_ref, ga_ref,
    gt, dg, pq, me_w, me_d, near_w, near_d,
    d_ref, w_ref, n_ref, x_ref, send_c, recv_c, send_l, recv_l, keep, og, rb, od, rx, rxd, rz, rzd,
    send_sem, recv_sem, load_sem, own_sem,
):
    where = place()
    y, x, p, l, c = where
    peer = peers_of(x, y, p, l, c)
    red = Reduction(where)
    net = Plan(send_sem, recv_sem)
    wide_of, deep_of, second_of = {}, {}, {}
    t = 2 * l + c
    two = KINDS[:2]
    own = []
    for n, kind in enumerate(two):
        wide = []
        for k in range(2):
            away = chip_slot(*red.place(kind, k, True), *red.z[kind])
            here = chip_slot(*red.place(kind, k, False), *red.z[kind])
            for m, ref in enumerate((gg, gu)):
                wide.append((ref.at[rows_at(away, 64)], rb.at[n, k, m]))
                own.append(pltpu.make_async_copy(ref.at[rows_at(here, 64)], og.at[n, k, m], own_sem.at[len(own)]))
        wide_of[kind] = net.add(peer[red.first_peer(kind)], wide)
        away = 1 - red.kept(kind)
        second_of[kind] = net.add(peer[red.second_peer(kind)], [(og.at[n, away], rx.at[n]), (od_in.at[n, away], rxd.at[n])])
    go_far = net.add(peer["p"], [(fw_in, rz), (fd_in, rzd)])
    go_give_0 = net.add(peer["c"], [(send_c.at[0], recv_c.at[0])])
    go_give_1 = net.add(peer["c"], [(send_c.at[1], recv_c.at[1])])
    go_cross = net.add(peer["l"], [(send_l, recv_l)])

    loads = [
        pltpu.make_async_copy(src, dst, load_sem.at[k])
        for k, (src, dst) in enumerate([(d_in, d_ref), (w_in, w_ref), (n_in, n_ref), (od_in, od), (xs.at[rows_at(t, OWN)], x_ref)])
    ]
    for copy in loads:
        copy.start()
    for copy in own:
        copy.start()
    greet(list(peer.values()))
    net.start(wide_of[ME], wide_of[NEAR], go_far)

    def project(ll, cc, write):
        part = d_ref[rows_at(2 * ll + cc, OWN), :]

        def chunk(k, carry):
            cols = rows_at(k, 256)
            write(cols, dot(part, w_ref[cols, :], NT))
            return carry

        lax.fori_loop(0, 4, chunk, 0)

    def give(k):
        def write(cols, value):
            send_c[k, :, cols] = value.astype(jnp.bfloat16)

        return write

    def hold(k):
        def write(cols, value):
            keep[k, :, cols] = value

        return write

    loads[0].wait()
    loads[1].wait()
    project(1 - l, 1 - c, give(0))
    net.start(go_give_0)
    project(1 - l, c, hold(0))
    net.arrived(go_give_0)
    send_l[...] = (keep[0] + recv_c[0].astype(jnp.float32)).astype(jnp.bfloat16)
    net.start(go_cross)
    project(l, 1 - c, give(1))
    net.start(go_give_1)
    project(l, c, hold(1))
    for copy in own:
        copy.wait()
    for copy in loads[2:]:
        copy.wait()
    for n, kind in enumerate(two):
        net.arrived(wide_of[kind])
        for k in range(2):

            def wide(r, carry):
                rows = rows_at(r, 16)
                for m in range(2):
                    total = og[n, k, m, rows, :].astype(jnp.float32) + rb[n, k, m, rows, :].astype(jnp.float32)
                    og[n, k, m, rows, :] = total.astype(jnp.bfloat16)
                return carry

            lax.fori_loop(0, 4, wide, 0)
        net.start(second_of[kind])

    def grad_qkv(k, carry):
        cols = rows_at(k, 256)
        pq[cols, :] = dot(n_ref[:, cols], d_ref[...], TN).astype(jnp.bfloat16)
        return carry

    lax.fori_loop(0, 4, grad_qkv, 0)
    net.arrived(go_give_1, go_cross)

    dg[...] = jnp.zeros_like(dg)

    def rows_back(k, carry):
        rows = rows_at(k, 64)
        value = x_ref[rows, :].astype(jnp.float32)
        grad = keep[1, rows, :] + recv_c[1, rows, :].astype(jnp.float32) + recv_l[rows, :].astype(jnp.float32)
        r = lax.rsqrt(jnp.mean(value * value, axis=-1, keepdims=True) + EPS)
        scaled = value * r
        gained = grad * ga_ref[...]
        back = r * (gained - scaled * jnp.mean(scaled * gained, axis=-1, keepdims=True))
        gt[rows, :] = (dr_ref[rows, :] + back).astype(jnp.bfloat16)
        dg[...] += jnp.sum((grad * scaled).reshape(-1, 8, MODEL_DIM), axis=0)
        return carry

    lax.fori_loop(0, 8, rows_back, 0)
    net.arrived(second_of[NEAR])
    u = red.kept(NEAR)
    near_w[...] = (og[1, u].astype(jnp.float32) + rx[1].astype(jnp.float32)).astype(jnp.bfloat16)
    near_d[...] = (od[1, u].astype(jnp.float32) + rxd[1].astype(jnp.float32)).astype(jnp.bfloat16)
    net.arrived(second_of[ME], go_far)
    u = red.kept(ME)
    me_w[...] = og[0, u].astype(jnp.float32) + rx[0].astype(jnp.float32) + rz[...].astype(jnp.float32)
    me_d[...] = od[0, u].astype(jnp.float32) + rxd[0].astype(jnp.float32) + rzd[...].astype(jnp.float32)
    net.sent()


def normed_back(d, w, normed, xs, gg, gu, fw, fd, od, d_resid, g_attn):
    bf16, f32 = jnp.bfloat16, jnp.float32
    any_spec = pl.BlockSpec(memory_space=pl.ANY)
    vmem = pl.BlockSpec(memory_space=pltpu.VMEM)
    copies = 24
    wide, deep = (2, 64, HALF_FF), (192, 512)

    def vm(a):
        return pltpu.VMEM(a.shape, a.dtype)

    return pl.pallas_call(
        normed_kernel,
        out_shape=(
            jax.ShapeDtypeStruct((OWN, MODEL_DIM), bf16),
            jax.ShapeDtypeStruct((8, MODEL_DIM), f32),
            jax.ShapeDtypeStruct((1024, 1024), bf16),
            jax.ShapeDtypeStruct(wide, f32),
            jax.ShapeDtypeStruct(deep, f32),
            jax.ShapeDtypeStruct(wide, bf16),
            jax.ShapeDtypeStruct(deep, bf16),
        ),
        in_specs=[any_spec] * 9 + [vmem] * 2,
        out_specs=[vmem] * 7,
        scratch_shapes=[
            vm(d), vm(w), vm(normed),
            pltpu.VMEM((OWN, MODEL_DIM), bf16),
            pltpu.VMEM((2, OWN, MODEL_DIM), bf16),
            pltpu.VMEM((2, OWN, MODEL_DIM), bf16),
            pltpu.VMEM((OWN, MODEL_DIM), bf16),
            pltpu.VMEM((OWN, MODEL_DIM), bf16),
            pltpu.VMEM((2, OWN, MODEL_DIM), f32),
            pltpu.VMEM((2, 2) + wide, bf16),
            pltpu.VMEM((2, 2) + wide, bf16),
            pltpu.VMEM((2, 2) + deep, bf16),
            pltpu.VMEM((2,) + wide, bf16),
            pltpu.VMEM((2,) + deep, bf16),
            pltpu.VMEM(wide, bf16),
            pltpu.VMEM(deep, bf16),
            pltpu.SemaphoreType.DMA((copies,)),
            pltpu.SemaphoreType.DMA((copies,)),
            pltpu.SemaphoreType.DMA((6,)),
            pltpu.SemaphoreType.DMA((8,)),
        ],
        compiler_params=pltpu.CompilerParams(
            collective_id=5, has_side_effects=True, vmem_limit_bytes=58 * 1024 * 1024
        ),
        name="normed_back",
    )(d, w, normed, xs, gg, gu, fw, fd, od, d_resid, g_attn)


def back_kernel(
    pq, go, gp, near_w, near_d, me_w, me_d, gt,
    out_query, out_key, out_value, out_out, out_gate, out_up, out_down, gout, tokens,
    work, wgo, wgp, ry, ryo, ryg, ox, oxo, oxg, rs, rso, rsg, rq, rqo, rqg,
    zw, zd, total_w, total_d, fw, fd, landed,
    send_sem, recv_sem, back_send, back_recv,
):
    where = place()
    y, x, p, l, c = where
    peer = peers_of(x, y, p, l, c)
    net = Plan(send_sem, recv_sem)
    me = 2 * l + c
    home = Return(where, gt, landed, back_send, back_recv)

    def group(yy, xx, pp):
        return (yy * 2 + xx) * 2 + pp

    def moved(sources, groups, targets, at=0):
        return [
            (src.at[one], dst.at[at + k])
            for k, one in enumerate(groups)
            for src, dst in zip(sources, targets)
        ]

    source, working, small = (pq, go, gp), (work, wgo, wgp), (rs, rso, rsg)
    go_own_y = net.add(peer["y"], moved(source, (group(1 - y, 0, p), group(1 - y, 1, p)), (ry, ryo, ryg)))
    go_other_x = net.add(peer["x"], moved(source, (group(0, 1 - x, 1 - p), group(1, 1 - x, 1 - p)), (ox, oxo, oxg)))
    go_own_x = net.add(peer["x"], moved(working, (group(y, 1 - x, p),), small, 0))
    go_other_y = net.add(peer["y"], moved(working, (group(1 - y, x, 1 - p),), small, 1))
    go_across = net.add(peer["p"], moved(working, (group(y, x, 1 - p),), small, 2))
    base = group(y, x, p)

    def parts(q):
        return [
            (work.at[base, rows_at(q, 32)], rq.at[me]),
            (wgo.at[base, rows_at(q, 64)], rqo.at[me]),
            (wgp.at[base, q], rqg.at[me]),
        ]

    go_last_l = net.add(peer["l"], parts(2 * (1 - l) + c))
    go_last_d = net.add(peer["d"], parts(2 * (1 - l) + 1 - c))
    go_last_c = net.add(peer["c"], parts(2 * l + 1 - c))
    go_near = net.add(peer["l"], [(near_w, zw), (near_d, zd)])
    go_halves = net.add(peer["c"], [(total_w.at[1 - c], fw.at[c]), (total_d.at[1 - c], fd.at[c])])
    greet(line_peers(p, l, c) + [peer["x"], peer["y"]])
    net.start(go_own_y, go_other_x, go_near)
    home.start()

    def add(at, left, right, place_at):
        for target, a, b in zip(working, left, right):
            total = a[at].astype(jnp.float32) + b[place_at].astype(jnp.float32)
            target[at] = total.astype(target.dtype)

    net.arrived(go_own_y)
    for xx in (0, 1):
        add(group(y, xx, p), source, (ry, ryo, ryg), xx)
    net.start(go_own_x)
    net.arrived(go_other_x)
    for yy in (0, 1):
        add(group(yy, x, 1 - p), source, (ox, oxo, oxg), yy)
    net.start(go_other_y)
    net.arrived(go_near)
    for cc in range(2):
        rows = pl.ds(32 * cc, 32)
        total_w[cc] = me_w[:, rows, :] + zw[:, rows, :].astype(jnp.float32)
        rows = pl.ds(96 * cc, 96)
        total_d[cc] = me_d[rows, :] + zd[rows, :].astype(jnp.float32)
    net.start(go_halves)
    net.arrived(go_other_y)
    add(group(y, x, 1 - p), working, small, 1)
    net.start(go_across)
    net.arrived(go_own_x)
    add(base, working, small, 0)
    fw[c] = total_w[c]
    fd[c] = total_d[c]
    net.arrived(go_halves)
    for half in range(2):
        cols = slice(half * HALF_FF, (half + 1) * HALF_FF)
        out_gate[:, cols] = fw[half, 0]
        out_up[:, cols] = fw[half, 1]
        out_down[:, half * 512 : (half + 1) * 512] = fd[half]
    net.arrived(go_across)
    add(base, working, small, 2)
    net.start(go_last_l, go_last_d, go_last_c)
    rq[me] = work[base, rows_at(me, 32), :]
    rqo[me] = wgo[base, rows_at(me, 64), :]
    rqg[me] = wgp[base, me]
    home.wait()
    tokens[...] = landed[...].astype(jnp.float32)
    net.arrived(go_last_l, go_last_d, go_last_c)
    for q in range(4):
        value = rq[q].astype(jnp.float32)
        out_query[:, 512 * q : 512 * (q + 1)] = value[:, :512]
        out_key[:, 256 * q : 256 * (q + 1)] = value[:, 512:768]
        out_value[:, 256 * q : 256 * (q + 1)] = value[:, 768:]
        out_out[:, 256 * q : 256 * (q + 1)] = rqo[q].astype(jnp.float32)
    gout[...] = rqg[0] + rqg[1] + rqg[2] + rqg[3]
    net.sent()


def back(pq, goq, gp, near_w, near_d, me_w, me_d, gt):
    bf16, f32 = jnp.bfloat16, jnp.float32
    vmem = pl.BlockSpec(memory_space=pltpu.VMEM)
    copies = 40

    def three(*lead):
        return [
            pltpu.VMEM(lead + (128, 1024), bf16),
            pltpu.VMEM(lead + (256, 256), bf16),
            pltpu.VMEM(lead + (4, 8, 128), f32),
        ]

    wide, deep = (2, 64, HALF_FF), (192, 512)
    return pl.pallas_call(
        back_kernel,
        out_shape=(
            jax.ShapeDtypeStruct((32, 2048), f32),
            jax.ShapeDtypeStruct((32, 1024), f32),
            jax.ShapeDtypeStruct((32, 1024), f32),
            jax.ShapeDtypeStruct((64, 1024), f32),
            jax.ShapeDtypeStruct((32, FF), f32),
            jax.ShapeDtypeStruct((32, FF), f32),
            jax.ShapeDtypeStruct((96, 1024), f32),
            jax.ShapeDtypeStruct((8, 128), f32),
            jax.ShapeDtypeStruct((2, ROWS, MODEL_DIM), f32),
        ),
        in_specs=[vmem] * 8,
        out_specs=[vmem] * 9,
        scratch_shapes=three(8) + three(2) + three(2) + three(3)
        + [
            pltpu.VMEM((4, 32, 1024), bf16),
            pltpu.VMEM((4, 64, 256), bf16),
            pltpu.VMEM((4, 8, 128), f32),
            pltpu.VMEM(wide, bf16),
            pltpu.VMEM(deep, bf16),
            pltpu.VMEM((2, 2, 32, HALF_FF), f32),
            pltpu.VMEM((2, 96, 512), f32),
            pltpu.VMEM((2, 2, 32, HALF_FF), f32),
            pltpu.VMEM((2, 96, 512), f32),
            pltpu.VMEM((2, ROWS, MODEL_DIM), bf16),
            pltpu.SemaphoreType.DMA((copies,)),
            pltpu.SemaphoreType.DMA((copies,)),
            pltpu.SemaphoreType.DMA((2,)),
            pltpu.SemaphoreType.DMA((2,)),
        ],
        compiler_params=pltpu.CompilerParams(
            collective_id=1, has_side_effects=True, vmem_limit_bytes=58 * 1024 * 1024
        ),
        name="back_reduce",
    )(pq.reshape(8, 128, 1024), goq.reshape(8, 256, 256), gp.reshape(8, 4, 8, 128), near_w, near_d, me_w, me_d, gt)


def pick(value, index):
    return lax.dynamic_index_in_dim(value, index, 0, keepdims=False)


def fast_device(tokens, cotangent, starts, w_query, key_matrix, value_matrix, w_out, w_gate, w_up, w_down, gains):
    p = lax.axis_index("p")
    gn = jnp.pad(gains.astype(jnp.float32), (0, 952)).reshape(8, 128)
    half_steps = jnp.arange(HEAD_DIM // 2, dtype=jnp.float32)
    inverse = THETA ** (-2.0 * half_steps / HEAD_DIM)
    inverse = jnp.broadcast_to(jnp.concatenate([inverse, inverse])[None], (8, HEAD_DIM))
    own_starts = pick(starts, p)
    block_at = jnp.arange(SEQ_ROWS // PIECE, dtype=jnp.int32) * PIECE
    flags = jnp.any(own_starts[None, :] == block_at[:, None], axis=1).astype(jnp.int32)
    xs, w_qkv, woq, gf, wgu, wdn, cosine, sine = front(
        tokens, w_query, key_matrix, value_matrix, w_out, gn, w_gate, w_up, w_down, inverse
    )
    xs = xs.reshape(SEQ_ROWS, MODEL_DIM)
    gain_all = gf.reshape(32, 1024)[:, :72].reshape(2304)
    g_attn = gain_all[None, :1024]
    g_mlp = gain_all[None, 1024:2048]
    g_q = gain_all[None, 2048:2176]
    g_k = gain_all[None, 2176:]
    normed, q, k, v, q_raw, k_raw, attn, lse, wo, wgu, wdn = attend(
        flags, xs, w_qkv, g_attn, g_q, g_k, cosine, sine, woq, wgu, wdn
    )
    resid, mlp_in, wgu, wdn, wdx, wdo, dy = finish_resid(attn, wo, g_mlp, xs, cotangent, wgu, wdn)
    grad_gate, grad_up, grad_down, d_resid, d_branch, result, d_g_mlp = feed_forward(
        mlp_in.reshape(1024, MODEL_DIM), dy.reshape(1024, MODEL_DIM), wgu, wdo, wdx, resid, g_mlp
    )
    d_qkv, goq, fw, fd, od, output, d_g_heads = attend_back(
        flags, q, k, v, attn, d_branch, wo, lse, q_raw, k_raw, cosine, sine, grad_gate, grad_up, grad_down, result, g_q, g_k
    )
    gt, d_g_attn, pq, me_w, me_d, near_w, near_d = normed_back(
        d_qkv, w_qkv, normed, xs, grad_gate, grad_up, fw, fd, od, d_resid, g_attn
    )
    d_gains = jnp.concatenate([jnp.sum(d_g_attn, axis=0), jnp.sum(d_g_mlp, axis=0), jnp.sum(d_g_heads, axis=1).reshape(256)])
    gp = jnp.pad(d_gains.reshape(32, 72), ((0, 0), (0, 952))).reshape(32, 8, 128)
    *grads, gains_sum, grad_tokens = back(pq, goq, gp, near_w, near_d, me_w, me_d, gt)
    return (output, grad_tokens, *grads, gains_sum.reshape(1024)[:72])


def fast_solution(mesh):
    wide = Mesh(mesh.devices.reshape(2, 2, 2, 2, 2), AXES)
    rows = ("y", "x")
    places = ("p", "l", "c")
    weight = P(AXES, None)
    return jax.shard_map(
        fast_device,
        mesh=wide,
        in_specs=(P(rows, places, None), P(rows, places, None), P(rows, None)) + (weight,) * 7 + (P(AXES),),
        out_specs=(P(rows, places, None), P(rows, places, None)) + (weight,) * 7 + (P(AXES),),
        check_vma=False,
    )


def solution(mesh):
    if dict(mesh.shape) == {"dp": 4, "ctx": 8}:
        return fast_solution(mesh)
    return generic_solution(mesh)
```

```python
import functools
import math

import jax
import jax.numpy as jnp
from jax import lax
from jax.experimental import pallas as pl
from jax.experimental.pallas import tpu as pltpu
from jax.sharding import Mesh
from jax.sharding import PartitionSpec as P

MODEL_DIM = 1024
QUERY_HEADS = 16
KEY_VALUE_HEADS = 8
HEAD_DIM = 128
SEQUENCE_TOKENS = 2048
PIECE = 256
NPIECE = 4


EPS = 1e-06
THETA = 1000000.0
NEG = -1e30


def rms_norm(incoming_values, gain_vector):
    return (
        incoming_values
        * lax.rsqrt(jnp.mean(incoming_values * incoming_values, axis=-1, keepdims=True) + EPS)
        * gain_vector
    )


def rope_tables(positions):
    half_steps = jnp.arange(HEAD_DIM // 2, dtype=jnp.float32)
    inverse = THETA ** (-2.0 * half_steps / HEAD_DIM)
    angles = positions.astype(jnp.float32)[:, None] * inverse[None, :]
    angles = jnp.concatenate([angles, angles], axis=-1)
    return (jnp.cos(angles), jnp.sin(angles))


def rotate(incoming_values, cosine_table, sine_table):
    half_dim = HEAD_DIM // 2
    turned = jnp.concatenate(
        [-incoming_values[..., half_dim:], incoming_values[..., :half_dim]], axis=-1
    )
    return incoming_values * cosine_table[:, None, :] + turned * sine_table[:, None, :]


def per_head_route(unrotated_projection, gain_vector, cosine_table, sine_table, head_count):
    shaped = unrotated_projection.reshape(unrotated_projection.shape[:-1] + (head_count, HEAD_DIM))
    return rotate(rms_norm(shaped, gain_vector), cosine_table, sine_table).reshape(
        unrotated_projection.shape
    )


def piece_ids(positions, piece_starts):
    inside = (positions[:, None] >= piece_starts[None, :]) & (
        positions[:, None] < piece_starts[None, :] + PIECE
    )
    number = jnp.arange(1, NPIECE + 1, dtype=jnp.int32)
    return jnp.sum(jnp.where(inside, number[None, :], 0), axis=1) - 1


def visible(query_pos, query_id, key_pos, key_id):
    causal = key_pos[None, :] <= query_pos[:, None]
    same_piece = (query_id[:, None] == key_id[None, :]) & (query_id[:, None] >= 0)
    return causal | same_piece


def swiglu(gate_proj, up_proj):
    return jax.nn.silu(gate_proj) * up_proj


def block_extent(kv_count, per_head):
    target = max(1, 512 // per_head)
    chosen = 1
    for candidate in range(1, kv_count + 1):
        if kv_count % candidate == 0 and candidate <= target:
            chosen = candidate
    return chosen


def attend_forward(incoming_query, incoming_keys, incoming_values, allowed, head_group_block):
    sequence_rows = incoming_query.shape[0]
    query_group_factor = QUERY_HEADS // KEY_VALUE_HEADS
    scaling = 1.0 / math.sqrt(HEAD_DIM)
    query_per_head = incoming_query.reshape(
        sequence_rows, KEY_VALUE_HEADS, query_group_factor, HEAD_DIM
    )
    key_per_head = incoming_keys.reshape(incoming_keys.shape[0], KEY_VALUE_HEADS, HEAD_DIM)
    value_per_head = incoming_values.reshape(incoming_values.shape[0], KEY_VALUE_HEADS, HEAD_DIM)
    mixed_parts = []
    total_parts = []
    for head_offset in range(0, KEY_VALUE_HEADS, head_group_block):
        q_part = query_per_head[:, head_offset : head_offset + head_group_block]
        k_part = key_per_head[:, head_offset : head_offset + head_group_block]
        v_part = value_per_head[:, head_offset : head_offset + head_group_block]
        scores = (
            jnp.einsum("tagd,kad->agtk", q_part, k_part, preferred_element_type=jnp.float32)
            * scaling
        )
        scores = jnp.where(allowed[None, None], scores, NEG)
        row_max = jnp.max(scores, axis=-1, keepdims=True)
        exp_scores = jnp.exp(scores - row_max)
        summed = jnp.sum(exp_scores, axis=-1, keepdims=True)
        prob_low = (exp_scores / summed).astype(jnp.bfloat16)
        mixed_parts.append(
            jnp.einsum("agtk,kad->tagd", prob_low, v_part, preferred_element_type=jnp.float32)
        )
        total_parts.append(row_max + jnp.log(summed))
    mixed_out = jnp.concatenate(mixed_parts, axis=1).reshape(sequence_rows, QUERY_HEADS * HEAD_DIM)
    return (mixed_out, jnp.concatenate(total_parts, axis=0))


def attend_backward(
    incoming_query,
    incoming_keys,
    incoming_values,
    allowed,
    log_total,
    mixed_gradient,
    head_group_block,
):
    sequence_rows = incoming_query.shape[0]
    key_row_matrix = incoming_keys.shape[0]
    query_group_factor = QUERY_HEADS // KEY_VALUE_HEADS
    scaling = 1.0 / math.sqrt(HEAD_DIM)
    query_per_head = incoming_query.reshape(
        sequence_rows, KEY_VALUE_HEADS, query_group_factor, HEAD_DIM
    )
    gradient_per_head = mixed_gradient.reshape(
        sequence_rows, KEY_VALUE_HEADS, query_group_factor, HEAD_DIM
    )
    key_per_head = incoming_keys.reshape(key_row_matrix, KEY_VALUE_HEADS, HEAD_DIM)
    value_per_head = incoming_values.reshape(key_row_matrix, KEY_VALUE_HEADS, HEAD_DIM)
    dq_parts = []
    key_gradient_pieces = []
    value_gradient_pieces = []
    for head_offset in range(0, KEY_VALUE_HEADS, head_group_block):
        q_part = query_per_head[:, head_offset : head_offset + head_group_block]
        g_part = gradient_per_head[:, head_offset : head_offset + head_group_block]
        k_part = key_per_head[:, head_offset : head_offset + head_group_block]
        v_part = value_per_head[:, head_offset : head_offset + head_group_block]
        scores = (
            jnp.einsum("tagd,kad->agtk", q_part, k_part, preferred_element_type=jnp.float32)
            * scaling
        )
        scores = jnp.where(allowed[None, None], scores, NEG)
        prob_all = jnp.exp(scores - log_total[head_offset : head_offset + head_group_block])
        prob_low = prob_all.astype(jnp.bfloat16)
        d_probs = jnp.einsum("tagd,kad->agtk", g_part, v_part, preferred_element_type=jnp.float32)
        row_dot = jnp.sum(prob_all * d_probs, axis=-1, keepdims=True)
        d_scores = (prob_all * (d_probs - row_dot)).astype(jnp.bfloat16)
        dq_parts.append(
            jnp.einsum("agtk,kad->tagd", d_scores, k_part, preferred_element_type=jnp.float32)
            * scaling
        )
        key_gradient_pieces.append(
            jnp.einsum("agtk,tagd->kad", d_scores, q_part, preferred_element_type=jnp.float32)
            * scaling
        )
        value_gradient_pieces.append(
            jnp.einsum("agtk,tagd->kad", prob_low, g_part, preferred_element_type=jnp.float32)
        )
    d_query = jnp.concatenate(dq_parts, axis=1).reshape(sequence_rows, QUERY_HEADS * HEAD_DIM)
    key_gradient = jnp.concatenate(key_gradient_pieces, axis=1).reshape(
        key_row_matrix, KEY_VALUE_HEADS * HEAD_DIM
    )
    value_gradient = jnp.concatenate(value_gradient_pieces, axis=1).reshape(
        key_row_matrix, KEY_VALUE_HEADS * HEAD_DIM
    )
    return (d_query, key_gradient, value_gradient)


def generic_device(
    tokens, cotangent, starts, w_query, key_matrix, value_matrix, w_out, w_gate, w_up, w_down, gains
):
    sequence_count, sequence_rows, model_width = tokens.shape
    number_of_rows = sequence_count * sequence_rows
    head_group_block = block_extent(KEY_VALUE_HEADS, QUERY_HEADS // KEY_VALUE_HEADS * sequence_rows)
    attn_set = (
        lax.all_gather(w_query, ("dp", "ctx"), axis=0, tiled=True),
        lax.all_gather(key_matrix, ("dp", "ctx"), axis=0, tiled=True),
        lax.all_gather(value_matrix, ("dp", "ctx"), axis=0, tiled=True),
        lax.all_gather(w_out, ("dp", "ctx"), axis=0, tiled=True),
        lax.all_gather(gains, ("dp", "ctx"), axis=0, tiled=True),
    )
    mlp_set = (
        lax.all_gather(w_gate, ("dp", "ctx"), axis=0, tiled=True),
        lax.all_gather(w_up, ("dp", "ctx"), axis=0, tiled=True),
        lax.all_gather(w_down, ("dp", "ctx"), axis=0, tiled=True),
    )
    gain_all = attn_set[4].astype(jnp.float32)
    g_attn = gain_all[:MODEL_DIM]
    g_mlp = gain_all[MODEL_DIM : 2 * MODEL_DIM]
    g_query = gain_all[2 * MODEL_DIM : 2 * MODEL_DIM + HEAD_DIM]
    key_grad_total = gain_all[2 * MODEL_DIM + HEAD_DIM :]
    positions = lax.axis_index("ctx") * sequence_rows + jnp.arange(sequence_rows, dtype=jnp.int32)
    key_places = jnp.arange(SEQUENCE_TOKENS, dtype=jnp.int32)
    cosine_table, sine_table = rope_tables(positions)

    def query_map(unrotated_projection, gain_vector):
        return per_head_route(
            unrotated_projection, gain_vector, cosine_table, sine_table, QUERY_HEADS
        )

    def key_map(unrotated_projection, gain_vector):
        return per_head_route(
            unrotated_projection, gain_vector, cosine_table, sine_table, KEY_VALUE_HEADS
        )

    flat_in = tokens.reshape(number_of_rows, model_width).astype(jnp.float32)
    normed = rms_norm(flat_in, g_attn).astype(jnp.bfloat16)
    query_raw = jnp.dot(normed, attn_set[0], preferred_element_type=jnp.float32).reshape(
        sequence_count, sequence_rows, QUERY_HEADS * HEAD_DIM
    )
    key_unrotated = jnp.dot(normed, attn_set[1], preferred_element_type=jnp.float32).reshape(
        sequence_count, sequence_rows, KEY_VALUE_HEADS * HEAD_DIM
    )
    value_reduced = jnp.dot(normed, attn_set[2], preferred_element_type=jnp.float32).astype(
        jnp.bfloat16
    )
    value_reduced = value_reduced.reshape(sequence_count, sequence_rows, KEY_VALUE_HEADS * HEAD_DIM)
    query_reduced = query_map(query_raw, g_query).astype(jnp.bfloat16)
    key_reduced = key_map(key_unrotated, key_grad_total).astype(jnp.bfloat16)
    mask_list = []
    mixed_list = []
    total_list = []
    for seq_index in range(sequence_count):
        query_ids = piece_ids(positions, starts[seq_index])
        key_ids = piece_ids(key_places, starts[seq_index])
        allowed = visible(positions, query_ids, key_places, key_ids)
        key_full, value_full = (
            lax.all_gather(key_reduced[seq_index], "ctx", axis=0, tiled=True),
            lax.all_gather(value_reduced[seq_index], "ctx", axis=0, tiled=True),
        )
        mixed_out, log_total = attend_forward(
            query_reduced[seq_index], key_full, value_full, allowed, head_group_block
        )
        mask_list.append(allowed)
        mixed_list.append(mixed_out)
        total_list.append(log_total)
    attn_low = (
        jnp.stack(mixed_list).reshape(number_of_rows, QUERY_HEADS * HEAD_DIM).astype(jnp.bfloat16)
    )
    residual = flat_in + jnp.dot(attn_low, attn_set[3], preferred_element_type=jnp.float32)
    mlp_in = rms_norm(residual, g_mlp).astype(jnp.bfloat16)
    gate_proj = jnp.dot(mlp_in, mlp_set[0], preferred_element_type=jnp.float32)
    up_proj = jnp.dot(mlp_in, mlp_set[1], preferred_element_type=jnp.float32)
    hidden = swiglu(gate_proj, up_proj).astype(jnp.bfloat16)
    result = residual + jnp.dot(hidden, mlp_set[2], preferred_element_type=jnp.float32)
    output = result.astype(jnp.bfloat16).reshape(tokens.shape)
    mlp_back = (
        lax.all_gather(w_gate, ("dp", "ctx"), axis=0, tiled=True),
        lax.all_gather(w_up, ("dp", "ctx"), axis=0, tiled=True),
        lax.all_gather(w_down, ("dp", "ctx"), axis=0, tiled=True),
    )
    grad_flat = cotangent.reshape(number_of_rows, model_width)
    grad_down = jnp.dot(hidden.T, grad_flat, preferred_element_type=jnp.float32)
    d_hidden = jnp.dot(grad_flat, mlp_back[2].T, preferred_element_type=jnp.float32)
    swiglu_pull = jax.vjp(swiglu, gate_proj, up_proj)[1]
    d_gate, d_up = swiglu_pull(d_hidden)
    d_gate = d_gate.astype(jnp.bfloat16)
    d_up = d_up.astype(jnp.bfloat16)
    grad_gate = jnp.dot(mlp_in.T, d_gate, preferred_element_type=jnp.float32)
    grad_up = jnp.dot(mlp_in.T, d_up, preferred_element_type=jnp.float32)
    mlp_grads = (
        lax.psum_scatter(grad_gate, ("dp", "ctx"), scatter_dimension=0, tiled=True),
        lax.psum_scatter(grad_up, ("dp", "ctx"), scatter_dimension=0, tiled=True),
        lax.psum_scatter(grad_down, ("dp", "ctx"), scatter_dimension=0, tiled=True),
    )
    d_mlp_in = jnp.dot(d_gate, mlp_back[0].T, preferred_element_type=jnp.float32)
    d_mlp_in = d_mlp_in + jnp.dot(d_up, mlp_back[1].T, preferred_element_type=jnp.float32)
    mlp_norm_pull = jax.vjp(rms_norm, residual, g_mlp)[1]
    d_resid_norm, d_g_mlp = mlp_norm_pull(d_mlp_in)
    d_resid = grad_flat.astype(jnp.float32) + d_resid_norm
    attn_back = (
        lax.all_gather(w_query, ("dp", "ctx"), axis=0, tiled=True),
        lax.all_gather(key_matrix, ("dp", "ctx"), axis=0, tiled=True),
        lax.all_gather(value_matrix, ("dp", "ctx"), axis=0, tiled=True),
        lax.all_gather(w_out, ("dp", "ctx"), axis=0, tiled=True),
        lax.all_gather(gains, ("dp", "ctx"), axis=0, tiled=True),
    )
    d_branch = d_resid.astype(jnp.bfloat16)
    grad_out = jnp.dot(attn_low.T, d_branch, preferred_element_type=jnp.float32)
    d_attn = jnp.dot(d_branch, attn_back[3].T, preferred_element_type=jnp.float32).astype(
        jnp.bfloat16
    )
    d_attn = d_attn.reshape(sequence_count, sequence_rows, QUERY_HEADS * HEAD_DIM)
    dq_list = []
    dk_list = []
    value_gradient_list = []
    for seq_index in range(sequence_count):
        key_full, value_full = (
            lax.all_gather(key_reduced[seq_index], "ctx", axis=0, tiled=True),
            lax.all_gather(value_reduced[seq_index], "ctx", axis=0, tiled=True),
        )
        d_query_seq, d_key_full, d_value_full = attend_backward(
            query_reduced[seq_index],
            key_full,
            value_full,
            mask_list[seq_index],
            total_list[seq_index],
            d_attn[seq_index],
            head_group_block,
        )
        d_key_seq, d_value_seq = (
            lax.psum_scatter(
                d_key_full.astype(jnp.bfloat16), "ctx", scatter_dimension=0, tiled=True
            ).astype(jnp.float32),
            lax.psum_scatter(
                d_value_full.astype(jnp.bfloat16), "ctx", scatter_dimension=0, tiled=True
            ).astype(jnp.float32),
        )
        dq_list.append(d_query_seq)
        dk_list.append(d_key_seq)
        value_gradient_list.append(d_value_seq)
    d_query = jnp.stack(dq_list)
    key_gradient = jnp.stack(dk_list)
    value_gradient_reduced = (
        jnp.stack(value_gradient_list)
        .reshape(number_of_rows, KEY_VALUE_HEADS * HEAD_DIM)
        .astype(jnp.bfloat16)
    )
    query_pull = jax.vjp(query_map, query_raw, g_query)[1]
    d_query_raw, d_g_query = query_pull(d_query)
    key_pull = jax.vjp(key_map, key_unrotated, key_grad_total)[1]
    key_gradient_unrotated, d_g_key = key_pull(key_gradient)
    d_query_low = d_query_raw.reshape(number_of_rows, QUERY_HEADS * HEAD_DIM).astype(jnp.bfloat16)
    key_gradient_reduced = key_gradient_unrotated.reshape(
        number_of_rows, KEY_VALUE_HEADS * HEAD_DIM
    ).astype(jnp.bfloat16)
    grad_query = jnp.dot(normed.T, d_query_low, preferred_element_type=jnp.float32)
    grad_key = jnp.dot(normed.T, key_gradient_reduced, preferred_element_type=jnp.float32)
    grad_value = jnp.dot(normed.T, value_gradient_reduced, preferred_element_type=jnp.float32)
    d_normed = jnp.dot(d_query_low, attn_back[0].T, preferred_element_type=jnp.float32)
    d_normed = d_normed + jnp.dot(
        key_gradient_reduced, attn_back[1].T, preferred_element_type=jnp.float32
    )
    d_normed = d_normed + jnp.dot(
        value_gradient_reduced, attn_back[2].T, preferred_element_type=jnp.float32
    )
    input_pull = jax.vjp(rms_norm, flat_in, g_attn)[1]
    d_input_norm, d_g_attn = input_pull(d_normed)
    grad_tokens = (d_resid + d_input_norm).reshape(tokens.shape)
    grad_gains = jnp.concatenate([d_g_attn, d_g_mlp, d_g_query, d_g_key])
    attn_grads = (
        lax.psum_scatter(grad_query, ("dp", "ctx"), scatter_dimension=0, tiled=True),
        lax.psum_scatter(grad_key, ("dp", "ctx"), scatter_dimension=0, tiled=True),
        lax.psum_scatter(grad_value, ("dp", "ctx"), scatter_dimension=0, tiled=True),
        lax.psum_scatter(grad_out, ("dp", "ctx"), scatter_dimension=0, tiled=True),
        lax.psum_scatter(grad_gains, ("dp", "ctx"), scatter_dimension=0, tiled=True),
    )
    return (
        output,
        grad_tokens,
        attn_grads[0],
        attn_grads[1],
        attn_grads[2],
        attn_grads[3],
        mlp_grads[0],
        mlp_grads[1],
        mlp_grads[2],
        attn_grads[4],
    )


def generic_solution(mesh):
    return jax.shard_map(
        generic_device,
        mesh=mesh,
        in_specs=(
            P("dp", "ctx", None),
            P("dp", "ctx", None),
            P("dp", None),
            P(("dp", "ctx"), None),
            P(("dp", "ctx"), None),
            P(("dp", "ctx"), None),
            P(("dp", "ctx"), None),
            P(("dp", "ctx"), None),
            P(("dp", "ctx"), None),
            P(("dp", "ctx"), None),
            P(("dp", "ctx")),
        ),
        out_specs=(
            P("dp", "ctx", None),
            P("dp", "ctx", None),
            P(("dp", "ctx"), None),
            P(("dp", "ctx"), None),
            P(("dp", "ctx"), None),
            P(("dp", "ctx"), None),
            P(("dp", "ctx"), None),
            P(("dp", "ctx"), None),
            P(("dp", "ctx"), None),
            P(("dp", "ctx")),
        ),
        check_vma=False,
    )


AXES = ("y", "x", "p", "l", "c")
FF = 3072
HALF_FF = FF // 2
ROWS = 256
SEQ_ROWS = SEQUENCE_TOKENS
OWN = SEQ_ROWS // 4
BLK = 512
NBLK = SEQ_ROWS // BLK
QH = 4
KH = 2
MESH = pl.DeviceIdType.MESH
SCALE = 1.0 / math.sqrt(HEAD_DIM)
LOG2E = 1.4426950408889634
NT = (((1,), (1,)), ((), ()))
TN = (((0,), (0,)), ((), ()))


def dot(a, b, dims=None):
    if dims is None:
        dims = (((1,), (0,)), ((), ()))
    return lax.dot_general(a, b, dims, preferred_element_type=jnp.float32)


def greet(peers):
    barrier = pltpu.get_barrier_semaphore()
    for peer in peers:
        pl.semaphore_signal(barrier, inc=1, device_id=peer, device_id_type=MESH)
    pl.semaphore_wait(barrier, len(peers))


class Plan:
    def __init__(self, send_sem, recv_sem):
        self.send_sem = send_sem
        self.recv_sem = recv_sem
        self.count = 0
        self.entries = []

    def add(self, peer, pairs):
        self.entries.append((peer, pairs, self.count))
        self.count += len(pairs)
        return len(self.entries) - 1

    def copies(self, name):
        peer, pairs, at = self.entries[name]
        return [
            pltpu.make_async_remote_copy(
                src_ref=src,
                dst_ref=dst,
                send_sem=self.send_sem.at[at + k],
                recv_sem=self.recv_sem.at[at + k],
                device_id=peer,
                device_id_type=MESH,
            )
            for k, (src, dst) in enumerate(pairs)
        ]

    def start(self, *names):
        for name in names:
            for copy in self.copies(name):
                copy.start()

    def arrived(self, *names):
        for name in names:
            for copy in self.copies(name):
                copy.wait_recv()

    def sent(self):
        for name in range(len(self.entries)):
            for copy in self.copies(name):
                copy.wait_send()


def place():
    return tuple(lax.axis_index(name) for name in AXES)


def peers_of(x, y, p, l, c):
    return {
        "c": {"c": 1 - c},
        "l": {"l": 1 - l},
        "d": {"l": 1 - l, "c": 1 - c},
        "p": {"p": 1 - p},
        "x": {"x": 1 - x},
        "y": {"y": 1 - y},
    }


def owned(p, l, c):
    return 2 * c + (p + l + c) % 2


def rows_at(index, size, count=1):
    return pl.ds(pl.multiple_of(index * size, size), size * count)


def in_place(*refs):
    return [(ref, ref) for ref in refs]


def front_kernel(tok, wq, wk, wv, wo, gn, wg, wu, wd, inverse, xs, wa, woq, gf, wgu, wdn, cosine, sine, send_sem, recv_sem, in_sem, local_sem, *staged):
    y, x, p, l, c = place()
    peer = peers_of(x, y, p, l, c)
    block = 4 * p + 2 * l + c
    group = (y * 2 + x) * 8
    me = group + block
    t = 2 * l + c
    net = Plan(send_sem, recv_sem)

    def quarter(q):
        return [
            (wq.at[:, rows_at(q, 512)], wa.at[rows_at(me, 32), pl.ds(0, 512)]),
            (wk.at[:, rows_at(q, 256)], wa.at[rows_at(me, 32), pl.ds(512, 256)]),
            (wv.at[:, rows_at(q, 256)], wa.at[rows_at(me, 32), pl.ds(768, 256)]),
            (wo.at[:, rows_at(q, 256)], woq.at[rows_at(me, 64)]),
            (gn, gf.at[me]),
        ]

    def half(h):
        return [
            (wg.at[:, rows_at(h, HALF_FF)], wgu.at[0, rows_at(me, 32)]),
            (wu.at[:, rows_at(h, HALF_FF)], wgu.at[1, rows_at(me, 32)]),
            (wd.at[:, rows_at(h, 512)], wdn.at[rows_at(me, 96)]),
        ]

    def span(base, piece):
        if piece < 2:
            return in_place(wa.at[rows_at(base // 2 + piece, 64)])
        return in_place(woq.at[rows_at(base // 4, 256)], gf.at[pl.ds(base, 4)])

    def chip(yy, xx, pp, ll):
        slot = (yy * 2 + xx) * 4 + 2 * pp + ll
        return in_place(wgu.at[:, rows_at(slot, 64)], wdn.at[rows_at(slot, 192)])

    mine, other = group + 4 * p, group + 4 * (1 - p)
    go_first_l = net.add(peer["l"], quarter(2 * (1 - l) + c))
    go_first_d = net.add(peer["d"], quarter(2 * (1 - l) + 1 - c))
    go_first_c = net.add(peer["c"], quarter(2 * l + 1 - c))
    go_near = net.add(peer["l"], [(tok.at[p], xs.at[block])])
    upper, lower = pl.ds(0, ROWS // 2), pl.ds(ROWS // 2, ROWS // 2)
    go_far_0 = net.add(peer["p"], [(tok.at[1 - p, upper], xs.at[block, upper])])
    go_far_1 = net.add(peer["p"], [(tok.at[1 - p, lower], xs.at[block, lower])])
    go_near_c = net.add(peer["c"], [(tok.at[p], xs.at[block])])
    pieces = range(3)
    go_across = [net.add(peer["p"], span(mine, k)) for k in pieces]
    go_own_x = [net.add(peer["x"], span(mine, k)) for k in pieces]
    go_near_relay = net.add(peer["c"], in_place(xs.at[block ^ 2]))
    go_own_y = [net.add(peer["y"], span(mine, k) + span((y * 2 + 1 - x) * 8 + 4 * p, k)) for k in pieces]
    go_other_y = [net.add(peer["y"], span(other, k)) for k in pieces]
    go_far_l0 = net.add(peer["l"], in_place(xs.at[block ^ 4, upper]))
    go_far_l1 = net.add(peer["l"], in_place(xs.at[block ^ 4, lower]))
    go_far_relay = net.add(peer["c"], in_place(xs.at[block ^ 4]))
    go_other_x = [net.add(peer["x"], span(other, k) + span(((1 - y) * 2 + x) * 8 + 4 * (1 - p), k)) for k in pieces]
    go_far_l_relay = net.add(peer["c"], in_place(xs.at[block ^ 6]))
    go_mlp_c = net.add(peer["c"], half(1 - c))
    go_mlp_near = net.add(peer["l"], chip(y, x, p, l))
    go_mlp_x = net.add(peer["x"], chip(y, x, p, l))
    moves = quarter(t) + half(c) + [(tok.at[p], xs.at[block])]
    taken = [pltpu.make_async_copy(src, stage, in_sem.at[k]) for k, ((src, dst), stage) in enumerate(zip(moves, staged))]
    own = [pltpu.make_async_copy(stage, dst, local_sem.at[k]) for k, ((src, dst), stage) in enumerate(zip(moves, staged))]
    for copy in taken:
        copy.start()
    greet(list(peer.values()))
    net.start(go_first_l, go_first_d, go_first_c, go_far_0, go_near_c, go_mlp_c)
    for copy in taken:
        copy.wait()
    for copy in own:
        copy.start()

    def table(first, last):
        def chunk(k, carry):
            rows = rows_at(k, 64)
            position = (lax.broadcasted_iota(jnp.int32, (64, HEAD_DIM), 0) + k * 64).astype(jnp.float32)
            lane = lax.broadcasted_iota(jnp.int32, (64, HEAD_DIM), 1)
            angle = position * inverse[0:1, :]
            cosine[rows, :] = jnp.cos(angle)
            sine[rows, :] = jnp.where(lane < HEAD_DIM // 2, -1.0, 1.0) * jnp.sin(angle)
            return carry

        lax.fori_loop(first, last, chunk, 0)

    for copy in own:
        copy.wait()
    net.arrived(go_first_l, go_first_d, go_first_c)
    net.start(*go_across, *go_own_x, go_near)
    table(0, 12)
    for k in pieces:
        net.arrived(go_across[k])
        net.start(go_other_y[k])
    net.start(go_far_1)
    net.arrived(go_mlp_c)
    net.start(go_mlp_x)
    net.arrived(go_near)
    net.start(go_near_relay)
    for k in pieces:
        net.arrived(go_other_y[k])
        net.start(go_other_x[k])
    net.arrived(*go_own_x)
    net.start(*go_own_y, go_mlp_near)
    net.arrived(go_far_0)
    net.start(go_far_l0)
    table(12, 32)
    net.arrived(go_far_1)
    net.start(go_far_l1, go_far_relay)
    net.arrived(go_far_l0, go_far_l1)
    net.start(go_far_l_relay)
    net.arrived(go_near_c, go_near_relay, go_far_relay, go_far_l_relay, *go_own_y, *go_other_x, go_mlp_x, go_mlp_near)
    net.sent()


def front(tok, wq, wk, wv, wo, gn, wg, wu, wd, inverse):
    any_spec = pl.BlockSpec(memory_space=pl.ANY)
    copies = 64
    bf16 = jnp.bfloat16
    return pl.pallas_call(
        front_kernel,
        out_shape=(
            jax.ShapeDtypeStruct((8, ROWS, MODEL_DIM), bf16),
            jax.ShapeDtypeStruct((1024, 1024), bf16),
            jax.ShapeDtypeStruct((2048, 256), bf16),
            jax.ShapeDtypeStruct((32, 8, 128), jnp.float32),
            jax.ShapeDtypeStruct((2, MODEL_DIM, HALF_FF), bf16),
            jax.ShapeDtypeStruct((FF, 512), bf16),
            jax.ShapeDtypeStruct((SEQ_ROWS, HEAD_DIM), jnp.float32),
            jax.ShapeDtypeStruct((SEQ_ROWS, HEAD_DIM), jnp.float32),
        ),
        in_specs=[any_spec] * 9 + [pl.BlockSpec(memory_space=pltpu.VMEM)],
        out_specs=[any_spec] * 6 + [pl.BlockSpec(memory_space=pltpu.VMEM)] * 2,
        scratch_shapes=[
            pltpu.SemaphoreType.DMA((copies,)),
            pltpu.SemaphoreType.DMA((copies,)),
            pltpu.SemaphoreType.DMA((9,)),
            pltpu.SemaphoreType.DMA((9,)),
            pltpu.VMEM((32, 512), bf16),
            pltpu.VMEM((32, 256), bf16),
            pltpu.VMEM((32, 256), bf16),
            pltpu.VMEM((64, 256), bf16),
            pltpu.VMEM((8, 128), jnp.float32),
            pltpu.VMEM((32, HALF_FF), bf16),
            pltpu.VMEM((32, HALF_FF), bf16),
            pltpu.VMEM((96, 512), bf16),
            pltpu.VMEM((ROWS, MODEL_DIM), bf16),
        ],
        compiler_params=pltpu.CompilerParams(collective_id=0, has_side_effects=True),
        name="front_gather",
    )(tok, wq, wk, wv, wo, gn, wg, wu, wd, inverse)


def line_peers(p, l, c):
    return [
        {"p": (p + a) % 2, "l": (l + b) % 2, "c": (c + d) % 2}
        for a in range(2)
        for b in range(2)
        for d in range(2)
        if a + b + d > 0
    ]


class Return:
    def __init__(self, where, src, dst, send_sem, recv_sem):
        self.where = where[2:]
        self.src, self.dst, self.send_sem, self.recv_sem = src, dst, send_sem, recv_sem

    def stays(self, index):
        p, l, c = self.where
        return (p == c) & (index == c)

    def local(self, c0):
        p, l, c = self.where
        return pltpu.make_async_copy(self.src.at[pl.ds(c0 * ROWS, ROWS)], self.dst.at[p], self.send_sem.at[c0])

    def remote(self, c0):
        p, l, c = self.where
        return pltpu.make_async_remote_copy(
            src_ref=self.src.at[pl.ds(c0 * ROWS, ROWS)],
            dst_ref=self.dst.at[p],
            send_sem=self.send_sem.at[c0],
            recv_sem=self.recv_sem.at[p],
            device_id={"p": c, "l": (p + l + c) % 2, "c": c0},
            device_id_type=MESH,
        )

    def start_one(self, c0):
        here = self.stays(c0)

        @pl.when(here)
        def _():
            self.local(c0).start()

        @pl.when(jnp.logical_not(here))
        def _():
            self.remote(c0).start()

    def start(self):
        for c0 in range(2):
            self.start_one(c0)

    def wait(self):
        p, l, c = self.where
        for c0 in range(2):
            here = self.stays(c0)

            @pl.when(here)
            def _():
                self.local(c0).wait()

            @pl.when(jnp.logical_not(here))
            def _():
                self.remote(c0).wait_send()

        for seq in range(2):

            @pl.when(jnp.logical_not(self.stays(seq)))
            def _():
                pltpu.make_async_remote_copy(
                    src_ref=self.src.at[pl.ds(0, ROWS)],
                    dst_ref=self.dst.at[seq],
                    send_sem=self.send_sem.at[0],
                    recv_sem=self.recv_sem.at[seq],
                    device_id={"p": 1 - p},
                    device_id_type=MESH,
                ).wait_recv()


class Spread:
    def __init__(self, where, src, dst, send_sem, recv_sem):
        self.where = where[2:]
        self.src, self.dst, self.send_sem, self.recv_sem = src, dst, send_sem, recv_sem

    def here(self, index):
        p, l, c = self.where
        return (p == c) & (index == c)

    def local(self, seq):
        p, l, c = self.where
        return pltpu.make_async_copy(self.src.at[seq], self.dst.at[p, c], self.send_sem.at[seq])

    def remote(self, seq):
        p, l, c = self.where
        return pltpu.make_async_remote_copy(
            src_ref=self.src.at[seq],
            dst_ref=self.dst.at[p, c],
            send_sem=self.send_sem.at[seq],
            recv_sem=self.recv_sem.at[c],
            device_id={"p": seq, "l": (seq + l + p) % 2, "c": p},
            device_id_type=MESH,
        )

    def start(self):
        for seq in range(2):

            @pl.when(self.here(seq))
            def _():
                self.local(seq).start()

            @pl.when(jnp.logical_not(self.here(seq)))
            def _():
                self.remote(seq).start()

    def wait(self):
        p, l, c = self.where
        for seq in range(2):

            @pl.when(self.here(seq))
            def _():
                self.local(seq).wait()

            @pl.when(jnp.logical_not(self.here(seq)))
            def _():
                self.remote(seq).wait_send()

        for block in range(2):

            @pl.when(jnp.logical_not(self.here(block)))
            def _():
                pltpu.make_async_remote_copy(
                    src_ref=self.src.at[0],
                    dst_ref=self.dst.at[c, block],
                    send_sem=self.send_sem.at[0],
                    recv_sem=self.recv_sem.at[block],
                    device_id={"p": 1 - p},
                    device_id_type=MESH,
                ).wait_recv()


def turn(value):
    return pltpu.roll(value, HEAD_DIM // 2, 1)


def block_mask(key_dim, flags, index):
    shape = (BLK, BLK)
    key = lax.broadcasted_iota(jnp.int32, shape, key_dim)
    query = lax.broadcasted_iota(jnp.int32, shape, 1 - key_dim)
    upper = query // PIECE
    piece = jnp.where(upper == 0, flags[2 * index], flags[2 * index + 1])
    return (key <= query) | ((key // PIECE == upper) & (piece > 0))


PROJECT = 8


def attend_kernel(
    flags, x_ref, w_ref, ga_ref, gq_ref, gk_ref, cos_ref, sin_ref, woq, wgu_in, wdn_in,
    n_ref, q_ref, k_ref, v_ref, qr_ref, kr_ref, o_ref, lse_ref, wo, wgu, wdn,
    stage, send_sem, recv_sem, local_sem,
):
    y, x, p, l, c = place()
    peer = peers_of(x, y, p, l, c)
    t = 2 * l + c
    net = Plan(send_sem, recv_sem)

    def chip(yy, xx, pp, ll):
        slot = (yy * 2 + xx) * 4 + 2 * pp + ll
        return in_place(wgu.at[:, rows_at(slot, 64)], wdn.at[rows_at(slot, 192)])

    def rows_of(q):
        return woq.at[rows_at(q, 512)], wo.at[:, rows_at(t, 256)]

    go_mlp_y = net.add(peer["y"], chip(y, x, p, l) + chip(y, 1 - x, p, l))
    go_mlp_x = net.add(peer["x"], chip(y, x, p, 1 - l) + chip(1 - y, x, p, 1 - l))
    go_far = [net.add(peer["p"], [pair]) for pair in chip(y, x, p, l)]
    go_far_l = [net.add(peer["l"], [pair]) for pair in chip(y, x, 1 - p, l)]
    go_near_y = net.add(peer["y"], chip(y, x, p, 1 - l))
    go_wo_l = net.add(peer["l"], [rows_of(2 * (1 - l) + c)])
    go_wo_d = net.add(peer["d"], [rows_of(2 * (1 - l) + 1 - c)])
    go_wo_c = net.add(peer["c"], [rows_of(2 * l + 1 - c)])
    step = pl.program_id(0)

    @pl.when(step == 0)
    def _():
        greet(list(peer.values()))
        net.start(go_near_y, *go_far, go_wo_l, go_wo_d, go_wo_c)
        copy = pltpu.make_async_copy(rows_of(t)[0], stage, local_sem.at[0])
        copy.start()
        copy.wait()
        pltpu.make_async_copy(stage, rows_of(t)[1], local_sem.at[1]).start()

    @pl.when(step < PROJECT)
    def _():
        value = x_ref[...].astype(jnp.float32)
        r = lax.rsqrt(jnp.mean(value * value, axis=-1, keepdims=True) + EPS)
        normed = (value * r * ga_ref[...]).astype(jnp.bfloat16)
        n_ref[...] = normed
        full = dot(normed, w_ref[...])
        cosine, sine = cos_ref[...], sin_ref[...]
        rows = rows_at(jnp.minimum(step, PROJECT - 1), 256)
        for h in range(QH + KH):
            u = full[:, h * HEAD_DIM : (h + 1) * HEAD_DIM]
            raw_ref, out_ref, g_ref, at = (qr_ref, q_ref, gq_ref, h) if h < QH else (kr_ref, k_ref, gk_ref, h - QH)
            raw_ref[at] = u
            n = u * lax.rsqrt(jnp.mean(u * u, axis=-1, keepdims=True) + EPS) * g_ref[...]
            out_ref[at, rows, :] = (n * cosine + turn(n) * sine).astype(jnp.bfloat16)
        for h in range(KH):
            at = (QH + KH + h) * HEAD_DIM
            v_ref[h, rows, :] = full[:, at : at + HEAD_DIM].astype(jnp.bfloat16)

    @pl.when(step == PROJECT)
    def _():
        net.arrived(go_near_y)
        net.start(go_mlp_x, go_mlp_y)

    for k, at in enumerate((PROJECT + 2, PROJECT + 4)):

        @pl.when(step == at)
        def _():
            net.arrived(go_far[k])
            net.start(go_far_l[k])

    @pl.when(step >= PROJECT)
    def _():
        order = jnp.maximum(step - PROJECT, 0)
        g, i = order // NBLK, order % NBLK
        ones = jnp.ones((BLK, HEAD_DIM), jnp.bfloat16)
        mask = block_mask(1, flags, i)

        def values(j):
            return jnp.concatenate([v_ref[g, rows_at(j, BLK), :], ones], axis=1)

        queries = [q_ref[2 * g + h, rows_at(i, BLK), :] for h in range(2)]

        def part(j, masked):
            keys, both = k_ref[g, rows_at(j, BLK), :], values(j)
            found = []
            for q in queries:
                probs = jnp.exp2(dot(q, keys, NT) * (SCALE * LOG2E))
                if masked:
                    probs = jnp.where(mask, probs, 0.0)
                found.append(dot(probs.astype(jnp.bfloat16), both))
            return found

        def one(j, accs):
            return tuple(acc + more for acc, more in zip(accs, part(j, False)))

        accs = lax.fori_loop(0, i, one, tuple(part(i, True)))
        for h, acc in enumerate(accs):
            total = acc[:, HEAD_DIM:]
            o_ref[:, h * HEAD_DIM : (h + 1) * HEAD_DIM] = (acc[:, :HEAD_DIM] / total).astype(jnp.bfloat16)
            lse_ref[h] = jnp.log2(total).T[0:8, :]

    @pl.when(step == PROJECT + 2 * NBLK - 1)
    def _():
        pltpu.make_async_copy(stage, rows_of(t)[1], local_sem.at[1]).wait()
        net.arrived(go_mlp_y, go_mlp_x, *go_far_l, go_wo_l, go_wo_d, go_wo_c)
        net.sent()


def attend(flags, x, w, ga, gq, gk, cosine, sine, woq, wgu, wdn):
    bf16, f32 = jnp.bfloat16, jnp.float32

    def early(s):
        return jnp.minimum(s, PROJECT - 1)

    def late(s):
        return jnp.maximum(s - PROJECT, 0)

    def row(width):
        return pl.BlockSpec((256, width), lambda s, f: (early(s), 0))

    def whole(shape):
        return pl.BlockSpec(shape, lambda s, f: (0,) * len(shape))

    def heads(n):
        return pl.BlockSpec((n, 256, HEAD_DIM), lambda s, f: (0, early(s), 0))

    def shape(n, dtype):
        return jax.ShapeDtypeStruct((n, SEQ_ROWS, HEAD_DIM), dtype)

    any_spec = pl.BlockSpec(memory_space=pl.ANY)
    copies = 20
    return pl.pallas_call(
        attend_kernel,
        out_shape=(
            jax.ShapeDtypeStruct((SEQ_ROWS, MODEL_DIM), bf16),
            shape(QH, bf16),
            shape(KH, bf16),
            shape(KH, bf16),
            shape(QH, f32),
            shape(KH, f32),
            jax.ShapeDtypeStruct((SEQ_ROWS, QH * HEAD_DIM), bf16),
            jax.ShapeDtypeStruct((QH, 8, SEQ_ROWS), f32),
            jax.ShapeDtypeStruct((512, MODEL_DIM), bf16),
            jax.ShapeDtypeStruct(wgu.shape, bf16),
            jax.ShapeDtypeStruct(wdn.shape, bf16),
        ),
        grid_spec=pltpu.PrefetchScalarGridSpec(
            num_scalar_prefetch=1,
            grid=(PROJECT + KH * NBLK,),
            in_specs=[row(MODEL_DIM), whole(w.shape), whole(ga.shape), whole(gq.shape), whole(gk.shape), row(HEAD_DIM), row(HEAD_DIM)]
            + [any_spec] * 3,
            out_specs=[
                row(MODEL_DIM),
                whole((QH, SEQ_ROWS, HEAD_DIM)),
                whole((KH, SEQ_ROWS, HEAD_DIM)),
                whole((KH, SEQ_ROWS, HEAD_DIM)),
                heads(QH),
                heads(KH),
                pl.BlockSpec((BLK, 2 * HEAD_DIM), lambda s, f: (late(s) % NBLK, late(s) // NBLK)),
                pl.BlockSpec((2, 8, BLK), lambda s, f: (late(s) // NBLK, 0, late(s) % NBLK)),
            ]
            + [any_spec] * 3,
            scratch_shapes=[pltpu.VMEM((512, 256), bf16)]
            + [pltpu.SemaphoreType.DMA((copies,))] * 2
            + [pltpu.SemaphoreType.DMA((2,))],
        ),
        input_output_aliases={9: 9, 10: 10},
        compiler_params=pltpu.CompilerParams(
            collective_id=2, has_side_effects=True, vmem_limit_bytes=48 * 1024 * 1024
        ),
        cost_estimate=pl.CostEstimate(
            flops=4 * QH * SEQ_ROWS * SEQ_ROWS * HEAD_DIM, bytes_accessed=24 << 20, transcendentals=QH * SEQ_ROWS * SEQ_ROWS
        ),
        name="attend",
    )(flags, x, w, ga, gq, gk, cosine, sine, woq, wgu, wdn)


def resid_kernel(
    attn, wo, g_mlp, xs, cot, wgu_in, wdn_in,
    resid, mlp_in, wgu, wdn, wdx, dy,
    send_c, recv_c, send_l, recv_l, keep, x_own, send_sem, recv_sem, local_sem, dy_send, dy_recv,
):
    where = place()
    y, x, p, l, c = where
    peer = peers_of(x, y, p, l, c)
    net = Plan(send_sem, recv_sem)

    def chip(yy, xx, pp, ll):
        slot = (yy * 2 + xx) * 4 + 2 * pp + ll
        return in_place(wgu.at[:, rows_at(slot, 64)], wdn.at[rows_at(slot, 192)])

    def down(pp, ll):
        found = []
        for xx in range(2):
            slot = xx * 4 + 2 * pp + ll
            found.append((wdn.at[rows_at((1 - c) * 8 + slot, 192)], wdx.at[rows_at(slot, 192)]))
        return found

    def hop(name, *chips):
        found = [chip(*one) for one in chips]
        return [net.add(peer[name], [pairs[k] for pairs in found]) for k in range(2)]

    go_far_x = hop("x", (y, x, 1 - p, l))
    go_far_y = hop("y", (y, x, 1 - p, l), (y, 1 - x, 1 - p, l))
    go_fal_y = hop("y", (y, x, 1 - p, 1 - l))
    go_fal_x = hop("x", (y, x, 1 - p, 1 - l), (1 - y, x, 1 - p, 1 - l))
    go_down_me = net.add(peer["c"], down(p, l))
    go_down_near = net.add(peer["c"], down(p, 1 - l))
    go_down_far = net.add(peer["c"], down(1 - p, l))
    go_down_fal = net.add(peer["c"], down(1 - p, 1 - l))
    go_give_0 = net.add(peer["c"], [(send_c.at[0], recv_c.at[0])])
    go_give_1 = net.add(peer["c"], [(send_c.at[1], recv_c.at[1])])
    go_cross = net.add(peer["l"], [(send_l, recv_l)])
    go_share = net.add(peer["c"], in_place(mlp_in.at[c]))
    go_dy_c = net.add(peer["c"], in_place(dy.at[c]))
    spread = Spread(where, cot, dy, dy_send, dy_recv)
    greet(line_peers(p, l, c) + [peer["x"], peer["y"]])
    spread.start()
    net.start(go_far_x[1], go_fal_y[1], go_far_x[0], go_fal_y[0], go_down_me, go_down_near)
    fetch = pltpu.make_async_copy(xs.at[rows_at(owned(p, l, c), OWN)], x_own, local_sem.at[0])
    fetch.start()

    def project(ll, cc, write):
        part = attn[rows_at(owned(p, ll, cc), OWN), :]

        def chunk(k, carry):
            cols = rows_at(k, 256)
            write(cols, dot(part, wo[:, cols]))
            return carry

        lax.fori_loop(0, 4, chunk, 0)

    def give(k):
        def write(cols, value):
            send_c[k, :, cols] = value.astype(jnp.bfloat16)

        return write

    def hold(k):
        def write(cols, value):
            keep[k, :, cols] = value

        return write

    def relay_hop(k):
        net.arrived(go_far_x[k])
        net.start(go_far_y[k])
        net.arrived(go_fal_y[k])
        net.start(go_fal_x[k])

    project(1 - l, 1 - c, give(0))
    net.start(go_give_0)
    project(1 - l, c, hold(0))
    net.arrived(go_give_0)
    send_l[...] = (keep[0] + recv_c[0].astype(jnp.float32)).astype(jnp.bfloat16)
    net.start(go_cross)
    relay_hop(1)
    project(l, 1 - c, give(1))
    net.start(go_give_1)
    project(l, c, hold(1))
    fetch.wait()
    relay_hop(0)
    net.arrived(go_give_1)
    keep[1] += recv_c[1].astype(jnp.float32) + x_own[...].astype(jnp.float32)
    net.arrived(go_cross)
    total = keep[1] + recv_l[...].astype(jnp.float32)
    resid[...] = total
    r = lax.rsqrt(jnp.mean(total * total, axis=-1, keepdims=True) + EPS)
    mlp_in[c] = (total * r * g_mlp[...]).astype(jnp.bfloat16)
    net.start(go_share)
    net.arrived(go_far_y[1])
    net.start(go_down_far)
    spread.wait()
    net.start(go_dy_c)
    net.arrived(go_fal_x[1])
    net.start(go_down_fal)
    net.arrived(go_far_y[0], go_fal_x[0])
    net.arrived(go_down_me, go_down_near, go_down_far, go_down_fal, go_share, go_dy_c)
    net.sent()


def finish_resid(attn, wo, g_mlp, xs, cot, wgu, wdn):
    bf16, f32 = jnp.bfloat16, jnp.float32
    any_spec = pl.BlockSpec(memory_space=pl.ANY)
    vmem = pl.BlockSpec(memory_space=pltpu.VMEM)
    copies = 32
    return pl.pallas_call(
        resid_kernel,
        out_shape=(
            jax.ShapeDtypeStruct((OWN, MODEL_DIM), f32),
            jax.ShapeDtypeStruct((2, OWN, MODEL_DIM), bf16),
            jax.ShapeDtypeStruct(wgu.shape, bf16),
            jax.ShapeDtypeStruct(wdn.shape, bf16),
            jax.ShapeDtypeStruct((HALF_FF, 512), bf16),
            jax.ShapeDtypeStruct((2, 2, ROWS, MODEL_DIM), bf16),
        ),
        in_specs=[vmem] * 3 + [any_spec] * 4,
        out_specs=[vmem] * 2 + [any_spec] * 4,
        scratch_shapes=[
            pltpu.VMEM((2, OWN, MODEL_DIM), bf16),
            pltpu.VMEM((2, OWN, MODEL_DIM), bf16),
            pltpu.VMEM((OWN, MODEL_DIM), bf16),
            pltpu.VMEM((OWN, MODEL_DIM), bf16),
            pltpu.VMEM((2, OWN, MODEL_DIM), f32),
            pltpu.VMEM((OWN, MODEL_DIM), bf16),
            pltpu.SemaphoreType.DMA((copies,)),
            pltpu.SemaphoreType.DMA((copies,)),
            pltpu.SemaphoreType.DMA((1,)),
            pltpu.SemaphoreType.DMA((2,)),
            pltpu.SemaphoreType.DMA((2,)),
        ],
        input_output_aliases={5: 2, 6: 3},
        compiler_params=pltpu.CompilerParams(
            collective_id=3, has_side_effects=True, vmem_limit_bytes=48 * 1024 * 1024
        ),
        name="residual",
    )(attn, wo, g_mlp, xs, cot, wgu, wdn)


CHUNK = 512
EARLY = 1024


def forward_kernel(
    m_ref, dy_ref, w_ref, wdn, wx_ref, resid, g_mlp,
    ggu, gdb, rb, d_resid, db, res, dg,
    mt, dyt, hid, dgt, dup, d_in, down, give, take, all_down, ggv, gdv, send_sem, recv_sem, load_sem, out_sem,
):
    where = place()
    y, x, p, l, c = where
    peer = peers_of(x, y, p, l, c)
    red = Reduction(where)
    net = Plan(send_sem, recv_sem)
    go_d_in = net.add(peer["c"], [(give.at[0], take.at[0])])
    go_down = net.add(peer["c"], [(give.at[1], take.at[1])])
    go_gd, go_wide, outs = [], [], []
    for f in range(HALF_FF // CHUNK):
        part_f = pl.ds(f * CHUNK, CHUNK)
        go_gd.append(net.add(peer["c"], [(gdv.at[part_f, rows_at(1 - c, 512)], gdb.at[c, part_f])]))
        outs.append(
            [
                pltpu.make_async_copy(ggv.at[:, :, part_f], ggu.at[:, :, part_f], out_sem.at[2 * f]),
                pltpu.make_async_copy(gdv.at[part_f, rows_at(c, 512)], gdb.at[c, part_f], out_sem.at[2 * f + 1]),
            ]
        )
        go_wide.append([])
        if f * CHUNK < EARLY:
            for n, kind in enumerate(KINDS):
                pairs = []
                for k in range(2):
                    slot = chip_slot(*red.place(kind, k, True), *red.z[kind])
                    pairs.append((ggv.at[:, rows_at(slot, 64), part_f], rb.at[n, k, :, :, part_f]))
                go_wide[f].append(net.add(peer[red.first_peer(kind)], pairs))
    step = pl.program_id(0)
    fetch = pltpu.make_async_copy(wdn.at[rows_at(c, HALF_FF)], all_down, load_sem.at[0])

    @pl.when(step == 0)
    def _():
        fetch.start()
        greet([peer["c"], peer["x"], peer["y"]])

        def flip(k, carry):
            rows = rows_at(k, 256)
            mt[:, rows] = m_ref[rows, :].T
            dyt[:, rows] = dy_ref[rows, :].T
            return carry

        lax.fori_loop(0, 4, flip, 0)
        d_in[...] = jnp.zeros_like(d_in)
        down[...] = jnp.zeros_like(down)
        fetch.wait()

    wo_ref = all_down.at[rows_at(step, CHUNK)]
    own_cols, other_cols = rows_at(c, 512), rows_at(1 - c, 512)

    def part(r, carry):
        rows = rows_at(r, 512)
        value, grad = m_ref[rows, :], dy_ref
        gate, up = dot(value, w_ref[0]), dot(value, w_ref[1])
        d_hidden = dot(grad[rows, own_cols], wo_ref[...], NT) + dot(grad[rows, other_cols], wx_ref[...], NT)
        s = 1.0 / (1.0 + jnp.exp(-gate))
        silu = gate * s
        hidden = (silu * up).astype(jnp.bfloat16)
        d_up = (d_hidden * silu).astype(jnp.bfloat16)
        d_gate = (d_hidden * up * (s * (1.0 + gate * (1.0 - s)))).astype(jnp.bfloat16)
        hid[rows, :] = hidden
        dup[rows, :] = d_up
        dgt[rows, :] = d_gate
        d_in[rows, :] += dot(d_gate, w_ref[0], NT) + dot(d_up, w_ref[1], NT)
        down[rows, own_cols] += dot(hidden, wo_ref[...])
        down[rows, other_cols] += dot(hidden, wx_ref[...])
        return carry

    lax.fori_loop(0, 2, part, 0)

    @pl.when(step == pl.num_programs(0) - 1)
    def _():
        give[0] = d_in[rows_at(1 - c, OWN), :].astype(jnp.bfloat16)
        give[1] = down[rows_at(1 - c, OWN), :].astype(jnp.bfloat16)
        net.start(go_d_in, go_down)

    now = rows_at(step, CHUNK)

    def weights(k, carry):
        rows = rows_at(k, 512)
        ggv[0, rows, now] = dot(mt[rows, :], dgt[...]).astype(jnp.bfloat16)
        ggv[1, rows, now] = dot(mt[rows, :], dup[...]).astype(jnp.bfloat16)
        gdv[now, rows] = dot(dyt[rows, :], hid[...]).T.astype(jnp.bfloat16)
        return carry

    lax.fori_loop(0, 2, weights, 0)
    for f in range(HALF_FF // CHUNK):

        @pl.when(step == f)
        def _():
            net.start(*go_wide[f], go_gd[f])
            for copy in outs[f]:
                copy.start()

    @pl.when(step == pl.num_programs(0) - 1)
    def _():
        net.arrived(go_d_in, go_down)
        dg[...] = jnp.zeros_like(dg)

        def finish(k, carry):
            rows = rows_at(k, 64)
            here = pl.ds(pl.multiple_of(c * OWN + k * 64, 64), 64)
            value = resid[rows, :]
            grad = d_in[here, :] + take[0, rows, :].astype(jnp.float32)
            r = lax.rsqrt(jnp.mean(value * value, axis=-1, keepdims=True) + EPS)
            scaled = value * r
            gained = grad * g_mlp[...]
            total = dy_ref[here, :].astype(jnp.float32) + r * (gained - scaled * jnp.mean(scaled * gained, axis=-1, keepdims=True))
            d_resid[rows, :] = total
            db[rows, :] = total.astype(jnp.bfloat16)
            dg[...] += jnp.sum((grad * scaled).reshape(-1, 8, MODEL_DIM), axis=0)
            res[rows, :] = (value + down[here, :] + take[1, rows, :].astype(jnp.float32)).astype(jnp.bfloat16)
            return carry

        lax.fori_loop(0, 8, finish, 0)
        for f in range(HALF_FF // CHUNK):
            net.arrived(*go_wide[f], go_gd[f])
            for copy in outs[f]:
                copy.wait()
        net.sent()


def feed_forward(mlp_in, dy, wgu, wdn, wdx, resid, g_mlp):
    bf16, f32 = jnp.bfloat16, jnp.float32

    def whole(shape):
        return pl.BlockSpec(shape, lambda f: (0,) * len(shape), pipeline_mode=pl.Buffered(1))

    down = pl.BlockSpec((CHUNK, 512), lambda f: (f, 0))
    copies = 24
    rows = (1024, MODEL_DIM)
    own = (OWN, MODEL_DIM)
    return pl.pallas_call(
        forward_kernel,
        grid=(HALF_FF // CHUNK,),
        out_shape=(
            jax.ShapeDtypeStruct((2, MODEL_DIM, HALF_FF), bf16),
            jax.ShapeDtypeStruct((2, HALF_FF, 512), bf16),
            jax.ShapeDtypeStruct((4, 2, 2, 64, EARLY), bf16),
            jax.ShapeDtypeStruct(own, f32),
            jax.ShapeDtypeStruct(own, bf16),
            jax.ShapeDtypeStruct(own, bf16),
            jax.ShapeDtypeStruct((8, MODEL_DIM), f32),
        ),
        in_specs=[whole(rows), whole(rows), pl.BlockSpec((2, MODEL_DIM, CHUNK), lambda f: (0, 0, f))]
        + [pl.BlockSpec(memory_space=pl.ANY), down]
        + [whole(own), whole((1, MODEL_DIM))],
        out_specs=[pl.BlockSpec(memory_space=pl.ANY)] * 3
        + [whole(own), whole(own), whole(own), whole((8, MODEL_DIM))],
        scratch_shapes=[
            pltpu.VMEM(rows, bf16),
            pltpu.VMEM(rows, bf16),
            pltpu.VMEM((1024, CHUNK), bf16),
            pltpu.VMEM((1024, CHUNK), bf16),
            pltpu.VMEM((1024, CHUNK), bf16),
            pltpu.VMEM(rows, f32),
            pltpu.VMEM(rows, f32),
            pltpu.VMEM((2,) + own, bf16),
            pltpu.VMEM((2,) + own, bf16),
            pltpu.VMEM((HALF_FF, 512), bf16),
            pltpu.VMEM((2, MODEL_DIM, HALF_FF), bf16),
            pltpu.VMEM((HALF_FF, MODEL_DIM), bf16),
            pltpu.SemaphoreType.DMA((copies,)),
            pltpu.SemaphoreType.DMA((copies,)),
            pltpu.SemaphoreType.DMA((1,)),
            pltpu.SemaphoreType.DMA((6,)),
        ],
        compiler_params=pltpu.CompilerParams(
            collective_id=6, has_side_effects=True, vmem_limit_bytes=60 * 1024 * 1024
        ),
        name="feed_forward",
    )(mlp_in, dy, wgu, wdn, wdx, resid, g_mlp)


KINDS = ME, NEAR, FAR, FAL = range(4)


def chip_slot(yy, xx, pp, ll):
    return (yy * 2 + xx) * 4 + 2 * pp + ll


class Reduction:
    def __init__(self, where):
        y, x, p, l, c = where
        self.z = ((p, l), (p, 1 - l), (1 - p, l), (1 - p, 1 - l))
        self.y, self.x = y, x

    def y_first(self, kind):
        return kind in (ME, FAR)

    def first_peer(self, kind):
        return "y" if self.y_first(kind) else "x"

    def second_peer(self, kind):
        return "x" if self.y_first(kind) else "y"

    def place(self, kind, index, given):
        if self.y_first(kind):
            return (1 - self.y if given else self.y), index
        return index, (1 - self.x if given else self.x)

    def kept(self, kind):
        return self.x if self.y_first(kind) else self.y


def attend_back_kernel(
    flags, q_in, k_in, v_in, o_in, db_in, wo_in, lse_in, qr_in, kr_in, cos_in, sin_in, ggu, gdb, rb_in, res, gq_ref, gk_ref,
    d_out, goq, og_out, od_out, fw_out, fd_out, out, dg_ref,
    q_ref, k_ref, v_ref, o_ref, dall, wo, lse_ref, qr_ref, kr_ref, cos_ref, sin_ref,
    da, delta, dbuf, dq_acc, dk_acc, dv_acc, og, od, rb, rbd, rc, rcd, rz, rzd, go,
    send_sem, recv_sem, load_sem, own_sem, out_sem, back_send, back_recv,
):
    where = place()
    y, x, p, l, c = where
    peer = peers_of(x, y, p, l, c)
    red = Reduction(where)
    net = Plan(send_sem, recv_sem)
    t = 2 * l + c

    def block(index):
        return dall.at[rows_at(index, OWN)]

    mine = owned(p, l, c)
    go_db_l = net.add(peer["l"], [(db_in, block(mine))])
    go_db_c = net.add(peer["c"], [(db_in, block(mine))])
    go_db_r = net.add(peer["c"], in_place(block(owned(p, 1 - l, c))))
    early, late = pl.ds(0, EARLY), pl.ds(EARLY, HALF_FF - EARLY)
    first_of, second_a, second_b = {}, {}, {}
    for n, kind in enumerate(KINDS):
        pairs = []
        for k in range(2):
            yy, xx = red.place(kind, k, True)
            slot = chip_slot(yy, xx, *red.z[kind])
            pairs.append((ggu.at[:, rows_at(slot, 64), late], rb.at[n, k, :, :, late]))
            pairs.append((gdb.at[yy, rows_at(xx * 4 + 2 * red.z[kind][0] + red.z[kind][1], 192)], rbd.at[n, k]))
        first_of[kind] = net.add(peer[red.first_peer(kind)], pairs)
        if n >= 2:
            away, link = 1 - red.kept(kind), peer[red.second_peer(kind)]
            second_a[kind] = net.add(link, [(og.at[n, away, :, :, early], rc.at[n - 2, :, :, early])])
            second_b[kind] = net.add(link, [(og.at[n, away, :, :, late], rc.at[n - 2, :, :, late]), (od.at[n, away], rcd.at[n - 2])])
    u_far, u_fal = red.kept(FAR), red.kept(FAL)
    go_fal_a = net.add(peer["l"], [(og.at[FAL, u_fal, :, :, early], rz.at[:, :, early])])
    go_fal_b = net.add(peer["l"], [(og.at[FAL, u_fal, :, :, late], rz.at[:, :, late]), (od.at[FAL, u_fal], rzd)])
    go_far_a = net.add(peer["p"], [(og.at[FAR, u_far, :, :, early], fw_out.at[:, :, early])])
    go_far_b = net.add(peer["p"], [(og.at[FAR, u_far, :, :, late], fw_out.at[:, :, late]), (od.at[FAR, u_far], fd_out)])
    home = Return(where, res, out, back_send, back_recv)

    def columns(q):
        return [(go.at[:, rows_at(q, 256)], goq.at[rows_at(t, 512)])]

    go_go_l = net.add(peer["l"], columns(2 * (1 - l) + c))
    go_go_d = net.add(peer["d"], columns(2 * (1 - l) + 1 - c))
    go_go_c = net.add(peer["c"], columns(2 * l + 1 - c))
    own_go = pltpu.make_async_copy(*columns(t)[0], out_sem.at[1])
    loads = [
        pltpu.make_async_copy(src, dst, load_sem.at[k])
        for k, (src, dst) in enumerate(
            [
                (db_in, block(mine)), (wo_in, wo), (o_in, o_ref), (q_in, q_ref), (k_in, k_ref), (v_in, v_ref), (lse_in, lse_ref),
                (cos_in, cos_ref), (sin_in, sin_ref), (qr_in, qr_ref), (kr_in, kr_ref),
            ]
        )
    ]
    own = [pltpu.make_async_copy(rb_in, rb.at[:, :, :, :, early], own_sem.at[0])]
    for n, kind in enumerate(KINDS):
        for k in range(2):
            yy, xx = red.place(kind, k, False)
            slot = chip_slot(yy, xx, *red.z[kind])
            own.append(pltpu.make_async_copy(ggu.at[:, rows_at(slot, 64)], og.at[n, k], own_sem.at[len(own)]))
            rows = rows_at(xx * 4 + 2 * red.z[kind][0] + red.z[kind][1], 192)
            own.append(pltpu.make_async_copy(gdb.at[yy, rows], od.at[n, k], own_sem.at[len(own)]))

    def plus(target, other):
        target[...] = (target[...].astype(jnp.float32) + other[...].astype(jnp.float32)).astype(jnp.bfloat16)

    def wide_sum(n, cols):
        def wide(r, carry):
            k, m, rows = r // 4, (r // 2) % 2, rows_at(r % 2, 32)
            plus(og.at[n, k, m, rows, cols], rb.at[n, k, m, rows, cols])
            return carry

        lax.fori_loop(0, 8, wide, 0)

    def deep_sum(n):
        def deep(r, carry):
            k, rows = r // 3, rows_at(r % 3, 64)
            plus(od.at[n, k, rows, :], rbd.at[n, k, rows, :])
            return carry

        lax.fori_loop(0, 6, deep, 0)

    def branch(index):
        rows = rows_at(index, OWN)
        value = dot(dall[rows, :], wo[...], NT).astype(jnp.bfloat16)
        da[rows, :] = value
        for h in range(QH):
            cols = slice(h * HEAD_DIM, (h + 1) * HEAD_DIM)
            prod = value[:, cols].astype(jnp.float32) * o_ref[rows, cols].astype(jnp.float32)
            delta[h, :, rows] = jnp.broadcast_to(jnp.sum(prod.T, axis=0, keepdims=True), (8, BLK))

    def unrope(grad, u, gain, rows):
        grad = grad * SCALE
        e = grad * cos_ref[rows, :] + turn(grad * sin_ref[rows, :])
        r = lax.rsqrt(jnp.mean(u * u, axis=-1, keepdims=True) + EPS)
        ur = u * r
        ge = e * gain
        d = r * (ge - ur * jnp.mean(ur * ge, axis=-1, keepdims=True))
        return d.astype(jnp.bfloat16), jnp.sum((e * ur).reshape(-1, 8, HEAD_DIM), axis=0)

    step = pl.program_id(0)
    b, g = step // KH, step % KH
    i = owned(p, (l + b // 2) % 2, b % 2)

    @pl.when(step == 0)
    def _():
        for copy in loads[:3]:
            copy.start()
        for copy in own:
            copy.start()
        for copy in loads[3:]:
            copy.start()
        greet(line_peers(p, l, c) + [peer["x"], peer["y"]])
        net.start(go_db_l, go_db_c, first_of[FAR], first_of[FAL])
        dk_acc[...] = jnp.zeros_like(dk_acc)
        dv_acc[...] = jnp.zeros_like(dv_acc)
        dg_ref[...] = jnp.zeros_like(dg_ref)
        for copy in own:
            copy.wait()
        for kind in (FAR, FAL):
            wide_sum(kind, early)
            net.start(second_a[kind])
        for copy in loads[:3]:
            copy.wait()
        branch(mine)
        net.arrived(go_db_c)
        branch(owned(p, l, 1 - c))
        for copy in loads[3:]:
            copy.wait()

    @pl.when(step == 1)
    def _():
        net.arrived(second_a[FAL])
        plus(og.at[FAL, u_fal, :, :, early], rc.at[1, :, :, early])
        net.start(go_fal_a)
        net.arrived(second_a[FAR])
        plus(og.at[FAR, u_far, :, :, early], rc.at[0, :, :, early])

    @pl.when(step == 2)
    def _():
        home.start()

    @pl.when(step == 2)
    def _():
        for kind in (FAR, FAL):
            net.arrived(first_of[kind])
            wide_sum(kind, late)
            deep_sum(kind)
            net.start(second_b[kind])
        net.start(first_of[ME], first_of[NEAR])

    @pl.when(step == 2 * KH)
    def _():
        net.arrived(go_db_l)
        net.start(go_db_r)
        branch(owned(p, 1 - l, c))
        net.arrived(go_db_r)
        branch(owned(p, 1 - l, 1 - c))

    @pl.when(step == 3)
    def _():
        net.arrived(go_fal_a)
        plus(og.at[FAR, u_far, :, :, early], rz.at[:, :, early])
        net.start(go_far_a)

    @pl.when(step == 4)
    def _():
        net.arrived(second_b[FAL])
        plus(og.at[FAL, u_fal, :, :, late], rc.at[1, :, :, late])
        plus(od.at[FAL, u_fal], rcd.at[1])
        net.start(go_fal_b)
        net.arrived(second_b[FAR])
        plus(og.at[FAR, u_far, :, :, late], rc.at[0, :, :, late])
        plus(od.at[FAR, u_far], rcd.at[0])

    @pl.when(step == 5)
    def _():
        net.arrived(go_fal_b)
        plus(og.at[FAR, u_far, :, :, late], rz.at[:, :, late])
        plus(od.at[FAR, u_far], rzd)
        net.start(go_far_b)

    @pl.when(step == 3 * KH)
    def _():
        def grad_out(k, carry):
            cols = rows_at(k, 256)
            go[cols, :] = dot(o_ref[:, cols], dall[...], TN).astype(jnp.bfloat16)
            return carry

        lax.fori_loop(0, 2, grad_out, 0)
        net.start(go_go_l, go_go_d, go_go_c)
        own_go.start()

    dq_acc[...] = jnp.zeros_like(dq_acc)
    rows = rows_at(i, BLK)
    heads = [2 * g + n for n in range(2)]
    spans = [rows_at(h, HEAD_DIM) for h in heads]
    queries = [q_ref[h, rows, :] for h in heads]
    grads = [da[rows, span] for span in spans]

    def tile(j, mask=None):
        keys = rows_at(j, BLK)
        k, v = k_ref[g, keys, :], v_ref[g, keys, :]
        dv, dk = None, None
        for n, h in enumerate(heads):
            probs = jnp.exp2(dot(k, queries[n], NT) * (SCALE * LOG2E) - lse_ref[h, 0:1, rows])
            if mask is not None:
                probs = jnp.where(mask, probs, 0.0)
            d_scores = (probs * (dot(v, grads[n], NT) - delta[h, 0:1, rows])).astype(jnp.bfloat16)
            dv_more, dk_more = dot(probs.astype(jnp.bfloat16), grads[n]), dot(d_scores, queries[n])
            dv, dk = (dv_more, dk_more) if dv is None else (dv + dv_more, dk + dk_more)
            dq_acc[n] += dot(d_scores, k, TN)
        dv_acc[g, keys, :] += dv
        dk_acc[g, keys, :] += dk

    def loop(j, carry):
        tile(j)
        return carry

    tile(i, block_mask(0, flags, i))
    lax.fori_loop(0, i, loop, 0)
    for n, h in enumerate(heads):
        low, total = unrope(dq_acc[n], qr_ref[h, rows, :], gq_ref[...], rows)
        dbuf[rows, spans[n]] = low
        dg_ref[0] += total

    @pl.when(step == 4 * KH - 1)
    def _():
        for gg_at in range(KH):

            def finish(r, carry):
                rows = rows_at(r, 256)
                low, total = unrope(dk_acc[gg_at, rows, :], kr_ref[gg_at, rows, :], gk_ref[...], rows)
                dbuf[rows, pl.ds((QH + gg_at) * HEAD_DIM, HEAD_DIM)] = low
                dbuf[rows, pl.ds((QH + KH + gg_at) * HEAD_DIM, HEAD_DIM)] = dv_acc[gg_at, rows, :].astype(jnp.bfloat16)
                dg_ref[1] += total
                return carry

            lax.fori_loop(0, 8, finish, 0)
        outs = [pltpu.make_async_copy(dbuf, d_out, out_sem.at[0])]
        outs[0].start()
        for kind in (ME, NEAR):
            wide_sum(kind, early)
            net.arrived(first_of[kind])
            wide_sum(kind, late)
            deep_sum(kind)
        outs += [
            pltpu.make_async_copy(og.at[pl.ds(0, 2)], og_out, out_sem.at[2]),
            pltpu.make_async_copy(od.at[pl.ds(0, 2)], od_out, out_sem.at[3]),
        ]
        for copy in outs[1:]:
            copy.start()
        net.arrived(go_go_l, go_go_d, go_go_c, go_far_a, go_far_b)
        own_go.wait()
        net.sent()
        home.wait()
        for copy in outs:
            copy.wait()


def attend_back(flags, q, k, v, o, db, wo, lse, qr, kr, cosine, sine, ggu, gdb, rb, res, gq, gk):
    bf16, f32 = jnp.bfloat16, jnp.float32
    any_spec = pl.BlockSpec(memory_space=pl.ANY)
    gain = pl.BlockSpec((1, HEAD_DIM), lambda s, f: (0, 0))
    copies = 40

    def vm(a):
        return pltpu.VMEM(a.shape, a.dtype)

    return pl.pallas_call(
        attend_back_kernel,
        out_shape=(
            jax.ShapeDtypeStruct((SEQ_ROWS, 1024), bf16),
            jax.ShapeDtypeStruct((2048, 256), bf16),
            jax.ShapeDtypeStruct((2, 2, 2, 64, HALF_FF), bf16),
            jax.ShapeDtypeStruct((2, 2, 192, 512), bf16),
            jax.ShapeDtypeStruct((2, 64, HALF_FF), bf16),
            jax.ShapeDtypeStruct((192, 512), bf16),
            jax.ShapeDtypeStruct((2, ROWS, MODEL_DIM), bf16),
            jax.ShapeDtypeStruct((2, 8, HEAD_DIM), f32),
        ),
        grid_spec=pltpu.PrefetchScalarGridSpec(
            num_scalar_prefetch=1,
            grid=(4 * KH,),
            in_specs=[any_spec] * 15 + [gain] * 2,
            out_specs=[any_spec] * 7 + [pl.BlockSpec((2, 8, HEAD_DIM), lambda s, f: (0, 0, 0))],
            scratch_shapes=[vm(q), vm(k), vm(v), vm(o), pltpu.VMEM((SEQ_ROWS, MODEL_DIM), bf16), vm(wo), vm(lse), vm(qr), vm(kr)]
            + [vm(cosine), vm(sine)]
            + [
                pltpu.VMEM((SEQ_ROWS, QH * HEAD_DIM), bf16),
                pltpu.VMEM((QH, 8, SEQ_ROWS), f32),
                pltpu.VMEM((SEQ_ROWS, 1024), bf16),
                pltpu.VMEM((2, BLK, HEAD_DIM), f32),
                pltpu.VMEM((KH, SEQ_ROWS, HEAD_DIM), f32),
                pltpu.VMEM((KH, SEQ_ROWS, HEAD_DIM), f32),
                pltpu.VMEM((4, 2, 2, 64, HALF_FF), bf16),
                pltpu.VMEM((4, 2, 192, 512), bf16),
                pltpu.VMEM((4, 2, 2, 64, HALF_FF), bf16),
                pltpu.VMEM((4, 2, 192, 512), bf16),
                pltpu.VMEM((2, 2, 64, HALF_FF), bf16),
                pltpu.VMEM((2, 192, 512), bf16),
                pltpu.VMEM((2, 64, HALF_FF), bf16),
                pltpu.VMEM((192, 512), bf16),
                pltpu.VMEM((512, MODEL_DIM), bf16),
                pltpu.SemaphoreType.DMA((copies,)),
                pltpu.SemaphoreType.DMA((copies,)),
                pltpu.SemaphoreType.DMA((11,)),
                pltpu.SemaphoreType.DMA((17,)),
                pltpu.SemaphoreType.DMA((4,)),
                pltpu.SemaphoreType.DMA((2,)),
                pltpu.SemaphoreType.DMA((2,)),
            ],
        ),
        compiler_params=pltpu.CompilerParams(
            collective_id=4, has_side_effects=True, vmem_limit_bytes=60 * 1024 * 1024
        ),
        cost_estimate=pl.CostEstimate(
            flops=10 * QH * SEQ_ROWS * SEQ_ROWS * HEAD_DIM, bytes_accessed=40 << 20, transcendentals=QH * SEQ_ROWS * SEQ_ROWS
        ),
        name="attend_back",
    )(flags, q, k, v, o, db, wo, lse, qr, kr, cosine, sine, ggu, gdb, rb, res, gq, gk)


def tail_kernel(
    d_in, w_in, n_in, xs, og_in, od_in, fw_in, fd_in, goq_in, dr_ref, ga_ref, dgm_ref, dgh_ref,
    out_query, out_key, out_value, out_out, out_gate, out_up, out_down, gout, tokens,
    d_ref, w_ref, n_ref, x_ref, goq, send_c, recv_c, send_l, recv_l, keep, gt, landed,
    og, od, rx, rxd, rz, rzd, total_w, total_d, fw, fd,
    pq, work, wgo, ry, ryo, ox, oxo, rs, rso, rq, rqo, gs, gr,
    send_sem, recv_sem, load_sem, back_send, back_recv,
):
    where = place()
    y, x, p, l, c = where
    peer = peers_of(x, y, p, l, c)
    red = Reduction(where)
    net = Plan(send_sem, recv_sem)
    second_of = {}
    t = 2 * l + c
    for n, kind in enumerate(KINDS[:2]):
        away = 1 - red.kept(kind)
        second_of[kind] = net.add(peer[red.second_peer(kind)], [(og_in.at[n, away], rx.at[n]), (od_in.at[n, away], rxd.at[n])])
    u_me, u_near = red.kept(ME), red.kept(NEAR)
    go_near = net.add(peer["l"], [(og.at[1], rz.at[1]), (od.at[1], rzd.at[1])])
    go_halves = net.add(peer["c"], [(total_w.at[1 - c], fw.at[c]), (total_d.at[1 - c], fd.at[c])])
    go_give_0 = net.add(peer["c"], [(send_c.at[0], recv_c.at[0])])
    go_give_1 = net.add(peer["c"], [(send_c.at[1], recv_c.at[1])])
    halves = [pl.ds(k * ROWS, ROWS) for k in range(2)]
    go_cross = [net.add(peer["l"], [(send_l.at[half], recv_l.at[half])]) for half in halves]

    def group(yy, xx, pp):
        return (yy * 2 + xx) * 2 + pp

    def moved(sources, groups, targets, at=0):
        return [(src.at[one], dst.at[at + k]) for k, one in enumerate(groups) for src, dst in zip(sources, targets)]

    source, working, small = (pq, goq), (work, wgo), (rs, rso)
    base, across = group(y, x, p), group(y, x, 1 - p)
    give_y = (group(1 - y, 0, p), group(1 - y, 1, p))
    give_x = (group(0, 1 - x, 1 - p), group(1, 1 - x, 1 - p))
    go_own_y = [[net.add(peer["y"], moved((a,), give_y[k : k + 1], (b,), k)) for k in range(2)] for a, b in ((pq, ry), (goq_in, ryo))]
    go_other_x = [[net.add(peer["x"], moved((a,), give_x[k : k + 1], (b,), k)) for k in range(2)] for a, b in ((pq, ox), (goq_in, oxo))]
    go_own_x = [net.add(peer["x"], moved(working[k : k + 1], (group(y, 1 - x, p),), small[k : k + 1], 0)) for k in range(2)]
    go_other_y = [net.add(peer["y"], moved(working[k : k + 1], (group(1 - y, x, 1 - p),), small[k : k + 1], 1)) for k in range(2)]
    go_across = [net.add(peer["p"], moved(working[k : k + 1], (across,), small[k : k + 1], 2)) for k in range(2)]

    def parts(q):
        return [(work.at[base, rows_at(q, 32)], rq.at[t]), (wgo.at[base, rows_at(q, 64)], rqo.at[t])]

    go_last_l = net.add(peer["l"], parts(2 * (1 - l) + c))
    go_last_d = net.add(peer["d"], parts(2 * (1 - l) + 1 - c))
    go_last_c = net.add(peer["c"], parts(2 * l + 1 - c))
    go_gain = [net.add(peer[name], [(gs.at[k], gr.at[k])]) for k, name in enumerate(("c", "x", "y", "p", "l"))]
    home = Return(where, gt, landed, back_send, back_recv)

    def gain_hop(k):
        net.arrived(go_gain[k])
        gs[k + 1] = gs[k] + gr[k]
        if k + 1 < len(AXES):
            net.start(go_gain[k + 1])

    loads = [
        pltpu.make_async_copy(src, dst, load_sem.at[k])
        for k, (src, dst) in enumerate(
            [
                (d_in, d_ref), (w_in, w_ref), (n_in, n_ref), (goq_in, goq), (xs.at[rows_at(owned(p, l, c), OWN)], x_ref),
                (og_in.at[0, u_me], og.at[0]), (og_in.at[1, u_near], og.at[1]),
                (od_in.at[0, u_me], od.at[0]), (od_in.at[1, u_near], od.at[1]),
                (fw_in, rz.at[0]), (fd_in, rzd.at[0]),
            ]
        )
    ]
    for copy in loads:
        copy.start()
    greet(line_peers(p, l, c) + [peer["x"], peer["y"]])
    net.start(second_of[NEAR], second_of[ME], *go_own_y[1], *go_other_x[1])

    def project(ll, cc, write):
        part = d_ref[rows_at(owned(p, ll, cc), OWN), :]

        def chunk(k, carry):
            cols = rows_at(k, 256)
            write(cols, dot(part, w_ref[cols, :], NT))
            return carry

        lax.fori_loop(0, 4, chunk, 0)

    def give(k):
        def write(cols, value):
            send_c[k, :, cols] = value.astype(jnp.bfloat16)

        return write

    def hold(k):
        def write(cols, value):
            keep[k, :, cols] = value

        return write

    def add(k, at, left, right, place_at):
        total = left[at].astype(jnp.float32) + right[place_at].astype(jnp.float32)
        working[k][at] = total.astype(jnp.bfloat16)

    def first_sums(k):
        net.arrived(*go_other_x[k])
        for yy in (0, 1):
            add(k, group(yy, x, 1 - p), source[k], (ox, oxo)[k], yy)
        net.start(go_other_y[k])
        net.arrived(*go_own_y[k])
        for xx in (0, 1):
            add(k, group(y, xx, p), source[k], (ry, ryo)[k], xx)
        net.start(go_own_x[k])

    def second_sums(k):
        net.arrived(go_other_y[k])
        add(k, across, working[k], small[k], 1)
        net.start(go_across[k])
        net.arrived(go_own_x[k])
        add(k, base, working[k], small[k], 0)

    loads[0].wait()
    loads[1].wait()
    project(1 - l, 1 - c, give(0))
    net.start(go_give_0)
    project(1 - l, c, hold(0))
    net.arrived(go_give_0)
    send_l[...] = (keep[0] + recv_c[0].astype(jnp.float32)).astype(jnp.bfloat16)
    net.start(*go_cross)
    for copy in loads[2:]:
        copy.wait()

    def grad_qkv(yy, xx):
        k = yy * 2 + xx
        value = dot(n_ref[:, rows_at(k, 256)], d_ref[...], TN).astype(jnp.bfloat16)
        pq[2 * k] = value[:128]
        pq[2 * k + 1] = value[128:]

    def start_if(index, groups):
        for k in range(2):

            @pl.when(index == k)
            def _():
                net.start(groups[k])

    def one_chunk(k, carry):
        yy, xx = jnp.where(k % 2 == 0, 1 - y, y), jnp.where(k < 2, 1 - x, x)
        grad_qkv(yy, xx)

        @pl.when(k < 2)
        def _():
            start_if(yy, go_other_x[0])

        @pl.when(k % 2 == 0)
        def _():
            start_if(xx, go_own_y[0])

        return carry

    lax.fori_loop(0, 4, one_chunk, 0)
    first_sums(1)
    project(l, 1 - c, give(1))
    net.start(go_give_1)
    project(l, c, hold(1))
    net.arrived(second_of[NEAR])
    og[1] = (og[1].astype(jnp.float32) + rx[1].astype(jnp.float32)).astype(jnp.bfloat16)
    od[1] = (od[1].astype(jnp.float32) + rxd[1].astype(jnp.float32)).astype(jnp.bfloat16)
    net.start(go_near)
    second_sums(1)
    net.arrived(go_give_1)
    gs[0] = jnp.zeros_like(gs[0])

    def rows_back(k, total):
        rows = rows_at(k, 64)
        value = x_ref[rows, :].astype(jnp.float32)
        grad = keep[1, rows, :] + recv_c[1, rows, :].astype(jnp.float32) + recv_l[rows, :].astype(jnp.float32)
        r = lax.rsqrt(jnp.mean(value * value, axis=-1, keepdims=True) + EPS)
        scaled = value * r
        gained = grad * ga_ref[...]
        back = r * (gained - scaled * jnp.mean(scaled * gained, axis=-1, keepdims=True))
        gt[rows, :] = (dr_ref[rows, :] + back).astype(jnp.bfloat16)
        return total + jnp.sum(grad * scaled, axis=0, keepdims=True)

    d_attn = jnp.zeros((1, MODEL_DIM), jnp.float32)
    for k in range(2):
        net.arrived(go_cross[k])
        d_attn = lax.fori_loop(4 * k, 4 * k + 4, rows_back, d_attn)
        home.start_one(k)
        if k == 0:
            first_sums(0)
    d_mlp = jnp.sum(dgm_ref[...], axis=0, keepdims=True)
    for k in range(8):
        lanes = slice(k * 128, (k + 1) * 128)
        gs[0, k : k + 1, :] = d_attn[:, lanes]
        gs[0, 8 + k : 9 + k, :] = d_mlp[:, lanes]
    for k in range(2):
        gs[0, 16 + k : 17 + k, :] = jnp.sum(dgh_ref[k], axis=0, keepdims=True)
    net.start(go_gain[0])
    second_sums(0)
    gain_hop(0)
    net.arrived(second_of[ME])
    gain_hop(1)
    net.arrived(go_near)
    for cc in range(2):
        rows = pl.ds(32 * cc, 32)
        total_w[cc] = (
            og[0, :, rows, :].astype(jnp.float32) + rx[0, :, rows, :].astype(jnp.float32)
            + rz[0, :, rows, :].astype(jnp.float32) + rz[1, :, rows, :].astype(jnp.float32)
        )
        rows = pl.ds(96 * cc, 96)
        total_d[cc] = (
            od[0, rows, :].astype(jnp.float32) + rxd[0, rows, :].astype(jnp.float32)
            + rzd[0, rows, :].astype(jnp.float32) + rzd[1, rows, :].astype(jnp.float32)
        )
    net.start(go_halves)
    fw[c] = total_w[c]
    fd[c] = total_d[c]
    gain_hop(2)
    net.arrived(go_halves)
    for half in range(2):
        cols = slice(half * HALF_FF, (half + 1) * HALF_FF)
        out_gate[:, cols] = fw[half, 0]
        out_up[:, cols] = fw[half, 1]
        out_down[:, half * 512 : (half + 1) * 512] = fd[half]
    for k in (1, 0):
        net.arrived(go_across[k])
        add(k, base, working[k], small[k], 2)
    net.start(go_last_l, go_last_d, go_last_c)
    rq[t] = work[base, rows_at(t, 32), :]
    rqo[t] = wgo[base, rows_at(t, 64), :]
    gain_hop(3)
    home.wait()
    tokens[...] = landed[...].astype(jnp.float32)
    gain_hop(4)
    gout[...] = gs[len(AXES)]
    net.arrived(go_last_l, go_last_d, go_last_c)
    for q in range(4):
        value = rq[q].astype(jnp.float32)
        out_query[:, 512 * q : 512 * (q + 1)] = value[:, :512]
        out_key[:, 256 * q : 256 * (q + 1)] = value[:, 512:768]
        out_value[:, 256 * q : 256 * (q + 1)] = value[:, 768:]
        out_out[:, 256 * q : 256 * (q + 1)] = rqo[q].astype(jnp.float32)
    net.sent()


def tail(d, w, normed, xs, og, od, fw, fd, goq, d_resid, g_attn, d_g_mlp, d_g_heads):
    bf16, f32 = jnp.bfloat16, jnp.float32
    any_spec = pl.BlockSpec(memory_space=pl.ANY)
    vmem = pl.BlockSpec(memory_space=pltpu.VMEM)
    copies = 48
    wide, deep = (2, 64, HALF_FF), (192, 512)
    own = (OWN, MODEL_DIM)
    big, tall = (128, 1024), (256, 256)

    def vm(a):
        return pltpu.VMEM(a.shape, a.dtype)

    def low(*shape):
        return pltpu.VMEM(shape, bf16)

    goq = goq.reshape(8, 256, 256)
    return pl.pallas_call(
        tail_kernel,
        out_shape=(
            jax.ShapeDtypeStruct((32, 2048), f32),
            jax.ShapeDtypeStruct((32, 1024), f32),
            jax.ShapeDtypeStruct((32, 1024), f32),
            jax.ShapeDtypeStruct((64, 1024), f32),
            jax.ShapeDtypeStruct((32, FF), f32),
            jax.ShapeDtypeStruct((32, FF), f32),
            jax.ShapeDtypeStruct((96, 1024), f32),
            jax.ShapeDtypeStruct((24, 128), f32),
            jax.ShapeDtypeStruct((2, ROWS, MODEL_DIM), f32),
        ),
        in_specs=[any_spec] * 9 + [vmem] * 4,
        out_specs=[vmem] * 9,
        scratch_shapes=[
            vm(d), vm(w), vm(normed), low(*own), vm(goq),
            low(2, *own), low(2, *own), low(*own), low(*own),
            pltpu.VMEM((2,) + own, f32),
            low(*own), low(2, ROWS, MODEL_DIM),
            low(2, *wide), low(2, *deep),
            low(2, *wide), low(2, *deep), low(2, *wide), low(2, *deep),
            pltpu.VMEM((2, 2, 32, HALF_FF), f32), pltpu.VMEM((2, 96, 512), f32),
            pltpu.VMEM((2, 2, 32, HALF_FF), f32), pltpu.VMEM((2, 96, 512), f32),
            low(8, *big), low(8, *big), low(8, *tall),
            low(2, *big), low(2, *tall), low(2, *big), low(2, *tall), low(3, *big), low(3, *tall),
            low(4, 32, 1024), low(4, 64, 256),
            pltpu.VMEM((6, 24, 128), f32), pltpu.VMEM((5, 24, 128), f32),
            pltpu.SemaphoreType.DMA((copies,)),
            pltpu.SemaphoreType.DMA((copies,)),
            pltpu.SemaphoreType.DMA((11,)),
            pltpu.SemaphoreType.DMA((2,)),
            pltpu.SemaphoreType.DMA((2,)),
        ],
        compiler_params=pltpu.CompilerParams(
            collective_id=5, has_side_effects=True, vmem_limit_bytes=60 * 1024 * 1024
        ),
        name="tail_reduce",
    )(d, w, normed, xs, og, od, fw, fd, goq, d_resid, g_attn, d_g_mlp, d_g_heads)


def pick(value, index):
    return lax.dynamic_index_in_dim(value, index, 0, keepdims=False)


def fast_device(tokens, cotangent, starts, w_query, key_matrix, value_matrix, w_out, w_gate, w_up, w_down, gains):
    p = lax.axis_index("p")
    gn = jnp.pad(gains.astype(jnp.float32), (0, 952)).reshape(8, 128)
    half_steps = jnp.arange(HEAD_DIM // 2, dtype=jnp.float32)
    inverse = THETA ** (-2.0 * half_steps / HEAD_DIM)
    inverse = jnp.broadcast_to(jnp.concatenate([inverse, inverse])[None], (8, HEAD_DIM))
    own_starts = pick(starts, p)
    block_at = jnp.arange(SEQ_ROWS // PIECE, dtype=jnp.int32) * PIECE
    flags = jnp.any(own_starts[None, :] == block_at[:, None], axis=1).astype(jnp.int32)
    xs, w_qkv, woq, gf, wgu, wdn, cosine, sine = front(
        tokens, w_query, key_matrix, value_matrix, w_out, gn, w_gate, w_up, w_down, inverse
    )
    xs = xs.reshape(SEQ_ROWS, MODEL_DIM)
    gain_all = gf.reshape(32, 1024)[:, :72].reshape(2304)
    g_attn = gain_all[None, :1024]
    g_mlp = gain_all[None, 1024:2048]
    g_q = gain_all[None, 2048:2176]
    g_k = gain_all[None, 2176:]
    normed, q, k, v, q_raw, k_raw, attn, lse, wo, wgu, wdn = attend(
        flags, xs, w_qkv, g_attn, g_q, g_k, cosine, sine, woq, wgu, wdn
    )
    resid, mlp_in, wgu, wdn, wdx, dy = finish_resid(attn, wo, g_mlp, xs, cotangent, wgu, wdn)
    ggu, gdb, rb, d_resid, d_branch, result, d_g_mlp = feed_forward(
        mlp_in.reshape(1024, MODEL_DIM), dy.reshape(1024, MODEL_DIM), wgu, wdn, wdx, resid, g_mlp
    )
    d_qkv, goq, og, od, fw, fd, output, d_g_heads = attend_back(
        flags, q, k, v, attn, d_branch, wo, lse, q_raw, k_raw, cosine, sine, ggu, gdb, rb, result, g_q, g_k
    )
    *grads, gains_sum, grad_tokens = tail(
        d_qkv, w_qkv, normed, xs, og, od, fw, fd, goq, d_resid, g_attn, d_g_mlp, d_g_heads
    )
    device = lax.axis_index(AXES)
    out_gains = lax.dynamic_slice(gains_sum.reshape(3072), (device * 72,), (72,))
    return (output, grad_tokens, *grads, out_gains)


def fast_solution(mesh):
    wide = Mesh(mesh.devices.reshape(2, 2, 2, 2, 2), AXES)
    rows = ("y", "x")
    places = ("p", "l", "c")
    weight = P(AXES, None)
    return jax.shard_map(
        fast_device,
        mesh=wide,
        in_specs=(P(rows, places, None), P(rows, places, None), P(rows, None)) + (weight,) * 7 + (P(AXES),),
        out_specs=(P(rows, places, None), P(rows, places, None)) + (weight,) * 7 + (P(AXES),),
        check_vma=False,
    )


def solution(mesh):
    if dict(mesh.shape) == {"dp": 4, "ctx": 8}:
        return fast_solution(mesh)
    return generic_solution(mesh)
```

```python
import functools
import math

import jax
import jax.numpy as jnp
from jax import lax
from jax.experimental import pallas as pl
from jax.experimental.pallas import tpu as pltpu
from jax.sharding import Mesh
from jax.sharding import PartitionSpec as P

MODEL_DIM = 1024
QUERY_HEADS = 16
KEY_VALUE_HEADS = 8
HEAD_DIM = 128
SEQUENCE_TOKENS = 2048
PIECE = 256
NPIECE = 4


EPS = 1e-06
THETA = 1000000.0
NEG = -1e30


def rms_norm(incoming_values, gain_vector):
    return (
        incoming_values
        * lax.rsqrt(jnp.mean(incoming_values * incoming_values, axis=-1, keepdims=True) + EPS)
        * gain_vector
    )


def rope_tables(positions):
    half_steps = jnp.arange(HEAD_DIM // 2, dtype=jnp.float32)
    inverse = THETA ** (-2.0 * half_steps / HEAD_DIM)
    angles = positions.astype(jnp.float32)[:, None] * inverse[None, :]
    angles = jnp.concatenate([angles, angles], axis=-1)
    return (jnp.cos(angles), jnp.sin(angles))


def rotate(incoming_values, cosine_table, sine_table):
    half_dim = HEAD_DIM // 2
    turned = jnp.concatenate(
        [-incoming_values[..., half_dim:], incoming_values[..., :half_dim]], axis=-1
    )
    return incoming_values * cosine_table[:, None, :] + turned * sine_table[:, None, :]


def per_head_route(unrotated_projection, gain_vector, cosine_table, sine_table, head_count):
    shaped = unrotated_projection.reshape(unrotated_projection.shape[:-1] + (head_count, HEAD_DIM))
    return rotate(rms_norm(shaped, gain_vector), cosine_table, sine_table).reshape(
        unrotated_projection.shape
    )


def piece_ids(positions, piece_starts):
    inside = (positions[:, None] >= piece_starts[None, :]) & (
        positions[:, None] < piece_starts[None, :] + PIECE
    )
    number = jnp.arange(1, NPIECE + 1, dtype=jnp.int32)
    return jnp.sum(jnp.where(inside, number[None, :], 0), axis=1) - 1


def visible(query_pos, query_id, key_pos, key_id):
    causal = key_pos[None, :] <= query_pos[:, None]
    same_piece = (query_id[:, None] == key_id[None, :]) & (query_id[:, None] >= 0)
    return causal | same_piece


def swiglu(gate_proj, up_proj):
    return jax.nn.silu(gate_proj) * up_proj


def block_extent(kv_count, per_head):
    target = max(1, 512 // per_head)
    chosen = 1
    for candidate in range(1, kv_count + 1):
        if kv_count % candidate == 0 and candidate <= target:
            chosen = candidate
    return chosen


def attend_forward(incoming_query, incoming_keys, incoming_values, allowed, head_group_block):
    sequence_rows = incoming_query.shape[0]
    query_group_factor = QUERY_HEADS // KEY_VALUE_HEADS
    scaling = 1.0 / math.sqrt(HEAD_DIM)
    query_per_head = incoming_query.reshape(
        sequence_rows, KEY_VALUE_HEADS, query_group_factor, HEAD_DIM
    )
    key_per_head = incoming_keys.reshape(incoming_keys.shape[0], KEY_VALUE_HEADS, HEAD_DIM)
    value_per_head = incoming_values.reshape(incoming_values.shape[0], KEY_VALUE_HEADS, HEAD_DIM)
    mixed_parts = []
    total_parts = []
    for head_offset in range(0, KEY_VALUE_HEADS, head_group_block):
        q_part = query_per_head[:, head_offset : head_offset + head_group_block]
        k_part = key_per_head[:, head_offset : head_offset + head_group_block]
        v_part = value_per_head[:, head_offset : head_offset + head_group_block]
        scores = (
            jnp.einsum("tagd,kad->agtk", q_part, k_part, preferred_element_type=jnp.float32)
            * scaling
        )
        scores = jnp.where(allowed[None, None], scores, NEG)
        row_max = jnp.max(scores, axis=-1, keepdims=True)
        exp_scores = jnp.exp(scores - row_max)
        summed = jnp.sum(exp_scores, axis=-1, keepdims=True)
        prob_low = (exp_scores / summed).astype(jnp.bfloat16)
        mixed_parts.append(
            jnp.einsum("agtk,kad->tagd", prob_low, v_part, preferred_element_type=jnp.float32)
        )
        total_parts.append(row_max + jnp.log(summed))
    mixed_out = jnp.concatenate(mixed_parts, axis=1).reshape(sequence_rows, QUERY_HEADS * HEAD_DIM)
    return (mixed_out, jnp.concatenate(total_parts, axis=0))


def attend_backward(
    incoming_query,
    incoming_keys,
    incoming_values,
    allowed,
    log_total,
    mixed_gradient,
    head_group_block,
):
    sequence_rows = incoming_query.shape[0]
    key_row_matrix = incoming_keys.shape[0]
    query_group_factor = QUERY_HEADS // KEY_VALUE_HEADS
    scaling = 1.0 / math.sqrt(HEAD_DIM)
    query_per_head = incoming_query.reshape(
        sequence_rows, KEY_VALUE_HEADS, query_group_factor, HEAD_DIM
    )
    gradient_per_head = mixed_gradient.reshape(
        sequence_rows, KEY_VALUE_HEADS, query_group_factor, HEAD_DIM
    )
    key_per_head = incoming_keys.reshape(key_row_matrix, KEY_VALUE_HEADS, HEAD_DIM)
    value_per_head = incoming_values.reshape(key_row_matrix, KEY_VALUE_HEADS, HEAD_DIM)
    dq_parts = []
    key_gradient_pieces = []
    value_gradient_pieces = []
    for head_offset in range(0, KEY_VALUE_HEADS, head_group_block):
        q_part = query_per_head[:, head_offset : head_offset + head_group_block]
        g_part = gradient_per_head[:, head_offset : head_offset + head_group_block]
        k_part = key_per_head[:, head_offset : head_offset + head_group_block]
        v_part = value_per_head[:, head_offset : head_offset + head_group_block]
        scores = (
            jnp.einsum("tagd,kad->agtk", q_part, k_part, preferred_element_type=jnp.float32)
            * scaling
        )
        scores = jnp.where(allowed[None, None], scores, NEG)
        prob_all = jnp.exp(scores - log_total[head_offset : head_offset + head_group_block])
        prob_low = prob_all.astype(jnp.bfloat16)
        d_probs = jnp.einsum("tagd,kad->agtk", g_part, v_part, preferred_element_type=jnp.float32)
        row_dot = jnp.sum(prob_all * d_probs, axis=-1, keepdims=True)
        d_scores = (prob_all * (d_probs - row_dot)).astype(jnp.bfloat16)
        dq_parts.append(
            jnp.einsum("agtk,kad->tagd", d_scores, k_part, preferred_element_type=jnp.float32)
            * scaling
        )
        key_gradient_pieces.append(
            jnp.einsum("agtk,tagd->kad", d_scores, q_part, preferred_element_type=jnp.float32)
            * scaling
        )
        value_gradient_pieces.append(
            jnp.einsum("agtk,tagd->kad", prob_low, g_part, preferred_element_type=jnp.float32)
        )
    d_query = jnp.concatenate(dq_parts, axis=1).reshape(sequence_rows, QUERY_HEADS * HEAD_DIM)
    key_gradient = jnp.concatenate(key_gradient_pieces, axis=1).reshape(
        key_row_matrix, KEY_VALUE_HEADS * HEAD_DIM
    )
    value_gradient = jnp.concatenate(value_gradient_pieces, axis=1).reshape(
        key_row_matrix, KEY_VALUE_HEADS * HEAD_DIM
    )
    return (d_query, key_gradient, value_gradient)


def generic_device(
    tokens, cotangent, starts, w_query, key_matrix, value_matrix, w_out, w_gate, w_up, w_down, gains
):
    sequence_count, sequence_rows, model_width = tokens.shape
    number_of_rows = sequence_count * sequence_rows
    head_group_block = block_extent(KEY_VALUE_HEADS, QUERY_HEADS // KEY_VALUE_HEADS * sequence_rows)
    attn_set = (
        lax.all_gather(w_query, ("dp", "ctx"), axis=0, tiled=True),
        lax.all_gather(key_matrix, ("dp", "ctx"), axis=0, tiled=True),
        lax.all_gather(value_matrix, ("dp", "ctx"), axis=0, tiled=True),
        lax.all_gather(w_out, ("dp", "ctx"), axis=0, tiled=True),
        lax.all_gather(gains, ("dp", "ctx"), axis=0, tiled=True),
    )
    mlp_set = (
        lax.all_gather(w_gate, ("dp", "ctx"), axis=0, tiled=True),
        lax.all_gather(w_up, ("dp", "ctx"), axis=0, tiled=True),
        lax.all_gather(w_down, ("dp", "ctx"), axis=0, tiled=True),
    )
    gain_all = attn_set[4].astype(jnp.float32)
    g_attn = gain_all[:MODEL_DIM]
    g_mlp = gain_all[MODEL_DIM : 2 * MODEL_DIM]
    g_query = gain_all[2 * MODEL_DIM : 2 * MODEL_DIM + HEAD_DIM]
    key_grad_total = gain_all[2 * MODEL_DIM + HEAD_DIM :]
    positions = lax.axis_index("ctx") * sequence_rows + jnp.arange(sequence_rows, dtype=jnp.int32)
    key_places = jnp.arange(SEQUENCE_TOKENS, dtype=jnp.int32)
    cosine_table, sine_table = rope_tables(positions)

    def query_map(unrotated_projection, gain_vector):
        return per_head_route(
            unrotated_projection, gain_vector, cosine_table, sine_table, QUERY_HEADS
        )

    def key_map(unrotated_projection, gain_vector):
        return per_head_route(
            unrotated_projection, gain_vector, cosine_table, sine_table, KEY_VALUE_HEADS
        )

    flat_in = tokens.reshape(number_of_rows, model_width).astype(jnp.float32)
    normed = rms_norm(flat_in, g_attn).astype(jnp.bfloat16)
    query_raw = jnp.dot(normed, attn_set[0], preferred_element_type=jnp.float32).reshape(
        sequence_count, sequence_rows, QUERY_HEADS * HEAD_DIM
    )
    key_unrotated = jnp.dot(normed, attn_set[1], preferred_element_type=jnp.float32).reshape(
        sequence_count, sequence_rows, KEY_VALUE_HEADS * HEAD_DIM
    )
    value_reduced = jnp.dot(normed, attn_set[2], preferred_element_type=jnp.float32).astype(
        jnp.bfloat16
    )
    value_reduced = value_reduced.reshape(sequence_count, sequence_rows, KEY_VALUE_HEADS * HEAD_DIM)
    query_reduced = query_map(query_raw, g_query).astype(jnp.bfloat16)
    key_reduced = key_map(key_unrotated, key_grad_total).astype(jnp.bfloat16)
    mask_list = []
    mixed_list = []
    total_list = []
    for seq_index in range(sequence_count):
        query_ids = piece_ids(positions, starts[seq_index])
        key_ids = piece_ids(key_places, starts[seq_index])
        allowed = visible(positions, query_ids, key_places, key_ids)
        key_full, value_full = (
            lax.all_gather(key_reduced[seq_index], "ctx", axis=0, tiled=True),
            lax.all_gather(value_reduced[seq_index], "ctx", axis=0, tiled=True),
        )
        mixed_out, log_total = attend_forward(
            query_reduced[seq_index], key_full, value_full, allowed, head_group_block
        )
        mask_list.append(allowed)
        mixed_list.append(mixed_out)
        total_list.append(log_total)
    attn_low = (
        jnp.stack(mixed_list).reshape(number_of_rows, QUERY_HEADS * HEAD_DIM).astype(jnp.bfloat16)
    )
    residual = flat_in + jnp.dot(attn_low, attn_set[3], preferred_element_type=jnp.float32)
    mlp_in = rms_norm(residual, g_mlp).astype(jnp.bfloat16)
    gate_proj = jnp.dot(mlp_in, mlp_set[0], preferred_element_type=jnp.float32)
    up_proj = jnp.dot(mlp_in, mlp_set[1], preferred_element_type=jnp.float32)
    hidden = swiglu(gate_proj, up_proj).astype(jnp.bfloat16)
    result = residual + jnp.dot(hidden, mlp_set[2], preferred_element_type=jnp.float32)
    output = result.astype(jnp.bfloat16).reshape(tokens.shape)
    mlp_back = (
        lax.all_gather(w_gate, ("dp", "ctx"), axis=0, tiled=True),
        lax.all_gather(w_up, ("dp", "ctx"), axis=0, tiled=True),
        lax.all_gather(w_down, ("dp", "ctx"), axis=0, tiled=True),
    )
    grad_flat = cotangent.reshape(number_of_rows, model_width)
    grad_down = jnp.dot(hidden.T, grad_flat, preferred_element_type=jnp.float32)
    d_hidden = jnp.dot(grad_flat, mlp_back[2].T, preferred_element_type=jnp.float32)
    swiglu_pull = jax.vjp(swiglu, gate_proj, up_proj)[1]
    d_gate, d_up = swiglu_pull(d_hidden)
    d_gate = d_gate.astype(jnp.bfloat16)
    d_up = d_up.astype(jnp.bfloat16)
    grad_gate = jnp.dot(mlp_in.T, d_gate, preferred_element_type=jnp.float32)
    grad_up = jnp.dot(mlp_in.T, d_up, preferred_element_type=jnp.float32)
    mlp_grads = (
        lax.psum_scatter(grad_gate, ("dp", "ctx"), scatter_dimension=0, tiled=True),
        lax.psum_scatter(grad_up, ("dp", "ctx"), scatter_dimension=0, tiled=True),
        lax.psum_scatter(grad_down, ("dp", "ctx"), scatter_dimension=0, tiled=True),
    )
    d_mlp_in = jnp.dot(d_gate, mlp_back[0].T, preferred_element_type=jnp.float32)
    d_mlp_in = d_mlp_in + jnp.dot(d_up, mlp_back[1].T, preferred_element_type=jnp.float32)
    mlp_norm_pull = jax.vjp(rms_norm, residual, g_mlp)[1]
    d_resid_norm, d_g_mlp = mlp_norm_pull(d_mlp_in)
    d_resid = grad_flat.astype(jnp.float32) + d_resid_norm
    attn_back = (
        lax.all_gather(w_query, ("dp", "ctx"), axis=0, tiled=True),
        lax.all_gather(key_matrix, ("dp", "ctx"), axis=0, tiled=True),
        lax.all_gather(value_matrix, ("dp", "ctx"), axis=0, tiled=True),
        lax.all_gather(w_out, ("dp", "ctx"), axis=0, tiled=True),
        lax.all_gather(gains, ("dp", "ctx"), axis=0, tiled=True),
    )
    d_branch = d_resid.astype(jnp.bfloat16)
    grad_out = jnp.dot(attn_low.T, d_branch, preferred_element_type=jnp.float32)
    d_attn = jnp.dot(d_branch, attn_back[3].T, preferred_element_type=jnp.float32).astype(
        jnp.bfloat16
    )
    d_attn = d_attn.reshape(sequence_count, sequence_rows, QUERY_HEADS * HEAD_DIM)
    dq_list = []
    dk_list = []
    value_gradient_list = []
    for seq_index in range(sequence_count):
        key_full, value_full = (
            lax.all_gather(key_reduced[seq_index], "ctx", axis=0, tiled=True),
            lax.all_gather(value_reduced[seq_index], "ctx", axis=0, tiled=True),
        )
        d_query_seq, d_key_full, d_value_full = attend_backward(
            query_reduced[seq_index],
            key_full,
            value_full,
            mask_list[seq_index],
            total_list[seq_index],
            d_attn[seq_index],
            head_group_block,
        )
        d_key_seq, d_value_seq = (
            lax.psum_scatter(
                d_key_full.astype(jnp.bfloat16), "ctx", scatter_dimension=0, tiled=True
            ).astype(jnp.float32),
            lax.psum_scatter(
                d_value_full.astype(jnp.bfloat16), "ctx", scatter_dimension=0, tiled=True
            ).astype(jnp.float32),
        )
        dq_list.append(d_query_seq)
        dk_list.append(d_key_seq)
        value_gradient_list.append(d_value_seq)
    d_query = jnp.stack(dq_list)
    key_gradient = jnp.stack(dk_list)
    value_gradient_reduced = (
        jnp.stack(value_gradient_list)
        .reshape(number_of_rows, KEY_VALUE_HEADS * HEAD_DIM)
        .astype(jnp.bfloat16)
    )
    query_pull = jax.vjp(query_map, query_raw, g_query)[1]
    d_query_raw, d_g_query = query_pull(d_query)
    key_pull = jax.vjp(key_map, key_unrotated, key_grad_total)[1]
    key_gradient_unrotated, d_g_key = key_pull(key_gradient)
    d_query_low = d_query_raw.reshape(number_of_rows, QUERY_HEADS * HEAD_DIM).astype(jnp.bfloat16)
    key_gradient_reduced = key_gradient_unrotated.reshape(
        number_of_rows, KEY_VALUE_HEADS * HEAD_DIM
    ).astype(jnp.bfloat16)
    grad_query = jnp.dot(normed.T, d_query_low, preferred_element_type=jnp.float32)
    grad_key = jnp.dot(normed.T, key_gradient_reduced, preferred_element_type=jnp.float32)
    grad_value = jnp.dot(normed.T, value_gradient_reduced, preferred_element_type=jnp.float32)
    d_normed = jnp.dot(d_query_low, attn_back[0].T, preferred_element_type=jnp.float32)
    d_normed = d_normed + jnp.dot(
        key_gradient_reduced, attn_back[1].T, preferred_element_type=jnp.float32
    )
    d_normed = d_normed + jnp.dot(
        value_gradient_reduced, attn_back[2].T, preferred_element_type=jnp.float32
    )
    input_pull = jax.vjp(rms_norm, flat_in, g_attn)[1]
    d_input_norm, d_g_attn = input_pull(d_normed)
    grad_tokens = (d_resid + d_input_norm).reshape(tokens.shape)
    grad_gains = jnp.concatenate([d_g_attn, d_g_mlp, d_g_query, d_g_key])
    attn_grads = (
        lax.psum_scatter(grad_query, ("dp", "ctx"), scatter_dimension=0, tiled=True),
        lax.psum_scatter(grad_key, ("dp", "ctx"), scatter_dimension=0, tiled=True),
        lax.psum_scatter(grad_value, ("dp", "ctx"), scatter_dimension=0, tiled=True),
        lax.psum_scatter(grad_out, ("dp", "ctx"), scatter_dimension=0, tiled=True),
        lax.psum_scatter(grad_gains, ("dp", "ctx"), scatter_dimension=0, tiled=True),
    )
    return (
        output,
        grad_tokens,
        attn_grads[0],
        attn_grads[1],
        attn_grads[2],
        attn_grads[3],
        mlp_grads[0],
        mlp_grads[1],
        mlp_grads[2],
        attn_grads[4],
    )


def generic_solution(mesh):
    return jax.shard_map(
        generic_device,
        mesh=mesh,
        in_specs=(
            P("dp", "ctx", None),
            P("dp", "ctx", None),
            P("dp", None),
            P(("dp", "ctx"), None),
            P(("dp", "ctx"), None),
            P(("dp", "ctx"), None),
            P(("dp", "ctx"), None),
            P(("dp", "ctx"), None),
            P(("dp", "ctx"), None),
            P(("dp", "ctx"), None),
            P(("dp", "ctx")),
        ),
        out_specs=(
            P("dp", "ctx", None),
            P("dp", "ctx", None),
            P(("dp", "ctx"), None),
            P(("dp", "ctx"), None),
            P(("dp", "ctx"), None),
            P(("dp", "ctx"), None),
            P(("dp", "ctx"), None),
            P(("dp", "ctx"), None),
            P(("dp", "ctx"), None),
            P(("dp", "ctx")),
        ),
        check_vma=False,
    )


AXES = ("y", "x", "p", "l", "c")
FF = 3072
HALF_FF = FF // 2
ROWS = 256
SEQ_ROWS = SEQUENCE_TOKENS
OWN = SEQ_ROWS // 4
BLK = 512
NBLK = SEQ_ROWS // BLK
QH = 4
KH = 2
MESH = pl.DeviceIdType.MESH
SCALE = 1.0 / math.sqrt(HEAD_DIM)
LOG2E = 1.4426950408889634
VMEM_LIMIT = 62 * 1024 * 1024
NT = (((1,), (1,)), ((), ()))
TN = (((0,), (0,)), ((), ()))


def dot(a, b, dims=None):
    if dims is None:
        dims = (((1,), (0,)), ((), ()))
    return lax.dot_general(a, b, dims, preferred_element_type=jnp.float32)


def greet(peers):
    barrier = pltpu.get_barrier_semaphore()
    for peer in peers:
        pl.semaphore_signal(barrier, inc=1, device_id=peer, device_id_type=MESH)
    pl.semaphore_wait(barrier, len(peers))


class Plan:
    def __init__(self, send_sem, recv_sem):
        self.send_sem = send_sem
        self.recv_sem = recv_sem
        self.count = 0
        self.entries = []

    def add(self, peer, pairs):
        self.entries.append((peer, pairs, self.count))
        self.count += len(pairs)
        return len(self.entries) - 1

    def copies(self, name):
        peer, pairs, at = self.entries[name]
        return [
            pltpu.make_async_remote_copy(
                src_ref=src,
                dst_ref=dst,
                send_sem=self.send_sem.at[at + k],
                recv_sem=self.recv_sem.at[at + k],
                device_id=peer,
                device_id_type=MESH,
            )
            for k, (src, dst) in enumerate(pairs)
        ]

    def start(self, *names):
        for name in names:
            for copy in self.copies(name):
                copy.start()

    def arrived(self, *names):
        for name in names:
            for copy in self.copies(name):
                copy.wait_recv()

    def sent(self):
        for name in range(len(self.entries)):
            for copy in self.copies(name):
                copy.wait_send()


def place():
    return tuple(lax.axis_index(name) for name in AXES)


def peers_of(x, y, p, l, c):
    return {
        "c": {"c": 1 - c},
        "l": {"l": 1 - l},
        "d": {"l": 1 - l, "c": 1 - c},
        "p": {"p": 1 - p},
        "x": {"x": 1 - x},
        "y": {"y": 1 - y},
    }


def owned(p, l, c):
    return 2 * c + (p + l + c) % 2


def rows_at(index, size, count=1):
    return pl.ds(pl.multiple_of(index * size, size), size * count)


def in_place(*refs):
    return [(ref, ref) for ref in refs]


def front_kernel(tok, wq, wk, wv, wo, gn, wg, wu, wd, inverse, xs, wa, woq, gf, wgu, wdn, cosine, sine, send_sem, recv_sem, in_sem, local_sem, *staged):
    y, x, p, l, c = place()
    peer = peers_of(x, y, p, l, c)
    block = 4 * p + 2 * l + c
    group = (y * 2 + x) * 8
    me = group + block
    t = 2 * l + c
    net = Plan(send_sem, recv_sem)

    def quarter(q):
        return [
            (wq.at[:, rows_at(q, 512)], wa.at[rows_at(me, 32), pl.ds(0, 512)]),
            (wk.at[:, rows_at(q, 256)], wa.at[rows_at(me, 32), pl.ds(512, 256)]),
            (wv.at[:, rows_at(q, 256)], wa.at[rows_at(me, 32), pl.ds(768, 256)]),
            (wo.at[:, rows_at(q, 256)], woq.at[rows_at(me, 64)]),
            (gn, gf.at[me]),
        ]

    def half(h):
        return [
            (wg.at[:, rows_at(h, HALF_FF)], wgu.at[0, rows_at(me, 32)]),
            (wu.at[:, rows_at(h, HALF_FF)], wgu.at[1, rows_at(me, 32)]),
            (wd.at[:, rows_at(h, 512)], wdn.at[rows_at(me, 96)]),
        ]

    def span(base, piece):
        if piece < 2:
            return in_place(wa.at[rows_at(base // 2 + piece, 64)])
        return in_place(woq.at[rows_at(base // 4, 256)], gf.at[pl.ds(base, 4)])

    def chip(yy, xx, pp, ll):
        slot = (yy * 2 + xx) * 4 + 2 * pp + ll
        return in_place(wgu.at[:, rows_at(slot, 64)], wdn.at[rows_at(slot, 192)])

    mine, other = group + 4 * p, group + 4 * (1 - p)
    go_first_l = net.add(peer["l"], quarter(2 * (1 - l) + c))
    go_first_d = net.add(peer["d"], quarter(2 * (1 - l) + 1 - c))
    go_first_c = net.add(peer["c"], quarter(2 * l + 1 - c))
    go_near = net.add(peer["l"], [(tok.at[p], xs.at[block])])
    upper, lower = pl.ds(0, ROWS // 2), pl.ds(ROWS // 2, ROWS // 2)
    go_far_0 = net.add(peer["p"], [(tok.at[1 - p, upper], xs.at[block, upper])])
    go_far_1 = net.add(peer["p"], [(tok.at[1 - p, lower], xs.at[block, lower])])
    go_near_c = net.add(peer["c"], [(tok.at[p], xs.at[block])])
    pieces = range(3)
    go_across = [net.add(peer["p"], span(mine, k)) for k in pieces]
    go_own_x = [net.add(peer["x"], span(mine, k)) for k in pieces]
    go_near_relay = net.add(peer["c"], in_place(xs.at[block ^ 2]))
    go_own_y = [net.add(peer["y"], span(mine, k) + span((y * 2 + 1 - x) * 8 + 4 * p, k)) for k in pieces]
    go_other_y = [net.add(peer["y"], span(other, k)) for k in pieces]
    go_far_l0 = net.add(peer["l"], in_place(xs.at[block ^ 4, upper]))
    go_far_l1 = net.add(peer["l"], in_place(xs.at[block ^ 4, lower]))
    go_far_relay = net.add(peer["c"], in_place(xs.at[block ^ 4]))
    go_other_x = [net.add(peer["x"], span(other, k) + span(((1 - y) * 2 + x) * 8 + 4 * (1 - p), k)) for k in pieces]
    go_far_l_relay = net.add(peer["c"], in_place(xs.at[block ^ 6]))
    go_mlp_c = net.add(peer["c"], half(1 - c))
    go_mlp_near = net.add(peer["l"], chip(y, x, p, l))
    go_mlp_x = net.add(peer["x"], chip(y, x, p, l))
    moves = quarter(t) + half(c) + [(tok.at[p], xs.at[block])]
    taken = [pltpu.make_async_copy(src, stage, in_sem.at[k]) for k, ((src, dst), stage) in enumerate(zip(moves, staged))]
    own = [pltpu.make_async_copy(stage, dst, local_sem.at[k]) for k, ((src, dst), stage) in enumerate(zip(moves, staged))]
    for copy in taken:
        copy.start()
    greet(list(peer.values()))
    net.start(go_first_l, go_first_d, go_first_c, go_far_0, go_near_c, go_mlp_c)
    for copy in taken:
        copy.wait()
    for copy in own:
        copy.start()

    def table(first, last):
        def chunk(k, carry):
            rows = rows_at(k, 64)
            position = (lax.broadcasted_iota(jnp.int32, (64, HEAD_DIM), 0) + k * 64).astype(jnp.float32)
            lane = lax.broadcasted_iota(jnp.int32, (64, HEAD_DIM), 1)
            angle = position * inverse[0:1, :]
            cosine[rows, :] = jnp.cos(angle)
            sine[rows, :] = jnp.where(lane < HEAD_DIM // 2, -1.0, 1.0) * jnp.sin(angle)
            return carry

        lax.fori_loop(first, last, chunk, 0)

    for copy in own:
        copy.wait()
    net.arrived(go_first_l, go_first_d, go_first_c)
    net.start(*go_across, *go_own_x, go_near)
    table(0, 12)
    for k in pieces:
        net.arrived(go_across[k])
        net.start(go_other_y[k])
    net.start(go_far_1)
    net.arrived(go_mlp_c)
    net.start(go_mlp_x)
    net.arrived(go_near)
    net.start(go_near_relay)
    for k in pieces:
        net.arrived(go_other_y[k])
        net.start(go_other_x[k])
    net.arrived(*go_own_x)
    net.start(*go_own_y, go_mlp_near)
    net.arrived(go_far_0)
    net.start(go_far_l0)
    table(12, 32)
    net.arrived(go_far_1)
    net.start(go_far_l1, go_far_relay)
    net.arrived(go_far_l0, go_far_l1)
    net.start(go_far_l_relay)
    net.arrived(go_near_c, go_near_relay, go_far_relay, go_far_l_relay, *go_own_y, *go_other_x, go_mlp_x, go_mlp_near)
    net.sent()


def front(tok, wq, wk, wv, wo, gn, wg, wu, wd, inverse):
    any_spec = pl.BlockSpec(memory_space=pl.ANY)
    copies = 64
    bf16 = jnp.bfloat16
    return pl.pallas_call(
        front_kernel,
        out_shape=(
            jax.ShapeDtypeStruct((8, ROWS, MODEL_DIM), bf16),
            jax.ShapeDtypeStruct((1024, 1024), bf16),
            jax.ShapeDtypeStruct((2048, 256), bf16),
            jax.ShapeDtypeStruct((32, 8, 128), jnp.float32),
            jax.ShapeDtypeStruct((2, MODEL_DIM, HALF_FF), bf16),
            jax.ShapeDtypeStruct((FF, 512), bf16),
            jax.ShapeDtypeStruct((SEQ_ROWS, HEAD_DIM), jnp.float32),
            jax.ShapeDtypeStruct((SEQ_ROWS, HEAD_DIM), jnp.float32),
        ),
        in_specs=[any_spec] * 9 + [pl.BlockSpec(memory_space=pltpu.VMEM)],
        out_specs=[any_spec] * 6 + [pl.BlockSpec(memory_space=pltpu.VMEM)] * 2,
        scratch_shapes=[
            pltpu.SemaphoreType.DMA((copies,)),
            pltpu.SemaphoreType.DMA((copies,)),
            pltpu.SemaphoreType.DMA((9,)),
            pltpu.SemaphoreType.DMA((9,)),
            pltpu.VMEM((32, 512), bf16),
            pltpu.VMEM((32, 256), bf16),
            pltpu.VMEM((32, 256), bf16),
            pltpu.VMEM((64, 256), bf16),
            pltpu.VMEM((8, 128), jnp.float32),
            pltpu.VMEM((32, HALF_FF), bf16),
            pltpu.VMEM((32, HALF_FF), bf16),
            pltpu.VMEM((96, 512), bf16),
            pltpu.VMEM((ROWS, MODEL_DIM), bf16),
        ],
        compiler_params=pltpu.CompilerParams(
            collective_id=0, has_side_effects=True, vmem_limit_bytes=VMEM_LIMIT
        ),
        name="front_gather",
    )(tok, wq, wk, wv, wo, gn, wg, wu, wd, inverse)


def line_peers(p, l, c):
    return [
        {"p": (p + a) % 2, "l": (l + b) % 2, "c": (c + d) % 2}
        for a in range(2)
        for b in range(2)
        for d in range(2)
        if a + b + d > 0
    ]


class Return:
    def __init__(self, where, src, dst, send_sem, recv_sem):
        self.where = where[2:]
        self.src, self.dst, self.send_sem, self.recv_sem = src, dst, send_sem, recv_sem

    def stays(self, index):
        p, l, c = self.where
        return (p == c) & (index == c)

    def local(self, c0):
        p, l, c = self.where
        return pltpu.make_async_copy(self.src.at[pl.ds(c0 * ROWS, ROWS)], self.dst.at[p], self.send_sem.at[c0])

    def remote(self, c0):
        p, l, c = self.where
        return pltpu.make_async_remote_copy(
            src_ref=self.src.at[pl.ds(c0 * ROWS, ROWS)],
            dst_ref=self.dst.at[p],
            send_sem=self.send_sem.at[c0],
            recv_sem=self.recv_sem.at[p],
            device_id={"p": c, "l": (p + l + c) % 2, "c": c0},
            device_id_type=MESH,
        )

    def start_one(self, c0):
        here = self.stays(c0)

        @pl.when(here)
        def _():
            self.local(c0).start()

        @pl.when(jnp.logical_not(here))
        def _():
            self.remote(c0).start()

    def start(self):
        for c0 in range(2):
            self.start_one(c0)

    def wait(self):
        p, l, c = self.where
        for c0 in range(2):
            here = self.stays(c0)

            @pl.when(here)
            def _():
                self.local(c0).wait()

            @pl.when(jnp.logical_not(here))
            def _():
                self.remote(c0).wait_send()

        for seq in range(2):

            @pl.when(jnp.logical_not(self.stays(seq)))
            def _():
                pltpu.make_async_remote_copy(
                    src_ref=self.src.at[pl.ds(0, ROWS)],
                    dst_ref=self.dst.at[seq],
                    send_sem=self.send_sem.at[0],
                    recv_sem=self.recv_sem.at[seq],
                    device_id={"p": 1 - p},
                    device_id_type=MESH,
                ).wait_recv()


class Spread:
    def __init__(self, where, src, dst, send_sem, recv_sem):
        self.where = where[2:]
        self.src, self.dst, self.send_sem, self.recv_sem = src, dst, send_sem, recv_sem

    def here(self, index):
        p, l, c = self.where
        return (p == c) & (index == c)

    def local(self, seq):
        p, l, c = self.where
        return pltpu.make_async_copy(self.src.at[seq], self.dst.at[p, c], self.send_sem.at[seq])

    def remote(self, seq):
        p, l, c = self.where
        return pltpu.make_async_remote_copy(
            src_ref=self.src.at[seq],
            dst_ref=self.dst.at[p, c],
            send_sem=self.send_sem.at[seq],
            recv_sem=self.recv_sem.at[c],
            device_id={"p": seq, "l": (seq + l + p) % 2, "c": p},
            device_id_type=MESH,
        )

    def start(self):
        for seq in range(2):

            @pl.when(self.here(seq))
            def _():
                self.local(seq).start()

            @pl.when(jnp.logical_not(self.here(seq)))
            def _():
                self.remote(seq).start()

    def wait(self):
        p, l, c = self.where
        for seq in range(2):

            @pl.when(self.here(seq))
            def _():
                self.local(seq).wait()

            @pl.when(jnp.logical_not(self.here(seq)))
            def _():
                self.remote(seq).wait_send()

        for block in range(2):

            @pl.when(jnp.logical_not(self.here(block)))
            def _():
                pltpu.make_async_remote_copy(
                    src_ref=self.src.at[0],
                    dst_ref=self.dst.at[c, block],
                    send_sem=self.send_sem.at[0],
                    recv_sem=self.recv_sem.at[block],
                    device_id={"p": 1 - p},
                    device_id_type=MESH,
                ).wait_recv()


def turn(value):
    return pltpu.roll(value, HEAD_DIM // 2, 1)


def block_mask(key_dim, flags, index):
    shape = (BLK, BLK)
    key = lax.broadcasted_iota(jnp.int32, shape, key_dim)
    query = lax.broadcasted_iota(jnp.int32, shape, 1 - key_dim)
    upper = query // PIECE
    piece = jnp.where(upper == 0, flags[2 * index], flags[2 * index + 1])
    return (key <= query) | ((key // PIECE == upper) & (piece > 0))


PROJECT = 8


def attend_kernel(
    flags, x_ref, w_ref, ga_ref, gq_ref, gk_ref, cos_ref, sin_ref, woq, wgu_in, wdn_in,
    n_ref, q_ref, k_ref, v_ref, qr_ref, kr_ref, o_ref, lse_ref, wo, wgu, wdn,
    stage, send_sem, recv_sem, local_sem,
):
    y, x, p, l, c = place()
    peer = peers_of(x, y, p, l, c)
    t = 2 * l + c
    net = Plan(send_sem, recv_sem)

    def chip(yy, xx, pp, ll):
        slot = (yy * 2 + xx) * 4 + 2 * pp + ll
        return in_place(wgu.at[:, rows_at(slot, 64)], wdn.at[rows_at(slot, 192)])

    def rows_of(q):
        return woq.at[rows_at(q, 512)], wo.at[:, rows_at(t, 256)]

    go_mlp_y = net.add(peer["y"], chip(y, x, p, l) + chip(y, 1 - x, p, l))
    go_mlp_x = net.add(peer["x"], chip(y, x, p, 1 - l) + chip(1 - y, x, p, 1 - l))
    go_far = [net.add(peer["p"], [pair]) for pair in chip(y, x, p, l)]
    go_far_l = [net.add(peer["l"], [pair]) for pair in chip(y, x, 1 - p, l)]
    go_near_y = net.add(peer["y"], chip(y, x, p, 1 - l))
    go_wo_l = net.add(peer["l"], [rows_of(2 * (1 - l) + c)])
    go_wo_d = net.add(peer["d"], [rows_of(2 * (1 - l) + 1 - c)])
    go_wo_c = net.add(peer["c"], [rows_of(2 * l + 1 - c)])
    step = pl.program_id(0)

    @pl.when(step == 0)
    def _():
        greet(list(peer.values()))
        net.start(go_near_y, *go_far, go_wo_l, go_wo_d, go_wo_c)
        copy = pltpu.make_async_copy(rows_of(t)[0], stage, local_sem.at[0])
        copy.start()
        copy.wait()
        pltpu.make_async_copy(stage, rows_of(t)[1], local_sem.at[1]).start()

    @pl.when(step < PROJECT)
    def _():
        value = x_ref[...].astype(jnp.float32)
        r = lax.rsqrt(jnp.mean(value * value, axis=-1, keepdims=True) + EPS)
        normed = (value * r * ga_ref[...]).astype(jnp.bfloat16)
        n_ref[...] = normed
        full = dot(normed, w_ref[...])
        cosine, sine = cos_ref[...], sin_ref[...]
        rows = rows_at(jnp.minimum(step, PROJECT - 1), 256)
        for h in range(QH + KH):
            u = full[:, h * HEAD_DIM : (h + 1) * HEAD_DIM]
            raw_ref, out_ref, g_ref, at = (qr_ref, q_ref, gq_ref, h) if h < QH else (kr_ref, k_ref, gk_ref, h - QH)
            raw_ref[at] = u
            n = u * lax.rsqrt(jnp.mean(u * u, axis=-1, keepdims=True) + EPS) * g_ref[...]
            out_ref[at, rows, :] = (n * cosine + turn(n) * sine).astype(jnp.bfloat16)
        for h in range(KH):
            at = (QH + KH + h) * HEAD_DIM
            v_ref[h, rows, :] = full[:, at : at + HEAD_DIM].astype(jnp.bfloat16)

    @pl.when(step == PROJECT)
    def _():
        net.arrived(go_near_y)
        net.start(go_mlp_x, go_mlp_y)

    for k, at in enumerate((PROJECT + 2, PROJECT + 4)):

        @pl.when(step == at)
        def _():
            net.arrived(go_far[k])
            net.start(go_far_l[k])

    @pl.when(step >= PROJECT)
    def _():
        order = jnp.maximum(step - PROJECT, 0)
        g, i = order // NBLK, order % NBLK
        ones = jnp.ones((BLK, HEAD_DIM), jnp.bfloat16)
        mask = block_mask(1, flags, i)

        def values(j):
            return jnp.concatenate([v_ref[g, rows_at(j, BLK), :], ones], axis=1)

        queries = [q_ref[2 * g + h, rows_at(i, BLK), :] for h in range(2)]

        def part(j, masked):
            keys, both = k_ref[g, rows_at(j, BLK), :], values(j)
            found = []
            for q in queries:
                probs = jnp.exp2(dot(q, keys, NT) * (SCALE * LOG2E))
                if masked:
                    probs = jnp.where(mask, probs, 0.0)
                found.append(dot(probs.astype(jnp.bfloat16), both))
            return found

        def one(j, accs):
            return tuple(acc + more for acc, more in zip(accs, part(j, False)))

        accs = lax.fori_loop(0, i, one, tuple(part(i, True)))
        for h, acc in enumerate(accs):
            total = acc[:, HEAD_DIM:]
            o_ref[:, h * HEAD_DIM : (h + 1) * HEAD_DIM] = (acc[:, :HEAD_DIM] / total).astype(jnp.bfloat16)
            lse_ref[h] = jnp.log2(total).T[0:8, :]

    @pl.when(step == PROJECT + 2 * NBLK - 1)
    def _():
        pltpu.make_async_copy(stage, rows_of(t)[1], local_sem.at[1]).wait()
        net.arrived(go_mlp_y, go_mlp_x, *go_far_l, go_wo_l, go_wo_d, go_wo_c)
        net.sent()


def attend(flags, x, w, ga, gq, gk, cosine, sine, woq, wgu, wdn):
    bf16, f32 = jnp.bfloat16, jnp.float32

    def early(s):
        return jnp.minimum(s, PROJECT - 1)

    def late(s):
        return jnp.maximum(s - PROJECT, 0)

    def row(width):
        return pl.BlockSpec((256, width), lambda s, f: (early(s), 0))

    def whole(shape):
        return pl.BlockSpec(shape, lambda s, f: (0,) * len(shape))

    def heads(n):
        return pl.BlockSpec((n, 256, HEAD_DIM), lambda s, f: (0, early(s), 0))

    def shape(n, dtype):
        return jax.ShapeDtypeStruct((n, SEQ_ROWS, HEAD_DIM), dtype)

    any_spec = pl.BlockSpec(memory_space=pl.ANY)
    copies = 20
    return pl.pallas_call(
        attend_kernel,
        out_shape=(
            jax.ShapeDtypeStruct((SEQ_ROWS, MODEL_DIM), bf16),
            shape(QH, bf16),
            shape(KH, bf16),
            shape(KH, bf16),
            shape(QH, f32),
            shape(KH, f32),
            jax.ShapeDtypeStruct((SEQ_ROWS, QH * HEAD_DIM), bf16),
            jax.ShapeDtypeStruct((QH, 8, SEQ_ROWS), f32),
            jax.ShapeDtypeStruct((512, MODEL_DIM), bf16),
            jax.ShapeDtypeStruct(wgu.shape, bf16),
            jax.ShapeDtypeStruct(wdn.shape, bf16),
        ),
        grid_spec=pltpu.PrefetchScalarGridSpec(
            num_scalar_prefetch=1,
            grid=(PROJECT + KH * NBLK,),
            in_specs=[row(MODEL_DIM), whole(w.shape), whole(ga.shape), whole(gq.shape), whole(gk.shape), row(HEAD_DIM), row(HEAD_DIM)]
            + [any_spec] * 3,
            out_specs=[
                row(MODEL_DIM),
                whole((QH, SEQ_ROWS, HEAD_DIM)),
                whole((KH, SEQ_ROWS, HEAD_DIM)),
                whole((KH, SEQ_ROWS, HEAD_DIM)),
                heads(QH),
                heads(KH),
                pl.BlockSpec((BLK, 2 * HEAD_DIM), lambda s, f: (late(s) % NBLK, late(s) // NBLK)),
                pl.BlockSpec((2, 8, BLK), lambda s, f: (late(s) // NBLK, 0, late(s) % NBLK)),
            ]
            + [any_spec] * 3,
            scratch_shapes=[pltpu.VMEM((512, 256), bf16)]
            + [pltpu.SemaphoreType.DMA((copies,))] * 2
            + [pltpu.SemaphoreType.DMA((2,))],
        ),
        input_output_aliases={9: 9, 10: 10},
        compiler_params=pltpu.CompilerParams(
            collective_id=2, has_side_effects=True, vmem_limit_bytes=VMEM_LIMIT
        ),
        cost_estimate=pl.CostEstimate(
            flops=4 * QH * SEQ_ROWS * SEQ_ROWS * HEAD_DIM, bytes_accessed=24 << 20, transcendentals=QH * SEQ_ROWS * SEQ_ROWS
        ),
        name="attend",
    )(flags, x, w, ga, gq, gk, cosine, sine, woq, wgu, wdn)


def resid_kernel(
    attn, wo, g_mlp, xs, cot, wgu_in, wdn_in,
    resid, mlp_in, wgu, wdn, wdx, dy,
    send_c, recv_c, send_l, recv_l, keep, x_own, send_sem, recv_sem, local_sem, dy_send, dy_recv,
):
    where = place()
    y, x, p, l, c = where
    peer = peers_of(x, y, p, l, c)
    net = Plan(send_sem, recv_sem)

    def chip(yy, xx, pp, ll):
        slot = (yy * 2 + xx) * 4 + 2 * pp + ll
        return in_place(wgu.at[:, rows_at(slot, 64)], wdn.at[rows_at(slot, 192)])

    def down(pp, ll):
        found = []
        for xx in range(2):
            slot = xx * 4 + 2 * pp + ll
            found.append((wdn.at[rows_at((1 - c) * 8 + slot, 192)], wdx.at[rows_at(slot, 192)]))
        return found

    def hop(name, *chips):
        found = [chip(*one) for one in chips]
        return [net.add(peer[name], [pairs[k] for pairs in found]) for k in range(2)]

    go_far_x = hop("x", (y, x, 1 - p, l))
    go_far_y = hop("y", (y, x, 1 - p, l), (y, 1 - x, 1 - p, l))
    go_fal_y = hop("y", (y, x, 1 - p, 1 - l))
    go_fal_x = hop("x", (y, x, 1 - p, 1 - l), (1 - y, x, 1 - p, 1 - l))
    go_down_me = net.add(peer["c"], down(p, l))
    go_down_near = net.add(peer["c"], down(p, 1 - l))
    go_down_far = net.add(peer["c"], down(1 - p, l))
    go_down_fal = net.add(peer["c"], down(1 - p, 1 - l))
    halves = [pl.ds(n * ROWS, ROWS) for n in range(2)]
    go_give_0 = [net.add(peer["c"], [(send_c.at[0, half], recv_c.at[0, half])]) for half in halves]
    go_give_1 = net.add(peer["c"], [(send_c.at[1], recv_c.at[1])])
    go_cross = [net.add(peer["l"], [(send_l.at[half], recv_l.at[half])]) for half in halves]
    go_share = [net.add(peer["c"], in_place(mlp_in.at[c, half])) for half in halves]
    go_dy_c = net.add(peer["c"], in_place(dy.at[c]))
    spread = Spread(where, cot, dy, dy_send, dy_recv)
    greet(line_peers(p, l, c) + [peer["x"], peer["y"]])
    spread.start()
    net.start(go_far_x[1], go_fal_y[1], go_far_x[0], go_fal_y[0], go_down_me, go_down_near)
    fetch = pltpu.make_async_copy(xs.at[rows_at(owned(p, l, c), OWN)], x_own, local_sem.at[0])
    fetch.start()

    def project(ll, cc, write, first=0, count=OWN):
        part = attn[pl.ds(pl.multiple_of(owned(p, ll, cc) * OWN + first, ROWS), count), :]

        def chunk(n, carry):
            cols = rows_at(n, 256)
            write(pl.ds(first, count), cols, dot(part, wo[:, cols]))
            return carry

        lax.fori_loop(0, 4, chunk, 0)

    def give(n):
        def write(rows, cols, value):
            send_c[n, rows, cols] = value.astype(jnp.bfloat16)

        return write

    def hold(n):
        def write(rows, cols, value):
            keep[n, rows, cols] = value

        return write

    def relay_hop(k):
        net.arrived(go_far_x[k])
        net.start(go_far_y[k])
        net.arrived(go_fal_y[k])
        net.start(go_fal_x[k])

    for n, half in enumerate(halves):
        project(1 - l, 1 - c, give(0), n * ROWS, ROWS)
        net.start(go_give_0[n])
        project(1 - l, c, hold(0), n * ROWS, ROWS)
        net.arrived(go_give_0[n])
        send_l[half, :] = (keep[0, half, :] + recv_c[0, half, :].astype(jnp.float32)).astype(jnp.bfloat16)
        net.start(go_cross[n])
    relay_hop(1)
    project(l, 1 - c, give(1))
    net.start(go_give_1)
    project(l, c, hold(1))
    fetch.wait()
    relay_hop(0)
    net.arrived(go_give_1)
    keep[1] += recv_c[1].astype(jnp.float32) + x_own[...].astype(jnp.float32)
    for n, half in enumerate(halves):
        net.arrived(go_cross[n])
        total = keep[1, half, :] + recv_l[half, :].astype(jnp.float32)
        resid[half, :] = total
        r = lax.rsqrt(jnp.mean(total * total, axis=-1, keepdims=True) + EPS)
        mlp_in[c, half, :] = (total * r * g_mlp[...]).astype(jnp.bfloat16)
        net.start(go_share[n])
    net.arrived(go_far_y[1])
    net.start(go_down_far)
    spread.wait()
    net.start(go_dy_c)
    net.arrived(go_fal_x[1])
    net.start(go_down_fal)
    net.arrived(go_far_y[0], go_fal_x[0])
    net.arrived(go_down_me, go_down_near, go_down_far, go_down_fal, *go_share, go_dy_c)
    net.sent()


def finish_resid(attn, wo, g_mlp, xs, cot, wgu, wdn):
    bf16, f32 = jnp.bfloat16, jnp.float32
    any_spec = pl.BlockSpec(memory_space=pl.ANY)
    vmem = pl.BlockSpec(memory_space=pltpu.VMEM)
    copies = 32
    return pl.pallas_call(
        resid_kernel,
        out_shape=(
            jax.ShapeDtypeStruct((OWN, MODEL_DIM), f32),
            jax.ShapeDtypeStruct((2, OWN, MODEL_DIM), bf16),
            jax.ShapeDtypeStruct(wgu.shape, bf16),
            jax.ShapeDtypeStruct(wdn.shape, bf16),
            jax.ShapeDtypeStruct((HALF_FF, 512), bf16),
            jax.ShapeDtypeStruct((2, 2, ROWS, MODEL_DIM), bf16),
        ),
        in_specs=[vmem] * 3 + [any_spec] * 4,
        out_specs=[vmem] * 2 + [any_spec] * 4,
        scratch_shapes=[
            pltpu.VMEM((2, OWN, MODEL_DIM), bf16),
            pltpu.VMEM((2, OWN, MODEL_DIM), bf16),
            pltpu.VMEM((OWN, MODEL_DIM), bf16),
            pltpu.VMEM((OWN, MODEL_DIM), bf16),
            pltpu.VMEM((2, OWN, MODEL_DIM), f32),
            pltpu.VMEM((OWN, MODEL_DIM), bf16),
            pltpu.SemaphoreType.DMA((copies,)),
            pltpu.SemaphoreType.DMA((copies,)),
            pltpu.SemaphoreType.DMA((1,)),
            pltpu.SemaphoreType.DMA((2,)),
            pltpu.SemaphoreType.DMA((2,)),
        ],
        input_output_aliases={5: 2, 6: 3},
        compiler_params=pltpu.CompilerParams(
            collective_id=3, has_side_effects=True, vmem_limit_bytes=VMEM_LIMIT
        ),
        name="residual",
    )(attn, wo, g_mlp, xs, cot, wgu, wdn)


CHUNK = 512
EARLY = 1024


def forward_kernel(
    m_ref, dy_ref, w_ref, wdn, wx_ref, resid, g_mlp,
    ggu, gdb, rb, d_resid, db, res, dg,
    mt, dyt, hid, dgt, dup, d_in, down, give, take, all_down, ggv, gdv, send_sem, recv_sem, load_sem, out_sem,
):
    where = place()
    y, x, p, l, c = where
    peer = peers_of(x, y, p, l, c)
    red = Reduction(where)
    net = Plan(send_sem, recv_sem)
    go_d_in = net.add(peer["c"], [(give.at[0], take.at[0])])
    go_down = net.add(peer["c"], [(give.at[1], take.at[1])])
    go_gd, go_wide, outs = [], [], []
    for f in range(HALF_FF // CHUNK):
        part_f = pl.ds(f * CHUNK, CHUNK)
        go_gd.append(net.add(peer["c"], [(gdv.at[part_f, rows_at(1 - c, 512)], gdb.at[c, part_f])]))
        outs.append(
            [
                pltpu.make_async_copy(ggv.at[:, :, part_f], ggu.at[:, :, part_f], out_sem.at[2 * f]),
                pltpu.make_async_copy(gdv.at[part_f, rows_at(c, 512)], gdb.at[c, part_f], out_sem.at[2 * f + 1]),
            ]
        )
        go_wide.append([])
        if f * CHUNK < EARLY:
            for n, kind in enumerate(KINDS):
                pairs = []
                for k in range(2):
                    slot = chip_slot(*red.place(kind, k, True), *red.z[kind])
                    pairs.append((ggv.at[:, rows_at(slot, 64), part_f], rb.at[n, k, :, :, part_f]))
                go_wide[f].append(net.add(peer[red.first_peer(kind)], pairs))
    step = pl.program_id(0)
    fetch = pltpu.make_async_copy(wdn.at[rows_at(c, HALF_FF)], all_down, load_sem.at[0])

    @pl.when(step == 0)
    def _():
        fetch.start()
        greet([peer["c"], peer["x"], peer["y"]])

        def flip(k, carry):
            rows = rows_at(k, 256)
            mt[:, rows] = m_ref[rows, :].T
            dyt[:, rows] = dy_ref[rows, :].T
            return carry

        lax.fori_loop(0, 4, flip, 0)
        d_in[...] = jnp.zeros_like(d_in)
        down[...] = jnp.zeros_like(down)
        fetch.wait()

    wo_ref = all_down.at[rows_at(step, CHUNK)]
    own_cols, other_cols = rows_at(c, 512), rows_at(1 - c, 512)

    def part(r, carry):
        rows = rows_at(r, 512)
        value, grad = m_ref[rows, :], dy_ref
        gate, up = dot(value, w_ref[0]), dot(value, w_ref[1])
        d_hidden = dot(grad[rows, own_cols], wo_ref[...], NT) + dot(grad[rows, other_cols], wx_ref[...], NT)
        s = 1.0 / (1.0 + jnp.exp(-gate))
        silu = gate * s
        hidden = (silu * up).astype(jnp.bfloat16)
        d_up = (d_hidden * silu).astype(jnp.bfloat16)
        d_gate = (d_hidden * up * (s * (1.0 + gate * (1.0 - s)))).astype(jnp.bfloat16)
        hid[rows, :] = hidden
        dup[rows, :] = d_up
        dgt[rows, :] = d_gate
        d_in[rows, :] += dot(d_gate, w_ref[0], NT) + dot(d_up, w_ref[1], NT)
        down[rows, own_cols] += dot(hidden, wo_ref[...])
        down[rows, other_cols] += dot(hidden, wx_ref[...])
        return carry

    lax.fori_loop(0, 2, part, 0)

    @pl.when(step == pl.num_programs(0) - 1)
    def _():
        give[0] = d_in[rows_at(1 - c, OWN), :].astype(jnp.bfloat16)
        give[1] = down[rows_at(1 - c, OWN), :].astype(jnp.bfloat16)
        net.start(go_d_in, go_down)

    now = rows_at(step, CHUNK)

    def weights(k, carry):
        rows = rows_at(k, 512)
        ggv[0, rows, now] = dot(mt[rows, :], dgt[...]).astype(jnp.bfloat16)
        ggv[1, rows, now] = dot(mt[rows, :], dup[...]).astype(jnp.bfloat16)
        gdv[now, rows] = dot(dyt[rows, :], hid[...]).T.astype(jnp.bfloat16)
        return carry

    lax.fori_loop(0, 2, weights, 0)
    for f in range(HALF_FF // CHUNK):

        @pl.when(step == f)
        def _():
            net.start(*go_wide[f], go_gd[f])
            for copy in outs[f]:
                copy.start()

    @pl.when(step == pl.num_programs(0) - 1)
    def _():
        net.arrived(go_d_in, go_down)
        dg[...] = jnp.zeros_like(dg)

        def finish(k, carry):
            rows = rows_at(k, 64)
            here = pl.ds(pl.multiple_of(c * OWN + k * 64, 64), 64)
            value = resid[rows, :]
            grad = d_in[here, :] + take[0, rows, :].astype(jnp.float32)
            r = lax.rsqrt(jnp.mean(value * value, axis=-1, keepdims=True) + EPS)
            scaled = value * r
            gained = grad * g_mlp[...]
            total = dy_ref[here, :].astype(jnp.float32) + r * (gained - scaled * jnp.mean(scaled * gained, axis=-1, keepdims=True))
            d_resid[rows, :] = total
            db[rows, :] = total.astype(jnp.bfloat16)
            dg[...] += jnp.sum((grad * scaled).reshape(-1, 8, MODEL_DIM), axis=0)
            res[rows, :] = (value + down[here, :] + take[1, rows, :].astype(jnp.float32)).astype(jnp.bfloat16)
            return carry

        lax.fori_loop(0, 8, finish, 0)
        for f in range(HALF_FF // CHUNK):
            net.arrived(*go_wide[f], go_gd[f])
            for copy in outs[f]:
                copy.wait()
        net.sent()


def feed_forward(mlp_in, dy, wgu, wdn, wdx, resid, g_mlp):
    bf16, f32 = jnp.bfloat16, jnp.float32

    def whole(shape):
        return pl.BlockSpec(shape, lambda f: (0,) * len(shape), pipeline_mode=pl.Buffered(1))

    down = pl.BlockSpec((CHUNK, 512), lambda f: (f, 0))
    copies = 24
    rows = (1024, MODEL_DIM)
    own = (OWN, MODEL_DIM)
    return pl.pallas_call(
        forward_kernel,
        grid=(HALF_FF // CHUNK,),
        out_shape=(
            jax.ShapeDtypeStruct((2, MODEL_DIM, HALF_FF), bf16),
            jax.ShapeDtypeStruct((2, HALF_FF, 512), bf16),
            jax.ShapeDtypeStruct((4, 2, 2, 64, EARLY), bf16),
            jax.ShapeDtypeStruct(own, f32),
            jax.ShapeDtypeStruct(own, bf16),
            jax.ShapeDtypeStruct(own, bf16),
            jax.ShapeDtypeStruct((8, MODEL_DIM), f32),
        ),
        in_specs=[whole(rows), whole(rows), pl.BlockSpec((2, MODEL_DIM, CHUNK), lambda f: (0, 0, f))]
        + [pl.BlockSpec(memory_space=pl.ANY), down]
        + [whole(own), whole((1, MODEL_DIM))],
        out_specs=[pl.BlockSpec(memory_space=pl.ANY)] * 3
        + [whole(own), whole(own), whole(own), whole((8, MODEL_DIM))],
        scratch_shapes=[
            pltpu.VMEM(rows, bf16),
            pltpu.VMEM(rows, bf16),
            pltpu.VMEM((1024, CHUNK), bf16),
            pltpu.VMEM((1024, CHUNK), bf16),
            pltpu.VMEM((1024, CHUNK), bf16),
            pltpu.VMEM(rows, f32),
            pltpu.VMEM(rows, f32),
            pltpu.VMEM((2,) + own, bf16),
            pltpu.VMEM((2,) + own, bf16),
            pltpu.VMEM((HALF_FF, 512), bf16),
            pltpu.VMEM((2, MODEL_DIM, HALF_FF), bf16),
            pltpu.VMEM((HALF_FF, MODEL_DIM), bf16),
            pltpu.SemaphoreType.DMA((copies,)),
            pltpu.SemaphoreType.DMA((copies,)),
            pltpu.SemaphoreType.DMA((1,)),
            pltpu.SemaphoreType.DMA((6,)),
        ],
        compiler_params=pltpu.CompilerParams(
            collective_id=6, has_side_effects=True, vmem_limit_bytes=VMEM_LIMIT
        ),
        name="feed_forward",
    )(mlp_in, dy, wgu, wdn, wdx, resid, g_mlp)


KINDS = ME, NEAR, FAR, FAL = range(4)


def chip_slot(yy, xx, pp, ll):
    return (yy * 2 + xx) * 4 + 2 * pp + ll


class Reduction:
    def __init__(self, where):
        y, x, p, l, c = where
        self.z = ((p, l), (p, 1 - l), (1 - p, l), (1 - p, 1 - l))
        self.y, self.x = y, x

    def y_first(self, kind):
        return kind in (ME, FAR)

    def first_peer(self, kind):
        return "y" if self.y_first(kind) else "x"

    def second_peer(self, kind):
        return "x" if self.y_first(kind) else "y"

    def place(self, kind, index, given):
        if self.y_first(kind):
            return (1 - self.y if given else self.y), index
        return index, (1 - self.x if given else self.x)

    def kept(self, kind):
        return self.x if self.y_first(kind) else self.y


def attend_back_kernel(
    flags, q_in, k_in, v_in, o_in, db_in, wo_in, lse_in, qr_in, kr_in, cos_in, sin_in, ggu, gdb, rb_in, res, gq_ref, gk_ref,
    d_out, goq, og_out, od_out, fw_out, fd_out, out, dg_ref,
    q_ref, k_ref, v_ref, o_ref, dall, wo, lse_ref, qr_ref, kr_ref, cos_ref, sin_ref,
    da, delta, dbuf, dq_acc, dk_acc, dv_acc, og, od, rb, rbd, rc, rcd, rz, rzd, go,
    send_sem, recv_sem, load_sem, own_sem, out_sem, back_send, back_recv,
):
    where = place()
    y, x, p, l, c = where
    peer = peers_of(x, y, p, l, c)
    red = Reduction(where)
    net = Plan(send_sem, recv_sem)
    t = 2 * l + c

    def block(index):
        return dall.at[rows_at(index, OWN)]

    mine = owned(p, l, c)
    go_db_l = net.add(peer["l"], [(db_in, block(mine))])
    go_db_c = net.add(peer["c"], [(db_in, block(mine))])
    go_db_r = net.add(peer["c"], in_place(block(owned(p, 1 - l, c))))
    early, late = pl.ds(0, EARLY), pl.ds(EARLY, HALF_FF - EARLY)
    first_of, second_a, second_b = {}, {}, {}
    for n, kind in enumerate(KINDS):
        pairs = []
        for k in range(2):
            yy, xx = red.place(kind, k, True)
            slot = chip_slot(yy, xx, *red.z[kind])
            pairs.append((ggu.at[:, rows_at(slot, 64), late], rb.at[n, k, :, :, late]))
            pairs.append((gdb.at[yy, rows_at(xx * 4 + 2 * red.z[kind][0] + red.z[kind][1], 192)], rbd.at[n, k]))
        first_of[kind] = net.add(peer[red.first_peer(kind)], pairs)
        if n >= 2:
            away, link = 1 - red.kept(kind), peer[red.second_peer(kind)]
            second_a[kind] = net.add(link, [(og.at[n, away, :, :, early], rc.at[n - 2, :, :, early])])
            second_b[kind] = net.add(link, [(og.at[n, away, :, :, late], rc.at[n - 2, :, :, late]), (od.at[n, away], rcd.at[n - 2])])
    u_far, u_fal = red.kept(FAR), red.kept(FAL)
    go_fal_a = net.add(peer["l"], [(og.at[FAL, u_fal, :, :, early], rz.at[:, :, early])])
    go_fal_b = net.add(peer["l"], [(og.at[FAL, u_fal, :, :, late], rz.at[:, :, late]), (od.at[FAL, u_fal], rzd)])
    go_far_a = net.add(peer["p"], [(og.at[FAR, u_far, :, :, early], fw_out.at[:, :, early])])
    go_far_b = net.add(peer["p"], [(og.at[FAR, u_far, :, :, late], fw_out.at[:, :, late]), (od.at[FAR, u_far], fd_out)])
    home = Return(where, res, out, back_send, back_recv)

    def columns(q):
        return [(go.at[:, rows_at(q, 256)], goq.at[rows_at(t, 512)])]

    go_go_l = net.add(peer["l"], columns(2 * (1 - l) + c))
    go_go_d = net.add(peer["d"], columns(2 * (1 - l) + 1 - c))
    go_go_c = net.add(peer["c"], columns(2 * l + 1 - c))
    own_go = pltpu.make_async_copy(*columns(t)[0], out_sem.at[1])
    loads = [
        pltpu.make_async_copy(src, dst, load_sem.at[k])
        for k, (src, dst) in enumerate(
            [
                (db_in, block(mine)), (wo_in, wo), (o_in, o_ref), (q_in, q_ref), (k_in, k_ref), (v_in, v_ref), (lse_in, lse_ref),
                (cos_in, cos_ref), (sin_in, sin_ref), (qr_in, qr_ref), (kr_in, kr_ref),
            ]
        )
    ]
    own = [pltpu.make_async_copy(rb_in, rb.at[:, :, :, :, early], own_sem.at[0])]
    for n, kind in enumerate(KINDS):
        for k in range(2):
            yy, xx = red.place(kind, k, False)
            slot = chip_slot(yy, xx, *red.z[kind])
            own.append(pltpu.make_async_copy(ggu.at[:, rows_at(slot, 64)], og.at[n, k], own_sem.at[len(own)]))
            rows = rows_at(xx * 4 + 2 * red.z[kind][0] + red.z[kind][1], 192)
            own.append(pltpu.make_async_copy(gdb.at[yy, rows], od.at[n, k], own_sem.at[len(own)]))

    def plus(target, other):
        target[...] = (target[...].astype(jnp.float32) + other[...].astype(jnp.float32)).astype(jnp.bfloat16)

    def wide_sum(n, cols):
        def wide(r, carry):
            k, m, rows = r // 4, (r // 2) % 2, rows_at(r % 2, 32)
            plus(og.at[n, k, m, rows, cols], rb.at[n, k, m, rows, cols])
            return carry

        lax.fori_loop(0, 8, wide, 0)

    def deep_sum(n):
        def deep(r, carry):
            k, rows = r // 3, rows_at(r % 3, 64)
            plus(od.at[n, k, rows, :], rbd.at[n, k, rows, :])
            return carry

        lax.fori_loop(0, 6, deep, 0)

    def branch(index):
        rows = rows_at(index, OWN)
        value = dot(dall[rows, :], wo[...], NT).astype(jnp.bfloat16)
        da[rows, :] = value
        for h in range(QH):
            cols = slice(h * HEAD_DIM, (h + 1) * HEAD_DIM)
            prod = value[:, cols].astype(jnp.float32) * o_ref[rows, cols].astype(jnp.float32)
            delta[h, :, rows] = jnp.broadcast_to(jnp.sum(prod.T, axis=0, keepdims=True), (8, BLK))

    def unrope(grad, u, gain, rows):
        grad = grad * SCALE
        e = grad * cos_ref[rows, :] + turn(grad * sin_ref[rows, :])
        r = lax.rsqrt(jnp.mean(u * u, axis=-1, keepdims=True) + EPS)
        ur = u * r
        ge = e * gain
        d = r * (ge - ur * jnp.mean(ur * ge, axis=-1, keepdims=True))
        return d.astype(jnp.bfloat16), jnp.sum((e * ur).reshape(-1, 8, HEAD_DIM), axis=0)

    step = pl.program_id(0)
    b, g = step // KH, step % KH
    i = owned(p, (l + b // 2) % 2, b % 2)

    @pl.when(step == 0)
    def _():
        for copy in loads[:3]:
            copy.start()
        for copy in own:
            copy.start()
        for copy in loads[3:]:
            copy.start()
        greet(line_peers(p, l, c) + [peer["x"], peer["y"]])
        net.start(go_db_l, go_db_c, first_of[FAR], first_of[FAL])
        dk_acc[...] = jnp.zeros_like(dk_acc)
        dv_acc[...] = jnp.zeros_like(dv_acc)
        dg_ref[...] = jnp.zeros_like(dg_ref)
        for copy in own:
            copy.wait()
        for kind in (FAR, FAL):
            wide_sum(kind, early)
            net.start(second_a[kind])
        for copy in loads[:3]:
            copy.wait()
        branch(mine)
        net.arrived(go_db_c)
        branch(owned(p, l, 1 - c))
        for copy in loads[3:]:
            copy.wait()

    @pl.when(step == 2)
    def _():
        net.arrived(second_a[FAL])
        plus(og.at[FAL, u_fal, :, :, early], rc.at[1, :, :, early])
        net.start(go_fal_a)
        net.arrived(second_a[FAR])
        plus(og.at[FAR, u_far, :, :, early], rc.at[0, :, :, early])

    @pl.when(step == 1)
    def _():
        home.start()

    @pl.when(step == 3)
    def _():
        for kind in (FAR, FAL):
            net.arrived(first_of[kind])
            wide_sum(kind, late)
            deep_sum(kind)
            net.start(second_b[kind])
        net.start(first_of[ME], first_of[NEAR])

    @pl.when(step == 2 * KH)
    def _():
        net.arrived(go_db_l)
        net.start(go_db_r)
        branch(owned(p, 1 - l, c))
        net.arrived(go_db_r)
        branch(owned(p, 1 - l, 1 - c))

    @pl.when(step == 5)
    def _():
        net.arrived(go_fal_a)
        plus(og.at[FAR, u_far, :, :, early], rz.at[:, :, early])
        net.start(go_far_a)

    @pl.when(step == 5)
    def _():
        net.arrived(second_b[FAL])
        plus(og.at[FAL, u_fal, :, :, late], rc.at[1, :, :, late])
        plus(od.at[FAL, u_fal], rcd.at[1])
        net.start(go_fal_b)
        net.arrived(second_b[FAR])
        plus(og.at[FAR, u_far, :, :, late], rc.at[0, :, :, late])
        plus(od.at[FAR, u_far], rcd.at[0])

    @pl.when(step == 7)
    def _():
        net.arrived(go_fal_b)
        plus(og.at[FAR, u_far, :, :, late], rz.at[:, :, late])
        plus(od.at[FAR, u_far], rzd)
        net.start(go_far_b)

    @pl.when(step == 5)
    def _():
        def grad_out(k, carry):
            cols = rows_at(k, 256)
            go[cols, :] = dot(o_ref[:, cols], dall[...], TN).astype(jnp.bfloat16)
            return carry

        lax.fori_loop(0, 2, grad_out, 0)
        net.start(go_go_l, go_go_d, go_go_c)
        own_go.start()

    dq_acc[...] = jnp.zeros_like(dq_acc)
    rows = rows_at(i, BLK)
    heads = [2 * g + n for n in range(2)]
    spans = [rows_at(h, HEAD_DIM) for h in heads]
    queries = [q_ref[h, rows, :] for h in heads]
    grads = [da[rows, span] for span in spans]

    def tile(j, mask=None):
        keys = rows_at(j, BLK)
        k, v = k_ref[g, keys, :], v_ref[g, keys, :]
        turned = k.T
        dv, dk = None, None
        for n, h in enumerate(heads):
            probs = jnp.exp2(dot(k, queries[n], NT) * (SCALE * LOG2E) - lse_ref[h, 0:1, rows])
            if mask is not None:
                probs = jnp.where(mask, probs, 0.0)
            d_scores = (probs * (dot(v, grads[n], NT) - delta[h, 0:1, rows])).astype(jnp.bfloat16)
            dv_more, dk_more = dot(probs.astype(jnp.bfloat16), grads[n]), dot(d_scores, queries[n])
            dv, dk = (dv_more, dk_more) if dv is None else (dv + dv_more, dk + dk_more)
            dq_acc[n] += dot(turned, d_scores)
        dv_acc[g, keys, :] += dv
        dk_acc[g, keys, :] += dk

    def loop(j, carry):
        tile(j)
        return carry

    tile(i, block_mask(0, flags, i))
    lax.fori_loop(0, i, loop, 0)
    for n, h in enumerate(heads):
        low, total = unrope(dq_acc[n].T, qr_ref[h, rows, :], gq_ref[...], rows)
        dbuf[rows, spans[n]] = low
        dg_ref[0] += total

    @pl.when(step == 4 * KH - 1)
    def _():
        for gg_at in range(KH):

            def finish(r, carry):
                rows = rows_at(r, 256)
                low, total = unrope(dk_acc[gg_at, rows, :], kr_ref[gg_at, rows, :], gk_ref[...], rows)
                dbuf[rows, pl.ds((QH + gg_at) * HEAD_DIM, HEAD_DIM)] = low
                dbuf[rows, pl.ds((QH + KH + gg_at) * HEAD_DIM, HEAD_DIM)] = dv_acc[gg_at, rows, :].astype(jnp.bfloat16)
                dg_ref[1] += total
                return carry

            lax.fori_loop(0, 8, finish, 0)
        outs = [pltpu.make_async_copy(dbuf, d_out, out_sem.at[0])]
        outs[0].start()
        for kind in (ME, NEAR):
            wide_sum(kind, early)
            net.arrived(first_of[kind])
            wide_sum(kind, late)
            deep_sum(kind)
        outs += [
            pltpu.make_async_copy(og.at[pl.ds(0, 2)], og_out, out_sem.at[2]),
            pltpu.make_async_copy(od.at[pl.ds(0, 2)], od_out, out_sem.at[3]),
        ]
        for copy in outs[1:]:
            copy.start()
        net.arrived(go_go_l, go_go_d, go_go_c, go_far_a, go_far_b)
        own_go.wait()
        net.sent()
        home.wait()
        for copy in outs:
            copy.wait()


def attend_back(flags, q, k, v, o, db, wo, lse, qr, kr, cosine, sine, ggu, gdb, rb, res, gq, gk):
    bf16, f32 = jnp.bfloat16, jnp.float32
    any_spec = pl.BlockSpec(memory_space=pl.ANY)
    gain = pl.BlockSpec((1, HEAD_DIM), lambda s, f: (0, 0))
    copies = 40

    def vm(a):
        return pltpu.VMEM(a.shape, a.dtype)

    return pl.pallas_call(
        attend_back_kernel,
        out_shape=(
            jax.ShapeDtypeStruct((SEQ_ROWS, 1024), bf16),
            jax.ShapeDtypeStruct((2048, 256), bf16),
            jax.ShapeDtypeStruct((2, 2, 2, 64, HALF_FF), bf16),
            jax.ShapeDtypeStruct((2, 2, 192, 512), bf16),
            jax.ShapeDtypeStruct((2, 64, HALF_FF), bf16),
            jax.ShapeDtypeStruct((192, 512), bf16),
            jax.ShapeDtypeStruct((2, ROWS, MODEL_DIM), bf16),
            jax.ShapeDtypeStruct((2, 8, HEAD_DIM), f32),
        ),
        grid_spec=pltpu.PrefetchScalarGridSpec(
            num_scalar_prefetch=1,
            grid=(4 * KH,),
            in_specs=[any_spec] * 15 + [gain] * 2,
            out_specs=[any_spec] * 7 + [pl.BlockSpec((2, 8, HEAD_DIM), lambda s, f: (0, 0, 0))],
            scratch_shapes=[vm(q), vm(k), vm(v), vm(o), pltpu.VMEM((SEQ_ROWS, MODEL_DIM), bf16), vm(wo), vm(lse), vm(qr), vm(kr)]
            + [vm(cosine), vm(sine)]
            + [
                pltpu.VMEM((SEQ_ROWS, QH * HEAD_DIM), bf16),
                pltpu.VMEM((QH, 8, SEQ_ROWS), f32),
                pltpu.VMEM((SEQ_ROWS, 1024), bf16),
                pltpu.VMEM((2, HEAD_DIM, BLK), f32),
                pltpu.VMEM((KH, SEQ_ROWS, HEAD_DIM), f32),
                pltpu.VMEM((KH, SEQ_ROWS, HEAD_DIM), f32),
                pltpu.VMEM((4, 2, 2, 64, HALF_FF), bf16),
                pltpu.VMEM((4, 2, 192, 512), bf16),
                pltpu.VMEM((4, 2, 2, 64, HALF_FF), bf16),
                pltpu.VMEM((4, 2, 192, 512), bf16),
                pltpu.VMEM((2, 2, 64, HALF_FF), bf16),
                pltpu.VMEM((2, 192, 512), bf16),
                pltpu.VMEM((2, 64, HALF_FF), bf16),
                pltpu.VMEM((192, 512), bf16),
                pltpu.VMEM((512, MODEL_DIM), bf16),
                pltpu.SemaphoreType.DMA((copies,)),
                pltpu.SemaphoreType.DMA((copies,)),
                pltpu.SemaphoreType.DMA((11,)),
                pltpu.SemaphoreType.DMA((17,)),
                pltpu.SemaphoreType.DMA((4,)),
                pltpu.SemaphoreType.DMA((2,)),
                pltpu.SemaphoreType.DMA((2,)),
            ],
        ),
        compiler_params=pltpu.CompilerParams(
            collective_id=4, has_side_effects=True, vmem_limit_bytes=VMEM_LIMIT
        ),
        cost_estimate=pl.CostEstimate(
            flops=10 * QH * SEQ_ROWS * SEQ_ROWS * HEAD_DIM, bytes_accessed=40 << 20, transcendentals=QH * SEQ_ROWS * SEQ_ROWS
        ),
        name="attend_back",
    )(flags, q, k, v, o, db, wo, lse, qr, kr, cosine, sine, ggu, gdb, rb, res, gq, gk)


def tail_kernel(
    d_in, w_in, n_in, xs, og_in, od_in, fw_in, fd_in, goq_in, dr_ref, ga_ref, dgm_ref, dgh_ref,
    rq, rqo, fw, fd, gout, landed,
    d_ref, w_ref, n_ref, x_ref, goq, send_c, recv_c, send_l, recv_l, keep, gt,
    og, od, rx, rxd, rz, rzd, total_w, total_d,
    pq, work, wgo, ry, ryo, ox, oxo, rs, rso, gs, gr,
    send_sem, recv_sem, load_sem, back_send, back_recv,
):
    where = place()
    y, x, p, l, c = where
    peer = peers_of(x, y, p, l, c)
    red = Reduction(where)
    net = Plan(send_sem, recv_sem)
    second_of = {}
    t = 2 * l + c
    for n, kind in enumerate(KINDS[:2]):
        away = 1 - red.kept(kind)
        second_of[kind] = net.add(peer[red.second_peer(kind)], [(og_in.at[n, away], rx.at[n]), (od_in.at[n, away], rxd.at[n])])
    u_me, u_near = red.kept(ME), red.kept(NEAR)
    go_near = net.add(peer["l"], [(og.at[1], rz.at[1]), (od.at[1], rzd.at[1])])
    go_halves = net.add(peer["c"], [(total_w.at[1 - c], fw.at[c]), (total_d.at[1 - c], fd.at[c])])
    go_give_0 = net.add(peer["c"], [(send_c.at[0], recv_c.at[0])])
    go_give_1 = net.add(peer["c"], [(send_c.at[1], recv_c.at[1])])
    halves = [pl.ds(k * ROWS, ROWS) for k in range(2)]
    go_cross = [net.add(peer["l"], [(send_l.at[half], recv_l.at[half])]) for half in halves]

    def group(yy, xx, pp):
        return (yy * 2 + xx) * 2 + pp

    def moved(sources, groups, targets, at=0):
        return [(src.at[one], dst.at[at + k]) for k, one in enumerate(groups) for src, dst in zip(sources, targets)]

    source, working, small = (pq, goq), (work, wgo), (rs, rso)
    base, across = group(y, x, p), group(y, x, 1 - p)
    give_y = (group(1 - y, 0, p), group(1 - y, 1, p))
    give_x = (group(0, 1 - x, 1 - p), group(1, 1 - x, 1 - p))
    go_own_y = [[net.add(peer["y"], moved((a,), give_y[k : k + 1], (b,), k)) for k in range(2)] for a, b in ((pq, ry), (goq_in, ryo))]
    go_other_x = [[net.add(peer["x"], moved((a,), give_x[k : k + 1], (b,), k)) for k in range(2)] for a, b in ((pq, ox), (goq_in, oxo))]
    go_own_x = [net.add(peer["x"], moved(working[k : k + 1], (group(y, 1 - x, p),), small[k : k + 1], 0)) for k in range(2)]
    go_other_y = [net.add(peer["y"], moved(working[k : k + 1], (group(1 - y, x, 1 - p),), small[k : k + 1], 1)) for k in range(2)]
    go_across = [net.add(peer["p"], moved(working[k : k + 1], (across,), small[k : k + 1], 2)) for k in range(2)]

    def parts(q):
        return [(work.at[base, rows_at(q, 32)], rq.at[t]), (wgo.at[base, rows_at(q, 64)], rqo.at[t])]

    go_last_l = net.add(peer["l"], parts(2 * (1 - l) + c))
    go_last_d = net.add(peer["d"], parts(2 * (1 - l) + 1 - c))
    go_last_c = net.add(peer["c"], parts(2 * l + 1 - c))
    go_gain = [net.add(peer[name], [(gs.at[k], gr.at[k])]) for k, name in enumerate(("c", "x", "y", "p", "l"))]
    home = Return(where, gt, landed, back_send, back_recv)

    def gain_hop(k):
        net.arrived(go_gain[k])
        gs[k + 1] = gs[k] + gr[k]
        if k + 1 < len(AXES):
            net.start(go_gain[k + 1])

    loads = [
        pltpu.make_async_copy(src, dst, load_sem.at[k])
        for k, (src, dst) in enumerate(
            [
                (d_in, d_ref), (w_in, w_ref), (n_in, n_ref), (goq_in, goq), (xs.at[rows_at(owned(p, l, c), OWN)], x_ref),
                (og_in.at[0, u_me], og.at[0]), (og_in.at[1, u_near], og.at[1]),
                (od_in.at[0, u_me], od.at[0]), (od_in.at[1, u_near], od.at[1]),
                (fw_in, rz.at[0]), (fd_in, rzd.at[0]),
            ]
        )
    ]
    for copy in loads:
        copy.start()
    greet(line_peers(p, l, c) + [peer["x"], peer["y"]])
    net.start(second_of[NEAR], second_of[ME], *go_own_y[1], *go_other_x[1])

    def project(ll, cc, write):
        part = d_ref[rows_at(owned(p, ll, cc), OWN), :]

        def chunk(k, carry):
            cols = rows_at(k, 256)
            write(cols, dot(part, w_ref[cols, :], NT))
            return carry

        lax.fori_loop(0, 4, chunk, 0)

    def give(k):
        def write(cols, value):
            send_c[k, :, cols] = value.astype(jnp.bfloat16)

        return write

    def hold(k):
        def write(cols, value):
            keep[k, :, cols] = value

        return write

    def add(k, at, left, right, place_at):
        total = left[at].astype(jnp.float32) + right[place_at].astype(jnp.float32)
        working[k][at] = total.astype(jnp.bfloat16)

    def first_sums(k):
        net.arrived(*go_other_x[k])
        for yy in (0, 1):
            add(k, group(yy, x, 1 - p), source[k], (ox, oxo)[k], yy)
        net.start(go_other_y[k])
        net.arrived(*go_own_y[k])
        for xx in (0, 1):
            add(k, group(y, xx, p), source[k], (ry, ryo)[k], xx)
        net.start(go_own_x[k])

    def second_sums(k):
        net.arrived(go_other_y[k])
        add(k, across, working[k], small[k], 1)
        net.start(go_across[k])
        net.arrived(go_own_x[k])
        add(k, base, working[k], small[k], 0)

    loads[0].wait()
    loads[1].wait()
    project(1 - l, 1 - c, give(0))
    net.start(go_give_0)
    project(1 - l, c, hold(0))
    net.arrived(go_give_0)
    send_l[...] = (keep[0] + recv_c[0].astype(jnp.float32)).astype(jnp.bfloat16)
    net.start(go_cross[0])
    project(l, 1 - c, give(1))
    net.start(go_give_1)
    project(l, c, hold(1))
    for copy in loads[2:]:
        copy.wait()

    def grad_qkv(yy, xx):
        k = yy * 2 + xx
        value = dot(n_ref[:, rows_at(k, 256)], d_ref[...], TN).astype(jnp.bfloat16)
        pq[2 * k] = value[:128]
        pq[2 * k + 1] = value[128:]

    def start_if(index, groups):
        for k in range(2):

            @pl.when(index == k)
            def _():
                net.start(groups[k])

    def one_chunk(k, carry):
        yy, xx = jnp.where(k % 2 == 0, 1 - y, y), jnp.where(k < 2, 1 - x, x)
        grad_qkv(yy, xx)

        @pl.when(k < 2)
        def _():
            start_if(yy, go_other_x[0])

        @pl.when(k % 2 == 0)
        def _():
            start_if(xx, go_own_y[0])

        return carry

    gs[0] = jnp.zeros_like(gs[0])

    def rows_back(k, total):
        rows = rows_at(k, 64)
        value = x_ref[rows, :].astype(jnp.float32)
        grad = keep[1, rows, :] + recv_c[1, rows, :].astype(jnp.float32) + recv_l[rows, :].astype(jnp.float32)
        r = lax.rsqrt(jnp.mean(value * value, axis=-1, keepdims=True) + EPS)
        scaled = value * r
        gained = grad * ga_ref[...]
        back = r * (gained - scaled * jnp.mean(scaled * gained, axis=-1, keepdims=True))
        gt[rows, :] = (dr_ref[rows, :] + back).astype(jnp.bfloat16)
        return total + jnp.sum(grad * scaled, axis=0, keepdims=True)

    lax.fori_loop(0, 1, one_chunk, 0)
    net.start(go_cross[1])
    lax.fori_loop(1, 2, one_chunk, 0)
    net.arrived(go_give_1, go_cross[0])
    d_attn = lax.fori_loop(0, 4, rows_back, jnp.zeros((1, MODEL_DIM), jnp.float32))
    home.start_one(0)
    lax.fori_loop(2, 4, one_chunk, 0)
    first_sums(1)
    net.arrived(go_cross[1])
    d_attn = lax.fori_loop(4, 8, rows_back, d_attn)
    home.start_one(1)
    net.arrived(second_of[NEAR])
    og[1] = (og[1].astype(jnp.float32) + rx[1].astype(jnp.float32)).astype(jnp.bfloat16)
    od[1] = (od[1].astype(jnp.float32) + rxd[1].astype(jnp.float32)).astype(jnp.bfloat16)
    net.start(go_near)
    first_sums(0)
    second_sums(1)
    d_mlp = jnp.sum(dgm_ref[...], axis=0, keepdims=True)
    for k in range(8):
        lanes = slice(k * 128, (k + 1) * 128)
        gs[0, k : k + 1, :] = d_attn[:, lanes]
        gs[0, 8 + k : 9 + k, :] = d_mlp[:, lanes]
    for k in range(2):
        gs[0, 16 + k : 17 + k, :] = jnp.sum(dgh_ref[k], axis=0, keepdims=True)
    net.start(go_gain[0])
    second_sums(0)
    gain_hop(0)
    net.arrived(second_of[ME])
    gain_hop(1)
    net.arrived(go_near)
    for cc in range(2):
        rows = pl.ds(32 * cc, 32)
        total_w[cc] = (
            og[0, :, rows, :].astype(jnp.float32) + rx[0, :, rows, :].astype(jnp.float32)
            + rz[0, :, rows, :].astype(jnp.float32) + rz[1, :, rows, :].astype(jnp.float32)
        )
        rows = pl.ds(96 * cc, 96)
        total_d[cc] = (
            od[0, rows, :].astype(jnp.float32) + rxd[0, rows, :].astype(jnp.float32)
            + rzd[0, rows, :].astype(jnp.float32) + rzd[1, rows, :].astype(jnp.float32)
        )
    net.start(go_halves)
    fw[c] = total_w[c]
    fd[c] = total_d[c]
    gain_hop(2)
    net.arrived(go_halves)
    for k in (1, 0):
        net.arrived(go_across[k])
        add(k, base, working[k], small[k], 2)
    net.start(go_last_l, go_last_d, go_last_c)
    rq[t] = work[base, rows_at(t, 32), :]
    rqo[t] = wgo[base, rows_at(t, 64), :]
    gain_hop(3)
    home.wait()
    gain_hop(4)
    gout[...] = gs[len(AXES)]
    net.arrived(go_last_l, go_last_d, go_last_c)
    net.sent()


def finish_kernel(
    rq, rqo, fw, fd, landed, result,
    output, tokens, out_query, out_key, out_value, out_out, out_gate, out_up, out_down,
):
    output[...] = result[...]
    tokens[...] = landed[...].astype(jnp.float32)
    for half in range(2):
        cols = slice(half * HALF_FF, (half + 1) * HALF_FF)
        out_gate[:, cols] = fw[half, 0]
        out_up[:, cols] = fw[half, 1]
        out_down[:, half * 512 : (half + 1) * 512] = fd[half]
    for q in range(4):
        value = rq[q].astype(jnp.float32)
        out_query[:, 512 * q : 512 * (q + 1)] = value[:, :512]
        out_key[:, 256 * q : 256 * (q + 1)] = value[:, 512:768]
        out_value[:, 256 * q : 256 * (q + 1)] = value[:, 768:]
        out_out[:, 256 * q : 256 * (q + 1)] = rqo[q].astype(jnp.float32)


def finish(rq, rqo, fw, fd, landed, result):
    f32 = jnp.float32
    vmem = pl.BlockSpec(memory_space=pltpu.VMEM)
    return pl.pallas_call(
        finish_kernel,
        out_shape=(
            jax.ShapeDtypeStruct((2, ROWS, MODEL_DIM), jnp.bfloat16),
            jax.ShapeDtypeStruct((2, ROWS, MODEL_DIM), f32),
            jax.ShapeDtypeStruct((32, 2048), f32),
            jax.ShapeDtypeStruct((32, 1024), f32),
            jax.ShapeDtypeStruct((32, 1024), f32),
            jax.ShapeDtypeStruct((64, 1024), f32),
            jax.ShapeDtypeStruct((32, FF), f32),
            jax.ShapeDtypeStruct((32, FF), f32),
            jax.ShapeDtypeStruct((96, 1024), f32),
        ),
        in_specs=[vmem] * 6,
        out_specs=[vmem] * 9,
        compiler_params=pltpu.CompilerParams(vmem_limit_bytes=VMEM_LIMIT),
        name="finish",
    )(rq, rqo, fw, fd, landed, result)


def tail(d, w, normed, xs, og, od, fw, fd, goq, d_resid, g_attn, d_g_mlp, d_g_heads):
    bf16, f32 = jnp.bfloat16, jnp.float32
    any_spec = pl.BlockSpec(memory_space=pl.ANY)
    vmem = pl.BlockSpec(memory_space=pltpu.VMEM)
    copies = 48
    wide, deep = (2, 64, HALF_FF), (192, 512)
    own = (OWN, MODEL_DIM)
    big, tall = (128, 1024), (256, 256)

    def vm(a):
        return pltpu.VMEM(a.shape, a.dtype)

    def low(*shape):
        return pltpu.VMEM(shape, bf16)

    goq = goq.reshape(8, 256, 256)
    return pl.pallas_call(
        tail_kernel,
        out_shape=(
            jax.ShapeDtypeStruct((4, 32, 1024), bf16),
            jax.ShapeDtypeStruct((4, 64, 256), bf16),
            jax.ShapeDtypeStruct((2, 2, 32, HALF_FF), f32),
            jax.ShapeDtypeStruct((2, 96, 512), f32),
            jax.ShapeDtypeStruct((24, 128), f32),
            jax.ShapeDtypeStruct((2, ROWS, MODEL_DIM), bf16),
        ),
        in_specs=[any_spec] * 9 + [vmem] * 4,
        out_specs=[vmem] * 6,
        scratch_shapes=[
            vm(d), vm(w), vm(normed), low(*own), vm(goq),
            low(2, *own), low(2, *own), low(*own), low(*own),
            pltpu.VMEM((2,) + own, f32),
            low(*own),
            low(2, *wide), low(2, *deep),
            low(2, *wide), low(2, *deep), low(2, *wide), low(2, *deep),
            pltpu.VMEM((2, 2, 32, HALF_FF), f32), pltpu.VMEM((2, 96, 512), f32),
            low(8, *big), low(8, *big), low(8, *tall),
            low(2, *big), low(2, *tall), low(2, *big), low(2, *tall), low(3, *big), low(3, *tall),
            pltpu.VMEM((6, 24, 128), f32), pltpu.VMEM((5, 24, 128), f32),
            pltpu.SemaphoreType.DMA((copies,)),
            pltpu.SemaphoreType.DMA((copies,)),
            pltpu.SemaphoreType.DMA((11,)),
            pltpu.SemaphoreType.DMA((2,)),
            pltpu.SemaphoreType.DMA((2,)),
        ],
        compiler_params=pltpu.CompilerParams(
            collective_id=5, has_side_effects=True, vmem_limit_bytes=VMEM_LIMIT
        ),
        name="tail_reduce",
    )(d, w, normed, xs, og, od, fw, fd, goq, d_resid, g_attn, d_g_mlp, d_g_heads)


def pick(value, index):
    return lax.dynamic_index_in_dim(value, index, 0, keepdims=False)


def fast_device(tokens, cotangent, starts, w_query, key_matrix, value_matrix, w_out, w_gate, w_up, w_down, gains):
    p = lax.axis_index("p")
    gn = jnp.pad(gains.astype(jnp.float32), (0, 952)).reshape(8, 128)
    half_steps = jnp.arange(HEAD_DIM // 2, dtype=jnp.float32)
    inverse = THETA ** (-2.0 * half_steps / HEAD_DIM)
    inverse = jnp.broadcast_to(jnp.concatenate([inverse, inverse])[None], (8, HEAD_DIM))
    own_starts = pick(starts, p)
    block_at = jnp.arange(SEQ_ROWS // PIECE, dtype=jnp.int32) * PIECE
    flags = jnp.any(own_starts[None, :] == block_at[:, None], axis=1).astype(jnp.int32)
    xs, w_qkv, woq, gf, wgu, wdn, cosine, sine = front(
        tokens, w_query, key_matrix, value_matrix, w_out, gn, w_gate, w_up, w_down, inverse
    )
    xs = xs.reshape(SEQ_ROWS, MODEL_DIM)
    gain_all = gf.reshape(32, 1024)[:, :72].reshape(2304)
    g_attn = gain_all[None, :1024]
    g_mlp = gain_all[None, 1024:2048]
    g_q = gain_all[None, 2048:2176]
    g_k = gain_all[None, 2176:]
    normed, q, k, v, q_raw, k_raw, attn, lse, wo, wgu, wdn = attend(
        flags, xs, w_qkv, g_attn, g_q, g_k, cosine, sine, woq, wgu, wdn
    )
    resid, mlp_in, wgu, wdn, wdx, dy = finish_resid(attn, wo, g_mlp, xs, cotangent, wgu, wdn)
    ggu, gdb, rb, d_resid, d_branch, result, d_g_mlp = feed_forward(
        mlp_in.reshape(1024, MODEL_DIM), dy.reshape(1024, MODEL_DIM), wgu, wdn, wdx, resid, g_mlp
    )
    d_qkv, goq, og, od, fw, fd, output, d_g_heads = attend_back(
        flags, q, k, v, attn, d_branch, wo, lse, q_raw, k_raw, cosine, sine, ggu, gdb, rb, result, g_q, g_k
    )
    rq, rqo, wide, deep, gains_sum, landed = tail(
        d_qkv, w_qkv, normed, xs, og, od, fw, fd, goq, d_resid, g_attn, d_g_mlp, d_g_heads
    )
    device = lax.axis_index(AXES)
    out_gains = lax.dynamic_slice(gains_sum.reshape(3072), (device * 72,), (72,))
    return (*finish(rq, rqo, wide, deep, landed, output), out_gains)


def fast_solution(mesh):
    wide = Mesh(mesh.devices.reshape(2, 2, 2, 2, 2), AXES)
    rows = ("y", "x")
    places = ("p", "l", "c")
    weight = P(AXES, None)
    return jax.shard_map(
        fast_device,
        mesh=wide,
        in_specs=(P(rows, places, None), P(rows, places, None), P(rows, None)) + (weight,) * 7 + (P(AXES),),
        out_specs=(P(rows, places, None), P(rows, places, None)) + (weight,) * 7 + (P(AXES),),
        check_vma=False,
    )


def solution(mesh):
    if dict(mesh.shape) == {"dp": 4, "ctx": 8}:
        return fast_solution(mesh)
    return generic_solution(mesh)
```

```python
import functools
import math

import jax
import jax.numpy as jnp
from jax import lax
from jax.experimental import pallas as pl
from jax.experimental.pallas import tpu as pltpu
from jax.sharding import Mesh
from jax.sharding import PartitionSpec as P

MODEL_DIM = 1024
QUERY_HEADS = 16
KEY_VALUE_HEADS = 8
HEAD_DIM = 128
SEQUENCE_TOKENS = 2048
PIECE = 256
NPIECE = 4


EPS = 1e-06
THETA = 1000000.0
NEG = -1e30


def rms_norm(incoming_values, gain_vector):
    return (
        incoming_values
        * lax.rsqrt(jnp.mean(incoming_values * incoming_values, axis=-1, keepdims=True) + EPS)
        * gain_vector
    )


def rope_tables(positions):
    half_steps = jnp.arange(HEAD_DIM // 2, dtype=jnp.float32)
    inverse = THETA ** (-2.0 * half_steps / HEAD_DIM)
    angles = positions.astype(jnp.float32)[:, None] * inverse[None, :]
    angles = jnp.concatenate([angles, angles], axis=-1)
    return (jnp.cos(angles), jnp.sin(angles))


def rotate(incoming_values, cosine_table, sine_table):
    half_dim = HEAD_DIM // 2
    turned = jnp.concatenate(
        [-incoming_values[..., half_dim:], incoming_values[..., :half_dim]], axis=-1
    )
    return incoming_values * cosine_table[:, None, :] + turned * sine_table[:, None, :]


def per_head_route(unrotated_projection, gain_vector, cosine_table, sine_table, head_count):
    shaped = unrotated_projection.reshape(unrotated_projection.shape[:-1] + (head_count, HEAD_DIM))
    return rotate(rms_norm(shaped, gain_vector), cosine_table, sine_table).reshape(
        unrotated_projection.shape
    )


def piece_ids(positions, piece_starts):
    inside = (positions[:, None] >= piece_starts[None, :]) & (
        positions[:, None] < piece_starts[None, :] + PIECE
    )
    number = jnp.arange(1, NPIECE + 1, dtype=jnp.int32)
    return jnp.sum(jnp.where(inside, number[None, :], 0), axis=1) - 1


def visible(query_pos, query_id, key_pos, key_id):
    causal = key_pos[None, :] <= query_pos[:, None]
    same_piece = (query_id[:, None] == key_id[None, :]) & (query_id[:, None] >= 0)
    return causal | same_piece


def swiglu(gate_proj, up_proj):
    return jax.nn.silu(gate_proj) * up_proj


def block_extent(kv_count, per_head):
    target = max(1, 512 // per_head)
    chosen = 1
    for candidate in range(1, kv_count + 1):
        if kv_count % candidate == 0 and candidate <= target:
            chosen = candidate
    return chosen


def attend_forward(incoming_query, incoming_keys, incoming_values, allowed, head_group_block):
    sequence_rows = incoming_query.shape[0]
    query_group_factor = QUERY_HEADS // KEY_VALUE_HEADS
    scaling = 1.0 / math.sqrt(HEAD_DIM)
    query_per_head = incoming_query.reshape(
        sequence_rows, KEY_VALUE_HEADS, query_group_factor, HEAD_DIM
    )
    key_per_head = incoming_keys.reshape(incoming_keys.shape[0], KEY_VALUE_HEADS, HEAD_DIM)
    value_per_head = incoming_values.reshape(incoming_values.shape[0], KEY_VALUE_HEADS, HEAD_DIM)
    mixed_parts = []
    total_parts = []
    for head_offset in range(0, KEY_VALUE_HEADS, head_group_block):
        q_part = query_per_head[:, head_offset : head_offset + head_group_block]
        k_part = key_per_head[:, head_offset : head_offset + head_group_block]
        v_part = value_per_head[:, head_offset : head_offset + head_group_block]
        scores = (
            jnp.einsum("tagd,kad->agtk", q_part, k_part, preferred_element_type=jnp.float32)
            * scaling
        )
        scores = jnp.where(allowed[None, None], scores, NEG)
        row_max = jnp.max(scores, axis=-1, keepdims=True)
        exp_scores = jnp.exp(scores - row_max)
        summed = jnp.sum(exp_scores, axis=-1, keepdims=True)
        prob_low = (exp_scores / summed).astype(jnp.bfloat16)
        mixed_parts.append(
            jnp.einsum("agtk,kad->tagd", prob_low, v_part, preferred_element_type=jnp.float32)
        )
        total_parts.append(row_max + jnp.log(summed))
    mixed_out = jnp.concatenate(mixed_parts, axis=1).reshape(sequence_rows, QUERY_HEADS * HEAD_DIM)
    return (mixed_out, jnp.concatenate(total_parts, axis=0))


def attend_backward(
    incoming_query,
    incoming_keys,
    incoming_values,
    allowed,
    log_total,
    mixed_gradient,
    head_group_block,
):
    sequence_rows = incoming_query.shape[0]
    key_row_matrix = incoming_keys.shape[0]
    query_group_factor = QUERY_HEADS // KEY_VALUE_HEADS
    scaling = 1.0 / math.sqrt(HEAD_DIM)
    query_per_head = incoming_query.reshape(
        sequence_rows, KEY_VALUE_HEADS, query_group_factor, HEAD_DIM
    )
    gradient_per_head = mixed_gradient.reshape(
        sequence_rows, KEY_VALUE_HEADS, query_group_factor, HEAD_DIM
    )
    key_per_head = incoming_keys.reshape(key_row_matrix, KEY_VALUE_HEADS, HEAD_DIM)
    value_per_head = incoming_values.reshape(key_row_matrix, KEY_VALUE_HEADS, HEAD_DIM)
    dq_parts = []
    key_gradient_pieces = []
    value_gradient_pieces = []
    for head_offset in range(0, KEY_VALUE_HEADS, head_group_block):
        q_part = query_per_head[:, head_offset : head_offset + head_group_block]
        g_part = gradient_per_head[:, head_offset : head_offset + head_group_block]
        k_part = key_per_head[:, head_offset : head_offset + head_group_block]
        v_part = value_per_head[:, head_offset : head_offset + head_group_block]
        scores = (
            jnp.einsum("tagd,kad->agtk", q_part, k_part, preferred_element_type=jnp.float32)
            * scaling
        )
        scores = jnp.where(allowed[None, None], scores, NEG)
        prob_all = jnp.exp(scores - log_total[head_offset : head_offset + head_group_block])
        prob_low = prob_all.astype(jnp.bfloat16)
        d_probs = jnp.einsum("tagd,kad->agtk", g_part, v_part, preferred_element_type=jnp.float32)
        row_dot = jnp.sum(prob_all * d_probs, axis=-1, keepdims=True)
        d_scores = (prob_all * (d_probs - row_dot)).astype(jnp.bfloat16)
        dq_parts.append(
            jnp.einsum("agtk,kad->tagd", d_scores, k_part, preferred_element_type=jnp.float32)
            * scaling
        )
        key_gradient_pieces.append(
            jnp.einsum("agtk,tagd->kad", d_scores, q_part, preferred_element_type=jnp.float32)
            * scaling
        )
        value_gradient_pieces.append(
            jnp.einsum("agtk,tagd->kad", prob_low, g_part, preferred_element_type=jnp.float32)
        )
    d_query = jnp.concatenate(dq_parts, axis=1).reshape(sequence_rows, QUERY_HEADS * HEAD_DIM)
    key_gradient = jnp.concatenate(key_gradient_pieces, axis=1).reshape(
        key_row_matrix, KEY_VALUE_HEADS * HEAD_DIM
    )
    value_gradient = jnp.concatenate(value_gradient_pieces, axis=1).reshape(
        key_row_matrix, KEY_VALUE_HEADS * HEAD_DIM
    )
    return (d_query, key_gradient, value_gradient)


def generic_device(
    tokens, cotangent, starts, w_query, key_matrix, value_matrix, w_out, w_gate, w_up, w_down, gains
):
    sequence_count, sequence_rows, model_width = tokens.shape
    number_of_rows = sequence_count * sequence_rows
    head_group_block = block_extent(KEY_VALUE_HEADS, QUERY_HEADS // KEY_VALUE_HEADS * sequence_rows)
    attn_set = (
        lax.all_gather(w_query, ("dp", "ctx"), axis=0, tiled=True),
        lax.all_gather(key_matrix, ("dp", "ctx"), axis=0, tiled=True),
        lax.all_gather(value_matrix, ("dp", "ctx"), axis=0, tiled=True),
        lax.all_gather(w_out, ("dp", "ctx"), axis=0, tiled=True),
        lax.all_gather(gains, ("dp", "ctx"), axis=0, tiled=True),
    )
    mlp_set = (
        lax.all_gather(w_gate, ("dp", "ctx"), axis=0, tiled=True),
        lax.all_gather(w_up, ("dp", "ctx"), axis=0, tiled=True),
        lax.all_gather(w_down, ("dp", "ctx"), axis=0, tiled=True),
    )
    gain_all = attn_set[4].astype(jnp.float32)
    g_attn = gain_all[:MODEL_DIM]
    g_mlp = gain_all[MODEL_DIM : 2 * MODEL_DIM]
    g_query = gain_all[2 * MODEL_DIM : 2 * MODEL_DIM + HEAD_DIM]
    key_grad_total = gain_all[2 * MODEL_DIM + HEAD_DIM :]
    positions = lax.axis_index("ctx") * sequence_rows + jnp.arange(sequence_rows, dtype=jnp.int32)
    key_places = jnp.arange(SEQUENCE_TOKENS, dtype=jnp.int32)
    cosine_table, sine_table = rope_tables(positions)

    def query_map(unrotated_projection, gain_vector):
        return per_head_route(
            unrotated_projection, gain_vector, cosine_table, sine_table, QUERY_HEADS
        )

    def key_map(unrotated_projection, gain_vector):
        return per_head_route(
            unrotated_projection, gain_vector, cosine_table, sine_table, KEY_VALUE_HEADS
        )

    flat_in = tokens.reshape(number_of_rows, model_width).astype(jnp.float32)
    normed = rms_norm(flat_in, g_attn).astype(jnp.bfloat16)
    query_raw = jnp.dot(normed, attn_set[0], preferred_element_type=jnp.float32).reshape(
        sequence_count, sequence_rows, QUERY_HEADS * HEAD_DIM
    )
    key_unrotated = jnp.dot(normed, attn_set[1], preferred_element_type=jnp.float32).reshape(
        sequence_count, sequence_rows, KEY_VALUE_HEADS * HEAD_DIM
    )
    value_reduced = jnp.dot(normed, attn_set[2], preferred_element_type=jnp.float32).astype(
        jnp.bfloat16
    )
    value_reduced = value_reduced.reshape(sequence_count, sequence_rows, KEY_VALUE_HEADS * HEAD_DIM)
    query_reduced = query_map(query_raw, g_query).astype(jnp.bfloat16)
    key_reduced = key_map(key_unrotated, key_grad_total).astype(jnp.bfloat16)
    mask_list = []
    mixed_list = []
    total_list = []
    for seq_index in range(sequence_count):
        query_ids = piece_ids(positions, starts[seq_index])
        key_ids = piece_ids(key_places, starts[seq_index])
        allowed = visible(positions, query_ids, key_places, key_ids)
        key_full, value_full = (
            lax.all_gather(key_reduced[seq_index], "ctx", axis=0, tiled=True),
            lax.all_gather(value_reduced[seq_index], "ctx", axis=0, tiled=True),
        )
        mixed_out, log_total = attend_forward(
            query_reduced[seq_index], key_full, value_full, allowed, head_group_block
        )
        mask_list.append(allowed)
        mixed_list.append(mixed_out)
        total_list.append(log_total)
    attn_low = (
        jnp.stack(mixed_list).reshape(number_of_rows, QUERY_HEADS * HEAD_DIM).astype(jnp.bfloat16)
    )
    residual = flat_in + jnp.dot(attn_low, attn_set[3], preferred_element_type=jnp.float32)
    mlp_in = rms_norm(residual, g_mlp).astype(jnp.bfloat16)
    gate_proj = jnp.dot(mlp_in, mlp_set[0], preferred_element_type=jnp.float32)
    up_proj = jnp.dot(mlp_in, mlp_set[1], preferred_element_type=jnp.float32)
    hidden = swiglu(gate_proj, up_proj).astype(jnp.bfloat16)
    result = residual + jnp.dot(hidden, mlp_set[2], preferred_element_type=jnp.float32)
    output = result.astype(jnp.bfloat16).reshape(tokens.shape)
    mlp_back = (
        lax.all_gather(w_gate, ("dp", "ctx"), axis=0, tiled=True),
        lax.all_gather(w_up, ("dp", "ctx"), axis=0, tiled=True),
        lax.all_gather(w_down, ("dp", "ctx"), axis=0, tiled=True),
    )
    grad_flat = cotangent.reshape(number_of_rows, model_width)
    grad_down = jnp.dot(hidden.T, grad_flat, preferred_element_type=jnp.float32)
    d_hidden = jnp.dot(grad_flat, mlp_back[2].T, preferred_element_type=jnp.float32)
    swiglu_pull = jax.vjp(swiglu, gate_proj, up_proj)[1]
    d_gate, d_up = swiglu_pull(d_hidden)
    d_gate = d_gate.astype(jnp.bfloat16)
    d_up = d_up.astype(jnp.bfloat16)
    grad_gate = jnp.dot(mlp_in.T, d_gate, preferred_element_type=jnp.float32)
    grad_up = jnp.dot(mlp_in.T, d_up, preferred_element_type=jnp.float32)
    mlp_grads = (
        lax.psum_scatter(grad_gate, ("dp", "ctx"), scatter_dimension=0, tiled=True),
        lax.psum_scatter(grad_up, ("dp", "ctx"), scatter_dimension=0, tiled=True),
        lax.psum_scatter(grad_down, ("dp", "ctx"), scatter_dimension=0, tiled=True),
    )
    d_mlp_in = jnp.dot(d_gate, mlp_back[0].T, preferred_element_type=jnp.float32)
    d_mlp_in = d_mlp_in + jnp.dot(d_up, mlp_back[1].T, preferred_element_type=jnp.float32)
    mlp_norm_pull = jax.vjp(rms_norm, residual, g_mlp)[1]
    d_resid_norm, d_g_mlp = mlp_norm_pull(d_mlp_in)
    d_resid = grad_flat.astype(jnp.float32) + d_resid_norm
    attn_back = (
        lax.all_gather(w_query, ("dp", "ctx"), axis=0, tiled=True),
        lax.all_gather(key_matrix, ("dp", "ctx"), axis=0, tiled=True),
        lax.all_gather(value_matrix, ("dp", "ctx"), axis=0, tiled=True),
        lax.all_gather(w_out, ("dp", "ctx"), axis=0, tiled=True),
        lax.all_gather(gains, ("dp", "ctx"), axis=0, tiled=True),
    )
    d_branch = d_resid.astype(jnp.bfloat16)
    grad_out = jnp.dot(attn_low.T, d_branch, preferred_element_type=jnp.float32)
    d_attn = jnp.dot(d_branch, attn_back[3].T, preferred_element_type=jnp.float32).astype(
        jnp.bfloat16
    )
    d_attn = d_attn.reshape(sequence_count, sequence_rows, QUERY_HEADS * HEAD_DIM)
    dq_list = []
    dk_list = []
    value_gradient_list = []
    for seq_index in range(sequence_count):
        key_full, value_full = (
            lax.all_gather(key_reduced[seq_index], "ctx", axis=0, tiled=True),
            lax.all_gather(value_reduced[seq_index], "ctx", axis=0, tiled=True),
        )
        d_query_seq, d_key_full, d_value_full = attend_backward(
            query_reduced[seq_index],
            key_full,
            value_full,
            mask_list[seq_index],
            total_list[seq_index],
            d_attn[seq_index],
            head_group_block,
        )
        d_key_seq, d_value_seq = (
            lax.psum_scatter(
                d_key_full.astype(jnp.bfloat16), "ctx", scatter_dimension=0, tiled=True
            ).astype(jnp.float32),
            lax.psum_scatter(
                d_value_full.astype(jnp.bfloat16), "ctx", scatter_dimension=0, tiled=True
            ).astype(jnp.float32),
        )
        dq_list.append(d_query_seq)
        dk_list.append(d_key_seq)
        value_gradient_list.append(d_value_seq)
    d_query = jnp.stack(dq_list)
    key_gradient = jnp.stack(dk_list)
    value_gradient_reduced = (
        jnp.stack(value_gradient_list)
        .reshape(number_of_rows, KEY_VALUE_HEADS * HEAD_DIM)
        .astype(jnp.bfloat16)
    )
    query_pull = jax.vjp(query_map, query_raw, g_query)[1]
    d_query_raw, d_g_query = query_pull(d_query)
    key_pull = jax.vjp(key_map, key_unrotated, key_grad_total)[1]
    key_gradient_unrotated, d_g_key = key_pull(key_gradient)
    d_query_low = d_query_raw.reshape(number_of_rows, QUERY_HEADS * HEAD_DIM).astype(jnp.bfloat16)
    key_gradient_reduced = key_gradient_unrotated.reshape(
        number_of_rows, KEY_VALUE_HEADS * HEAD_DIM
    ).astype(jnp.bfloat16)
    grad_query = jnp.dot(normed.T, d_query_low, preferred_element_type=jnp.float32)
    grad_key = jnp.dot(normed.T, key_gradient_reduced, preferred_element_type=jnp.float32)
    grad_value = jnp.dot(normed.T, value_gradient_reduced, preferred_element_type=jnp.float32)
    d_normed = jnp.dot(d_query_low, attn_back[0].T, preferred_element_type=jnp.float32)
    d_normed = d_normed + jnp.dot(
        key_gradient_reduced, attn_back[1].T, preferred_element_type=jnp.float32
    )
    d_normed = d_normed + jnp.dot(
        value_gradient_reduced, attn_back[2].T, preferred_element_type=jnp.float32
    )
    input_pull = jax.vjp(rms_norm, flat_in, g_attn)[1]
    d_input_norm, d_g_attn = input_pull(d_normed)
    grad_tokens = (d_resid + d_input_norm).reshape(tokens.shape)
    grad_gains = jnp.concatenate([d_g_attn, d_g_mlp, d_g_query, d_g_key])
    attn_grads = (
        lax.psum_scatter(grad_query, ("dp", "ctx"), scatter_dimension=0, tiled=True),
        lax.psum_scatter(grad_key, ("dp", "ctx"), scatter_dimension=0, tiled=True),
        lax.psum_scatter(grad_value, ("dp", "ctx"), scatter_dimension=0, tiled=True),
        lax.psum_scatter(grad_out, ("dp", "ctx"), scatter_dimension=0, tiled=True),
        lax.psum_scatter(grad_gains, ("dp", "ctx"), scatter_dimension=0, tiled=True),
    )
    return (
        output,
        grad_tokens,
        attn_grads[0],
        attn_grads[1],
        attn_grads[2],
        attn_grads[3],
        mlp_grads[0],
        mlp_grads[1],
        mlp_grads[2],
        attn_grads[4],
    )


def generic_solution(mesh):
    return jax.shard_map(
        generic_device,
        mesh=mesh,
        in_specs=(
            P("dp", "ctx", None),
            P("dp", "ctx", None),
            P("dp", None),
            P(("dp", "ctx"), None),
            P(("dp", "ctx"), None),
            P(("dp", "ctx"), None),
            P(("dp", "ctx"), None),
            P(("dp", "ctx"), None),
            P(("dp", "ctx"), None),
            P(("dp", "ctx"), None),
            P(("dp", "ctx")),
        ),
        out_specs=(
            P("dp", "ctx", None),
            P("dp", "ctx", None),
            P(("dp", "ctx"), None),
            P(("dp", "ctx"), None),
            P(("dp", "ctx"), None),
            P(("dp", "ctx"), None),
            P(("dp", "ctx"), None),
            P(("dp", "ctx"), None),
            P(("dp", "ctx"), None),
            P(("dp", "ctx")),
        ),
        check_vma=False,
    )


AXES = ("y", "x", "p", "l", "c")
FF = 3072
HALF_FF = FF // 2
ROWS = 256
SEQ_ROWS = SEQUENCE_TOKENS
OWN = SEQ_ROWS // 4
BLK = 512
NBLK = SEQ_ROWS // BLK
QH = 4
KH = 2
MESH = pl.DeviceIdType.MESH
SCALE = 1.0 / math.sqrt(HEAD_DIM)
LOG2E = 1.4426950408889634
VMEM_LIMIT = 62 * 1024 * 1024
NT = (((1,), (1,)), ((), ()))
TN = (((0,), (0,)), ((), ()))


def dot(a, b, dims=None):
    if dims is None:
        dims = (((1,), (0,)), ((), ()))
    return lax.dot_general(a, b, dims, preferred_element_type=jnp.float32)


def greet(peers):
    barrier = pltpu.get_barrier_semaphore()
    for peer in peers:
        pl.semaphore_signal(barrier, inc=1, device_id=peer, device_id_type=MESH)
    pl.semaphore_wait(barrier, len(peers))


class Plan:
    def __init__(self, send_sem, recv_sem):
        self.send_sem = send_sem
        self.recv_sem = recv_sem
        self.count = 0
        self.entries = []

    def add(self, peer, pairs):
        self.entries.append((peer, pairs, self.count))
        self.count += len(pairs)
        return len(self.entries) - 1

    def copies(self, name):
        peer, pairs, at = self.entries[name]
        return [
            pltpu.make_async_remote_copy(
                src_ref=src,
                dst_ref=dst,
                send_sem=self.send_sem.at[at + k],
                recv_sem=self.recv_sem.at[at + k],
                device_id=peer,
                device_id_type=MESH,
            )
            for k, (src, dst) in enumerate(pairs)
        ]

    def start(self, *names):
        for name in names:
            for copy in self.copies(name):
                copy.start()

    def arrived(self, *names):
        for name in names:
            for copy in self.copies(name):
                copy.wait_recv()

    def sent(self):
        for name in range(len(self.entries)):
            for copy in self.copies(name):
                copy.wait_send()


def place():
    return tuple(lax.axis_index(name) for name in AXES)


def peers_of(x, y, p, l, c):
    return {
        "c": {"c": 1 - c},
        "l": {"l": 1 - l},
        "d": {"l": 1 - l, "c": 1 - c},
        "p": {"p": 1 - p},
        "x": {"x": 1 - x},
        "y": {"y": 1 - y},
    }


def owned(p, l, c):
    return 2 * c + (p + l + c) % 2


def rows_at(index, size, count=1):
    return pl.ds(pl.multiple_of(index * size, size), size * count)


def in_place(*refs):
    return [(ref, ref) for ref in refs]


def front_kernel(tok, wq, wk, wv, wo, gn, wg, wu, wd, inverse, xs, wa, woq, gf, wgu, wdn, cosine, sine, send_sem, recv_sem, in_sem, local_sem, *staged):
    y, x, p, l, c = place()
    peer = peers_of(x, y, p, l, c)
    block = 4 * p + 2 * l + c
    group = (y * 2 + x) * 8
    me = group + block
    t = 2 * l + c
    net = Plan(send_sem, recv_sem)

    def quarter(q):
        return [
            (wq.at[:, rows_at(q, 512)], wa.at[rows_at(me, 32), pl.ds(0, 512)]),
            (wk.at[:, rows_at(q, 256)], wa.at[rows_at(me, 32), pl.ds(512, 256)]),
            (wv.at[:, rows_at(q, 256)], wa.at[rows_at(me, 32), pl.ds(768, 256)]),
            (wo.at[:, rows_at(q, 256)], woq.at[rows_at(me, 64)]),
            (gn, gf.at[me]),
        ]

    def half(h):
        return [
            (wg.at[:, rows_at(h, HALF_FF)], wgu.at[0, rows_at(me, 32)]),
            (wu.at[:, rows_at(h, HALF_FF)], wgu.at[1, rows_at(me, 32)]),
            (wd.at[:, rows_at(h, 512)], wdn.at[rows_at(me, 96)]),
        ]

    def span(base, piece):
        if piece < 2:
            return in_place(wa.at[rows_at(base // 2 + piece, 64)])
        return in_place(woq.at[rows_at(base // 4, 256)], gf.at[pl.ds(base, 4)])

    def chip(yy, xx, pp, ll):
        slot = (yy * 2 + xx) * 4 + 2 * pp + ll
        return in_place(wgu.at[:, rows_at(slot, 64)], wdn.at[rows_at(slot, 192)])

    mine, other = group + 4 * p, group + 4 * (1 - p)
    go_first_l = net.add(peer["l"], quarter(2 * (1 - l) + c))
    go_first_d = net.add(peer["d"], quarter(2 * (1 - l) + 1 - c))
    go_first_c = net.add(peer["c"], quarter(2 * l + 1 - c))
    go_near = net.add(peer["l"], [(tok.at[p], xs.at[block])])
    upper, lower = pl.ds(0, ROWS // 2), pl.ds(ROWS // 2, ROWS // 2)
    go_far_0 = net.add(peer["p"], [(tok.at[1 - p, upper], xs.at[block, upper])])
    go_far_1 = net.add(peer["p"], [(tok.at[1 - p, lower], xs.at[block, lower])])
    go_near_c = net.add(peer["c"], [(tok.at[p], xs.at[block])])
    pieces = range(3)
    go_across = [net.add(peer["p"], span(mine, k)) for k in pieces]
    go_own_x = [net.add(peer["x"], span(mine, k)) for k in pieces]
    go_near_relay = net.add(peer["c"], in_place(xs.at[block ^ 2]))
    go_own_y = [net.add(peer["y"], span(mine, k) + span((y * 2 + 1 - x) * 8 + 4 * p, k)) for k in pieces]
    go_other_y = [net.add(peer["y"], span(other, k)) for k in pieces]
    go_far_l0 = net.add(peer["l"], in_place(xs.at[block ^ 4, upper]))
    go_far_l1 = net.add(peer["l"], in_place(xs.at[block ^ 4, lower]))
    go_far_relay = net.add(peer["c"], in_place(xs.at[block ^ 4]))
    go_other_x = [net.add(peer["x"], span(other, k) + span(((1 - y) * 2 + x) * 8 + 4 * (1 - p), k)) for k in pieces]
    go_far_l_relay = net.add(peer["c"], in_place(xs.at[block ^ 6]))
    go_mlp_c = net.add(peer["c"], half(1 - c))
    go_mlp_near = net.add(peer["l"], chip(y, x, p, l))
    go_mlp_x = net.add(peer["x"], chip(y, x, p, l))
    moves = quarter(t) + half(c) + [(tok.at[p], xs.at[block])]
    taken = [pltpu.make_async_copy(src, stage, in_sem.at[k]) for k, ((src, dst), stage) in enumerate(zip(moves, staged))]
    own = [pltpu.make_async_copy(stage, dst, local_sem.at[k]) for k, ((src, dst), stage) in enumerate(zip(moves, staged))]
    for copy in taken:
        copy.start()
    greet(list(peer.values()))
    net.start(go_first_l, go_first_d, go_first_c, go_far_0, go_near_c, go_mlp_c)
    for copy in taken:
        copy.wait()
    for copy in own:
        copy.start()

    def table(first, last):
        def chunk(k, carry):
            rows = rows_at(k, 64)
            position = (lax.broadcasted_iota(jnp.int32, (64, HEAD_DIM), 0) + k * 64).astype(jnp.float32)
            lane = lax.broadcasted_iota(jnp.int32, (64, HEAD_DIM), 1)
            angle = position * inverse[0:1, :]
            cosine[rows, :] = jnp.cos(angle)
            sine[rows, :] = jnp.where(lane < HEAD_DIM // 2, -1.0, 1.0) * jnp.sin(angle)
            return carry

        lax.fori_loop(first, last, chunk, 0)

    for copy in own:
        copy.wait()
    net.arrived(go_first_l, go_first_d, go_first_c)
    net.start(*go_across, *go_own_x, go_near)
    table(0, 12)
    for k in pieces:
        net.arrived(go_across[k])
        net.start(go_other_y[k])
    net.start(go_far_1)
    net.arrived(go_mlp_c)
    net.start(go_mlp_x)
    net.arrived(go_near)
    net.start(go_near_relay)
    for k in pieces:
        net.arrived(go_other_y[k])
        net.start(go_other_x[k])
    net.arrived(*go_own_x)
    net.start(*go_own_y)
    net.arrived(go_far_0)
    net.start(go_far_l0)
    table(12, 32)
    net.arrived(go_far_1)
    net.start(go_far_l1, go_far_relay, go_mlp_near)
    net.arrived(go_far_l0, go_far_l1)
    net.start(go_far_l_relay)
    net.arrived(go_near_c, go_near_relay, go_far_relay, go_far_l_relay, *go_own_y, *go_other_x, go_mlp_x, go_mlp_near)
    net.sent()


def front(tok, wq, wk, wv, wo, gn, wg, wu, wd, inverse):
    any_spec = pl.BlockSpec(memory_space=pl.ANY)
    copies = 64
    bf16 = jnp.bfloat16
    return pl.pallas_call(
        front_kernel,
        out_shape=(
            jax.ShapeDtypeStruct((8, ROWS, MODEL_DIM), bf16),
            jax.ShapeDtypeStruct((1024, 1024), bf16),
            jax.ShapeDtypeStruct((2048, 256), bf16),
            jax.ShapeDtypeStruct((32, 8, 128), jnp.float32),
            jax.ShapeDtypeStruct((2, MODEL_DIM, HALF_FF), bf16),
            jax.ShapeDtypeStruct((FF, 512), bf16),
            jax.ShapeDtypeStruct((SEQ_ROWS, HEAD_DIM), jnp.float32),
            jax.ShapeDtypeStruct((SEQ_ROWS, HEAD_DIM), jnp.float32),
        ),
        in_specs=[any_spec] * 9 + [pl.BlockSpec(memory_space=pltpu.VMEM)],
        out_specs=[any_spec] * 6 + [pl.BlockSpec(memory_space=pltpu.VMEM)] * 2,
        scratch_shapes=[
            pltpu.SemaphoreType.DMA((copies,)),
            pltpu.SemaphoreType.DMA((copies,)),
            pltpu.SemaphoreType.DMA((9,)),
            pltpu.SemaphoreType.DMA((9,)),
            pltpu.VMEM((32, 512), bf16),
            pltpu.VMEM((32, 256), bf16),
            pltpu.VMEM((32, 256), bf16),
            pltpu.VMEM((64, 256), bf16),
            pltpu.VMEM((8, 128), jnp.float32),
            pltpu.VMEM((32, HALF_FF), bf16),
            pltpu.VMEM((32, HALF_FF), bf16),
            pltpu.VMEM((96, 512), bf16),
            pltpu.VMEM((ROWS, MODEL_DIM), bf16),
        ],
        compiler_params=pltpu.CompilerParams(
            collective_id=0, has_side_effects=True, vmem_limit_bytes=VMEM_LIMIT
        ),
        name="front_gather",
    )(tok, wq, wk, wv, wo, gn, wg, wu, wd, inverse)


def line_peers(p, l, c):
    return [
        {"p": (p + a) % 2, "l": (l + b) % 2, "c": (c + d) % 2}
        for a in range(2)
        for b in range(2)
        for d in range(2)
        if a + b + d > 0
    ]


class Return:
    def __init__(self, where, src, dst, send_sem, recv_sem):
        self.where = where[2:]
        self.src, self.dst, self.send_sem, self.recv_sem = src, dst, send_sem, recv_sem

    def stays(self, index):
        p, l, c = self.where
        return (p == c) & (index == c)

    def local(self, c0):
        p, l, c = self.where
        return pltpu.make_async_copy(self.src.at[pl.ds(c0 * ROWS, ROWS)], self.dst.at[p], self.send_sem.at[c0])

    def remote(self, c0):
        p, l, c = self.where
        return pltpu.make_async_remote_copy(
            src_ref=self.src.at[pl.ds(c0 * ROWS, ROWS)],
            dst_ref=self.dst.at[p],
            send_sem=self.send_sem.at[c0],
            recv_sem=self.recv_sem.at[p],
            device_id={"p": c, "l": (p + l + c) % 2, "c": c0},
            device_id_type=MESH,
        )

    def start_one(self, c0):
        here = self.stays(c0)

        @pl.when(here)
        def _():
            self.local(c0).start()

        @pl.when(jnp.logical_not(here))
        def _():
            self.remote(c0).start()

    def start(self):
        for c0 in range(2):
            self.start_one(c0)

    def wait(self):
        p, l, c = self.where
        for c0 in range(2):
            here = self.stays(c0)

            @pl.when(here)
            def _():
                self.local(c0).wait()

            @pl.when(jnp.logical_not(here))
            def _():
                self.remote(c0).wait_send()

        for seq in range(2):

            @pl.when(jnp.logical_not(self.stays(seq)))
            def _():
                pltpu.make_async_remote_copy(
                    src_ref=self.src.at[pl.ds(0, ROWS)],
                    dst_ref=self.dst.at[seq],
                    send_sem=self.send_sem.at[0],
                    recv_sem=self.recv_sem.at[seq],
                    device_id={"p": 1 - p},
                    device_id_type=MESH,
                ).wait_recv()


class Spread:
    def __init__(self, where, src, dst, send_sem, recv_sem):
        self.where = where[2:]
        self.src, self.dst, self.send_sem, self.recv_sem = src, dst, send_sem, recv_sem

    def here(self, index):
        p, l, c = self.where
        return (p == c) & (index == c)

    def local(self, seq):
        p, l, c = self.where
        return pltpu.make_async_copy(self.src.at[seq], self.dst.at[p, c], self.send_sem.at[seq])

    def remote(self, seq):
        p, l, c = self.where
        return pltpu.make_async_remote_copy(
            src_ref=self.src.at[seq],
            dst_ref=self.dst.at[p, c],
            send_sem=self.send_sem.at[seq],
            recv_sem=self.recv_sem.at[c],
            device_id={"p": seq, "l": (seq + l + p) % 2, "c": p},
            device_id_type=MESH,
        )

    def start(self):
        for seq in range(2):

            @pl.when(self.here(seq))
            def _():
                self.local(seq).start()

            @pl.when(jnp.logical_not(self.here(seq)))
            def _():
                self.remote(seq).start()

    def wait(self):
        p, l, c = self.where
        for seq in range(2):

            @pl.when(self.here(seq))
            def _():
                self.local(seq).wait()

            @pl.when(jnp.logical_not(self.here(seq)))
            def _():
                self.remote(seq).wait_send()

        for block in range(2):

            @pl.when(jnp.logical_not(self.here(block)))
            def _():
                pltpu.make_async_remote_copy(
                    src_ref=self.src.at[0],
                    dst_ref=self.dst.at[c, block],
                    send_sem=self.send_sem.at[0],
                    recv_sem=self.recv_sem.at[block],
                    device_id={"p": 1 - p},
                    device_id_type=MESH,
                ).wait_recv()


def turn(value):
    return pltpu.roll(value, HEAD_DIM // 2, 1)


def block_mask(key_dim, flags, index):
    shape = (BLK, BLK)
    key = lax.broadcasted_iota(jnp.int32, shape, key_dim)
    query = lax.broadcasted_iota(jnp.int32, shape, 1 - key_dim)
    upper = query // PIECE
    piece = jnp.where(upper == 0, flags[2 * index], flags[2 * index + 1])
    return (key <= query) | ((key // PIECE == upper) & (piece > 0))


PROJECT = 8


def attend_kernel(
    flags, x_ref, w_ref, ga_ref, gq_ref, gk_ref, cos_ref, sin_ref, woq, wgu_in, wdn_in,
    n_ref, q_ref, k_ref, v_ref, qr_ref, kr_ref, o_ref, lse_ref, wo, wgu, wdn,
    stage, send_sem, recv_sem, local_sem,
):
    y, x, p, l, c = place()
    peer = peers_of(x, y, p, l, c)
    t = 2 * l + c
    net = Plan(send_sem, recv_sem)

    def chip(yy, xx, pp, ll):
        slot = (yy * 2 + xx) * 4 + 2 * pp + ll
        return in_place(wgu.at[:, rows_at(slot, 64)], wdn.at[rows_at(slot, 192)])

    def rows_of(q):
        return woq.at[rows_at(q, 512)], wo.at[:, rows_at(t, 256)]

    go_mlp_y = net.add(peer["y"], chip(y, x, p, l) + chip(y, 1 - x, p, l))
    go_mlp_x = net.add(peer["x"], chip(y, x, p, 1 - l) + chip(1 - y, x, p, 1 - l))
    go_far = [net.add(peer["p"], [pair]) for pair in chip(y, x, p, l)]
    go_far_l = [net.add(peer["l"], [pair]) for pair in chip(y, x, 1 - p, l)]
    go_near_y = net.add(peer["y"], chip(y, x, p, 1 - l))
    go_wo_l = net.add(peer["l"], [rows_of(2 * (1 - l) + c)])
    go_wo_d = net.add(peer["d"], [rows_of(2 * (1 - l) + 1 - c)])
    go_wo_c = net.add(peer["c"], [rows_of(2 * l + 1 - c)])
    step = pl.program_id(0)

    @pl.when(step == 0)
    def _():
        greet(list(peer.values()))
        net.start(go_near_y, *go_far, go_wo_l, go_wo_d, go_wo_c)
        copy = pltpu.make_async_copy(rows_of(t)[0], stage, local_sem.at[0])
        copy.start()
        copy.wait()
        pltpu.make_async_copy(stage, rows_of(t)[1], local_sem.at[1]).start()

    @pl.when(step < PROJECT)
    def _():
        value = x_ref[...].astype(jnp.float32)
        r = lax.rsqrt(jnp.mean(value * value, axis=-1, keepdims=True) + EPS)
        normed = (value * r * ga_ref[...]).astype(jnp.bfloat16)
        n_ref[...] = normed
        full = dot(normed, w_ref[...])
        cosine, sine = cos_ref[...], sin_ref[...]
        rows = rows_at(jnp.minimum(step, PROJECT - 1), 256)
        for h in range(QH + KH):
            u = full[:, h * HEAD_DIM : (h + 1) * HEAD_DIM]
            raw_ref, out_ref, g_ref, at = (qr_ref, q_ref, gq_ref, h) if h < QH else (kr_ref, k_ref, gk_ref, h - QH)
            raw_ref[at] = u
            n = u * lax.rsqrt(jnp.mean(u * u, axis=-1, keepdims=True) + EPS) * g_ref[...]
            out_ref[at, rows, :] = (n * cosine + turn(n) * sine).astype(jnp.bfloat16)
        for h in range(KH):
            at = (QH + KH + h) * HEAD_DIM
            v_ref[h, rows, :] = full[:, at : at + HEAD_DIM].astype(jnp.bfloat16)

    @pl.when(step == PROJECT)
    def _():
        net.arrived(go_near_y)
        net.start(go_mlp_x, go_mlp_y)

    for k, at in enumerate((PROJECT + 3, PROJECT + 5)):

        @pl.when(step == at)
        def _():
            net.arrived(go_far[k])
            net.start(go_far_l[k])

    @pl.when(step >= PROJECT)
    def _():
        order = jnp.maximum(step - PROJECT, 0)
        g, i = order // NBLK, order % NBLK
        ones = jnp.ones((BLK, HEAD_DIM), jnp.bfloat16)
        mask = block_mask(1, flags, i)

        def values(j):
            return jnp.concatenate([v_ref[g, rows_at(j, BLK), :], ones], axis=1)

        queries = [q_ref[2 * g + h, rows_at(i, BLK), :] for h in range(2)]

        def part(j, masked):
            keys, both = k_ref[g, rows_at(j, BLK), :], values(j)
            found = []
            for q in queries:
                probs = jnp.exp2(dot(q, keys, NT) * (SCALE * LOG2E))
                if masked:
                    probs = jnp.where(mask, probs, 0.0)
                found.append(dot(probs.astype(jnp.bfloat16), both))
            return found

        def one(j, accs):
            return tuple(acc + more for acc, more in zip(accs, part(j, False)))

        accs = lax.fori_loop(0, i, one, tuple(part(i, True)))
        for h, acc in enumerate(accs):
            total = acc[:, HEAD_DIM:]
            o_ref[:, h * HEAD_DIM : (h + 1) * HEAD_DIM] = (acc[:, :HEAD_DIM] / total).astype(jnp.bfloat16)
            lse_ref[h] = jnp.log2(total).T[0:8, :]

    @pl.when(step == PROJECT + 2 * NBLK - 1)
    def _():
        pltpu.make_async_copy(stage, rows_of(t)[1], local_sem.at[1]).wait()
        net.arrived(go_mlp_y, go_mlp_x, *go_far_l, go_wo_l, go_wo_d, go_wo_c)
        net.sent()


def attend(flags, x, w, ga, gq, gk, cosine, sine, woq, wgu, wdn):
    bf16, f32 = jnp.bfloat16, jnp.float32

    def early(s):
        return jnp.minimum(s, PROJECT - 1)

    def late(s):
        return jnp.maximum(s - PROJECT, 0)

    def row(width):
        return pl.BlockSpec((256, width), lambda s, f: (early(s), 0))

    def whole(shape):
        return pl.BlockSpec(shape, lambda s, f: (0,) * len(shape))

    def heads(n):
        return pl.BlockSpec((n, 256, HEAD_DIM), lambda s, f: (0, early(s), 0))

    def shape(n, dtype):
        return jax.ShapeDtypeStruct((n, SEQ_ROWS, HEAD_DIM), dtype)

    any_spec = pl.BlockSpec(memory_space=pl.ANY)
    copies = 20
    return pl.pallas_call(
        attend_kernel,
        out_shape=(
            jax.ShapeDtypeStruct((SEQ_ROWS, MODEL_DIM), bf16),
            shape(QH, bf16),
            shape(KH, bf16),
            shape(KH, bf16),
            shape(QH, f32),
            shape(KH, f32),
            jax.ShapeDtypeStruct((SEQ_ROWS, QH * HEAD_DIM), bf16),
            jax.ShapeDtypeStruct((QH, 8, SEQ_ROWS), f32),
            jax.ShapeDtypeStruct((512, MODEL_DIM), bf16),
            jax.ShapeDtypeStruct(wgu.shape, bf16),
            jax.ShapeDtypeStruct(wdn.shape, bf16),
        ),
        grid_spec=pltpu.PrefetchScalarGridSpec(
            num_scalar_prefetch=1,
            grid=(PROJECT + KH * NBLK,),
            in_specs=[row(MODEL_DIM), whole(w.shape), whole(ga.shape), whole(gq.shape), whole(gk.shape), row(HEAD_DIM), row(HEAD_DIM)]
            + [any_spec] * 3,
            out_specs=[
                row(MODEL_DIM),
                whole((QH, SEQ_ROWS, HEAD_DIM)),
                whole((KH, SEQ_ROWS, HEAD_DIM)),
                whole((KH, SEQ_ROWS, HEAD_DIM)),
                heads(QH),
                heads(KH),
                pl.BlockSpec((BLK, 2 * HEAD_DIM), lambda s, f: (late(s) % NBLK, late(s) // NBLK)),
                pl.BlockSpec((2, 8, BLK), lambda s, f: (late(s) // NBLK, 0, late(s) % NBLK)),
            ]
            + [any_spec] * 3,
            scratch_shapes=[pltpu.VMEM((512, 256), bf16)]
            + [pltpu.SemaphoreType.DMA((copies,))] * 2
            + [pltpu.SemaphoreType.DMA((2,))],
        ),
        input_output_aliases={9: 9, 10: 10},
        compiler_params=pltpu.CompilerParams(
            collective_id=2, has_side_effects=True, vmem_limit_bytes=VMEM_LIMIT
        ),
        cost_estimate=pl.CostEstimate(
            flops=4 * QH * SEQ_ROWS * SEQ_ROWS * HEAD_DIM, bytes_accessed=24 << 20, transcendentals=QH * SEQ_ROWS * SEQ_ROWS
        ),
        name="attend",
    )(flags, x, w, ga, gq, gk, cosine, sine, woq, wgu, wdn)


def resid_kernel(
    attn, wo, g_mlp, xs, cot, wgu_in, wdn_in,
    resid, mlp_in, wgu, wdn, wdx, dy,
    send_c, recv_c, send_l, recv_l, keep, x_own, send_sem, recv_sem, local_sem, dy_send, dy_recv,
):
    where = place()
    y, x, p, l, c = where
    peer = peers_of(x, y, p, l, c)
    net = Plan(send_sem, recv_sem)

    def chip(yy, xx, pp, ll):
        slot = (yy * 2 + xx) * 4 + 2 * pp + ll
        return in_place(wgu.at[:, rows_at(slot, 64)], wdn.at[rows_at(slot, 192)])

    def down(pp, ll):
        found = []
        for xx in range(2):
            slot = xx * 4 + 2 * pp + ll
            found.append((wdn.at[rows_at((1 - c) * 8 + slot, 192)], wdx.at[rows_at(slot, 192)]))
        return found

    def hop(name, *chips):
        found = [chip(*one) for one in chips]
        return [net.add(peer[name], [pairs[k] for pairs in found]) for k in range(2)]

    go_far_x = hop("x", (y, x, 1 - p, l))
    go_far_y = hop("y", (y, x, 1 - p, l), (y, 1 - x, 1 - p, l))
    go_fal_y = hop("y", (y, x, 1 - p, 1 - l))
    go_fal_x = hop("x", (y, x, 1 - p, 1 - l), (1 - y, x, 1 - p, 1 - l))
    go_down_me = net.add(peer["c"], down(p, l))
    go_down_near = net.add(peer["c"], down(p, 1 - l))
    go_down_far = net.add(peer["c"], down(1 - p, l))
    go_down_fal = net.add(peer["c"], down(1 - p, 1 - l))
    halves = [pl.ds(n * ROWS, ROWS) for n in range(2)]
    go_give_0 = [net.add(peer["c"], [(send_c.at[0, half], recv_c.at[0, half])]) for half in halves]
    go_give_1 = net.add(peer["c"], [(send_c.at[1], recv_c.at[1])])
    go_cross = [net.add(peer["l"], [(send_l.at[half], recv_l.at[half])]) for half in halves]
    go_share = [net.add(peer["c"], in_place(mlp_in.at[c, half])) for half in halves]
    go_dy_c = net.add(peer["c"], in_place(dy.at[c]))
    spread = Spread(where, cot, dy, dy_send, dy_recv)
    greet(line_peers(p, l, c) + [peer["x"], peer["y"]])
    spread.start()
    net.start(go_far_x[1], go_fal_y[1], go_far_x[0], go_fal_y[0], go_down_me, go_down_near)
    fetch = pltpu.make_async_copy(xs.at[rows_at(owned(p, l, c), OWN)], x_own, local_sem.at[0])
    fetch.start()

    def project(ll, cc, write, first=0, count=OWN):
        part = attn[pl.ds(pl.multiple_of(owned(p, ll, cc) * OWN + first, ROWS), count), :]

        def chunk(n, carry):
            cols = rows_at(n, 256)
            write(pl.ds(first, count), cols, dot(part, wo[:, cols]))
            return carry

        lax.fori_loop(0, 4, chunk, 0)

    def give(n):
        def write(rows, cols, value):
            send_c[n, rows, cols] = value.astype(jnp.bfloat16)

        return write

    def hold(n):
        def write(rows, cols, value):
            keep[n, rows, cols] = value

        return write

    def relay_hop(k):
        net.arrived(go_far_x[k])
        net.start(go_far_y[k])
        net.arrived(go_fal_y[k])
        net.start(go_fal_x[k])

    for n, half in enumerate(halves):
        project(1 - l, 1 - c, give(0), n * ROWS, ROWS)
        net.start(go_give_0[n])
        project(1 - l, c, hold(0), n * ROWS, ROWS)
        net.arrived(go_give_0[n])
        send_l[half, :] = (keep[0, half, :] + recv_c[0, half, :].astype(jnp.float32)).astype(jnp.bfloat16)
        net.start(go_cross[n])
    relay_hop(1)
    project(l, 1 - c, give(1))
    net.start(go_give_1)
    project(l, c, hold(1))
    fetch.wait()
    relay_hop(0)
    net.arrived(go_give_1)
    keep[1] += recv_c[1].astype(jnp.float32) + x_own[...].astype(jnp.float32)
    for n, half in enumerate(halves):
        net.arrived(go_cross[n])
        total = keep[1, half, :] + recv_l[half, :].astype(jnp.float32)
        resid[half, :] = total
        r = lax.rsqrt(jnp.mean(total * total, axis=-1, keepdims=True) + EPS)
        mlp_in[c, half, :] = (total * r * g_mlp[...]).astype(jnp.bfloat16)
        net.start(go_share[n])
    net.arrived(go_far_y[1])
    net.start(go_down_far)
    spread.wait()
    net.start(go_dy_c)
    net.arrived(go_fal_x[1])
    net.start(go_down_fal)
    net.arrived(go_far_y[0], go_fal_x[0])
    net.arrived(go_down_me, go_down_near, go_down_far, go_down_fal, *go_share, go_dy_c)
    net.sent()


def finish_resid(attn, wo, g_mlp, xs, cot, wgu, wdn):
    bf16, f32 = jnp.bfloat16, jnp.float32
    any_spec = pl.BlockSpec(memory_space=pl.ANY)
    vmem = pl.BlockSpec(memory_space=pltpu.VMEM)
    copies = 32
    return pl.pallas_call(
        resid_kernel,
        out_shape=(
            jax.ShapeDtypeStruct((OWN, MODEL_DIM), f32),
            jax.ShapeDtypeStruct((2, OWN, MODEL_DIM), bf16),
            jax.ShapeDtypeStruct(wgu.shape, bf16),
            jax.ShapeDtypeStruct(wdn.shape, bf16),
            jax.ShapeDtypeStruct((HALF_FF, 512), bf16),
            jax.ShapeDtypeStruct((2, 2, ROWS, MODEL_DIM), bf16),
        ),
        in_specs=[vmem] * 3 + [any_spec] * 4,
        out_specs=[vmem] * 2 + [any_spec] * 4,
        scratch_shapes=[
            pltpu.VMEM((2, OWN, MODEL_DIM), bf16),
            pltpu.VMEM((2, OWN, MODEL_DIM), bf16),
            pltpu.VMEM((OWN, MODEL_DIM), bf16),
            pltpu.VMEM((OWN, MODEL_DIM), bf16),
            pltpu.VMEM((2, OWN, MODEL_DIM), f32),
            pltpu.VMEM((OWN, MODEL_DIM), bf16),
            pltpu.SemaphoreType.DMA((copies,)),
            pltpu.SemaphoreType.DMA((copies,)),
            pltpu.SemaphoreType.DMA((1,)),
            pltpu.SemaphoreType.DMA((2,)),
            pltpu.SemaphoreType.DMA((2,)),
        ],
        input_output_aliases={5: 2, 6: 3},
        compiler_params=pltpu.CompilerParams(
            collective_id=3, has_side_effects=True, vmem_limit_bytes=VMEM_LIMIT
        ),
        name="residual",
    )(attn, wo, g_mlp, xs, cot, wgu, wdn)


CHUNK = 512
EARLY = 1024


def forward_kernel(
    m_ref, dy_ref, w_ref, wdn, wx_ref, resid, g_mlp,
    ggu, gdb, rb, d_resid, db, res, dg,
    mt, dyt, hid, dgt, dup, d_in, down, give, take, all_down, ggv, gdv, send_sem, recv_sem, load_sem, out_sem,
):
    where = place()
    y, x, p, l, c = where
    peer = peers_of(x, y, p, l, c)
    red = Reduction(where)
    net = Plan(send_sem, recv_sem)
    go_d_in = net.add(peer["c"], [(give.at[0], take.at[0])])
    go_down = net.add(peer["c"], [(give.at[1], take.at[1])])
    go_gd, go_wide, outs = [], [], []
    for f in range(HALF_FF // CHUNK):
        part_f = pl.ds(f * CHUNK, CHUNK)
        go_gd.append(net.add(peer["c"], [(gdv.at[part_f, rows_at(1 - c, 512)], gdb.at[c, part_f])]))
        outs.append(
            [
                pltpu.make_async_copy(ggv.at[:, :, part_f], ggu.at[:, :, part_f], out_sem.at[2 * f]),
                pltpu.make_async_copy(gdv.at[part_f, rows_at(c, 512)], gdb.at[c, part_f], out_sem.at[2 * f + 1]),
            ]
        )
        go_wide.append([])
        if f * CHUNK < EARLY:
            for n, kind in enumerate(KINDS):
                pairs = []
                for k in range(2):
                    slot = chip_slot(*red.place(kind, k, True), *red.z[kind])
                    pairs.append((ggv.at[:, rows_at(slot, 64), part_f], rb.at[n, k, :, :, part_f]))
                go_wide[f].append(net.add(peer[red.first_peer(kind)], pairs))
    step = pl.program_id(0)
    fetch = pltpu.make_async_copy(wdn.at[rows_at(c, HALF_FF)], all_down, load_sem.at[0])

    @pl.when(step == 0)
    def _():
        fetch.start()
        greet([peer["c"], peer["x"], peer["y"]])

        def flip(k, carry):
            rows = rows_at(k, 256)
            mt[:, rows] = m_ref[rows, :].T
            dyt[:, rows] = dy_ref[rows, :].T
            return carry

        lax.fori_loop(0, 4, flip, 0)
        d_in[...] = jnp.zeros_like(d_in)
        down[...] = jnp.zeros_like(down)
        fetch.wait()

    wo_ref = all_down.at[rows_at(step, CHUNK)]
    own_cols, other_cols = rows_at(c, 512), rows_at(1 - c, 512)

    def part(r, carry):
        rows = rows_at(r, 512)
        value, grad = m_ref[rows, :], dy_ref
        gate, up = dot(value, w_ref[0]), dot(value, w_ref[1])
        d_hidden = dot(grad[rows, own_cols], wo_ref[...], NT) + dot(grad[rows, other_cols], wx_ref[...], NT)
        s = 1.0 / (1.0 + jnp.exp(-gate))
        silu = gate * s
        hidden = (silu * up).astype(jnp.bfloat16)
        d_up = (d_hidden * silu).astype(jnp.bfloat16)
        d_gate = (d_hidden * up * (s * (1.0 + gate * (1.0 - s)))).astype(jnp.bfloat16)
        hid[rows, :] = hidden
        dup[rows, :] = d_up
        dgt[rows, :] = d_gate
        d_in[rows, :] += dot(d_gate, w_ref[0], NT) + dot(d_up, w_ref[1], NT)
        down[rows, own_cols] += dot(hidden, wo_ref[...])
        down[rows, other_cols] += dot(hidden, wx_ref[...])
        return carry

    lax.fori_loop(0, 2, part, 0)

    @pl.when(step == pl.num_programs(0) - 1)
    def _():
        give[0] = d_in[rows_at(1 - c, OWN), :].astype(jnp.bfloat16)
        give[1] = down[rows_at(1 - c, OWN), :].astype(jnp.bfloat16)
        net.start(go_d_in, go_down)

    now = rows_at(step, CHUNK)

    def weights(k, carry):
        rows = rows_at(k, 512)
        ggv[0, rows, now] = dot(mt[rows, :], dgt[...]).astype(jnp.bfloat16)
        ggv[1, rows, now] = dot(mt[rows, :], dup[...]).astype(jnp.bfloat16)
        gdv[now, rows] = dot(dyt[rows, :], hid[...]).T.astype(jnp.bfloat16)
        return carry

    lax.fori_loop(0, 2, weights, 0)
    for f in range(HALF_FF // CHUNK):

        @pl.when(step == f)
        def _():
            net.start(*go_wide[f], go_gd[f])
            for copy in outs[f]:
                copy.start()

    @pl.when(step == pl.num_programs(0) - 1)
    def _():
        net.arrived(go_d_in, go_down)
        dg[...] = jnp.zeros_like(dg)

        def finish(k, carry):
            rows = rows_at(k, 64)
            here = pl.ds(pl.multiple_of(c * OWN + k * 64, 64), 64)
            value = resid[rows, :]
            grad = d_in[here, :] + take[0, rows, :].astype(jnp.float32)
            r = lax.rsqrt(jnp.mean(value * value, axis=-1, keepdims=True) + EPS)
            scaled = value * r
            gained = grad * g_mlp[...]
            total = dy_ref[here, :].astype(jnp.float32) + r * (gained - scaled * jnp.mean(scaled * gained, axis=-1, keepdims=True))
            d_resid[rows, :] = total
            db[rows, :] = total.astype(jnp.bfloat16)
            dg[...] += jnp.sum((grad * scaled).reshape(-1, 8, MODEL_DIM), axis=0)
            res[rows, :] = (value + down[here, :] + take[1, rows, :].astype(jnp.float32)).astype(jnp.bfloat16)
            return carry

        lax.fori_loop(0, 8, finish, 0)
        for f in range(HALF_FF // CHUNK):
            net.arrived(*go_wide[f], go_gd[f])
            for copy in outs[f]:
                copy.wait()
        net.sent()


def feed_forward(mlp_in, dy, wgu, wdn, wdx, resid, g_mlp):
    bf16, f32 = jnp.bfloat16, jnp.float32

    def whole(shape):
        return pl.BlockSpec(shape, lambda f: (0,) * len(shape), pipeline_mode=pl.Buffered(1))

    down = pl.BlockSpec((CHUNK, 512), lambda f: (f, 0))
    copies = 24
    rows = (1024, MODEL_DIM)
    own = (OWN, MODEL_DIM)
    return pl.pallas_call(
        forward_kernel,
        grid=(HALF_FF // CHUNK,),
        out_shape=(
            jax.ShapeDtypeStruct((2, MODEL_DIM, HALF_FF), bf16),
            jax.ShapeDtypeStruct((2, HALF_FF, 512), bf16),
            jax.ShapeDtypeStruct((4, 2, 2, 64, EARLY), bf16),
            jax.ShapeDtypeStruct(own, f32),
            jax.ShapeDtypeStruct(own, bf16),
            jax.ShapeDtypeStruct(own, bf16),
            jax.ShapeDtypeStruct((8, MODEL_DIM), f32),
        ),
        in_specs=[whole(rows), whole(rows), pl.BlockSpec((2, MODEL_DIM, CHUNK), lambda f: (0, 0, f))]
        + [pl.BlockSpec(memory_space=pl.ANY), down]
        + [whole(own), whole((1, MODEL_DIM))],
        out_specs=[pl.BlockSpec(memory_space=pl.ANY)] * 3
        + [whole(own), whole(own), whole(own), whole((8, MODEL_DIM))],
        scratch_shapes=[
            pltpu.VMEM(rows, bf16),
            pltpu.VMEM(rows, bf16),
            pltpu.VMEM((1024, CHUNK), bf16),
            pltpu.VMEM((1024, CHUNK), bf16),
            pltpu.VMEM((1024, CHUNK), bf16),
            pltpu.VMEM(rows, f32),
            pltpu.VMEM(rows, f32),
            pltpu.VMEM((2,) + own, bf16),
            pltpu.VMEM((2,) + own, bf16),
            pltpu.VMEM((HALF_FF, 512), bf16),
            pltpu.VMEM((2, MODEL_DIM, HALF_FF), bf16),
            pltpu.VMEM((HALF_FF, MODEL_DIM), bf16),
            pltpu.SemaphoreType.DMA((copies,)),
            pltpu.SemaphoreType.DMA((copies,)),
            pltpu.SemaphoreType.DMA((1,)),
            pltpu.SemaphoreType.DMA((6,)),
        ],
        compiler_params=pltpu.CompilerParams(
            collective_id=6, has_side_effects=True, vmem_limit_bytes=VMEM_LIMIT
        ),
        name="feed_forward",
    )(mlp_in, dy, wgu, wdn, wdx, resid, g_mlp)


KINDS = ME, NEAR, FAR, FAL = range(4)


def chip_slot(yy, xx, pp, ll):
    return (yy * 2 + xx) * 4 + 2 * pp + ll


class Reduction:
    def __init__(self, where):
        y, x, p, l, c = where
        self.z = ((p, l), (p, 1 - l), (1 - p, l), (1 - p, 1 - l))
        self.y, self.x = y, x

    def y_first(self, kind):
        return kind in (ME, FAR)

    def first_peer(self, kind):
        return "y" if self.y_first(kind) else "x"

    def second_peer(self, kind):
        return "x" if self.y_first(kind) else "y"

    def place(self, kind, index, given):
        if self.y_first(kind):
            return (1 - self.y if given else self.y), index
        return index, (1 - self.x if given else self.x)

    def kept(self, kind):
        return self.x if self.y_first(kind) else self.y


def attend_back_kernel(
    flags, q_in, k_in, v_in, o_in, db_in, wo_in, lse_in, qr_in, kr_in, cos_in, sin_in, ggu, gdb, rb_in, res, gq_ref, gk_ref,
    d_out, goq, og_out, od_out, fw_out, fd_out, out, dg_ref,
    q_ref, k_ref, v_ref, o_ref, dall, wo, lse_ref, qr_ref, kr_ref, cos_ref, sin_ref,
    da, delta, dbuf, dq_acc, dk_acc, dv_acc, og, od, rb, rbd, rc, rcd, rz, rzd, go,
    send_sem, recv_sem, load_sem, own_sem, out_sem, back_send, back_recv,
):
    where = place()
    y, x, p, l, c = where
    peer = peers_of(x, y, p, l, c)
    red = Reduction(where)
    net = Plan(send_sem, recv_sem)
    t = 2 * l + c

    def block(index):
        return dall.at[rows_at(index, OWN)]

    mine = owned(p, l, c)
    go_db_l = net.add(peer["l"], [(db_in, block(mine))])
    go_db_c = net.add(peer["c"], [(db_in, block(mine))])
    go_db_r = net.add(peer["c"], in_place(block(owned(p, 1 - l, c))))
    early, late = pl.ds(0, EARLY), pl.ds(EARLY, HALF_FF - EARLY)
    first_of, second_a, second_b = {}, {}, {}
    for n, kind in enumerate(KINDS):
        pairs = []
        for k in range(2):
            yy, xx = red.place(kind, k, True)
            slot = chip_slot(yy, xx, *red.z[kind])
            pairs.append((ggu.at[:, rows_at(slot, 64), late], rb.at[n, k, :, :, late]))
            pairs.append((gdb.at[yy, rows_at(xx * 4 + 2 * red.z[kind][0] + red.z[kind][1], 192)], rbd.at[n, k]))
        first_of[kind] = net.add(peer[red.first_peer(kind)], pairs)
        if n >= 2:
            away, link = 1 - red.kept(kind), peer[red.second_peer(kind)]
            second_a[kind] = net.add(link, [(og.at[n, away, :, :, early], rc.at[n - 2, :, :, early])])
            second_b[kind] = net.add(link, [(og.at[n, away, :, :, late], rc.at[n - 2, :, :, late]), (od.at[n, away], rcd.at[n - 2])])
    u_far, u_fal = red.kept(FAR), red.kept(FAL)
    go_fal_a = net.add(peer["l"], [(og.at[FAL, u_fal, :, :, early], rz.at[:, :, early])])
    go_fal_b = net.add(peer["l"], [(og.at[FAL, u_fal, :, :, late], rz.at[:, :, late]), (od.at[FAL, u_fal], rzd)])
    go_far_a = net.add(peer["p"], [(og.at[FAR, u_far, :, :, early], fw_out.at[:, :, early])])
    go_far_b = net.add(peer["p"], [(og.at[FAR, u_far, :, :, late], fw_out.at[:, :, late]), (od.at[FAR, u_far], fd_out)])
    home = Return(where, res, out, back_send, back_recv)

    def columns(q):
        return [(go.at[:, rows_at(q, 256)], goq.at[rows_at(t, 512)])]

    go_go_l = net.add(peer["l"], columns(2 * (1 - l) + c))
    go_go_d = net.add(peer["d"], columns(2 * (1 - l) + 1 - c))
    go_go_c = net.add(peer["c"], columns(2 * l + 1 - c))
    own_go = pltpu.make_async_copy(*columns(t)[0], out_sem.at[1])
    loads = [
        pltpu.make_async_copy(src, dst, load_sem.at[k])
        for k, (src, dst) in enumerate(
            [
                (db_in, block(mine)), (wo_in, wo), (o_in, o_ref), (q_in, q_ref), (k_in, k_ref), (v_in, v_ref), (lse_in, lse_ref),
                (cos_in, cos_ref), (sin_in, sin_ref), (qr_in, qr_ref), (kr_in, kr_ref),
            ]
        )
    ]
    own = [pltpu.make_async_copy(rb_in, rb.at[:, :, :, :, early], own_sem.at[0])]
    for n, kind in enumerate(KINDS):
        for k in range(2):
            yy, xx = red.place(kind, k, False)
            slot = chip_slot(yy, xx, *red.z[kind])
            own.append(pltpu.make_async_copy(ggu.at[:, rows_at(slot, 64)], og.at[n, k], own_sem.at[len(own)]))
            rows = rows_at(xx * 4 + 2 * red.z[kind][0] + red.z[kind][1], 192)
            own.append(pltpu.make_async_copy(gdb.at[yy, rows], od.at[n, k], own_sem.at[len(own)]))

    def plus(target, other):
        target[...] = (target[...].astype(jnp.float32) + other[...].astype(jnp.float32)).astype(jnp.bfloat16)

    def wide_sum(n, cols):
        def wide(r, carry):
            k, m, rows = r // 4, (r // 2) % 2, rows_at(r % 2, 32)
            plus(og.at[n, k, m, rows, cols], rb.at[n, k, m, rows, cols])
            return carry

        lax.fori_loop(0, 8, wide, 0)

    def deep_sum(n):
        def deep(r, carry):
            k, rows = r // 3, rows_at(r % 3, 64)
            plus(od.at[n, k, rows, :], rbd.at[n, k, rows, :])
            return carry

        lax.fori_loop(0, 6, deep, 0)

    def branch(index):
        rows = rows_at(index, OWN)
        value = dot(dall[rows, :], wo[...], NT).astype(jnp.bfloat16)
        da[rows, :] = value
        for h in range(QH):
            cols = slice(h * HEAD_DIM, (h + 1) * HEAD_DIM)
            prod = value[:, cols].astype(jnp.float32) * o_ref[rows, cols].astype(jnp.float32)
            delta[h, :, rows] = jnp.broadcast_to(jnp.sum(prod.T, axis=0, keepdims=True), (8, BLK))

    def unrope(grad, u, gain, rows):
        grad = grad * SCALE
        e = grad * cos_ref[rows, :] + turn(grad * sin_ref[rows, :])
        r = lax.rsqrt(jnp.mean(u * u, axis=-1, keepdims=True) + EPS)
        ur = u * r
        ge = e * gain
        d = r * (ge - ur * jnp.mean(ur * ge, axis=-1, keepdims=True))
        return d.astype(jnp.bfloat16), jnp.sum((e * ur).reshape(-1, 8, HEAD_DIM), axis=0)

    step = pl.program_id(0)
    b, g = step // KH, step % KH
    i = owned(p, (l + b // 2) % 2, b % 2)

    @pl.when(step == 0)
    def _():
        for copy in loads[:3]:
            copy.start()
        for copy in own:
            copy.start()
        for copy in loads[3:]:
            copy.start()
        greet(line_peers(p, l, c) + [peer["x"], peer["y"]])
        net.start(go_db_l, go_db_c, first_of[FAR], first_of[FAL])
        dk_acc[...] = jnp.zeros_like(dk_acc)
        dv_acc[...] = jnp.zeros_like(dv_acc)
        dg_ref[...] = jnp.zeros_like(dg_ref)
        for copy in own:
            copy.wait()
        for kind in (FAR, FAL):
            wide_sum(kind, early)
            net.start(second_a[kind])
        for copy in loads[:3]:
            copy.wait()
        branch(mine)
        net.arrived(go_db_c)
        branch(owned(p, l, 1 - c))
        for copy in loads[3:]:
            copy.wait()

    @pl.when(step == 2)
    def _():
        net.arrived(second_a[FAL])
        plus(og.at[FAL, u_fal, :, :, early], rc.at[1, :, :, early])
        net.start(go_fal_a)
        net.arrived(second_a[FAR])
        plus(og.at[FAR, u_far, :, :, early], rc.at[0, :, :, early])

    @pl.when(step == 0)
    def _():
        home.start()

    @pl.when(step == 3)
    def _():
        for kind in (FAR, FAL):
            net.arrived(first_of[kind])
            wide_sum(kind, late)
            deep_sum(kind)
            net.start(second_b[kind])
        net.start(first_of[ME], first_of[NEAR])

    @pl.when(step == 2 * KH)
    def _():
        net.arrived(go_db_l)
        net.start(go_db_r)
        branch(owned(p, 1 - l, c))
        net.arrived(go_db_r)
        branch(owned(p, 1 - l, 1 - c))

    @pl.when(step == 4)
    def _():
        net.arrived(go_fal_a)
        plus(og.at[FAR, u_far, :, :, early], rz.at[:, :, early])
        net.start(go_far_a)

    @pl.when(step == 5)
    def _():
        net.arrived(second_b[FAL])
        plus(og.at[FAL, u_fal, :, :, late], rc.at[1, :, :, late])
        plus(od.at[FAL, u_fal], rcd.at[1])
        net.start(go_fal_b)
        net.arrived(second_b[FAR])
        plus(og.at[FAR, u_far, :, :, late], rc.at[0, :, :, late])
        plus(od.at[FAR, u_far], rcd.at[0])

    @pl.when(step == 7)
    def _():
        net.arrived(go_fal_b)
        plus(og.at[FAR, u_far, :, :, late], rz.at[:, :, late])
        plus(od.at[FAR, u_far], rzd)
        net.start(go_far_b)

    @pl.when(step == 5)
    def _():
        def grad_out(k, carry):
            cols = rows_at(k, 256)
            go[cols, :] = dot(o_ref[:, cols], dall[...], TN).astype(jnp.bfloat16)
            return carry

        lax.fori_loop(0, 2, grad_out, 0)
        net.start(go_go_l, go_go_d, go_go_c)
        own_go.start()

    dq_acc[...] = jnp.zeros_like(dq_acc)
    rows = rows_at(i, BLK)
    heads = [2 * g + n for n in range(2)]
    spans = [rows_at(h, HEAD_DIM) for h in heads]
    queries = [q_ref[h, rows, :] for h in heads]
    grads = [da[rows, span] for span in spans]

    def tile(j, mask=None):
        keys = rows_at(j, BLK)
        k, v = k_ref[g, keys, :], v_ref[g, keys, :]
        turned = k.T
        dv, dk = None, None
        for n, h in enumerate(heads):
            probs = jnp.exp2(dot(k, queries[n], NT) * (SCALE * LOG2E) - lse_ref[h, 0:1, rows])
            if mask is not None:
                probs = jnp.where(mask, probs, 0.0)
            d_scores = (probs * (dot(v, grads[n], NT) - delta[h, 0:1, rows])).astype(jnp.bfloat16)
            dv_more, dk_more = dot(probs.astype(jnp.bfloat16), grads[n]), dot(d_scores, queries[n])
            dv, dk = (dv_more, dk_more) if dv is None else (dv + dv_more, dk + dk_more)
            dq_acc[n] += dot(turned, d_scores)
        dv_acc[g, keys, :] += dv
        dk_acc[g, keys, :] += dk

    def loop(j, carry):
        tile(j)
        return carry

    tile(i, block_mask(0, flags, i))
    lax.fori_loop(0, i, loop, 0)
    for n, h in enumerate(heads):
        low, total = unrope(dq_acc[n].T, qr_ref[h, rows, :], gq_ref[...], rows)
        dbuf[rows, spans[n]] = low
        dg_ref[0] += total

    @pl.when(step == 4 * KH - 1)
    def _():
        for gg_at in range(KH):

            def finish(r, carry):
                rows = rows_at(r, 256)
                low, total = unrope(dk_acc[gg_at, rows, :], kr_ref[gg_at, rows, :], gk_ref[...], rows)
                dbuf[rows, pl.ds((QH + gg_at) * HEAD_DIM, HEAD_DIM)] = low
                dbuf[rows, pl.ds((QH + KH + gg_at) * HEAD_DIM, HEAD_DIM)] = dv_acc[gg_at, rows, :].astype(jnp.bfloat16)
                dg_ref[1] += total
                return carry

            lax.fori_loop(0, 8, finish, 0)
        outs = [pltpu.make_async_copy(dbuf, d_out, out_sem.at[0])]
        outs[0].start()
        for kind in (ME, NEAR):
            wide_sum(kind, early)
            net.arrived(first_of[kind])
            wide_sum(kind, late)
            deep_sum(kind)
        outs += [
            pltpu.make_async_copy(og.at[pl.ds(0, 2)], og_out, out_sem.at[2]),
            pltpu.make_async_copy(od.at[pl.ds(0, 2)], od_out, out_sem.at[3]),
        ]
        for copy in outs[1:]:
            copy.start()
        net.arrived(go_go_l, go_go_d, go_go_c, go_far_a, go_far_b)
        own_go.wait()
        net.sent()
        home.wait()
        for copy in outs:
            copy.wait()


def attend_back(flags, q, k, v, o, db, wo, lse, qr, kr, cosine, sine, ggu, gdb, rb, res, gq, gk):
    bf16, f32 = jnp.bfloat16, jnp.float32
    any_spec = pl.BlockSpec(memory_space=pl.ANY)
    gain = pl.BlockSpec((1, HEAD_DIM), lambda s, f: (0, 0))
    copies = 40

    def vm(a):
        return pltpu.VMEM(a.shape, a.dtype)

    return pl.pallas_call(
        attend_back_kernel,
        out_shape=(
            jax.ShapeDtypeStruct((SEQ_ROWS, 1024), bf16),
            jax.ShapeDtypeStruct((2048, 256), bf16),
            jax.ShapeDtypeStruct((2, 2, 2, 64, HALF_FF), bf16),
            jax.ShapeDtypeStruct((2, 2, 192, 512), bf16),
            jax.ShapeDtypeStruct((2, 64, HALF_FF), bf16),
            jax.ShapeDtypeStruct((192, 512), bf16),
            jax.ShapeDtypeStruct((2, ROWS, MODEL_DIM), bf16),
            jax.ShapeDtypeStruct((2, 8, HEAD_DIM), f32),
        ),
        grid_spec=pltpu.PrefetchScalarGridSpec(
            num_scalar_prefetch=1,
            grid=(4 * KH,),
            in_specs=[any_spec] * 15 + [gain] * 2,
            out_specs=[any_spec] * 7 + [pl.BlockSpec((2, 8, HEAD_DIM), lambda s, f: (0, 0, 0))],
            scratch_shapes=[vm(q), vm(k), vm(v), vm(o), pltpu.VMEM((SEQ_ROWS, MODEL_DIM), bf16), vm(wo), vm(lse), vm(qr), vm(kr)]
            + [vm(cosine), vm(sine)]
            + [
                pltpu.VMEM((SEQ_ROWS, QH * HEAD_DIM), bf16),
                pltpu.VMEM((QH, 8, SEQ_ROWS), f32),
                pltpu.VMEM((SEQ_ROWS, 1024), bf16),
                pltpu.VMEM((2, HEAD_DIM, BLK), f32),
                pltpu.VMEM((KH, SEQ_ROWS, HEAD_DIM), f32),
                pltpu.VMEM((KH, SEQ_ROWS, HEAD_DIM), f32),
                pltpu.VMEM((4, 2, 2, 64, HALF_FF), bf16),
                pltpu.VMEM((4, 2, 192, 512), bf16),
                pltpu.VMEM((4, 2, 2, 64, HALF_FF), bf16),
                pltpu.VMEM((4, 2, 192, 512), bf16),
                pltpu.VMEM((2, 2, 64, HALF_FF), bf16),
                pltpu.VMEM((2, 192, 512), bf16),
                pltpu.VMEM((2, 64, HALF_FF), bf16),
                pltpu.VMEM((192, 512), bf16),
                pltpu.VMEM((512, MODEL_DIM), bf16),
                pltpu.SemaphoreType.DMA((copies,)),
                pltpu.SemaphoreType.DMA((copies,)),
                pltpu.SemaphoreType.DMA((11,)),
                pltpu.SemaphoreType.DMA((17,)),
                pltpu.SemaphoreType.DMA((4,)),
                pltpu.SemaphoreType.DMA((2,)),
                pltpu.SemaphoreType.DMA((2,)),
            ],
        ),
        compiler_params=pltpu.CompilerParams(
            collective_id=4, has_side_effects=True, vmem_limit_bytes=VMEM_LIMIT
        ),
        cost_estimate=pl.CostEstimate(
            flops=10 * QH * SEQ_ROWS * SEQ_ROWS * HEAD_DIM, bytes_accessed=40 << 20, transcendentals=QH * SEQ_ROWS * SEQ_ROWS
        ),
        name="attend_back",
    )(flags, q, k, v, o, db, wo, lse, qr, kr, cosine, sine, ggu, gdb, rb, res, gq, gk)


def tail_kernel(
    d_in, w_in, n_in, xs, og_in, od_in, fw_in, fd_in, goq_in, dr_ref, ga_ref, dgm_ref, dgh_ref,
    rq, rqo, fw, fd, gout, landed,
    d_ref, w_ref, n_ref, x_ref, goq, send_c, recv_c, send_l, recv_l, keep, gt,
    og, od, rx, rxd, rz, rzd, total_w, total_d,
    pq, work, wgo, ry, ryo, ox, oxo, rs, rso, gs, gr,
    send_sem, recv_sem, load_sem, back_send, back_recv,
):
    where = place()
    y, x, p, l, c = where
    peer = peers_of(x, y, p, l, c)
    red = Reduction(where)
    net = Plan(send_sem, recv_sem)
    second_of = {}
    t = 2 * l + c
    for n, kind in enumerate(KINDS[:2]):
        away = 1 - red.kept(kind)
        second_of[kind] = net.add(peer[red.second_peer(kind)], [(og_in.at[n, away], rx.at[n]), (od_in.at[n, away], rxd.at[n])])
    u_me, u_near = red.kept(ME), red.kept(NEAR)
    go_near = net.add(peer["l"], [(og.at[1], rz.at[1]), (od.at[1], rzd.at[1])])
    go_halves = net.add(peer["c"], [(total_w.at[1 - c], fw.at[c]), (total_d.at[1 - c], fd.at[c])])
    go_give_0 = net.add(peer["c"], [(send_c.at[0], recv_c.at[0])])
    go_give_1 = net.add(peer["c"], [(send_c.at[1], recv_c.at[1])])
    halves = [pl.ds(k * ROWS, ROWS) for k in range(2)]
    go_cross = [net.add(peer["l"], [(send_l.at[half], recv_l.at[half])]) for half in halves]

    def group(yy, xx, pp):
        return (yy * 2 + xx) * 2 + pp

    def moved(sources, groups, targets, at=0):
        return [(src.at[one], dst.at[at + k]) for k, one in enumerate(groups) for src, dst in zip(sources, targets)]

    source, working, small = (pq, goq), (work, wgo), (rs, rso)
    base, across = group(y, x, p), group(y, x, 1 - p)
    give_y = (group(1 - y, 0, p), group(1 - y, 1, p))
    give_x = (group(0, 1 - x, 1 - p), group(1, 1 - x, 1 - p))
    go_own_y = [[net.add(peer["y"], moved((a,), give_y[k : k + 1], (b,), k)) for k in range(2)] for a, b in ((pq, ry), (goq_in, ryo))]
    go_other_x = [[net.add(peer["x"], moved((a,), give_x[k : k + 1], (b,), k)) for k in range(2)] for a, b in ((pq, ox), (goq_in, oxo))]
    go_own_x = [net.add(peer["x"], moved(working[k : k + 1], (group(y, 1 - x, p),), small[k : k + 1], 0)) for k in range(2)]
    go_other_y = [net.add(peer["y"], moved(working[k : k + 1], (group(1 - y, x, 1 - p),), small[k : k + 1], 1)) for k in range(2)]
    go_across = [net.add(peer["p"], moved(working[k : k + 1], (across,), small[k : k + 1], 2)) for k in range(2)]

    def parts(q):
        return [(work.at[base, rows_at(q, 32)], rq.at[t]), (wgo.at[base, rows_at(q, 64)], rqo.at[t])]

    go_last_l = net.add(peer["l"], parts(2 * (1 - l) + c))
    go_last_d = net.add(peer["d"], parts(2 * (1 - l) + 1 - c))
    go_last_c = net.add(peer["c"], parts(2 * l + 1 - c))
    go_gain = [net.add(peer[name], [(gs.at[k], gr.at[k])]) for k, name in enumerate(("c", "x", "y", "p", "l"))]
    home = Return(where, gt, landed, back_send, back_recv)

    def gain_hop(k):
        net.arrived(go_gain[k])
        gs[k + 1] = gs[k] + gr[k]
        if k + 1 < len(AXES):
            net.start(go_gain[k + 1])

    loads = [
        pltpu.make_async_copy(src, dst, load_sem.at[k])
        for k, (src, dst) in enumerate(
            [
                (d_in, d_ref), (w_in, w_ref), (n_in, n_ref), (goq_in, goq), (xs.at[rows_at(owned(p, l, c), OWN)], x_ref),
                (og_in.at[0, u_me], og.at[0]), (og_in.at[1, u_near], og.at[1]),
                (od_in.at[0, u_me], od.at[0]), (od_in.at[1, u_near], od.at[1]),
                (fw_in, rz.at[0]), (fd_in, rzd.at[0]),
            ]
        )
    ]
    for copy in loads:
        copy.start()
    greet(line_peers(p, l, c) + [peer["x"], peer["y"]])
    net.start(second_of[NEAR], second_of[ME], *go_own_y[1], *go_other_x[1])

    def project(ll, cc, write):
        part = d_ref[rows_at(owned(p, ll, cc), OWN), :]

        def chunk(k, carry):
            cols = rows_at(k, 256)
            write(cols, dot(part, w_ref[cols, :], NT))
            return carry

        lax.fori_loop(0, 4, chunk, 0)

    def give(k):
        def write(cols, value):
            send_c[k, :, cols] = value.astype(jnp.bfloat16)

        return write

    def hold(k):
        def write(cols, value):
            keep[k, :, cols] = value

        return write

    def add(k, at, left, right, place_at):
        total = left[at].astype(jnp.float32) + right[place_at].astype(jnp.float32)
        working[k][at] = total.astype(jnp.bfloat16)

    def first_sums(k):
        net.arrived(*go_other_x[k])
        for yy in (0, 1):
            add(k, group(yy, x, 1 - p), source[k], (ox, oxo)[k], yy)
        net.start(go_other_y[k])
        net.arrived(*go_own_y[k])
        for xx in (0, 1):
            add(k, group(y, xx, p), source[k], (ry, ryo)[k], xx)
        net.start(go_own_x[k])

    def second_sums(k):
        net.arrived(go_other_y[k])
        add(k, across, working[k], small[k], 1)
        net.start(go_across[k])
        net.arrived(go_own_x[k])
        add(k, base, working[k], small[k], 0)

    loads[0].wait()
    loads[1].wait()
    project(1 - l, 1 - c, give(0))
    net.start(go_give_0)
    project(1 - l, c, hold(0))
    net.arrived(go_give_0)
    send_l[...] = (keep[0] + recv_c[0].astype(jnp.float32)).astype(jnp.bfloat16)
    net.start(*go_cross)
    project(l, 1 - c, give(1))
    net.start(go_give_1)
    project(l, c, hold(1))
    for copy in loads[2:]:
        copy.wait()

    def grad_qkv(yy, xx):
        k = yy * 2 + xx
        value = dot(n_ref[:, rows_at(k, 256)], d_ref[...], TN).astype(jnp.bfloat16)
        pq[2 * k] = value[:128]
        pq[2 * k + 1] = value[128:]

    def start_if(index, groups):
        for k in range(2):

            @pl.when(index == k)
            def _():
                net.start(groups[k])

    def one_chunk(k, carry):
        yy, xx = jnp.where(k % 2 == 0, 1 - y, y), jnp.where(k < 2, 1 - x, x)
        grad_qkv(yy, xx)

        @pl.when(k < 2)
        def _():
            start_if(yy, go_other_x[0])

        @pl.when(k % 2 == 0)
        def _():
            start_if(xx, go_own_y[0])

        return carry

    gs[0] = jnp.zeros_like(gs[0])

    def rows_back(k, total):
        rows = rows_at(k, 64)
        value = x_ref[rows, :].astype(jnp.float32)
        grad = keep[1, rows, :] + recv_c[1, rows, :].astype(jnp.float32) + recv_l[rows, :].astype(jnp.float32)
        r = lax.rsqrt(jnp.mean(value * value, axis=-1, keepdims=True) + EPS)
        scaled = value * r
        gained = grad * ga_ref[...]
        back = r * (gained - scaled * jnp.mean(scaled * gained, axis=-1, keepdims=True))
        gt[rows, :] = (dr_ref[rows, :] + back).astype(jnp.bfloat16)
        return total + jnp.sum(grad * scaled, axis=0, keepdims=True)

    lax.fori_loop(0, 2, one_chunk, 0)
    net.arrived(go_give_1, go_cross[0])
    d_attn = lax.fori_loop(0, 4, rows_back, jnp.zeros((1, MODEL_DIM), jnp.float32))
    home.start_one(0)
    lax.fori_loop(2, 4, one_chunk, 0)
    first_sums(1)
    net.arrived(go_cross[1])
    d_attn = lax.fori_loop(4, 8, rows_back, d_attn)
    home.start_one(1)
    net.arrived(second_of[NEAR])
    og[1] = (og[1].astype(jnp.float32) + rx[1].astype(jnp.float32)).astype(jnp.bfloat16)
    od[1] = (od[1].astype(jnp.float32) + rxd[1].astype(jnp.float32)).astype(jnp.bfloat16)
    net.start(go_near)
    first_sums(0)
    second_sums(1)
    d_mlp = jnp.sum(dgm_ref[...], axis=0, keepdims=True)
    for k in range(8):
        lanes = slice(k * 128, (k + 1) * 128)
        gs[0, k : k + 1, :] = d_attn[:, lanes]
        gs[0, 8 + k : 9 + k, :] = d_mlp[:, lanes]
    for k in range(2):
        gs[0, 16 + k : 17 + k, :] = jnp.sum(dgh_ref[k], axis=0, keepdims=True)
    net.start(go_gain[0])
    second_sums(0)
    gain_hop(0)
    net.arrived(second_of[ME])
    gain_hop(1)
    net.arrived(go_near)
    for cc in range(2):
        rows = pl.ds(32 * cc, 32)
        total_w[cc] = (
            og[0, :, rows, :].astype(jnp.float32) + rx[0, :, rows, :].astype(jnp.float32)
            + rz[0, :, rows, :].astype(jnp.float32) + rz[1, :, rows, :].astype(jnp.float32)
        )
        rows = pl.ds(96 * cc, 96)
        total_d[cc] = (
            od[0, rows, :].astype(jnp.float32) + rxd[0, rows, :].astype(jnp.float32)
            + rzd[0, rows, :].astype(jnp.float32) + rzd[1, rows, :].astype(jnp.float32)
        )
    net.start(go_halves)
    fw[c] = total_w[c]
    fd[c] = total_d[c]
    gain_hop(2)
    net.arrived(go_halves)
    for k in (1, 0):
        net.arrived(go_across[k])
        add(k, base, working[k], small[k], 2)
    net.start(go_last_l, go_last_d, go_last_c)
    rq[t] = work[base, rows_at(t, 32), :]
    rqo[t] = wgo[base, rows_at(t, 64), :]
    gain_hop(3)
    home.wait()
    gain_hop(4)
    gout[...] = gs[len(AXES)]
    net.arrived(go_last_l, go_last_d, go_last_c)
    net.sent()


def finish_kernel(
    rq, rqo, fw, fd, landed, result,
    output, tokens, out_query, out_key, out_value, out_out, out_gate, out_up, out_down,
):
    output[...] = result[...]
    tokens[...] = landed[...].astype(jnp.float32)
    for half in range(2):
        cols = slice(half * HALF_FF, (half + 1) * HALF_FF)
        out_gate[:, cols] = fw[half, 0]
        out_up[:, cols] = fw[half, 1]
        out_down[:, half * 512 : (half + 1) * 512] = fd[half]
    for q in range(4):
        value = rq[q].astype(jnp.float32)
        out_query[:, 512 * q : 512 * (q + 1)] = value[:, :512]
        out_key[:, 256 * q : 256 * (q + 1)] = value[:, 512:768]
        out_value[:, 256 * q : 256 * (q + 1)] = value[:, 768:]
        out_out[:, 256 * q : 256 * (q + 1)] = rqo[q].astype(jnp.float32)


def finish(rq, rqo, fw, fd, landed, result):
    f32 = jnp.float32
    vmem = pl.BlockSpec(memory_space=pltpu.VMEM)
    return pl.pallas_call(
        finish_kernel,
        out_shape=(
            jax.ShapeDtypeStruct((2, ROWS, MODEL_DIM), jnp.bfloat16),
            jax.ShapeDtypeStruct((2, ROWS, MODEL_DIM), f32),
            jax.ShapeDtypeStruct((32, 2048), f32),
            jax.ShapeDtypeStruct((32, 1024), f32),
            jax.ShapeDtypeStruct((32, 1024), f32),
            jax.ShapeDtypeStruct((64, 1024), f32),
            jax.ShapeDtypeStruct((32, FF), f32),
            jax.ShapeDtypeStruct((32, FF), f32),
            jax.ShapeDtypeStruct((96, 1024), f32),
        ),
        in_specs=[vmem] * 6,
        out_specs=[vmem] * 9,
        compiler_params=pltpu.CompilerParams(vmem_limit_bytes=VMEM_LIMIT),
        name="finish",
    )(rq, rqo, fw, fd, landed, result)


def tail(d, w, normed, xs, og, od, fw, fd, goq, d_resid, g_attn, d_g_mlp, d_g_heads):
    bf16, f32 = jnp.bfloat16, jnp.float32
    any_spec = pl.BlockSpec(memory_space=pl.ANY)
    vmem = pl.BlockSpec(memory_space=pltpu.VMEM)
    copies = 48
    wide, deep = (2, 64, HALF_FF), (192, 512)
    own = (OWN, MODEL_DIM)
    big, tall = (128, 1024), (256, 256)

    def vm(a):
        return pltpu.VMEM(a.shape, a.dtype)

    def low(*shape):
        return pltpu.VMEM(shape, bf16)

    goq = goq.reshape(8, 256, 256)
    return pl.pallas_call(
        tail_kernel,
        out_shape=(
            jax.ShapeDtypeStruct((4, 32, 1024), bf16),
            jax.ShapeDtypeStruct((4, 64, 256), bf16),
            jax.ShapeDtypeStruct((2, 2, 32, HALF_FF), f32),
            jax.ShapeDtypeStruct((2, 96, 512), f32),
            jax.ShapeDtypeStruct((24, 128), f32),
            jax.ShapeDtypeStruct((2, ROWS, MODEL_DIM), bf16),
        ),
        in_specs=[any_spec] * 9 + [vmem] * 4,
        out_specs=[vmem] * 6,
        scratch_shapes=[
            vm(d), vm(w), vm(normed), low(*own), vm(goq),
            low(2, *own), low(2, *own), low(*own), low(*own),
            pltpu.VMEM((2,) + own, f32),
            low(*own),
            low(2, *wide), low(2, *deep),
            low(2, *wide), low(2, *deep), low(2, *wide), low(2, *deep),
            pltpu.VMEM((2, 2, 32, HALF_FF), f32), pltpu.VMEM((2, 96, 512), f32),
            low(8, *big), low(8, *big), low(8, *tall),
            low(2, *big), low(2, *tall), low(2, *big), low(2, *tall), low(3, *big), low(3, *tall),
            pltpu.VMEM((6, 24, 128), f32), pltpu.VMEM((5, 24, 128), f32),
            pltpu.SemaphoreType.DMA((copies,)),
            pltpu.SemaphoreType.DMA((copies,)),
            pltpu.SemaphoreType.DMA((11,)),
            pltpu.SemaphoreType.DMA((2,)),
            pltpu.SemaphoreType.DMA((2,)),
        ],
        compiler_params=pltpu.CompilerParams(
            collective_id=5, has_side_effects=True, vmem_limit_bytes=VMEM_LIMIT
        ),
        name="tail_reduce",
    )(d, w, normed, xs, og, od, fw, fd, goq, d_resid, g_attn, d_g_mlp, d_g_heads)


def pick(value, index):
    return lax.dynamic_index_in_dim(value, index, 0, keepdims=False)


def fast_device(tokens, cotangent, starts, w_query, key_matrix, value_matrix, w_out, w_gate, w_up, w_down, gains):
    p = lax.axis_index("p")
    gn = jnp.pad(gains.astype(jnp.float32), (0, 952)).reshape(8, 128)
    half_steps = jnp.arange(HEAD_DIM // 2, dtype=jnp.float32)
    inverse = THETA ** (-2.0 * half_steps / HEAD_DIM)
    inverse = jnp.broadcast_to(jnp.concatenate([inverse, inverse])[None], (8, HEAD_DIM))
    own_starts = pick(starts, p)
    block_at = jnp.arange(SEQ_ROWS // PIECE, dtype=jnp.int32) * PIECE
    flags = jnp.any(own_starts[None, :] == block_at[:, None], axis=1).astype(jnp.int32)
    xs, w_qkv, woq, gf, wgu, wdn, cosine, sine = front(
        tokens, w_query, key_matrix, value_matrix, w_out, gn, w_gate, w_up, w_down, inverse
    )
    xs = xs.reshape(SEQ_ROWS, MODEL_DIM)
    gain_all = gf.reshape(32, 1024)[:, :72].reshape(2304)
    g_attn = gain_all[None, :1024]
    g_mlp = gain_all[None, 1024:2048]
    g_q = gain_all[None, 2048:2176]
    g_k = gain_all[None, 2176:]
    normed, q, k, v, q_raw, k_raw, attn, lse, wo, wgu, wdn = attend(
        flags, xs, w_qkv, g_attn, g_q, g_k, cosine, sine, woq, wgu, wdn
    )
    resid, mlp_in, wgu, wdn, wdx, dy = finish_resid(attn, wo, g_mlp, xs, cotangent, wgu, wdn)
    ggu, gdb, rb, d_resid, d_branch, result, d_g_mlp = feed_forward(
        mlp_in.reshape(1024, MODEL_DIM), dy.reshape(1024, MODEL_DIM), wgu, wdn, wdx, resid, g_mlp
    )
    d_qkv, goq, og, od, fw, fd, output, d_g_heads = attend_back(
        flags, q, k, v, attn, d_branch, wo, lse, q_raw, k_raw, cosine, sine, ggu, gdb, rb, result, g_q, g_k
    )
    rq, rqo, wide, deep, gains_sum, landed = tail(
        d_qkv, w_qkv, normed, xs, og, od, fw, fd, goq, d_resid, g_attn, d_g_mlp, d_g_heads
    )
    device = lax.axis_index(AXES)
    out_gains = lax.dynamic_slice(gains_sum.reshape(3072), (device * 72,), (72,))
    return (*finish(rq, rqo, wide, deep, landed, output), out_gains)


def fast_solution(mesh):
    wide = Mesh(mesh.devices.reshape(2, 2, 2, 2, 2), AXES)
    rows = ("y", "x")
    places = ("p", "l", "c")
    weight = P(AXES, None)
    return jax.shard_map(
        fast_device,
        mesh=wide,
        in_specs=(P(rows, places, None), P(rows, places, None), P(rows, None)) + (weight,) * 7 + (P(AXES),),
        out_specs=(P(rows, places, None), P(rows, places, None)) + (weight,) * 7 + (P(AXES),),
        check_vma=False,
    )


def solution(mesh):
    if dict(mesh.shape) == {"dp": 4, "ctx": 8}:
        return fast_solution(mesh)
    return generic_solution(mesh)
```

```python
import functools
import math

import jax
import jax.numpy as jnp
from jax import lax
from jax.experimental import pallas as pl
from jax.experimental.pallas import tpu as pltpu
from jax.sharding import Mesh
from jax.sharding import PartitionSpec as P

MODEL_DIM = 1024
QUERY_HEADS = 16
KEY_VALUE_HEADS = 8
HEAD_DIM = 128
SEQUENCE_TOKENS = 2048
PIECE = 256
NPIECE = 4


EPS = 1e-06
THETA = 1000000.0
NEG = -1e30


def rms_norm(incoming_values, gain_vector):
    return (
        incoming_values
        * lax.rsqrt(jnp.mean(incoming_values * incoming_values, axis=-1, keepdims=True) + EPS)
        * gain_vector
    )


def rope_tables(positions):
    half_steps = jnp.arange(HEAD_DIM // 2, dtype=jnp.float32)
    inverse = THETA ** (-2.0 * half_steps / HEAD_DIM)
    angles = positions.astype(jnp.float32)[:, None] * inverse[None, :]
    angles = jnp.concatenate([angles, angles], axis=-1)
    return (jnp.cos(angles), jnp.sin(angles))


def rotate(incoming_values, cosine_table, sine_table):
    half_dim = HEAD_DIM // 2
    turned = jnp.concatenate(
        [-incoming_values[..., half_dim:], incoming_values[..., :half_dim]], axis=-1
    )
    return incoming_values * cosine_table[:, None, :] + turned * sine_table[:, None, :]


def per_head_route(unrotated_projection, gain_vector, cosine_table, sine_table, head_count):
    shaped = unrotated_projection.reshape(unrotated_projection.shape[:-1] + (head_count, HEAD_DIM))
    return rotate(rms_norm(shaped, gain_vector), cosine_table, sine_table).reshape(
        unrotated_projection.shape
    )


def piece_ids(positions, piece_starts):
    inside = (positions[:, None] >= piece_starts[None, :]) & (
        positions[:, None] < piece_starts[None, :] + PIECE
    )
    number = jnp.arange(1, NPIECE + 1, dtype=jnp.int32)
    return jnp.sum(jnp.where(inside, number[None, :], 0), axis=1) - 1


def visible(query_pos, query_id, key_pos, key_id):
    causal = key_pos[None, :] <= query_pos[:, None]
    same_piece = (query_id[:, None] == key_id[None, :]) & (query_id[:, None] >= 0)
    return causal | same_piece


def swiglu(gate_proj, up_proj):
    return jax.nn.silu(gate_proj) * up_proj


def block_extent(kv_count, per_head):
    target = max(1, 512 // per_head)
    chosen = 1
    for candidate in range(1, kv_count + 1):
        if kv_count % candidate == 0 and candidate <= target:
            chosen = candidate
    return chosen


def attend_forward(incoming_query, incoming_keys, incoming_values, allowed, head_group_block):
    sequence_rows = incoming_query.shape[0]
    query_group_factor = QUERY_HEADS // KEY_VALUE_HEADS
    scaling = 1.0 / math.sqrt(HEAD_DIM)
    query_per_head = incoming_query.reshape(
        sequence_rows, KEY_VALUE_HEADS, query_group_factor, HEAD_DIM
    )
    key_per_head = incoming_keys.reshape(incoming_keys.shape[0], KEY_VALUE_HEADS, HEAD_DIM)
    value_per_head = incoming_values.reshape(incoming_values.shape[0], KEY_VALUE_HEADS, HEAD_DIM)
    mixed_parts = []
    total_parts = []
    for head_offset in range(0, KEY_VALUE_HEADS, head_group_block):
        q_part = query_per_head[:, head_offset : head_offset + head_group_block]
        k_part = key_per_head[:, head_offset : head_offset + head_group_block]
        v_part = value_per_head[:, head_offset : head_offset + head_group_block]
        scores = (
            jnp.einsum("tagd,kad->agtk", q_part, k_part, preferred_element_type=jnp.float32)
            * scaling
        )
        scores = jnp.where(allowed[None, None], scores, NEG)
        row_max = jnp.max(scores, axis=-1, keepdims=True)
        exp_scores = jnp.exp(scores - row_max)
        summed = jnp.sum(exp_scores, axis=-1, keepdims=True)
        prob_low = (exp_scores / summed).astype(jnp.bfloat16)
        mixed_parts.append(
            jnp.einsum("agtk,kad->tagd", prob_low, v_part, preferred_element_type=jnp.float32)
        )
        total_parts.append(row_max + jnp.log(summed))
    mixed_out = jnp.concatenate(mixed_parts, axis=1).reshape(sequence_rows, QUERY_HEADS * HEAD_DIM)
    return (mixed_out, jnp.concatenate(total_parts, axis=0))


def attend_backward(
    incoming_query,
    incoming_keys,
    incoming_values,
    allowed,
    log_total,
    mixed_gradient,
    head_group_block,
):
    sequence_rows = incoming_query.shape[0]
    key_row_matrix = incoming_keys.shape[0]
    query_group_factor = QUERY_HEADS // KEY_VALUE_HEADS
    scaling = 1.0 / math.sqrt(HEAD_DIM)
    query_per_head = incoming_query.reshape(
        sequence_rows, KEY_VALUE_HEADS, query_group_factor, HEAD_DIM
    )
    gradient_per_head = mixed_gradient.reshape(
        sequence_rows, KEY_VALUE_HEADS, query_group_factor, HEAD_DIM
    )
    key_per_head = incoming_keys.reshape(key_row_matrix, KEY_VALUE_HEADS, HEAD_DIM)
    value_per_head = incoming_values.reshape(key_row_matrix, KEY_VALUE_HEADS, HEAD_DIM)
    dq_parts = []
    key_gradient_pieces = []
    value_gradient_pieces = []
    for head_offset in range(0, KEY_VALUE_HEADS, head_group_block):
        q_part = query_per_head[:, head_offset : head_offset + head_group_block]
        g_part = gradient_per_head[:, head_offset : head_offset + head_group_block]
        k_part = key_per_head[:, head_offset : head_offset + head_group_block]
        v_part = value_per_head[:, head_offset : head_offset + head_group_block]
        scores = (
            jnp.einsum("tagd,kad->agtk", q_part, k_part, preferred_element_type=jnp.float32)
            * scaling
        )
        scores = jnp.where(allowed[None, None], scores, NEG)
        prob_all = jnp.exp(scores - log_total[head_offset : head_offset + head_group_block])
        prob_low = prob_all.astype(jnp.bfloat16)
        d_probs = jnp.einsum("tagd,kad->agtk", g_part, v_part, preferred_element_type=jnp.float32)
        row_dot = jnp.sum(prob_all * d_probs, axis=-1, keepdims=True)
        d_scores = (prob_all * (d_probs - row_dot)).astype(jnp.bfloat16)
        dq_parts.append(
            jnp.einsum("agtk,kad->tagd", d_scores, k_part, preferred_element_type=jnp.float32)
            * scaling
        )
        key_gradient_pieces.append(
            jnp.einsum("agtk,tagd->kad", d_scores, q_part, preferred_element_type=jnp.float32)
            * scaling
        )
        value_gradient_pieces.append(
            jnp.einsum("agtk,tagd->kad", prob_low, g_part, preferred_element_type=jnp.float32)
        )
    d_query = jnp.concatenate(dq_parts, axis=1).reshape(sequence_rows, QUERY_HEADS * HEAD_DIM)
    key_gradient = jnp.concatenate(key_gradient_pieces, axis=1).reshape(
        key_row_matrix, KEY_VALUE_HEADS * HEAD_DIM
    )
    value_gradient = jnp.concatenate(value_gradient_pieces, axis=1).reshape(
        key_row_matrix, KEY_VALUE_HEADS * HEAD_DIM
    )
    return (d_query, key_gradient, value_gradient)


def generic_device(
    tokens, cotangent, starts, w_query, key_matrix, value_matrix, w_out, w_gate, w_up, w_down, gains
):
    sequence_count, sequence_rows, model_width = tokens.shape
    number_of_rows = sequence_count * sequence_rows
    head_group_block = block_extent(KEY_VALUE_HEADS, QUERY_HEADS // KEY_VALUE_HEADS * sequence_rows)
    attn_set = (
        lax.all_gather(w_query, ("dp", "ctx"), axis=0, tiled=True),
        lax.all_gather(key_matrix, ("dp", "ctx"), axis=0, tiled=True),
        lax.all_gather(value_matrix, ("dp", "ctx"), axis=0, tiled=True),
        lax.all_gather(w_out, ("dp", "ctx"), axis=0, tiled=True),
        lax.all_gather(gains, ("dp", "ctx"), axis=0, tiled=True),
    )
    mlp_set = (
        lax.all_gather(w_gate, ("dp", "ctx"), axis=0, tiled=True),
        lax.all_gather(w_up, ("dp", "ctx"), axis=0, tiled=True),
        lax.all_gather(w_down, ("dp", "ctx"), axis=0, tiled=True),
    )
    gain_all = attn_set[4].astype(jnp.float32)
    g_attn = gain_all[:MODEL_DIM]
    g_mlp = gain_all[MODEL_DIM : 2 * MODEL_DIM]
    g_query = gain_all[2 * MODEL_DIM : 2 * MODEL_DIM + HEAD_DIM]
    key_grad_total = gain_all[2 * MODEL_DIM + HEAD_DIM :]
    positions = lax.axis_index("ctx") * sequence_rows + jnp.arange(sequence_rows, dtype=jnp.int32)
    key_places = jnp.arange(SEQUENCE_TOKENS, dtype=jnp.int32)
    cosine_table, sine_table = rope_tables(positions)

    def query_map(unrotated_projection, gain_vector):
        return per_head_route(
            unrotated_projection, gain_vector, cosine_table, sine_table, QUERY_HEADS
        )

    def key_map(unrotated_projection, gain_vector):
        return per_head_route(
            unrotated_projection, gain_vector, cosine_table, sine_table, KEY_VALUE_HEADS
        )

    flat_in = tokens.reshape(number_of_rows, model_width).astype(jnp.float32)
    normed = rms_norm(flat_in, g_attn).astype(jnp.bfloat16)
    query_raw = jnp.dot(normed, attn_set[0], preferred_element_type=jnp.float32).reshape(
        sequence_count, sequence_rows, QUERY_HEADS * HEAD_DIM
    )
    key_unrotated = jnp.dot(normed, attn_set[1], preferred_element_type=jnp.float32).reshape(
        sequence_count, sequence_rows, KEY_VALUE_HEADS * HEAD_DIM
    )
    value_reduced = jnp.dot(normed, attn_set[2], preferred_element_type=jnp.float32).astype(
        jnp.bfloat16
    )
    value_reduced = value_reduced.reshape(sequence_count, sequence_rows, KEY_VALUE_HEADS * HEAD_DIM)
    query_reduced = query_map(query_raw, g_query).astype(jnp.bfloat16)
    key_reduced = key_map(key_unrotated, key_grad_total).astype(jnp.bfloat16)
    mask_list = []
    mixed_list = []
    total_list = []
    for seq_index in range(sequence_count):
        query_ids = piece_ids(positions, starts[seq_index])
        key_ids = piece_ids(key_places, starts[seq_index])
        allowed = visible(positions, query_ids, key_places, key_ids)
        key_full, value_full = (
            lax.all_gather(key_reduced[seq_index], "ctx", axis=0, tiled=True),
            lax.all_gather(value_reduced[seq_index], "ctx", axis=0, tiled=True),
        )
        mixed_out, log_total = attend_forward(
            query_reduced[seq_index], key_full, value_full, allowed, head_group_block
        )
        mask_list.append(allowed)
        mixed_list.append(mixed_out)
        total_list.append(log_total)
    attn_low = (
        jnp.stack(mixed_list).reshape(number_of_rows, QUERY_HEADS * HEAD_DIM).astype(jnp.bfloat16)
    )
    residual = flat_in + jnp.dot(attn_low, attn_set[3], preferred_element_type=jnp.float32)
    mlp_in = rms_norm(residual, g_mlp).astype(jnp.bfloat16)
    gate_proj = jnp.dot(mlp_in, mlp_set[0], preferred_element_type=jnp.float32)
    up_proj = jnp.dot(mlp_in, mlp_set[1], preferred_element_type=jnp.float32)
    hidden = swiglu(gate_proj, up_proj).astype(jnp.bfloat16)
    result = residual + jnp.dot(hidden, mlp_set[2], preferred_element_type=jnp.float32)
    output = result.astype(jnp.bfloat16).reshape(tokens.shape)
    mlp_back = (
        lax.all_gather(w_gate, ("dp", "ctx"), axis=0, tiled=True),
        lax.all_gather(w_up, ("dp", "ctx"), axis=0, tiled=True),
        lax.all_gather(w_down, ("dp", "ctx"), axis=0, tiled=True),
    )
    grad_flat = cotangent.reshape(number_of_rows, model_width)
    grad_down = jnp.dot(hidden.T, grad_flat, preferred_element_type=jnp.float32)
    d_hidden = jnp.dot(grad_flat, mlp_back[2].T, preferred_element_type=jnp.float32)
    swiglu_pull = jax.vjp(swiglu, gate_proj, up_proj)[1]
    d_gate, d_up = swiglu_pull(d_hidden)
    d_gate = d_gate.astype(jnp.bfloat16)
    d_up = d_up.astype(jnp.bfloat16)
    grad_gate = jnp.dot(mlp_in.T, d_gate, preferred_element_type=jnp.float32)
    grad_up = jnp.dot(mlp_in.T, d_up, preferred_element_type=jnp.float32)
    mlp_grads = (
        lax.psum_scatter(grad_gate, ("dp", "ctx"), scatter_dimension=0, tiled=True),
        lax.psum_scatter(grad_up, ("dp", "ctx"), scatter_dimension=0, tiled=True),
        lax.psum_scatter(grad_down, ("dp", "ctx"), scatter_dimension=0, tiled=True),
    )
    d_mlp_in = jnp.dot(d_gate, mlp_back[0].T, preferred_element_type=jnp.float32)
    d_mlp_in = d_mlp_in + jnp.dot(d_up, mlp_back[1].T, preferred_element_type=jnp.float32)
    mlp_norm_pull = jax.vjp(rms_norm, residual, g_mlp)[1]
    d_resid_norm, d_g_mlp = mlp_norm_pull(d_mlp_in)
    d_resid = grad_flat.astype(jnp.float32) + d_resid_norm
    attn_back = (
        lax.all_gather(w_query, ("dp", "ctx"), axis=0, tiled=True),
        lax.all_gather(key_matrix, ("dp", "ctx"), axis=0, tiled=True),
        lax.all_gather(value_matrix, ("dp", "ctx"), axis=0, tiled=True),
        lax.all_gather(w_out, ("dp", "ctx"), axis=0, tiled=True),
        lax.all_gather(gains, ("dp", "ctx"), axis=0, tiled=True),
    )
    d_branch = d_resid.astype(jnp.bfloat16)
    grad_out = jnp.dot(attn_low.T, d_branch, preferred_element_type=jnp.float32)
    d_attn = jnp.dot(d_branch, attn_back[3].T, preferred_element_type=jnp.float32).astype(
        jnp.bfloat16
    )
    d_attn = d_attn.reshape(sequence_count, sequence_rows, QUERY_HEADS * HEAD_DIM)
    dq_list = []
    dk_list = []
    value_gradient_list = []
    for seq_index in range(sequence_count):
        key_full, value_full = (
            lax.all_gather(key_reduced[seq_index], "ctx", axis=0, tiled=True),
            lax.all_gather(value_reduced[seq_index], "ctx", axis=0, tiled=True),
        )
        d_query_seq, d_key_full, d_value_full = attend_backward(
            query_reduced[seq_index],
            key_full,
            value_full,
            mask_list[seq_index],
            total_list[seq_index],
            d_attn[seq_index],
            head_group_block,
        )
        d_key_seq, d_value_seq = (
            lax.psum_scatter(
                d_key_full.astype(jnp.bfloat16), "ctx", scatter_dimension=0, tiled=True
            ).astype(jnp.float32),
            lax.psum_scatter(
                d_value_full.astype(jnp.bfloat16), "ctx", scatter_dimension=0, tiled=True
            ).astype(jnp.float32),
        )
        dq_list.append(d_query_seq)
        dk_list.append(d_key_seq)
        value_gradient_list.append(d_value_seq)
    d_query = jnp.stack(dq_list)
    key_gradient = jnp.stack(dk_list)
    value_gradient_reduced = (
        jnp.stack(value_gradient_list)
        .reshape(number_of_rows, KEY_VALUE_HEADS * HEAD_DIM)
        .astype(jnp.bfloat16)
    )
    query_pull = jax.vjp(query_map, query_raw, g_query)[1]
    d_query_raw, d_g_query = query_pull(d_query)
    key_pull = jax.vjp(key_map, key_unrotated, key_grad_total)[1]
    key_gradient_unrotated, d_g_key = key_pull(key_gradient)
    d_query_low = d_query_raw.reshape(number_of_rows, QUERY_HEADS * HEAD_DIM).astype(jnp.bfloat16)
    key_gradient_reduced = key_gradient_unrotated.reshape(
        number_of_rows, KEY_VALUE_HEADS * HEAD_DIM
    ).astype(jnp.bfloat16)
    grad_query = jnp.dot(normed.T, d_query_low, preferred_element_type=jnp.float32)
    grad_key = jnp.dot(normed.T, key_gradient_reduced, preferred_element_type=jnp.float32)
    grad_value = jnp.dot(normed.T, value_gradient_reduced, preferred_element_type=jnp.float32)
    d_normed = jnp.dot(d_query_low, attn_back[0].T, preferred_element_type=jnp.float32)
    d_normed = d_normed + jnp.dot(
        key_gradient_reduced, attn_back[1].T, preferred_element_type=jnp.float32
    )
    d_normed = d_normed + jnp.dot(
        value_gradient_reduced, attn_back[2].T, preferred_element_type=jnp.float32
    )
    input_pull = jax.vjp(rms_norm, flat_in, g_attn)[1]
    d_input_norm, d_g_attn = input_pull(d_normed)
    grad_tokens = (d_resid + d_input_norm).reshape(tokens.shape)
    grad_gains = jnp.concatenate([d_g_attn, d_g_mlp, d_g_query, d_g_key])
    attn_grads = (
        lax.psum_scatter(grad_query, ("dp", "ctx"), scatter_dimension=0, tiled=True),
        lax.psum_scatter(grad_key, ("dp", "ctx"), scatter_dimension=0, tiled=True),
        lax.psum_scatter(grad_value, ("dp", "ctx"), scatter_dimension=0, tiled=True),
        lax.psum_scatter(grad_out, ("dp", "ctx"), scatter_dimension=0, tiled=True),
        lax.psum_scatter(grad_gains, ("dp", "ctx"), scatter_dimension=0, tiled=True),
    )
    return (
        output,
        grad_tokens,
        attn_grads[0],
        attn_grads[1],
        attn_grads[2],
        attn_grads[3],
        mlp_grads[0],
        mlp_grads[1],
        mlp_grads[2],
        attn_grads[4],
    )


def generic_solution(mesh):
    return jax.shard_map(
        generic_device,
        mesh=mesh,
        in_specs=(
            P("dp", "ctx", None),
            P("dp", "ctx", None),
            P("dp", None),
            P(("dp", "ctx"), None),
            P(("dp", "ctx"), None),
            P(("dp", "ctx"), None),
            P(("dp", "ctx"), None),
            P(("dp", "ctx"), None),
            P(("dp", "ctx"), None),
            P(("dp", "ctx"), None),
            P(("dp", "ctx")),
        ),
        out_specs=(
            P("dp", "ctx", None),
            P("dp", "ctx", None),
            P(("dp", "ctx"), None),
            P(("dp", "ctx"), None),
            P(("dp", "ctx"), None),
            P(("dp", "ctx"), None),
            P(("dp", "ctx"), None),
            P(("dp", "ctx"), None),
            P(("dp", "ctx"), None),
            P(("dp", "ctx")),
        ),
        check_vma=False,
    )


AXES = ("y", "x", "p", "l", "c")
FF = 3072
HALF_FF = FF // 2
ROWS = 256
SEQ_ROWS = SEQUENCE_TOKENS
OWN = SEQ_ROWS // 4
BLK = 512
NBLK = SEQ_ROWS // BLK
QH = 4
KH = 2
MESH = pl.DeviceIdType.MESH
SCALE = 1.0 / math.sqrt(HEAD_DIM)
LOG2E = 1.4426950408889634
VMEM_LIMIT = 62 * 1024 * 1024
NT = (((1,), (1,)), ((), ()))
TN = (((0,), (0,)), ((), ()))


def dot(a, b, dims=None):
    if dims is None:
        dims = (((1,), (0,)), ((), ()))
    return lax.dot_general(a, b, dims, preferred_element_type=jnp.float32)


def greet(peers):
    barrier = pltpu.get_barrier_semaphore()
    for peer in peers:
        pl.semaphore_signal(barrier, inc=1, device_id=peer, device_id_type=MESH)
    pl.semaphore_wait(barrier, len(peers))


class Plan:
    def __init__(self, send_sem, recv_sem):
        self.send_sem = send_sem
        self.recv_sem = recv_sem
        self.count = 0
        self.entries = []

    def add(self, peer, pairs):
        self.entries.append((peer, pairs, self.count))
        self.count += len(pairs)
        return len(self.entries) - 1

    def copies(self, name):
        peer, pairs, at = self.entries[name]
        return [
            pltpu.make_async_remote_copy(
                src_ref=src,
                dst_ref=dst,
                send_sem=self.send_sem.at[at + k],
                recv_sem=self.recv_sem.at[at + k],
                device_id=peer,
                device_id_type=MESH,
            )
            for k, (src, dst) in enumerate(pairs)
        ]

    def start(self, *names):
        for name in names:
            for copy in self.copies(name):
                copy.start()

    def arrived(self, *names):
        for name in names:
            for copy in self.copies(name):
                copy.wait_recv()

    def sent(self):
        for name in range(len(self.entries)):
            for copy in self.copies(name):
                copy.wait_send()


def place():
    return tuple(lax.axis_index(name) for name in AXES)


def peers_of(x, y, p, l, c):
    return {
        "c": {"c": 1 - c},
        "l": {"l": 1 - l},
        "d": {"l": 1 - l, "c": 1 - c},
        "p": {"p": 1 - p},
        "x": {"x": 1 - x},
        "y": {"y": 1 - y},
    }


def owned(p, l, c):
    return 2 * c + (p + l + c) % 2


def rows_at(index, size, count=1):
    return pl.ds(pl.multiple_of(index * size, size), size * count)


def in_place(*refs):
    return [(ref, ref) for ref in refs]


def front_kernel(tok, wq, wk, wv, wo, gn, wg, wu, wd, inverse, xs, wa, woq, gf, wgu, wdn, cosine, sine, send_sem, recv_sem, in_sem, local_sem, *staged):
    y, x, p, l, c = place()
    peer = peers_of(x, y, p, l, c)
    block = 4 * p + 2 * l + c
    group = (y * 2 + x) * 8
    me = group + block
    t = 2 * l + c
    net = Plan(send_sem, recv_sem)

    def quarter(q):
        return [
            (wq.at[:, rows_at(q, 512)], wa.at[rows_at(me, 32), pl.ds(0, 512)]),
            (wk.at[:, rows_at(q, 256)], wa.at[rows_at(me, 32), pl.ds(512, 256)]),
            (wv.at[:, rows_at(q, 256)], wa.at[rows_at(me, 32), pl.ds(768, 256)]),
            (wo.at[:, rows_at(q, 256)], woq.at[rows_at(me, 64)]),
            (gn, gf.at[me]),
        ]

    def half(h):
        return [
            (wg.at[:, rows_at(h, HALF_FF)], wgu.at[0, rows_at(me, 32)]),
            (wu.at[:, rows_at(h, HALF_FF)], wgu.at[1, rows_at(me, 32)]),
            (wd.at[:, rows_at(h, 512)], wdn.at[rows_at(me, 96)]),
        ]

    def span(base, piece):
        if piece < 2:
            return in_place(wa.at[rows_at(base // 2 + piece, 64)])
        return in_place(woq.at[rows_at(base // 4, 256)], gf.at[pl.ds(base, 4)])

    def chip(yy, xx, pp, ll):
        slot = (yy * 2 + xx) * 4 + 2 * pp + ll
        return in_place(wgu.at[:, rows_at(slot, 64)], wdn.at[rows_at(slot, 192)])

    mine, other = group + 4 * p, group + 4 * (1 - p)
    go_first_l = net.add(peer["l"], quarter(2 * (1 - l) + c))
    go_first_d = net.add(peer["d"], quarter(2 * (1 - l) + 1 - c))
    go_first_c = net.add(peer["c"], quarter(2 * l + 1 - c))
    go_near = net.add(peer["l"], [(tok.at[p], xs.at[block])])
    upper, lower = pl.ds(0, ROWS // 2), pl.ds(ROWS // 2, ROWS // 2)
    go_far_0 = net.add(peer["p"], [(tok.at[1 - p, upper], xs.at[block, upper])])
    go_far_1 = net.add(peer["p"], [(tok.at[1 - p, lower], xs.at[block, lower])])
    go_near_c = net.add(peer["c"], [(tok.at[p], xs.at[block])])
    pieces = range(3)
    go_across = [net.add(peer["p"], span(mine, k)) for k in pieces]
    go_own_x = [net.add(peer["x"], span(mine, k)) for k in pieces]
    go_near_relay = net.add(peer["c"], in_place(xs.at[block ^ 2]))
    go_own_y = [net.add(peer["y"], span(mine, k) + span((y * 2 + 1 - x) * 8 + 4 * p, k)) for k in pieces]
    go_other_y = [net.add(peer["y"], span(other, k)) for k in pieces]
    go_far_l0 = net.add(peer["l"], in_place(xs.at[block ^ 4, upper]))
    go_far_l1 = net.add(peer["l"], in_place(xs.at[block ^ 4, lower]))
    go_far_relay = net.add(peer["c"], in_place(xs.at[block ^ 4]))
    go_other_x = [net.add(peer["x"], span(other, k) + span(((1 - y) * 2 + x) * 8 + 4 * (1 - p), k)) for k in pieces]
    go_far_l_relay = net.add(peer["c"], in_place(xs.at[block ^ 6]))
    go_mlp_c = net.add(peer["c"], half(1 - c))
    go_mlp_near = net.add(peer["l"], chip(y, x, p, l))
    go_mlp_x = net.add(peer["x"], chip(y, x, p, l))
    moves = quarter(t) + half(c) + [(tok.at[p], xs.at[block])]
    taken = [pltpu.make_async_copy(src, stage, in_sem.at[k]) for k, ((src, dst), stage) in enumerate(zip(moves, staged))]
    own = [pltpu.make_async_copy(stage, dst, local_sem.at[k]) for k, ((src, dst), stage) in enumerate(zip(moves, staged))]
    for copy in taken:
        copy.start()
    greet(list(peer.values()))
    net.start(go_first_l, go_first_d, go_first_c, go_far_0, go_near_c, go_mlp_c)
    for copy in taken:
        copy.wait()
    for copy in own:
        copy.start()

    def table(first, last):
        def chunk(k, carry):
            rows = rows_at(k, 64)
            position = (lax.broadcasted_iota(jnp.int32, (64, HEAD_DIM), 0) + k * 64).astype(jnp.float32)
            lane = lax.broadcasted_iota(jnp.int32, (64, HEAD_DIM), 1)
            angle = position * inverse[0:1, :]
            cosine[rows, :] = jnp.cos(angle)
            sine[rows, :] = jnp.where(lane < HEAD_DIM // 2, -1.0, 1.0) * jnp.sin(angle)
            return carry

        lax.fori_loop(first, last, chunk, 0)

    for copy in own:
        copy.wait()
    net.arrived(go_first_l, go_first_d, go_first_c)
    net.start(*go_across, *go_own_x, go_near)
    table(0, 12)
    for k in pieces:
        net.arrived(go_across[k])
        net.start(go_other_y[k])
    net.start(go_far_1)
    net.arrived(go_mlp_c)
    net.start(go_mlp_x)
    net.arrived(go_near)
    net.start(go_near_relay)
    for k in pieces:
        net.arrived(go_other_y[k])
        net.start(go_other_x[k])
    net.arrived(*go_own_x)
    net.start(*go_own_y)
    net.arrived(go_far_0)
    net.start(go_far_l0)
    table(12, 32)
    net.arrived(go_far_1)
    net.start(go_far_l1, go_far_relay, go_mlp_near)
    net.arrived(go_far_l0, go_far_l1)
    net.start(go_far_l_relay)
    net.arrived(go_near_c, go_near_relay, go_far_relay, go_far_l_relay, *go_own_y, *go_other_x, go_mlp_x, go_mlp_near)
    net.sent()


def front(tok, wq, wk, wv, wo, gn, wg, wu, wd, inverse):
    any_spec = pl.BlockSpec(memory_space=pl.ANY)
    copies = 64
    bf16 = jnp.bfloat16
    return pl.pallas_call(
        front_kernel,
        out_shape=(
            jax.ShapeDtypeStruct((8, ROWS, MODEL_DIM), bf16),
            jax.ShapeDtypeStruct((1024, 1024), bf16),
            jax.ShapeDtypeStruct((2048, 256), bf16),
            jax.ShapeDtypeStruct((32, 8, 128), jnp.float32),
            jax.ShapeDtypeStruct((2, MODEL_DIM, HALF_FF), bf16),
            jax.ShapeDtypeStruct((FF, 512), bf16),
            jax.ShapeDtypeStruct((SEQ_ROWS, HEAD_DIM), jnp.float32),
            jax.ShapeDtypeStruct((SEQ_ROWS, HEAD_DIM), jnp.float32),
        ),
        in_specs=[any_spec] * 9 + [pl.BlockSpec(memory_space=pltpu.VMEM)],
        out_specs=[any_spec] * 6 + [pl.BlockSpec(memory_space=pltpu.VMEM)] * 2,
        scratch_shapes=[
            pltpu.SemaphoreType.DMA((copies,)),
            pltpu.SemaphoreType.DMA((copies,)),
            pltpu.SemaphoreType.DMA((9,)),
            pltpu.SemaphoreType.DMA((9,)),
            pltpu.VMEM((32, 512), bf16),
            pltpu.VMEM((32, 256), bf16),
            pltpu.VMEM((32, 256), bf16),
            pltpu.VMEM((64, 256), bf16),
            pltpu.VMEM((8, 128), jnp.float32),
            pltpu.VMEM((32, HALF_FF), bf16),
            pltpu.VMEM((32, HALF_FF), bf16),
            pltpu.VMEM((96, 512), bf16),
            pltpu.VMEM((ROWS, MODEL_DIM), bf16),
        ],
        compiler_params=pltpu.CompilerParams(
            collective_id=0, has_side_effects=True, vmem_limit_bytes=VMEM_LIMIT
        ),
        name="front_gather",
    )(tok, wq, wk, wv, wo, gn, wg, wu, wd, inverse)


def line_peers(p, l, c):
    return [
        {"p": (p + a) % 2, "l": (l + b) % 2, "c": (c + d) % 2}
        for a in range(2)
        for b in range(2)
        for d in range(2)
        if a + b + d > 0
    ]


class Return:
    def __init__(self, where, src, dst, send_sem, recv_sem):
        self.where = where[2:]
        self.src, self.dst, self.send_sem, self.recv_sem = src, dst, send_sem, recv_sem

    def stays(self, index):
        p, l, c = self.where
        return (p == c) & (index == c)

    def local(self, c0):
        p, l, c = self.where
        return pltpu.make_async_copy(self.src.at[pl.ds(c0 * ROWS, ROWS)], self.dst.at[p], self.send_sem.at[c0])

    def remote(self, c0):
        p, l, c = self.where
        return pltpu.make_async_remote_copy(
            src_ref=self.src.at[pl.ds(c0 * ROWS, ROWS)],
            dst_ref=self.dst.at[p],
            send_sem=self.send_sem.at[c0],
            recv_sem=self.recv_sem.at[p],
            device_id={"p": c, "l": (p + l + c) % 2, "c": c0},
            device_id_type=MESH,
        )

    def start_one(self, c0):
        here = self.stays(c0)

        @pl.when(here)
        def _():
            self.local(c0).start()

        @pl.when(jnp.logical_not(here))
        def _():
            self.remote(c0).start()

    def start(self):
        for c0 in range(2):
            self.start_one(c0)

    def wait(self):
        p, l, c = self.where
        for c0 in range(2):
            here = self.stays(c0)

            @pl.when(here)
            def _():
                self.local(c0).wait()

            @pl.when(jnp.logical_not(here))
            def _():
                self.remote(c0).wait_send()

        for seq in range(2):

            @pl.when(jnp.logical_not(self.stays(seq)))
            def _():
                pltpu.make_async_remote_copy(
                    src_ref=self.src.at[pl.ds(0, ROWS)],
                    dst_ref=self.dst.at[seq],
                    send_sem=self.send_sem.at[0],
                    recv_sem=self.recv_sem.at[seq],
                    device_id={"p": 1 - p},
                    device_id_type=MESH,
                ).wait_recv()


class Spread:
    def __init__(self, where, src, dst, send_sem, recv_sem):
        self.where = where[2:]
        self.src, self.dst, self.send_sem, self.recv_sem = src, dst, send_sem, recv_sem

    def here(self, index):
        p, l, c = self.where
        return (p == c) & (index == c)

    def local(self, seq):
        p, l, c = self.where
        return pltpu.make_async_copy(self.src.at[seq], self.dst.at[p, c], self.send_sem.at[seq])

    def remote(self, seq):
        p, l, c = self.where
        return pltpu.make_async_remote_copy(
            src_ref=self.src.at[seq],
            dst_ref=self.dst.at[p, c],
            send_sem=self.send_sem.at[seq],
            recv_sem=self.recv_sem.at[c],
            device_id={"p": seq, "l": (seq + l + p) % 2, "c": p},
            device_id_type=MESH,
        )

    def start(self):
        for seq in range(2):

            @pl.when(self.here(seq))
            def _():
                self.local(seq).start()

            @pl.when(jnp.logical_not(self.here(seq)))
            def _():
                self.remote(seq).start()

    def wait(self):
        p, l, c = self.where
        for seq in range(2):

            @pl.when(self.here(seq))
            def _():
                self.local(seq).wait()

            @pl.when(jnp.logical_not(self.here(seq)))
            def _():
                self.remote(seq).wait_send()

        for block in range(2):

            @pl.when(jnp.logical_not(self.here(block)))
            def _():
                pltpu.make_async_remote_copy(
                    src_ref=self.src.at[0],
                    dst_ref=self.dst.at[c, block],
                    send_sem=self.send_sem.at[0],
                    recv_sem=self.recv_sem.at[block],
                    device_id={"p": 1 - p},
                    device_id_type=MESH,
                ).wait_recv()


def turn(value):
    return pltpu.roll(value, HEAD_DIM // 2, 1)


def block_mask(key_dim, flags, index):
    shape = (BLK, BLK)
    key = lax.broadcasted_iota(jnp.int32, shape, key_dim)
    query = lax.broadcasted_iota(jnp.int32, shape, 1 - key_dim)
    upper = query // PIECE
    piece = jnp.where(upper == 0, flags[2 * index], flags[2 * index + 1])
    return (key <= query) | ((key // PIECE == upper) & (piece > 0))


PROJECT = 8


def attend_kernel(
    flags, x_ref, w_ref, ga_ref, gq_ref, gk_ref, cos_ref, sin_ref, woq, wgu_in, wdn_in,
    n_ref, q_ref, k_ref, v_ref, qr_ref, kr_ref, o_ref, lse_ref, wo, wgu, wdn,
    stage, send_sem, recv_sem, local_sem,
):
    y, x, p, l, c = place()
    peer = peers_of(x, y, p, l, c)
    t = 2 * l + c
    net = Plan(send_sem, recv_sem)

    def chip(yy, xx, pp, ll):
        slot = (yy * 2 + xx) * 4 + 2 * pp + ll
        return in_place(wgu.at[:, rows_at(slot, 64)], wdn.at[rows_at(slot, 192)])

    def rows_of(q):
        return woq.at[rows_at(q, 512)], wo.at[:, rows_at(t, 256)]

    go_mlp_y = net.add(peer["y"], chip(y, x, p, l) + chip(y, 1 - x, p, l))
    go_mlp_x = net.add(peer["x"], chip(y, x, p, 1 - l) + chip(1 - y, x, p, 1 - l))
    go_far = [net.add(peer["p"], [pair]) for pair in chip(y, x, p, l)]
    go_far_l = [net.add(peer["l"], [pair]) for pair in chip(y, x, 1 - p, l)]
    go_near_y = net.add(peer["y"], chip(y, x, p, 1 - l))
    go_wo_l = net.add(peer["l"], [rows_of(2 * (1 - l) + c)])
    go_wo_d = net.add(peer["d"], [rows_of(2 * (1 - l) + 1 - c)])
    go_wo_c = net.add(peer["c"], [rows_of(2 * l + 1 - c)])
    step = pl.program_id(0)

    @pl.when(step == 0)
    def _():
        greet(list(peer.values()))
        net.start(go_near_y, *go_far, go_wo_l, go_wo_d, go_wo_c)
        copy = pltpu.make_async_copy(rows_of(t)[0], stage, local_sem.at[0])
        copy.start()
        copy.wait()
        pltpu.make_async_copy(stage, rows_of(t)[1], local_sem.at[1]).start()

    @pl.when(step < PROJECT)
    def _():
        value = x_ref[...].astype(jnp.float32)
        r = lax.rsqrt(jnp.mean(value * value, axis=-1, keepdims=True) + EPS)
        normed = (value * r * ga_ref[...]).astype(jnp.bfloat16)
        n_ref[...] = normed
        full = dot(normed, w_ref[...])
        cosine, sine = cos_ref[...], sin_ref[...]
        rows = rows_at(jnp.minimum(step, PROJECT - 1), 256)
        for h in range(QH + KH):
            u = full[:, h * HEAD_DIM : (h + 1) * HEAD_DIM]
            raw_ref, out_ref, g_ref, at = (qr_ref, q_ref, gq_ref, h) if h < QH else (kr_ref, k_ref, gk_ref, h - QH)
            raw_ref[at] = u
            n = u * lax.rsqrt(jnp.mean(u * u, axis=-1, keepdims=True) + EPS) * g_ref[...]
            out_ref[at, rows, :] = (n * cosine + turn(n) * sine).astype(jnp.bfloat16)
        for h in range(KH):
            at = (QH + KH + h) * HEAD_DIM
            v_ref[h, rows, :] = full[:, at : at + HEAD_DIM].astype(jnp.bfloat16)

    @pl.when(step == PROJECT)
    def _():
        net.arrived(go_near_y)
        net.start(go_mlp_x, go_mlp_y)

    for k, at in enumerate((PROJECT + 3, PROJECT + 5)):

        @pl.when(step == at)
        def _():
            net.arrived(go_far[k])
            net.start(go_far_l[k])

    @pl.when(step >= PROJECT)
    def _():
        order = jnp.maximum(step - PROJECT, 0)
        g, i = order // NBLK, order % NBLK
        ones = jnp.ones((BLK, HEAD_DIM), jnp.bfloat16)
        mask = block_mask(1, flags, i)

        def values(j):
            return jnp.concatenate([v_ref[g, rows_at(j, BLK), :], ones], axis=1)

        queries = [q_ref[2 * g + h, rows_at(i, BLK), :] for h in range(2)]

        def part(j, masked):
            keys, both = k_ref[g, rows_at(j, BLK), :], values(j)
            found = []
            for q in queries:
                probs = jnp.exp2(dot(q, keys, NT) * (SCALE * LOG2E))
                if masked:
                    probs = jnp.where(mask, probs, 0.0)
                found.append(dot(probs.astype(jnp.bfloat16), both))
            return found

        def one(j, accs):
            return tuple(acc + more for acc, more in zip(accs, part(j, False)))

        accs = lax.fori_loop(0, i, one, tuple(part(i, True)))
        for h, acc in enumerate(accs):
            total = acc[:, HEAD_DIM:]
            o_ref[:, h * HEAD_DIM : (h + 1) * HEAD_DIM] = (acc[:, :HEAD_DIM] / total).astype(jnp.bfloat16)
            lse_ref[h] = jnp.log2(total).T[0:8, :]

    @pl.when(step == PROJECT + 2 * NBLK - 1)
    def _():
        pltpu.make_async_copy(stage, rows_of(t)[1], local_sem.at[1]).wait()
        net.arrived(go_mlp_y, go_mlp_x, *go_far_l, go_wo_l, go_wo_d, go_wo_c)
        net.sent()


def attend(flags, x, w, ga, gq, gk, cosine, sine, woq, wgu, wdn):
    bf16, f32 = jnp.bfloat16, jnp.float32

    def early(s):
        return jnp.minimum(s, PROJECT - 1)

    def late(s):
        return jnp.maximum(s - PROJECT, 0)

    def row(width):
        return pl.BlockSpec((256, width), lambda s, f: (early(s), 0))

    def whole(shape):
        return pl.BlockSpec(shape, lambda s, f: (0,) * len(shape))

    def heads(n):
        return pl.BlockSpec((n, 256, HEAD_DIM), lambda s, f: (0, early(s), 0))

    def shape(n, dtype):
        return jax.ShapeDtypeStruct((n, SEQ_ROWS, HEAD_DIM), dtype)

    any_spec = pl.BlockSpec(memory_space=pl.ANY)
    copies = 20
    return pl.pallas_call(
        attend_kernel,
        out_shape=(
            jax.ShapeDtypeStruct((SEQ_ROWS, MODEL_DIM), bf16),
            shape(QH, bf16),
            shape(KH, bf16),
            shape(KH, bf16),
            shape(QH, f32),
            shape(KH, f32),
            jax.ShapeDtypeStruct((SEQ_ROWS, QH * HEAD_DIM), bf16),
            jax.ShapeDtypeStruct((QH, 8, SEQ_ROWS), f32),
            jax.ShapeDtypeStruct((512, MODEL_DIM), bf16),
            jax.ShapeDtypeStruct(wgu.shape, bf16),
            jax.ShapeDtypeStruct(wdn.shape, bf16),
        ),
        grid_spec=pltpu.PrefetchScalarGridSpec(
            num_scalar_prefetch=1,
            grid=(PROJECT + KH * NBLK,),
            in_specs=[row(MODEL_DIM), whole(w.shape), whole(ga.shape), whole(gq.shape), whole(gk.shape), row(HEAD_DIM), row(HEAD_DIM)]
            + [any_spec] * 3,
            out_specs=[
                row(MODEL_DIM),
                whole((QH, SEQ_ROWS, HEAD_DIM)),
                whole((KH, SEQ_ROWS, HEAD_DIM)),
                whole((KH, SEQ_ROWS, HEAD_DIM)),
                heads(QH),
                heads(KH),
                pl.BlockSpec((BLK, 2 * HEAD_DIM), lambda s, f: (late(s) % NBLK, late(s) // NBLK)),
                pl.BlockSpec((2, 8, BLK), lambda s, f: (late(s) // NBLK, 0, late(s) % NBLK)),
            ]
            + [any_spec] * 3,
            scratch_shapes=[pltpu.VMEM((512, 256), bf16)]
            + [pltpu.SemaphoreType.DMA((copies,))] * 2
            + [pltpu.SemaphoreType.DMA((2,))],
        ),
        input_output_aliases={9: 9, 10: 10},
        compiler_params=pltpu.CompilerParams(
            collective_id=2, has_side_effects=True, vmem_limit_bytes=VMEM_LIMIT
        ),
        cost_estimate=pl.CostEstimate(
            flops=4 * QH * SEQ_ROWS * SEQ_ROWS * HEAD_DIM, bytes_accessed=24 << 20, transcendentals=QH * SEQ_ROWS * SEQ_ROWS
        ),
        name="attend",
    )(flags, x, w, ga, gq, gk, cosine, sine, woq, wgu, wdn)


def resid_kernel(
    attn, wo, g_mlp, xs, cot, wgu_in, wdn_in,
    resid, mlp_in, wgu, wdn, wdx, dy,
    send_c, recv_c, send_l, recv_l, keep, x_own, send_sem, recv_sem, local_sem, dy_send, dy_recv,
):
    where = place()
    y, x, p, l, c = where
    peer = peers_of(x, y, p, l, c)
    net = Plan(send_sem, recv_sem)

    def chip(yy, xx, pp, ll):
        slot = (yy * 2 + xx) * 4 + 2 * pp + ll
        return in_place(wgu.at[:, rows_at(slot, 64)], wdn.at[rows_at(slot, 192)])

    def down(pp, ll):
        found = []
        for xx in range(2):
            slot = xx * 4 + 2 * pp + ll
            found.append((wdn.at[rows_at((1 - c) * 8 + slot, 192)], wdx.at[rows_at(slot, 192)]))
        return found

    def hop(name, *chips):
        found = [chip(*one) for one in chips]
        return [net.add(peer[name], [pairs[k] for pairs in found]) for k in range(2)]

    go_far_x = hop("x", (y, x, 1 - p, l))
    go_far_y = hop("y", (y, x, 1 - p, l), (y, 1 - x, 1 - p, l))
    go_fal_y = hop("y", (y, x, 1 - p, 1 - l))
    go_fal_x = hop("x", (y, x, 1 - p, 1 - l), (1 - y, x, 1 - p, 1 - l))
    go_down_me = net.add(peer["c"], down(p, l))
    go_down_near = net.add(peer["c"], down(p, 1 - l))
    go_down_far = net.add(peer["c"], down(1 - p, l))
    go_down_fal = net.add(peer["c"], down(1 - p, 1 - l))
    halves = [pl.ds(n * ROWS, ROWS) for n in range(2)]
    go_give_0 = [net.add(peer["c"], [(send_c.at[0, half], recv_c.at[0, half])]) for half in halves]
    go_give_1 = net.add(peer["c"], [(send_c.at[1], recv_c.at[1])])
    go_cross = [net.add(peer["l"], [(send_l.at[half], recv_l.at[half])]) for half in halves]
    go_share = [net.add(peer["c"], in_place(mlp_in.at[c, half])) for half in halves]
    go_dy_c = net.add(peer["c"], in_place(dy.at[c]))
    spread = Spread(where, cot, dy, dy_send, dy_recv)
    greet(line_peers(p, l, c) + [peer["x"], peer["y"]])
    spread.start()
    net.start(go_far_x[1], go_fal_y[1], go_far_x[0], go_fal_y[0], go_down_me, go_down_near)
    fetch = pltpu.make_async_copy(xs.at[rows_at(owned(p, l, c), OWN)], x_own, local_sem.at[0])
    fetch.start()

    def project(ll, cc, write, first=0, count=OWN):
        part = attn[pl.ds(pl.multiple_of(owned(p, ll, cc) * OWN + first, ROWS), count), :]

        def chunk(n, carry):
            cols = rows_at(n, 256)
            write(pl.ds(first, count), cols, dot(part, wo[:, cols]))
            return carry

        lax.fori_loop(0, 4, chunk, 0)

    def give(n):
        def write(rows, cols, value):
            send_c[n, rows, cols] = value.astype(jnp.bfloat16)

        return write

    def hold(n):
        def write(rows, cols, value):
            keep[n, rows, cols] = value

        return write

    def relay_hop(k):
        net.arrived(go_far_x[k])
        net.start(go_far_y[k])
        net.arrived(go_fal_y[k])
        net.start(go_fal_x[k])

    for n, half in enumerate(halves):
        project(1 - l, 1 - c, give(0), n * ROWS, ROWS)
        net.start(go_give_0[n])
        project(1 - l, c, hold(0), n * ROWS, ROWS)
        net.arrived(go_give_0[n])
        send_l[half, :] = (keep[0, half, :] + recv_c[0, half, :].astype(jnp.float32)).astype(jnp.bfloat16)
        net.start(go_cross[n])
    relay_hop(1)
    project(l, 1 - c, give(1))
    net.start(go_give_1)
    project(l, c, hold(1))
    fetch.wait()
    relay_hop(0)
    net.arrived(go_give_1)
    keep[1] += recv_c[1].astype(jnp.float32) + x_own[...].astype(jnp.float32)
    for n, half in enumerate(halves):
        net.arrived(go_cross[n])
        total = keep[1, half, :] + recv_l[half, :].astype(jnp.float32)
        resid[half, :] = total
        r = lax.rsqrt(jnp.mean(total * total, axis=-1, keepdims=True) + EPS)
        mlp_in[c, half, :] = (total * r * g_mlp[...]).astype(jnp.bfloat16)
        net.start(go_share[n])
    net.arrived(go_far_y[1])
    net.start(go_down_far)
    spread.wait()
    net.start(go_dy_c)
    net.arrived(go_fal_x[1])
    net.start(go_down_fal)
    net.arrived(go_far_y[0], go_fal_x[0])
    net.arrived(go_down_me, go_down_near, go_down_far, go_down_fal, *go_share, go_dy_c)
    net.sent()


def finish_resid(attn, wo, g_mlp, xs, cot, wgu, wdn):
    bf16, f32 = jnp.bfloat16, jnp.float32
    any_spec = pl.BlockSpec(memory_space=pl.ANY)
    vmem = pl.BlockSpec(memory_space=pltpu.VMEM)
    copies = 32
    return pl.pallas_call(
        resid_kernel,
        out_shape=(
            jax.ShapeDtypeStruct((OWN, MODEL_DIM), f32),
            jax.ShapeDtypeStruct((2, OWN, MODEL_DIM), bf16),
            jax.ShapeDtypeStruct(wgu.shape, bf16),
            jax.ShapeDtypeStruct(wdn.shape, bf16),
            jax.ShapeDtypeStruct((HALF_FF, 512), bf16),
            jax.ShapeDtypeStruct((2, 2, ROWS, MODEL_DIM), bf16),
        ),
        in_specs=[vmem] * 3 + [any_spec] * 4,
        out_specs=[vmem] * 2 + [any_spec] * 4,
        scratch_shapes=[
            pltpu.VMEM((2, OWN, MODEL_DIM), bf16),
            pltpu.VMEM((2, OWN, MODEL_DIM), bf16),
            pltpu.VMEM((OWN, MODEL_DIM), bf16),
            pltpu.VMEM((OWN, MODEL_DIM), bf16),
            pltpu.VMEM((2, OWN, MODEL_DIM), f32),
            pltpu.VMEM((OWN, MODEL_DIM), bf16),
            pltpu.SemaphoreType.DMA((copies,)),
            pltpu.SemaphoreType.DMA((copies,)),
            pltpu.SemaphoreType.DMA((1,)),
            pltpu.SemaphoreType.DMA((2,)),
            pltpu.SemaphoreType.DMA((2,)),
        ],
        input_output_aliases={5: 2, 6: 3},
        compiler_params=pltpu.CompilerParams(
            collective_id=3, has_side_effects=True, vmem_limit_bytes=VMEM_LIMIT
        ),
        name="residual",
    )(attn, wo, g_mlp, xs, cot, wgu, wdn)


CHUNK = 512
EARLY = 1024


def forward_kernel(
    m_ref, dy_ref, w_ref, wdn, wx_ref, resid, g_mlp,
    ggu, gdb, rb, d_resid, db, res, dg,
    mt, hid, dgt, dup, d_in, down, give, take, all_down, ggv, gdv, send_sem, recv_sem, load_sem, out_sem,
):
    where = place()
    y, x, p, l, c = where
    peer = peers_of(x, y, p, l, c)
    red = Reduction(where)
    net = Plan(send_sem, recv_sem)
    go_d_in = net.add(peer["c"], [(give.at[0], take.at[0])])
    go_down = net.add(peer["c"], [(give.at[1], take.at[1])])
    go_gd, go_wide, outs = [], [], []
    for f in range(HALF_FF // CHUNK):
        part_f = pl.ds(f * CHUNK, CHUNK)
        go_gd.append(net.add(peer["c"], [(gdv.at[part_f, rows_at(1 - c, 512)], gdb.at[c, part_f])]))
        outs.append(
            [
                pltpu.make_async_copy(ggv.at[:, :, part_f], ggu.at[:, :, part_f], out_sem.at[2 * f]),
                pltpu.make_async_copy(gdv.at[part_f, rows_at(c, 512)], gdb.at[c, part_f], out_sem.at[2 * f + 1]),
            ]
        )
        go_wide.append([])
        if f * CHUNK < EARLY:
            for n, kind in enumerate(KINDS):
                pairs = []
                for k in range(2):
                    slot = chip_slot(*red.place(kind, k, True), *red.z[kind])
                    pairs.append((ggv.at[:, rows_at(slot, 64), part_f], rb.at[n, k, :, :, part_f]))
                go_wide[f].append(net.add(peer[red.first_peer(kind)], pairs))
    step = pl.program_id(0)
    fetch = pltpu.make_async_copy(wdn.at[rows_at(c, HALF_FF)], all_down, load_sem.at[0])

    @pl.when(step == 0)
    def _():
        fetch.start()
        greet([peer["c"], peer["x"], peer["y"]])

        def flip(k, carry):
            rows = rows_at(k, 256)
            mt[:, rows] = m_ref[rows, :].T
            return carry

        lax.fori_loop(0, 4, flip, 0)
        d_in[...] = jnp.zeros_like(d_in)
        down[...] = jnp.zeros_like(down)
        fetch.wait()

    wo_ref = all_down.at[rows_at(step, CHUNK)]
    own_cols, other_cols = rows_at(c, 512), rows_at(1 - c, 512)

    def part(r, carry):
        rows = rows_at(r, 512)
        value, grad = m_ref[rows, :], dy_ref
        gate, up = dot(value, w_ref[0]), dot(value, w_ref[1])
        d_hidden = dot(grad[rows, own_cols], wo_ref[...], NT) + dot(grad[rows, other_cols], wx_ref[...], NT)
        s = 1.0 / (1.0 + jnp.exp(-gate))
        silu = gate * s
        hidden = (silu * up).astype(jnp.bfloat16)
        d_up = (d_hidden * silu).astype(jnp.bfloat16)
        d_gate = (d_hidden * up * (s * (1.0 + gate * (1.0 - s)))).astype(jnp.bfloat16)
        hid[rows, :] = hidden
        dup[rows, :] = d_up
        dgt[rows, :] = d_gate
        d_in[rows, :] += dot(d_gate, w_ref[0], NT) + dot(d_up, w_ref[1], NT)
        down[rows, own_cols] += dot(hidden, wo_ref[...])
        down[rows, other_cols] += dot(hidden, wx_ref[...])
        return carry

    lax.fori_loop(0, 2, part, 0)

    @pl.when(step == pl.num_programs(0) - 1)
    def _():
        give[0] = d_in[rows_at(1 - c, OWN), :].astype(jnp.bfloat16)
        give[1] = down[rows_at(1 - c, OWN), :].astype(jnp.bfloat16)
        net.start(go_d_in, go_down)

    now = rows_at(step, CHUNK)

    def weights(k, carry):
        rows = rows_at(k, 1024)
        ggv[0, rows, now] = dot(mt[rows, :], dgt[...]).astype(jnp.bfloat16)
        ggv[1, rows, now] = dot(mt[rows, :], dup[...]).astype(jnp.bfloat16)
        gdv[now, rows] = dot(hid[...], dy_ref[:, rows], TN).astype(jnp.bfloat16)
        return carry

    lax.fori_loop(0, 1, weights, 0)
    for f in range(HALF_FF // CHUNK):

        @pl.when(step == f)
        def _():
            net.start(*go_wide[f], go_gd[f])
            for copy in outs[f]:
                copy.start()

    @pl.when(step == pl.num_programs(0) - 1)
    def _():
        net.arrived(go_d_in, go_down)
        dg[...] = jnp.zeros_like(dg)

        def finish(k, carry):
            rows = rows_at(k, 64)
            here = pl.ds(pl.multiple_of(c * OWN + k * 64, 64), 64)
            value = resid[rows, :]
            grad = d_in[here, :] + take[0, rows, :].astype(jnp.float32)
            r = lax.rsqrt(jnp.mean(value * value, axis=-1, keepdims=True) + EPS)
            scaled = value * r
            gained = grad * g_mlp[...]
            total = dy_ref[here, :].astype(jnp.float32) + r * (gained - scaled * jnp.mean(scaled * gained, axis=-1, keepdims=True))
            d_resid[rows, :] = total
            db[rows, :] = total.astype(jnp.bfloat16)
            dg[...] += jnp.sum((grad * scaled).reshape(-1, 8, MODEL_DIM), axis=0)
            res[rows, :] = (value + down[here, :] + take[1, rows, :].astype(jnp.float32)).astype(jnp.bfloat16)
            return carry

        lax.fori_loop(0, 8, finish, 0)
        for f in range(HALF_FF // CHUNK):
            net.arrived(*go_wide[f], go_gd[f])
            for copy in outs[f]:
                copy.wait()
        net.sent()


def feed_forward(mlp_in, dy, wgu, wdn, wdx, resid, g_mlp):
    bf16, f32 = jnp.bfloat16, jnp.float32

    def whole(shape):
        return pl.BlockSpec(shape, lambda f: (0,) * len(shape), pipeline_mode=pl.Buffered(1))

    down = pl.BlockSpec((CHUNK, 512), lambda f: (f, 0))
    copies = 24
    rows = (1024, MODEL_DIM)
    own = (OWN, MODEL_DIM)
    return pl.pallas_call(
        forward_kernel,
        grid=(HALF_FF // CHUNK,),
        out_shape=(
            jax.ShapeDtypeStruct((2, MODEL_DIM, HALF_FF), bf16),
            jax.ShapeDtypeStruct((2, HALF_FF, 512), bf16),
            jax.ShapeDtypeStruct((4, 2, 2, 64, EARLY), bf16),
            jax.ShapeDtypeStruct(own, f32),
            jax.ShapeDtypeStruct(own, bf16),
            jax.ShapeDtypeStruct(own, bf16),
            jax.ShapeDtypeStruct((8, MODEL_DIM), f32),
        ),
        in_specs=[whole(rows), whole(rows), pl.BlockSpec((2, MODEL_DIM, CHUNK), lambda f: (0, 0, f))]
        + [pl.BlockSpec(memory_space=pl.ANY), down]
        + [whole(own), whole((1, MODEL_DIM))],
        out_specs=[pl.BlockSpec(memory_space=pl.ANY)] * 3
        + [whole(own), whole(own), whole(own), whole((8, MODEL_DIM))],
        scratch_shapes=[
            pltpu.VMEM(rows, bf16),
            pltpu.VMEM((1024, CHUNK), bf16),
            pltpu.VMEM((1024, CHUNK), bf16),
            pltpu.VMEM((1024, CHUNK), bf16),
            pltpu.VMEM(rows, f32),
            pltpu.VMEM(rows, f32),
            pltpu.VMEM((2,) + own, bf16),
            pltpu.VMEM((2,) + own, bf16),
            pltpu.VMEM((HALF_FF, 512), bf16),
            pltpu.VMEM((2, MODEL_DIM, HALF_FF), bf16),
            pltpu.VMEM((HALF_FF, MODEL_DIM), bf16),
            pltpu.SemaphoreType.DMA((copies,)),
            pltpu.SemaphoreType.DMA((copies,)),
            pltpu.SemaphoreType.DMA((1,)),
            pltpu.SemaphoreType.DMA((6,)),
        ],
        compiler_params=pltpu.CompilerParams(
            collective_id=6, has_side_effects=True, vmem_limit_bytes=VMEM_LIMIT
        ),
        name="feed_forward",
    )(mlp_in, dy, wgu, wdn, wdx, resid, g_mlp)


KINDS = ME, NEAR, FAR, FAL = range(4)


def chip_slot(yy, xx, pp, ll):
    return (yy * 2 + xx) * 4 + 2 * pp + ll


class Reduction:
    def __init__(self, where):
        y, x, p, l, c = where
        self.z = ((p, l), (p, 1 - l), (1 - p, l), (1 - p, 1 - l))
        self.y, self.x = y, x

    def y_first(self, kind):
        return kind in (ME, FAR)

    def first_peer(self, kind):
        return "y" if self.y_first(kind) else "x"

    def second_peer(self, kind):
        return "x" if self.y_first(kind) else "y"

    def place(self, kind, index, given):
        if self.y_first(kind):
            return (1 - self.y if given else self.y), index
        return index, (1 - self.x if given else self.x)

    def kept(self, kind):
        return self.x if self.y_first(kind) else self.y


def attend_back_kernel(
    flags, q_in, k_in, v_in, o_in, db_in, wo_in, lse_in, qr_in, kr_in, cos_in, sin_in, ggu, gdb, rb_in, res, gq_ref, gk_ref,
    d_out, goq, og_out, od_out, fw_out, fd_out, out, dg_ref,
    q_ref, k_ref, v_ref, o_ref, dall, wo, lse_ref, qr_ref, kr_ref, cos_ref, sin_ref,
    da, delta, dbuf, dq_acc, dk_acc, dv_acc, og, od, rb, rbd, rc, rcd, rz, rzd, go,
    send_sem, recv_sem, load_sem, own_sem, out_sem, back_send, back_recv,
):
    where = place()
    y, x, p, l, c = where
    peer = peers_of(x, y, p, l, c)
    red = Reduction(where)
    net = Plan(send_sem, recv_sem)
    t = 2 * l + c

    def block(index):
        return dall.at[rows_at(index, OWN)]

    mine = owned(p, l, c)
    go_db_l = net.add(peer["l"], [(db_in, block(mine))])
    go_db_c = net.add(peer["c"], [(db_in, block(mine))])
    go_db_r = net.add(peer["c"], in_place(block(owned(p, 1 - l, c))))
    early, late = pl.ds(0, EARLY), pl.ds(EARLY, HALF_FF - EARLY)
    first_of, second_a, second_b = {}, {}, {}
    for n, kind in enumerate(KINDS):
        pairs = []
        for k in range(2):
            yy, xx = red.place(kind, k, True)
            slot = chip_slot(yy, xx, *red.z[kind])
            pairs.append((ggu.at[:, rows_at(slot, 64), late], rb.at[n, k, :, :, late]))
            pairs.append((gdb.at[yy, rows_at(xx * 4 + 2 * red.z[kind][0] + red.z[kind][1], 192)], rbd.at[n, k]))
        first_of[kind] = net.add(peer[red.first_peer(kind)], pairs)
        if n >= 2:
            away, link = 1 - red.kept(kind), peer[red.second_peer(kind)]
            second_a[kind] = net.add(link, [(og.at[n, away, :, :, early], rc.at[n - 2, :, :, early])])
            second_b[kind] = net.add(link, [(og.at[n, away, :, :, late], rc.at[n - 2, :, :, late]), (od.at[n, away], rcd.at[n - 2])])
    u_far, u_fal = red.kept(FAR), red.kept(FAL)
    go_fal_a = net.add(peer["l"], [(og.at[FAL, u_fal, :, :, early], rz.at[:, :, early])])
    go_fal_b = net.add(peer["l"], [(og.at[FAL, u_fal, :, :, late], rz.at[:, :, late]), (od.at[FAL, u_fal], rzd)])
    go_far_a = net.add(peer["p"], [(og.at[FAR, u_far, :, :, early], fw_out.at[:, :, early])])
    go_far_b = net.add(peer["p"], [(og.at[FAR, u_far, :, :, late], fw_out.at[:, :, late]), (od.at[FAR, u_far], fd_out)])
    home = Return(where, res, out, back_send, back_recv)

    def columns(q):
        return [(go.at[:, rows_at(q, 256)], goq.at[rows_at(t, 512)])]

    go_go_l = net.add(peer["l"], columns(2 * (1 - l) + c))
    go_go_d = net.add(peer["d"], columns(2 * (1 - l) + 1 - c))
    go_go_c = net.add(peer["c"], columns(2 * l + 1 - c))
    own_go = pltpu.make_async_copy(*columns(t)[0], out_sem.at[1])
    loads = [
        pltpu.make_async_copy(src, dst, load_sem.at[k])
        for k, (src, dst) in enumerate(
            [
                (db_in, block(mine)), (wo_in, wo), (o_in, o_ref), (q_in, q_ref), (k_in, k_ref), (v_in, v_ref), (lse_in, lse_ref),
                (cos_in, cos_ref), (sin_in, sin_ref), (qr_in, qr_ref), (kr_in, kr_ref),
            ]
        )
    ]
    own = [pltpu.make_async_copy(rb_in, rb.at[:, :, :, :, early], own_sem.at[0])]
    for n, kind in enumerate(KINDS):
        for k in range(2):
            yy, xx = red.place(kind, k, False)
            slot = chip_slot(yy, xx, *red.z[kind])
            own.append(pltpu.make_async_copy(ggu.at[:, rows_at(slot, 64)], og.at[n, k], own_sem.at[len(own)]))
            rows = rows_at(xx * 4 + 2 * red.z[kind][0] + red.z[kind][1], 192)
            own.append(pltpu.make_async_copy(gdb.at[yy, rows], od.at[n, k], own_sem.at[len(own)]))

    def plus(target, other):
        target[...] = (target[...].astype(jnp.float32) + other[...].astype(jnp.float32)).astype(jnp.bfloat16)

    def wide_sum(n, cols):
        def wide(r, carry):
            k, m, rows = r // 4, (r // 2) % 2, rows_at(r % 2, 32)
            plus(og.at[n, k, m, rows, cols], rb.at[n, k, m, rows, cols])
            return carry

        lax.fori_loop(0, 8, wide, 0)

    def deep_sum(n):
        def deep(r, carry):
            k, rows = r // 3, rows_at(r % 3, 64)
            plus(od.at[n, k, rows, :], rbd.at[n, k, rows, :])
            return carry

        lax.fori_loop(0, 6, deep, 0)

    def branch(index):
        rows = rows_at(index, OWN)
        value = dot(dall[rows, :], wo[...], NT).astype(jnp.bfloat16)
        da[rows, :] = value
        for h in range(QH):
            cols = slice(h * HEAD_DIM, (h + 1) * HEAD_DIM)
            prod = value[:, cols].astype(jnp.float32) * o_ref[rows, cols].astype(jnp.float32)
            delta[h, :, rows] = jnp.broadcast_to(jnp.sum(prod.T, axis=0, keepdims=True), (8, BLK))

    def unrope(grad, u, gain, rows):
        grad = grad * SCALE
        e = grad * cos_ref[rows, :] + turn(grad * sin_ref[rows, :])
        r = lax.rsqrt(jnp.mean(u * u, axis=-1, keepdims=True) + EPS)
        ur = u * r
        ge = e * gain
        d = r * (ge - ur * jnp.mean(ur * ge, axis=-1, keepdims=True))
        return d.astype(jnp.bfloat16), jnp.sum((e * ur).reshape(-1, 8, HEAD_DIM), axis=0)

    step = pl.program_id(0)
    b, g = step // KH, step % KH
    i = owned(p, (l + b // 2) % 2, b % 2)

    @pl.when(step == 0)
    def _():
        for copy in loads[:3]:
            copy.start()
        for copy in own:
            copy.start()
        for copy in loads[3:]:
            copy.start()
        greet(line_peers(p, l, c) + [peer["x"], peer["y"]])
        net.start(go_db_l, go_db_c, first_of[FAR], first_of[FAL])
        dk_acc[...] = jnp.zeros_like(dk_acc)
        dv_acc[...] = jnp.zeros_like(dv_acc)
        dg_ref[...] = jnp.zeros_like(dg_ref)
        for copy in own:
            copy.wait()
        for kind in (FAR, FAL):
            wide_sum(kind, early)
            net.start(second_a[kind])
        for copy in loads[:3]:
            copy.wait()
        branch(mine)
        net.arrived(go_db_c)
        branch(owned(p, l, 1 - c))
        for copy in loads[3:]:
            copy.wait()

    @pl.when(step == 2)
    def _():
        net.arrived(second_a[FAL])
        plus(og.at[FAL, u_fal, :, :, early], rc.at[1, :, :, early])
        net.start(go_fal_a)
        net.arrived(second_a[FAR])
        plus(og.at[FAR, u_far, :, :, early], rc.at[0, :, :, early])

    @pl.when(step == 0)
    def _():
        home.start()

    @pl.when(step == 3)
    def _():
        for kind in (FAR, FAL):
            net.arrived(first_of[kind])
            wide_sum(kind, late)
            deep_sum(kind)
            net.start(second_b[kind])
        net.start(first_of[ME], first_of[NEAR])

    @pl.when(step == 2 * KH)
    def _():
        net.arrived(go_db_l)
        net.start(go_db_r)
        branch(owned(p, 1 - l, c))
        net.arrived(go_db_r)
        branch(owned(p, 1 - l, 1 - c))

    @pl.when(step == 4)
    def _():
        net.arrived(go_fal_a)
        plus(og.at[FAR, u_far, :, :, early], rz.at[:, :, early])
        net.start(go_far_a)

    @pl.when(step == 5)
    def _():
        net.arrived(second_b[FAL])
        plus(og.at[FAL, u_fal, :, :, late], rc.at[1, :, :, late])
        plus(od.at[FAL, u_fal], rcd.at[1])
        net.start(go_fal_b)
        net.arrived(second_b[FAR])
        plus(og.at[FAR, u_far, :, :, late], rc.at[0, :, :, late])
        plus(od.at[FAR, u_far], rcd.at[0])

    @pl.when(step == 7)
    def _():
        net.arrived(go_fal_b)
        plus(og.at[FAR, u_far, :, :, late], rz.at[:, :, late])
        plus(od.at[FAR, u_far], rzd)
        net.start(go_far_b)

    @pl.when(step == 5)
    def _():
        def grad_out(k, carry):
            cols = rows_at(k, 256)
            go[cols, :] = dot(o_ref[:, cols], dall[...], TN).astype(jnp.bfloat16)
            return carry

        lax.fori_loop(0, 2, grad_out, 0)
        net.start(go_go_l, go_go_d, go_go_c)
        own_go.start()

    dq_acc[...] = jnp.zeros_like(dq_acc)
    rows = rows_at(i, BLK)
    heads = [2 * g + n for n in range(2)]
    spans = [rows_at(h, HEAD_DIM) for h in heads]
    queries = [q_ref[h, rows, :] for h in heads]
    grads = [da[rows, span] for span in spans]

    def tile(j, mask=None):
        keys = rows_at(j, BLK)
        k, v = k_ref[g, keys, :], v_ref[g, keys, :]
        turned = k.T
        dv, dk = None, None
        for n, h in enumerate(heads):
            probs = jnp.exp2(dot(k, queries[n], NT) * (SCALE * LOG2E) - lse_ref[h, 0:1, rows])
            if mask is not None:
                probs = jnp.where(mask, probs, 0.0)
            d_scores = (probs * (dot(v, grads[n], NT) - delta[h, 0:1, rows])).astype(jnp.bfloat16)
            dv_more, dk_more = dot(probs.astype(jnp.bfloat16), grads[n]), dot(d_scores, queries[n])
            dv, dk = (dv_more, dk_more) if dv is None else (dv + dv_more, dk + dk_more)
            dq_acc[n] += dot(turned, d_scores)
        dv_acc[g, keys, :] += dv
        dk_acc[g, keys, :] += dk

    def loop(j, carry):
        tile(j)
        return carry

    tile(i, block_mask(0, flags, i))
    lax.fori_loop(0, i, loop, 0)
    for n, h in enumerate(heads):
        low, total = unrope(dq_acc[n].T, qr_ref[h, rows, :], gq_ref[...], rows)
        dbuf[rows, spans[n]] = low
        dg_ref[0] += total

    @pl.when(step == 4 * KH - 1)
    def _():
        for gg_at in range(KH):

            def finish(r, carry):
                rows = rows_at(r, 256)
                low, total = unrope(dk_acc[gg_at, rows, :], kr_ref[gg_at, rows, :], gk_ref[...], rows)
                dbuf[rows, pl.ds((QH + gg_at) * HEAD_DIM, HEAD_DIM)] = low
                dbuf[rows, pl.ds((QH + KH + gg_at) * HEAD_DIM, HEAD_DIM)] = dv_acc[gg_at, rows, :].astype(jnp.bfloat16)
                dg_ref[1] += total
                return carry

            lax.fori_loop(0, 8, finish, 0)
        outs = [pltpu.make_async_copy(dbuf, d_out, out_sem.at[0])]
        outs[0].start()
        for kind in (ME, NEAR):
            wide_sum(kind, early)
            net.arrived(first_of[kind])
            wide_sum(kind, late)
            deep_sum(kind)
        outs += [
            pltpu.make_async_copy(og.at[pl.ds(0, 2)], og_out, out_sem.at[2]),
            pltpu.make_async_copy(od.at[pl.ds(0, 2)], od_out, out_sem.at[3]),
        ]
        for copy in outs[1:]:
            copy.start()
        net.arrived(go_go_l, go_go_d, go_go_c, go_far_a, go_far_b)
        own_go.wait()
        net.sent()
        home.wait()
        for copy in outs:
            copy.wait()


def attend_back(flags, q, k, v, o, db, wo, lse, qr, kr, cosine, sine, ggu, gdb, rb, res, gq, gk):
    bf16, f32 = jnp.bfloat16, jnp.float32
    any_spec = pl.BlockSpec(memory_space=pl.ANY)
    gain = pl.BlockSpec((1, HEAD_DIM), lambda s, f: (0, 0))
    copies = 40

    def vm(a):
        return pltpu.VMEM(a.shape, a.dtype)

    return pl.pallas_call(
        attend_back_kernel,
        out_shape=(
            jax.ShapeDtypeStruct((SEQ_ROWS, 1024), bf16),
            jax.ShapeDtypeStruct((2048, 256), bf16),
            jax.ShapeDtypeStruct((2, 2, 2, 64, HALF_FF), bf16),
            jax.ShapeDtypeStruct((2, 2, 192, 512), bf16),
            jax.ShapeDtypeStruct((2, 64, HALF_FF), bf16),
            jax.ShapeDtypeStruct((192, 512), bf16),
            jax.ShapeDtypeStruct((2, ROWS, MODEL_DIM), bf16),
            jax.ShapeDtypeStruct((2, 8, HEAD_DIM), f32),
        ),
        grid_spec=pltpu.PrefetchScalarGridSpec(
            num_scalar_prefetch=1,
            grid=(4 * KH,),
            in_specs=[any_spec] * 15 + [gain] * 2,
            out_specs=[any_spec] * 7 + [pl.BlockSpec((2, 8, HEAD_DIM), lambda s, f: (0, 0, 0))],
            scratch_shapes=[vm(q), vm(k), vm(v), vm(o), pltpu.VMEM((SEQ_ROWS, MODEL_DIM), bf16), vm(wo), vm(lse), vm(qr), vm(kr)]
            + [vm(cosine), vm(sine)]
            + [
                pltpu.VMEM((SEQ_ROWS, QH * HEAD_DIM), bf16),
                pltpu.VMEM((QH, 8, SEQ_ROWS), f32),
                pltpu.VMEM((SEQ_ROWS, 1024), bf16),
                pltpu.VMEM((2, HEAD_DIM, BLK), f32),
                pltpu.VMEM((KH, SEQ_ROWS, HEAD_DIM), f32),
                pltpu.VMEM((KH, SEQ_ROWS, HEAD_DIM), f32),
                pltpu.VMEM((4, 2, 2, 64, HALF_FF), bf16),
                pltpu.VMEM((4, 2, 192, 512), bf16),
                pltpu.VMEM((4, 2, 2, 64, HALF_FF), bf16),
                pltpu.VMEM((4, 2, 192, 512), bf16),
                pltpu.VMEM((2, 2, 64, HALF_FF), bf16),
                pltpu.VMEM((2, 192, 512), bf16),
                pltpu.VMEM((2, 64, HALF_FF), bf16),
                pltpu.VMEM((192, 512), bf16),
                pltpu.VMEM((512, MODEL_DIM), bf16),
                pltpu.SemaphoreType.DMA((copies,)),
                pltpu.SemaphoreType.DMA((copies,)),
                pltpu.SemaphoreType.DMA((11,)),
                pltpu.SemaphoreType.DMA((17,)),
                pltpu.SemaphoreType.DMA((4,)),
                pltpu.SemaphoreType.DMA((2,)),
                pltpu.SemaphoreType.DMA((2,)),
            ],
        ),
        compiler_params=pltpu.CompilerParams(
            collective_id=4, has_side_effects=True, vmem_limit_bytes=VMEM_LIMIT
        ),
        cost_estimate=pl.CostEstimate(
            flops=10 * QH * SEQ_ROWS * SEQ_ROWS * HEAD_DIM, bytes_accessed=40 << 20, transcendentals=QH * SEQ_ROWS * SEQ_ROWS
        ),
        name="attend_back",
    )(flags, q, k, v, o, db, wo, lse, qr, kr, cosine, sine, ggu, gdb, rb, res, gq, gk)


def tail_kernel(
    d_in, w_in, n_in, xs, og_in, od_in, fw_in, fd_in, goq_in, dr_ref, ga_ref, dgm_ref, dgh_ref,
    rq, rqo, fw, fd, gout, landed,
    d_ref, w_ref, n_ref, x_ref, goq, send_c, recv_c, send_l, recv_l, keep, gt,
    og, od, rx, rxd, rz, rzd, total_w, total_d,
    pq, work, wgo, ry, ryo, ox, oxo, rs, rso, gs, gr,
    send_sem, recv_sem, load_sem, back_send, back_recv,
):
    where = place()
    y, x, p, l, c = where
    peer = peers_of(x, y, p, l, c)
    red = Reduction(where)
    net = Plan(send_sem, recv_sem)
    second_of = {}
    t = 2 * l + c
    for n, kind in enumerate(KINDS[:2]):
        away = 1 - red.kept(kind)
        second_of[kind] = net.add(peer[red.second_peer(kind)], [(og_in.at[n, away], rx.at[n]), (od_in.at[n, away], rxd.at[n])])
    u_me, u_near = red.kept(ME), red.kept(NEAR)
    go_near = net.add(peer["l"], [(og.at[1], rz.at[1]), (od.at[1], rzd.at[1])])
    go_halves = net.add(peer["c"], [(total_w.at[1 - c], fw.at[c]), (total_d.at[1 - c], fd.at[c])])
    go_give_0 = net.add(peer["c"], [(send_c.at[0], recv_c.at[0])])
    go_give_1 = net.add(peer["c"], [(send_c.at[1], recv_c.at[1])])
    halves = [pl.ds(k * ROWS, ROWS) for k in range(2)]
    go_cross = [net.add(peer["l"], [(send_l.at[half], recv_l.at[half])]) for half in halves]

    def group(yy, xx, pp):
        return (yy * 2 + xx) * 2 + pp

    def moved(sources, groups, targets, at=0):
        return [(src.at[one], dst.at[at + k]) for k, one in enumerate(groups) for src, dst in zip(sources, targets)]

    source, working, small = (pq, goq), (work, wgo), (rs, rso)
    base, across = group(y, x, p), group(y, x, 1 - p)
    give_y = (group(1 - y, 0, p), group(1 - y, 1, p))
    give_x = (group(0, 1 - x, 1 - p), group(1, 1 - x, 1 - p))
    go_own_y = [[net.add(peer["y"], moved((a,), give_y[k : k + 1], (b,), k)) for k in range(2)] for a, b in ((pq, ry), (goq_in, ryo))]
    go_other_x = [[net.add(peer["x"], moved((a,), give_x[k : k + 1], (b,), k)) for k in range(2)] for a, b in ((pq, ox), (goq_in, oxo))]
    go_own_x = [net.add(peer["x"], moved(working[k : k + 1], (group(y, 1 - x, p),), small[k : k + 1], 0)) for k in range(2)]
    go_other_y = [net.add(peer["y"], moved(working[k : k + 1], (group(1 - y, x, 1 - p),), small[k : k + 1], 1)) for k in range(2)]
    go_across = [net.add(peer["p"], moved(working[k : k + 1], (across,), small[k : k + 1], 2)) for k in range(2)]

    def parts(q):
        return [(work.at[base, rows_at(q, 32)], rq.at[t]), (wgo.at[base, rows_at(q, 64)], rqo.at[t])]

    go_last_l = net.add(peer["l"], parts(2 * (1 - l) + c))
    go_last_d = net.add(peer["d"], parts(2 * (1 - l) + 1 - c))
    go_last_c = net.add(peer["c"], parts(2 * l + 1 - c))
    go_gain = [net.add(peer[name], [(gs.at[k], gr.at[k])]) for k, name in enumerate(("c", "x", "y", "p", "l"))]
    home = Return(where, gt, landed, back_send, back_recv)

    def gain_hop(k):
        net.arrived(go_gain[k])
        gs[k + 1] = gs[k] + gr[k]
        if k + 1 < len(AXES):
            net.start(go_gain[k + 1])

    loads = [
        pltpu.make_async_copy(src, dst, load_sem.at[k])
        for k, (src, dst) in enumerate(
            [
                (d_in, d_ref), (w_in, w_ref), (n_in, n_ref), (goq_in, goq), (xs.at[rows_at(owned(p, l, c), OWN)], x_ref),
                (og_in.at[0, u_me], og.at[0]), (og_in.at[1, u_near], og.at[1]),
                (od_in.at[0, u_me], od.at[0]), (od_in.at[1, u_near], od.at[1]),
                (fw_in, rz.at[0]), (fd_in, rzd.at[0]),
            ]
        )
    ]
    for copy in loads:
        copy.start()
    greet(line_peers(p, l, c) + [peer["x"], peer["y"]])
    net.start(second_of[NEAR], second_of[ME], *go_own_y[1], *go_other_x[1])

    def project(ll, cc, write):
        part = d_ref[rows_at(owned(p, ll, cc), OWN), :]

        def chunk(k, carry):
            cols = rows_at(k, 256)
            write(cols, dot(part, w_ref[cols, :], NT))
            return carry

        lax.fori_loop(0, 4, chunk, 0)

    def give(k):
        def write(cols, value):
            send_c[k, :, cols] = value.astype(jnp.bfloat16)

        return write

    def hold(k):
        def write(cols, value):
            keep[k, :, cols] = value

        return write

    def add(k, at, left, right, place_at):
        total = left[at].astype(jnp.float32) + right[place_at].astype(jnp.float32)
        working[k][at] = total.astype(jnp.bfloat16)

    def first_sums(k):
        net.arrived(*go_other_x[k])
        for yy in (0, 1):
            add(k, group(yy, x, 1 - p), source[k], (ox, oxo)[k], yy)
        net.start(go_other_y[k])
        net.arrived(*go_own_y[k])
        for xx in (0, 1):
            add(k, group(y, xx, p), source[k], (ry, ryo)[k], xx)
        net.start(go_own_x[k])

    def second_sums(k):
        net.arrived(go_other_y[k])
        add(k, across, working[k], small[k], 1)
        net.start(go_across[k])
        net.arrived(go_own_x[k])
        add(k, base, working[k], small[k], 0)

    loads[0].wait()
    loads[1].wait()
    project(1 - l, 1 - c, give(0))
    net.start(go_give_0)
    project(1 - l, c, hold(0))
    net.arrived(go_give_0)
    send_l[...] = (keep[0] + recv_c[0].astype(jnp.float32)).astype(jnp.bfloat16)
    net.start(*go_cross)
    project(l, 1 - c, give(1))
    net.start(go_give_1)
    project(l, c, hold(1))
    for copy in loads[2:]:
        copy.wait()

    def grad_qkv(yy, xx):
        k = yy * 2 + xx
        value = dot(n_ref[:, rows_at(k, 256)], d_ref[...], TN).astype(jnp.bfloat16)
        pq[2 * k] = value[:128]
        pq[2 * k + 1] = value[128:]

    def start_if(index, groups):
        for k in range(2):

            @pl.when(index == k)
            def _():
                net.start(groups[k])

    def one_chunk(k, carry):
        yy, xx = jnp.where(k % 2 == 0, 1 - y, y), jnp.where(k < 2, 1 - x, x)
        grad_qkv(yy, xx)

        @pl.when(k < 2)
        def _():
            start_if(yy, go_other_x[0])

        @pl.when(k % 2 == 0)
        def _():
            start_if(xx, go_own_y[0])

        return carry

    gs[0] = jnp.zeros_like(gs[0])

    def rows_back(k, total):
        rows = rows_at(k, 64)
        value = x_ref[rows, :].astype(jnp.float32)
        grad = keep[1, rows, :] + recv_c[1, rows, :].astype(jnp.float32) + recv_l[rows, :].astype(jnp.float32)
        r = lax.rsqrt(jnp.mean(value * value, axis=-1, keepdims=True) + EPS)
        scaled = value * r
        gained = grad * ga_ref[...]
        back = r * (gained - scaled * jnp.mean(scaled * gained, axis=-1, keepdims=True))
        gt[rows, :] = (dr_ref[rows, :] + back).astype(jnp.bfloat16)
        return total + jnp.sum(grad * scaled, axis=0, keepdims=True)

    lax.fori_loop(0, 2, one_chunk, 0)
    net.arrived(go_give_1, go_cross[0])
    d_attn = lax.fori_loop(0, 4, rows_back, jnp.zeros((1, MODEL_DIM), jnp.float32))
    home.start_one(0)
    lax.fori_loop(2, 4, one_chunk, 0)
    first_sums(1)
    net.arrived(go_cross[1])
    d_attn = lax.fori_loop(4, 8, rows_back, d_attn)
    home.start_one(1)
    net.arrived(second_of[NEAR])
    og[1] = (og[1].astype(jnp.float32) + rx[1].astype(jnp.float32)).astype(jnp.bfloat16)
    od[1] = (od[1].astype(jnp.float32) + rxd[1].astype(jnp.float32)).astype(jnp.bfloat16)
    net.start(go_near)
    first_sums(0)
    second_sums(1)
    d_mlp = jnp.sum(dgm_ref[...], axis=0, keepdims=True)
    for k in range(8):
        lanes = slice(k * 128, (k + 1) * 128)
        gs[0, k : k + 1, :] = d_attn[:, lanes]
        gs[0, 8 + k : 9 + k, :] = d_mlp[:, lanes]
    for k in range(2):
        gs[0, 16 + k : 17 + k, :] = jnp.sum(dgh_ref[k], axis=0, keepdims=True)
    net.start(go_gain[0])
    second_sums(0)
    gain_hop(0)
    net.arrived(second_of[ME])
    gain_hop(1)
    net.arrived(go_near)
    for cc in range(2):
        rows = pl.ds(32 * cc, 32)
        total_w[cc] = (
            og[0, :, rows, :].astype(jnp.float32) + rx[0, :, rows, :].astype(jnp.float32)
            + rz[0, :, rows, :].astype(jnp.float32) + rz[1, :, rows, :].astype(jnp.float32)
        )
        rows = pl.ds(96 * cc, 96)
        total_d[cc] = (
            od[0, rows, :].astype(jnp.float32) + rxd[0, rows, :].astype(jnp.float32)
            + rzd[0, rows, :].astype(jnp.float32) + rzd[1, rows, :].astype(jnp.float32)
        )
    net.start(go_halves)
    fw[c] = total_w[c]
    fd[c] = total_d[c]
    gain_hop(2)
    net.arrived(go_halves)
    for k in (1, 0):
        net.arrived(go_across[k])
        add(k, base, working[k], small[k], 2)
    net.start(go_last_l, go_last_d, go_last_c)
    rq[t] = work[base, rows_at(t, 32), :]
    rqo[t] = wgo[base, rows_at(t, 64), :]
    gain_hop(3)
    home.wait()
    gain_hop(4)
    gout[...] = gs[len(AXES)]
    net.arrived(go_last_l, go_last_d, go_last_c)
    net.sent()


def finish_kernel(
    rq, rqo, fw, fd, landed, result,
    output, tokens, out_query, out_key, out_value, out_out, out_gate, out_up, out_down,
):
    output[...] = result[...]
    tokens[...] = landed[...].astype(jnp.float32)
    for half in range(2):
        cols = slice(half * HALF_FF, (half + 1) * HALF_FF)
        out_gate[:, cols] = fw[half, 0]
        out_up[:, cols] = fw[half, 1]
        out_down[:, half * 512 : (half + 1) * 512] = fd[half]
    for q in range(4):
        value = rq[q].astype(jnp.float32)
        out_query[:, 512 * q : 512 * (q + 1)] = value[:, :512]
        out_key[:, 256 * q : 256 * (q + 1)] = value[:, 512:768]
        out_value[:, 256 * q : 256 * (q + 1)] = value[:, 768:]
        out_out[:, 256 * q : 256 * (q + 1)] = rqo[q].astype(jnp.float32)


def finish(rq, rqo, fw, fd, landed, result):
    f32 = jnp.float32
    vmem = pl.BlockSpec(memory_space=pltpu.VMEM)
    return pl.pallas_call(
        finish_kernel,
        out_shape=(
            jax.ShapeDtypeStruct((2, ROWS, MODEL_DIM), jnp.bfloat16),
            jax.ShapeDtypeStruct((2, ROWS, MODEL_DIM), f32),
            jax.ShapeDtypeStruct((32, 2048), f32),
            jax.ShapeDtypeStruct((32, 1024), f32),
            jax.ShapeDtypeStruct((32, 1024), f32),
            jax.ShapeDtypeStruct((64, 1024), f32),
            jax.ShapeDtypeStruct((32, FF), f32),
            jax.ShapeDtypeStruct((32, FF), f32),
            jax.ShapeDtypeStruct((96, 1024), f32),
        ),
        in_specs=[vmem] * 6,
        out_specs=[vmem] * 9,
        compiler_params=pltpu.CompilerParams(vmem_limit_bytes=VMEM_LIMIT),
        name="finish",
    )(rq, rqo, fw, fd, landed, result)


def tail(d, w, normed, xs, og, od, fw, fd, goq, d_resid, g_attn, d_g_mlp, d_g_heads):
    bf16, f32 = jnp.bfloat16, jnp.float32
    any_spec = pl.BlockSpec(memory_space=pl.ANY)
    vmem = pl.BlockSpec(memory_space=pltpu.VMEM)
    copies = 48
    wide, deep = (2, 64, HALF_FF), (192, 512)
    own = (OWN, MODEL_DIM)
    big, tall = (128, 1024), (256, 256)

    def vm(a):
        return pltpu.VMEM(a.shape, a.dtype)

    def low(*shape):
        return pltpu.VMEM(shape, bf16)

    goq = goq.reshape(8, 256, 256)
    return pl.pallas_call(
        tail_kernel,
        out_shape=(
            jax.ShapeDtypeStruct((4, 32, 1024), bf16),
            jax.ShapeDtypeStruct((4, 64, 256), bf16),
            jax.ShapeDtypeStruct((2, 2, 32, HALF_FF), f32),
            jax.ShapeDtypeStruct((2, 96, 512), f32),
            jax.ShapeDtypeStruct((24, 128), f32),
            jax.ShapeDtypeStruct((2, ROWS, MODEL_DIM), bf16),
        ),
        in_specs=[any_spec] * 9 + [vmem] * 4,
        out_specs=[vmem] * 6,
        scratch_shapes=[
            vm(d), vm(w), vm(normed), low(*own), vm(goq),
            low(2, *own), low(2, *own), low(*own), low(*own),
            pltpu.VMEM((2,) + own, f32),
            low(*own),
            low(2, *wide), low(2, *deep),
            low(2, *wide), low(2, *deep), low(2, *wide), low(2, *deep),
            pltpu.VMEM((2, 2, 32, HALF_FF), f32), pltpu.VMEM((2, 96, 512), f32),
            low(8, *big), low(8, *big), low(8, *tall),
            low(2, *big), low(2, *tall), low(2, *big), low(2, *tall), low(3, *big), low(3, *tall),
            pltpu.VMEM((6, 24, 128), f32), pltpu.VMEM((5, 24, 128), f32),
            pltpu.SemaphoreType.DMA((copies,)),
            pltpu.SemaphoreType.DMA((copies,)),
            pltpu.SemaphoreType.DMA((11,)),
            pltpu.SemaphoreType.DMA((2,)),
            pltpu.SemaphoreType.DMA((2,)),
        ],
        compiler_params=pltpu.CompilerParams(
            collective_id=5, has_side_effects=True, vmem_limit_bytes=VMEM_LIMIT
        ),
        name="tail_reduce",
    )(d, w, normed, xs, og, od, fw, fd, goq, d_resid, g_attn, d_g_mlp, d_g_heads)


def pick(value, index):
    return lax.dynamic_index_in_dim(value, index, 0, keepdims=False)


def fast_device(tokens, cotangent, starts, w_query, key_matrix, value_matrix, w_out, w_gate, w_up, w_down, gains):
    p = lax.axis_index("p")
    gn = jnp.pad(gains.astype(jnp.float32), (0, 952)).reshape(8, 128)
    half_steps = jnp.arange(HEAD_DIM // 2, dtype=jnp.float32)
    inverse = THETA ** (-2.0 * half_steps / HEAD_DIM)
    inverse = jnp.broadcast_to(jnp.concatenate([inverse, inverse])[None], (8, HEAD_DIM))
    own_starts = pick(starts, p)
    block_at = jnp.arange(SEQ_ROWS // PIECE, dtype=jnp.int32) * PIECE
    flags = jnp.any(own_starts[None, :] == block_at[:, None], axis=1).astype(jnp.int32)
    xs, w_qkv, woq, gf, wgu, wdn, cosine, sine = front(
        tokens, w_query, key_matrix, value_matrix, w_out, gn, w_gate, w_up, w_down, inverse
    )
    xs = xs.reshape(SEQ_ROWS, MODEL_DIM)
    gain_all = gf.reshape(32, 1024)[:, :72].reshape(2304)
    g_attn = gain_all[None, :1024]
    g_mlp = gain_all[None, 1024:2048]
    g_q = gain_all[None, 2048:2176]
    g_k = gain_all[None, 2176:]
    normed, q, k, v, q_raw, k_raw, attn, lse, wo, wgu, wdn = attend(
        flags, xs, w_qkv, g_attn, g_q, g_k, cosine, sine, woq, wgu, wdn
    )
    resid, mlp_in, wgu, wdn, wdx, dy = finish_resid(attn, wo, g_mlp, xs, cotangent, wgu, wdn)
    ggu, gdb, rb, d_resid, d_branch, result, d_g_mlp = feed_forward(
        mlp_in.reshape(1024, MODEL_DIM), dy.reshape(1024, MODEL_DIM), wgu, wdn, wdx, resid, g_mlp
    )
    d_qkv, goq, og, od, fw, fd, output, d_g_heads = attend_back(
        flags, q, k, v, attn, d_branch, wo, lse, q_raw, k_raw, cosine, sine, ggu, gdb, rb, result, g_q, g_k
    )
    rq, rqo, wide, deep, gains_sum, landed = tail(
        d_qkv, w_qkv, normed, xs, og, od, fw, fd, goq, d_resid, g_attn, d_g_mlp, d_g_heads
    )
    device = lax.axis_index(AXES)
    out_gains = lax.dynamic_slice(gains_sum.reshape(3072), (device * 72,), (72,))
    return (*finish(rq, rqo, wide, deep, landed, output), out_gains)


def fast_solution(mesh):
    wide = Mesh(mesh.devices.reshape(2, 2, 2, 2, 2), AXES)
    rows = ("y", "x")
    places = ("p", "l", "c")
    weight = P(AXES, None)
    return jax.shard_map(
        fast_device,
        mesh=wide,
        in_specs=(P(rows, places, None), P(rows, places, None), P(rows, None)) + (weight,) * 7 + (P(AXES),),
        out_specs=(P(rows, places, None), P(rows, places, None)) + (weight,) * 7 + (P(AXES),),
        check_vma=False,
    )


def solution(mesh):
    if dict(mesh.shape) == {"dp": 4, "ctx": 8}:
        return fast_solution(mesh)
    return generic_solution(mesh)
```

```python
import functools
import math

import jax
import jax.numpy as jnp
from jax import lax
from jax.experimental import pallas as pl
from jax.experimental.pallas import tpu as pltpu
from jax.sharding import Mesh
from jax.sharding import PartitionSpec as P

MODEL_DIM = 1024
QUERY_HEADS = 16
KEY_VALUE_HEADS = 8
HEAD_DIM = 128
SEQUENCE_TOKENS = 2048
PIECE = 256
NPIECE = 4


EPS = 1e-06
THETA = 1000000.0
NEG = -1e30


def rms_norm(incoming_values, gain_vector):
    return (
        incoming_values
        * lax.rsqrt(jnp.mean(incoming_values * incoming_values, axis=-1, keepdims=True) + EPS)
        * gain_vector
    )


def rope_tables(positions):
    half_steps = jnp.arange(HEAD_DIM // 2, dtype=jnp.float32)
    inverse = THETA ** (-2.0 * half_steps / HEAD_DIM)
    angles = positions.astype(jnp.float32)[:, None] * inverse[None, :]
    angles = jnp.concatenate([angles, angles], axis=-1)
    return (jnp.cos(angles), jnp.sin(angles))


def rotate(incoming_values, cosine_table, sine_table):
    half_dim = HEAD_DIM // 2
    turned = jnp.concatenate(
        [-incoming_values[..., half_dim:], incoming_values[..., :half_dim]], axis=-1
    )
    return incoming_values * cosine_table[:, None, :] + turned * sine_table[:, None, :]


def per_head_route(unrotated_projection, gain_vector, cosine_table, sine_table, head_count):
    shaped = unrotated_projection.reshape(unrotated_projection.shape[:-1] + (head_count, HEAD_DIM))
    return rotate(rms_norm(shaped, gain_vector), cosine_table, sine_table).reshape(
        unrotated_projection.shape
    )


def piece_ids(positions, piece_starts):
    inside = (positions[:, None] >= piece_starts[None, :]) & (
        positions[:, None] < piece_starts[None, :] + PIECE
    )
    number = jnp.arange(1, NPIECE + 1, dtype=jnp.int32)
    return jnp.sum(jnp.where(inside, number[None, :], 0), axis=1) - 1


def visible(query_pos, query_id, key_pos, key_id):
    causal = key_pos[None, :] <= query_pos[:, None]
    same_piece = (query_id[:, None] == key_id[None, :]) & (query_id[:, None] >= 0)
    return causal | same_piece


def swiglu(gate_proj, up_proj):
    return jax.nn.silu(gate_proj) * up_proj


def block_extent(kv_count, per_head):
    target = max(1, 512 // per_head)
    chosen = 1
    for candidate in range(1, kv_count + 1):
        if kv_count % candidate == 0 and candidate <= target:
            chosen = candidate
    return chosen


def attend_forward(incoming_query, incoming_keys, incoming_values, allowed, head_group_block):
    sequence_rows = incoming_query.shape[0]
    query_group_factor = QUERY_HEADS // KEY_VALUE_HEADS
    scaling = 1.0 / math.sqrt(HEAD_DIM)
    query_per_head = incoming_query.reshape(
        sequence_rows, KEY_VALUE_HEADS, query_group_factor, HEAD_DIM
    )
    key_per_head = incoming_keys.reshape(incoming_keys.shape[0], KEY_VALUE_HEADS, HEAD_DIM)
    value_per_head = incoming_values.reshape(incoming_values.shape[0], KEY_VALUE_HEADS, HEAD_DIM)
    mixed_parts = []
    total_parts = []
    for head_offset in range(0, KEY_VALUE_HEADS, head_group_block):
        q_part = query_per_head[:, head_offset : head_offset + head_group_block]
        k_part = key_per_head[:, head_offset : head_offset + head_group_block]
        v_part = value_per_head[:, head_offset : head_offset + head_group_block]
        scores = (
            jnp.einsum("tagd,kad->agtk", q_part, k_part, preferred_element_type=jnp.float32)
            * scaling
        )
        scores = jnp.where(allowed[None, None], scores, NEG)
        row_max = jnp.max(scores, axis=-1, keepdims=True)
        exp_scores = jnp.exp(scores - row_max)
        summed = jnp.sum(exp_scores, axis=-1, keepdims=True)
        prob_low = (exp_scores / summed).astype(jnp.bfloat16)
        mixed_parts.append(
            jnp.einsum("agtk,kad->tagd", prob_low, v_part, preferred_element_type=jnp.float32)
        )
        total_parts.append(row_max + jnp.log(summed))
    mixed_out = jnp.concatenate(mixed_parts, axis=1).reshape(sequence_rows, QUERY_HEADS * HEAD_DIM)
    return (mixed_out, jnp.concatenate(total_parts, axis=0))


def attend_backward(
    incoming_query,
    incoming_keys,
    incoming_values,
    allowed,
    log_total,
    mixed_gradient,
    head_group_block,
):
    sequence_rows = incoming_query.shape[0]
    key_row_matrix = incoming_keys.shape[0]
    query_group_factor = QUERY_HEADS // KEY_VALUE_HEADS
    scaling = 1.0 / math.sqrt(HEAD_DIM)
    query_per_head = incoming_query.reshape(
        sequence_rows, KEY_VALUE_HEADS, query_group_factor, HEAD_DIM
    )
    gradient_per_head = mixed_gradient.reshape(
        sequence_rows, KEY_VALUE_HEADS, query_group_factor, HEAD_DIM
    )
    key_per_head = incoming_keys.reshape(key_row_matrix, KEY_VALUE_HEADS, HEAD_DIM)
    value_per_head = incoming_values.reshape(key_row_matrix, KEY_VALUE_HEADS, HEAD_DIM)
    dq_parts = []
    key_gradient_pieces = []
    value_gradient_pieces = []
    for head_offset in range(0, KEY_VALUE_HEADS, head_group_block):
        q_part = query_per_head[:, head_offset : head_offset + head_group_block]
        g_part = gradient_per_head[:, head_offset : head_offset + head_group_block]
        k_part = key_per_head[:, head_offset : head_offset + head_group_block]
        v_part = value_per_head[:, head_offset : head_offset + head_group_block]
        scores = (
            jnp.einsum("tagd,kad->agtk", q_part, k_part, preferred_element_type=jnp.float32)
            * scaling
        )
        scores = jnp.where(allowed[None, None], scores, NEG)
        prob_all = jnp.exp(scores - log_total[head_offset : head_offset + head_group_block])
        prob_low = prob_all.astype(jnp.bfloat16)
        d_probs = jnp.einsum("tagd,kad->agtk", g_part, v_part, preferred_element_type=jnp.float32)
        row_dot = jnp.sum(prob_all * d_probs, axis=-1, keepdims=True)
        d_scores = (prob_all * (d_probs - row_dot)).astype(jnp.bfloat16)
        dq_parts.append(
            jnp.einsum("agtk,kad->tagd", d_scores, k_part, preferred_element_type=jnp.float32)
            * scaling
        )
        key_gradient_pieces.append(
            jnp.einsum("agtk,tagd->kad", d_scores, q_part, preferred_element_type=jnp.float32)
            * scaling
        )
        value_gradient_pieces.append(
            jnp.einsum("agtk,tagd->kad", prob_low, g_part, preferred_element_type=jnp.float32)
        )
    d_query = jnp.concatenate(dq_parts, axis=1).reshape(sequence_rows, QUERY_HEADS * HEAD_DIM)
    key_gradient = jnp.concatenate(key_gradient_pieces, axis=1).reshape(
        key_row_matrix, KEY_VALUE_HEADS * HEAD_DIM
    )
    value_gradient = jnp.concatenate(value_gradient_pieces, axis=1).reshape(
        key_row_matrix, KEY_VALUE_HEADS * HEAD_DIM
    )
    return (d_query, key_gradient, value_gradient)


def generic_device(
    tokens, cotangent, starts, w_query, key_matrix, value_matrix, w_out, w_gate, w_up, w_down, gains
):
    sequence_count, sequence_rows, model_width = tokens.shape
    number_of_rows = sequence_count * sequence_rows
    head_group_block = block_extent(KEY_VALUE_HEADS, QUERY_HEADS // KEY_VALUE_HEADS * sequence_rows)
    attn_set = (
        lax.all_gather(w_query, ("dp", "ctx"), axis=0, tiled=True),
        lax.all_gather(key_matrix, ("dp", "ctx"), axis=0, tiled=True),
        lax.all_gather(value_matrix, ("dp", "ctx"), axis=0, tiled=True),
        lax.all_gather(w_out, ("dp", "ctx"), axis=0, tiled=True),
        lax.all_gather(gains, ("dp", "ctx"), axis=0, tiled=True),
    )
    mlp_set = (
        lax.all_gather(w_gate, ("dp", "ctx"), axis=0, tiled=True),
        lax.all_gather(w_up, ("dp", "ctx"), axis=0, tiled=True),
        lax.all_gather(w_down, ("dp", "ctx"), axis=0, tiled=True),
    )
    gain_all = attn_set[4].astype(jnp.float32)
    g_attn = gain_all[:MODEL_DIM]
    g_mlp = gain_all[MODEL_DIM : 2 * MODEL_DIM]
    g_query = gain_all[2 * MODEL_DIM : 2 * MODEL_DIM + HEAD_DIM]
    key_grad_total = gain_all[2 * MODEL_DIM + HEAD_DIM :]
    positions = lax.axis_index("ctx") * sequence_rows + jnp.arange(sequence_rows, dtype=jnp.int32)
    key_places = jnp.arange(SEQUENCE_TOKENS, dtype=jnp.int32)
    cosine_table, sine_table = rope_tables(positions)

    def query_map(unrotated_projection, gain_vector):
        return per_head_route(
            unrotated_projection, gain_vector, cosine_table, sine_table, QUERY_HEADS
        )

    def key_map(unrotated_projection, gain_vector):
        return per_head_route(
            unrotated_projection, gain_vector, cosine_table, sine_table, KEY_VALUE_HEADS
        )

    flat_in = tokens.reshape(number_of_rows, model_width).astype(jnp.float32)
    normed = rms_norm(flat_in, g_attn).astype(jnp.bfloat16)
    query_raw = jnp.dot(normed, attn_set[0], preferred_element_type=jnp.float32).reshape(
        sequence_count, sequence_rows, QUERY_HEADS * HEAD_DIM
    )
    key_unrotated = jnp.dot(normed, attn_set[1], preferred_element_type=jnp.float32).reshape(
        sequence_count, sequence_rows, KEY_VALUE_HEADS * HEAD_DIM
    )
    value_reduced = jnp.dot(normed, attn_set[2], preferred_element_type=jnp.float32).astype(
        jnp.bfloat16
    )
    value_reduced = value_reduced.reshape(sequence_count, sequence_rows, KEY_VALUE_HEADS * HEAD_DIM)
    query_reduced = query_map(query_raw, g_query).astype(jnp.bfloat16)
    key_reduced = key_map(key_unrotated, key_grad_total).astype(jnp.bfloat16)
    mask_list = []
    mixed_list = []
    total_list = []
    for seq_index in range(sequence_count):
        query_ids = piece_ids(positions, starts[seq_index])
        key_ids = piece_ids(key_places, starts[seq_index])
        allowed = visible(positions, query_ids, key_places, key_ids)
        key_full, value_full = (
            lax.all_gather(key_reduced[seq_index], "ctx", axis=0, tiled=True),
            lax.all_gather(value_reduced[seq_index], "ctx", axis=0, tiled=True),
        )
        mixed_out, log_total = attend_forward(
            query_reduced[seq_index], key_full, value_full, allowed, head_group_block
        )
        mask_list.append(allowed)
        mixed_list.append(mixed_out)
        total_list.append(log_total)
    attn_low = (
        jnp.stack(mixed_list).reshape(number_of_rows, QUERY_HEADS * HEAD_DIM).astype(jnp.bfloat16)
    )
    residual = flat_in + jnp.dot(attn_low, attn_set[3], preferred_element_type=jnp.float32)
    mlp_in = rms_norm(residual, g_mlp).astype(jnp.bfloat16)
    gate_proj = jnp.dot(mlp_in, mlp_set[0], preferred_element_type=jnp.float32)
    up_proj = jnp.dot(mlp_in, mlp_set[1], preferred_element_type=jnp.float32)
    hidden = swiglu(gate_proj, up_proj).astype(jnp.bfloat16)
    result = residual + jnp.dot(hidden, mlp_set[2], preferred_element_type=jnp.float32)
    output = result.astype(jnp.bfloat16).reshape(tokens.shape)
    mlp_back = (
        lax.all_gather(w_gate, ("dp", "ctx"), axis=0, tiled=True),
        lax.all_gather(w_up, ("dp", "ctx"), axis=0, tiled=True),
        lax.all_gather(w_down, ("dp", "ctx"), axis=0, tiled=True),
    )
    grad_flat = cotangent.reshape(number_of_rows, model_width)
    grad_down = jnp.dot(hidden.T, grad_flat, preferred_element_type=jnp.float32)
    d_hidden = jnp.dot(grad_flat, mlp_back[2].T, preferred_element_type=jnp.float32)
    swiglu_pull = jax.vjp(swiglu, gate_proj, up_proj)[1]
    d_gate, d_up = swiglu_pull(d_hidden)
    d_gate = d_gate.astype(jnp.bfloat16)
    d_up = d_up.astype(jnp.bfloat16)
    grad_gate = jnp.dot(mlp_in.T, d_gate, preferred_element_type=jnp.float32)
    grad_up = jnp.dot(mlp_in.T, d_up, preferred_element_type=jnp.float32)
    mlp_grads = (
        lax.psum_scatter(grad_gate, ("dp", "ctx"), scatter_dimension=0, tiled=True),
        lax.psum_scatter(grad_up, ("dp", "ctx"), scatter_dimension=0, tiled=True),
        lax.psum_scatter(grad_down, ("dp", "ctx"), scatter_dimension=0, tiled=True),
    )
    d_mlp_in = jnp.dot(d_gate, mlp_back[0].T, preferred_element_type=jnp.float32)
    d_mlp_in = d_mlp_in + jnp.dot(d_up, mlp_back[1].T, preferred_element_type=jnp.float32)
    mlp_norm_pull = jax.vjp(rms_norm, residual, g_mlp)[1]
    d_resid_norm, d_g_mlp = mlp_norm_pull(d_mlp_in)
    d_resid = grad_flat.astype(jnp.float32) + d_resid_norm
    attn_back = (
        lax.all_gather(w_query, ("dp", "ctx"), axis=0, tiled=True),
        lax.all_gather(key_matrix, ("dp", "ctx"), axis=0, tiled=True),
        lax.all_gather(value_matrix, ("dp", "ctx"), axis=0, tiled=True),
        lax.all_gather(w_out, ("dp", "ctx"), axis=0, tiled=True),
        lax.all_gather(gains, ("dp", "ctx"), axis=0, tiled=True),
    )
    d_branch = d_resid.astype(jnp.bfloat16)
    grad_out = jnp.dot(attn_low.T, d_branch, preferred_element_type=jnp.float32)
    d_attn = jnp.dot(d_branch, attn_back[3].T, preferred_element_type=jnp.float32).astype(
        jnp.bfloat16
    )
    d_attn = d_attn.reshape(sequence_count, sequence_rows, QUERY_HEADS * HEAD_DIM)
    dq_list = []
    dk_list = []
    value_gradient_list = []
    for seq_index in range(sequence_count):
        key_full, value_full = (
            lax.all_gather(key_reduced[seq_index], "ctx", axis=0, tiled=True),
            lax.all_gather(value_reduced[seq_index], "ctx", axis=0, tiled=True),
        )
        d_query_seq, d_key_full, d_value_full = attend_backward(
            query_reduced[seq_index],
            key_full,
            value_full,
            mask_list[seq_index],
            total_list[seq_index],
            d_attn[seq_index],
            head_group_block,
        )
        d_key_seq, d_value_seq = (
            lax.psum_scatter(
                d_key_full.astype(jnp.bfloat16), "ctx", scatter_dimension=0, tiled=True
            ).astype(jnp.float32),
            lax.psum_scatter(
                d_value_full.astype(jnp.bfloat16), "ctx", scatter_dimension=0, tiled=True
            ).astype(jnp.float32),
        )
        dq_list.append(d_query_seq)
        dk_list.append(d_key_seq)
        value_gradient_list.append(d_value_seq)
    d_query = jnp.stack(dq_list)
    key_gradient = jnp.stack(dk_list)
    value_gradient_reduced = (
        jnp.stack(value_gradient_list)
        .reshape(number_of_rows, KEY_VALUE_HEADS * HEAD_DIM)
        .astype(jnp.bfloat16)
    )
    query_pull = jax.vjp(query_map, query_raw, g_query)[1]
    d_query_raw, d_g_query = query_pull(d_query)
    key_pull = jax.vjp(key_map, key_unrotated, key_grad_total)[1]
    key_gradient_unrotated, d_g_key = key_pull(key_gradient)
    d_query_low = d_query_raw.reshape(number_of_rows, QUERY_HEADS * HEAD_DIM).astype(jnp.bfloat16)
    key_gradient_reduced = key_gradient_unrotated.reshape(
        number_of_rows, KEY_VALUE_HEADS * HEAD_DIM
    ).astype(jnp.bfloat16)
    grad_query = jnp.dot(normed.T, d_query_low, preferred_element_type=jnp.float32)
    grad_key = jnp.dot(normed.T, key_gradient_reduced, preferred_element_type=jnp.float32)
    grad_value = jnp.dot(normed.T, value_gradient_reduced, preferred_element_type=jnp.float32)
    d_normed = jnp.dot(d_query_low, attn_back[0].T, preferred_element_type=jnp.float32)
    d_normed = d_normed + jnp.dot(
        key_gradient_reduced, attn_back[1].T, preferred_element_type=jnp.float32
    )
    d_normed = d_normed + jnp.dot(
        value_gradient_reduced, attn_back[2].T, preferred_element_type=jnp.float32
    )
    input_pull = jax.vjp(rms_norm, flat_in, g_attn)[1]
    d_input_norm, d_g_attn = input_pull(d_normed)
    grad_tokens = (d_resid + d_input_norm).reshape(tokens.shape)
    grad_gains = jnp.concatenate([d_g_attn, d_g_mlp, d_g_query, d_g_key])
    attn_grads = (
        lax.psum_scatter(grad_query, ("dp", "ctx"), scatter_dimension=0, tiled=True),
        lax.psum_scatter(grad_key, ("dp", "ctx"), scatter_dimension=0, tiled=True),
        lax.psum_scatter(grad_value, ("dp", "ctx"), scatter_dimension=0, tiled=True),
        lax.psum_scatter(grad_out, ("dp", "ctx"), scatter_dimension=0, tiled=True),
        lax.psum_scatter(grad_gains, ("dp", "ctx"), scatter_dimension=0, tiled=True),
    )
    return (
        output,
        grad_tokens,
        attn_grads[0],
        attn_grads[1],
        attn_grads[2],
        attn_grads[3],
        mlp_grads[0],
        mlp_grads[1],
        mlp_grads[2],
        attn_grads[4],
    )


def generic_solution(mesh):
    return jax.shard_map(
        generic_device,
        mesh=mesh,
        in_specs=(
            P("dp", "ctx", None),
            P("dp", "ctx", None),
            P("dp", None),
            P(("dp", "ctx"), None),
            P(("dp", "ctx"), None),
            P(("dp", "ctx"), None),
            P(("dp", "ctx"), None),
            P(("dp", "ctx"), None),
            P(("dp", "ctx"), None),
            P(("dp", "ctx"), None),
            P(("dp", "ctx")),
        ),
        out_specs=(
            P("dp", "ctx", None),
            P("dp", "ctx", None),
            P(("dp", "ctx"), None),
            P(("dp", "ctx"), None),
            P(("dp", "ctx"), None),
            P(("dp", "ctx"), None),
            P(("dp", "ctx"), None),
            P(("dp", "ctx"), None),
            P(("dp", "ctx"), None),
            P(("dp", "ctx")),
        ),
        check_vma=False,
    )


AXES = ("y", "x", "p", "l", "c")
FF = 3072
HALF_FF = FF // 2
ROWS = 256
SEQ_ROWS = SEQUENCE_TOKENS
OWN = SEQ_ROWS // 4
BLK = 512
NBLK = SEQ_ROWS // BLK
QH = 4
KH = 2
MESH = pl.DeviceIdType.MESH
SCALE = 1.0 / math.sqrt(HEAD_DIM)
LOG2E = 1.4426950408889634
VMEM_LIMIT = 62 * 1024 * 1024
NT = (((1,), (1,)), ((), ()))
TN = (((0,), (0,)), ((), ()))


def dot(a, b, dims=None):
    if dims is None:
        dims = (((1,), (0,)), ((), ()))
    return lax.dot_general(a, b, dims, preferred_element_type=jnp.float32)


def greet(peers):
    barrier = pltpu.get_barrier_semaphore()
    for peer in peers:
        pl.semaphore_signal(barrier, inc=1, device_id=peer, device_id_type=MESH)
    pl.semaphore_wait(barrier, len(peers))


class Plan:
    def __init__(self, send_sem, recv_sem):
        self.send_sem = send_sem
        self.recv_sem = recv_sem
        self.count = 0
        self.entries = []

    def add(self, peer, pairs):
        self.entries.append((peer, pairs, self.count))
        self.count += len(pairs)
        return len(self.entries) - 1

    def copies(self, name):
        peer, pairs, at = self.entries[name]
        return [
            pltpu.make_async_remote_copy(
                src_ref=src,
                dst_ref=dst,
                send_sem=self.send_sem.at[at + k],
                recv_sem=self.recv_sem.at[at + k],
                device_id=peer,
                device_id_type=MESH,
            )
            for k, (src, dst) in enumerate(pairs)
        ]

    def start(self, *names):
        for name in names:
            for copy in self.copies(name):
                copy.start()

    def arrived(self, *names):
        for name in names:
            for copy in self.copies(name):
                copy.wait_recv()

    def sent(self):
        for name in range(len(self.entries)):
            for copy in self.copies(name):
                copy.wait_send()


def place():
    return tuple(lax.axis_index(name) for name in AXES)


def peers_of(x, y, p, l, c):
    return {
        "c": {"c": 1 - c},
        "l": {"l": 1 - l},
        "d": {"l": 1 - l, "c": 1 - c},
        "p": {"p": 1 - p},
        "x": {"x": 1 - x},
        "y": {"y": 1 - y},
    }


def owned(p, l, c):
    return 2 * c + (p + l + c) % 2


def rows_at(index, size, count=1):
    return pl.ds(pl.multiple_of(index * size, size), size * count)


def in_place(*refs):
    return [(ref, ref) for ref in refs]


def front_kernel(tok, wq, wk, wv, wo, gn, wg, wu, wd, inverse, xs, wa, woq, gf, wgu, wdn, cosine, sine, send_sem, recv_sem, in_sem, local_sem, *staged):
    y, x, p, l, c = place()
    peer = peers_of(x, y, p, l, c)
    block = 4 * p + 2 * l + c
    group = (y * 2 + x) * 8
    me = group + block
    t = 2 * l + c
    net = Plan(send_sem, recv_sem)

    def quarter(q):
        return [
            (wq.at[:, rows_at(q, 512)], wa.at[rows_at(me, 32), pl.ds(0, 512)]),
            (wk.at[:, rows_at(q, 256)], wa.at[rows_at(me, 32), pl.ds(512, 256)]),
            (wv.at[:, rows_at(q, 256)], wa.at[rows_at(me, 32), pl.ds(768, 256)]),
            (wo.at[:, rows_at(q, 256)], woq.at[rows_at(me, 64)]),
            (gn, gf.at[me]),
        ]

    def half(h):
        return [
            (wg.at[:, rows_at(h, HALF_FF)], wgu.at[0, rows_at(me, 32)]),
            (wu.at[:, rows_at(h, HALF_FF)], wgu.at[1, rows_at(me, 32)]),
            (wd.at[:, rows_at(h, 512)], wdn.at[rows_at(me, 96)]),
        ]

    def span(base, piece):
        if piece < 2:
            return in_place(wa.at[rows_at(base // 2 + piece, 64)])
        return in_place(woq.at[rows_at(base // 4, 256)], gf.at[pl.ds(base, 4)])

    def chip(yy, xx, pp, ll):
        slot = (yy * 2 + xx) * 4 + 2 * pp + ll
        return in_place(wgu.at[:, rows_at(slot, 64)], wdn.at[rows_at(slot, 192)])

    mine, other = group + 4 * p, group + 4 * (1 - p)
    go_first_l = net.add(peer["l"], quarter(2 * (1 - l) + c))
    go_first_d = net.add(peer["d"], quarter(2 * (1 - l) + 1 - c))
    go_first_c = net.add(peer["c"], quarter(2 * l + 1 - c))
    go_near = net.add(peer["l"], [(tok.at[p], xs.at[block])])
    upper, lower = pl.ds(0, ROWS // 2), pl.ds(ROWS // 2, ROWS // 2)
    go_far_0 = net.add(peer["p"], [(tok.at[1 - p, upper], xs.at[block, upper])])
    go_far_1 = net.add(peer["p"], [(tok.at[1 - p, lower], xs.at[block, lower])])
    go_near_c = net.add(peer["c"], [(tok.at[p], xs.at[block])])
    pieces = range(3)
    go_across = [net.add(peer["p"], span(mine, k)) for k in pieces]
    go_own_x = [net.add(peer["x"], span(mine, k)) for k in pieces]
    go_near_relay = net.add(peer["c"], in_place(xs.at[block ^ 2]))
    go_own_y = [net.add(peer["y"], span(mine, k) + span((y * 2 + 1 - x) * 8 + 4 * p, k)) for k in pieces]
    go_other_y = [net.add(peer["y"], span(other, k)) for k in pieces]
    go_far_l0 = net.add(peer["l"], in_place(xs.at[block ^ 4, upper]))
    go_far_l1 = net.add(peer["l"], in_place(xs.at[block ^ 4, lower]))
    go_far_relay = net.add(peer["c"], in_place(xs.at[block ^ 4]))
    go_other_x = [net.add(peer["x"], span(other, k) + span(((1 - y) * 2 + x) * 8 + 4 * (1 - p), k)) for k in pieces]
    go_far_l_relay = net.add(peer["c"], in_place(xs.at[block ^ 6]))
    go_mlp_c = net.add(peer["c"], half(1 - c))
    go_mlp_near = net.add(peer["l"], chip(y, x, p, l))
    go_mlp_x = net.add(peer["x"], chip(y, x, p, l))
    moves = quarter(t) + half(c) + [(tok.at[p], xs.at[block])]
    taken = [pltpu.make_async_copy(src, stage, in_sem.at[k]) for k, ((src, dst), stage) in enumerate(zip(moves, staged))]
    own = [pltpu.make_async_copy(stage, dst, local_sem.at[k]) for k, ((src, dst), stage) in enumerate(zip(moves, staged))]
    for copy in taken:
        copy.start()
    greet(list(peer.values()))
    net.start(go_first_l, go_first_d, go_first_c, go_far_0, go_near_c, go_mlp_c)
    for copy in taken:
        copy.wait()
    for copy in own:
        copy.start()

    def table(first, last):
        def chunk(k, carry):
            rows = rows_at(k, 64)
            position = (lax.broadcasted_iota(jnp.int32, (64, HEAD_DIM), 0) + k * 64).astype(jnp.float32)
            lane = lax.broadcasted_iota(jnp.int32, (64, HEAD_DIM), 1)
            angle = position * inverse[0:1, :]
            cosine[rows, :] = jnp.cos(angle)
            sine[rows, :] = jnp.where(lane < HEAD_DIM // 2, -1.0, 1.0) * jnp.sin(angle)
            return carry

        lax.fori_loop(first, last, chunk, 0)

    for copy in own:
        copy.wait()
    net.arrived(go_first_l, go_first_d, go_first_c)
    net.start(*go_across, *go_own_x, go_near)
    table(0, 12)
    for k in pieces:
        net.arrived(go_across[k])
        net.start(go_other_y[k])
    net.start(go_far_1)
    net.arrived(go_mlp_c)
    net.start(go_mlp_x)
    net.arrived(go_near)
    net.start(go_near_relay)
    for k in pieces:
        net.arrived(go_other_y[k])
        net.start(go_other_x[k])
    net.arrived(*go_own_x)
    net.start(*go_own_y)
    net.arrived(go_far_0)
    net.start(go_far_l0)
    table(12, 32)
    net.arrived(go_far_1)
    net.start(go_far_l1, go_far_relay, go_mlp_near)
    net.arrived(go_far_l0, go_far_l1)
    net.start(go_far_l_relay)
    net.arrived(go_near_c, go_near_relay, go_far_relay, go_far_l_relay, *go_own_y, *go_other_x, go_mlp_x, go_mlp_near)
    net.sent()


def front(tok, wq, wk, wv, wo, gn, wg, wu, wd, inverse):
    any_spec = pl.BlockSpec(memory_space=pl.ANY)
    copies = 64
    bf16 = jnp.bfloat16
    return pl.pallas_call(
        front_kernel,
        out_shape=(
            jax.ShapeDtypeStruct((8, ROWS, MODEL_DIM), bf16),
            jax.ShapeDtypeStruct((1024, 1024), bf16),
            jax.ShapeDtypeStruct((2048, 256), bf16),
            jax.ShapeDtypeStruct((32, 8, 128), jnp.float32),
            jax.ShapeDtypeStruct((2, MODEL_DIM, HALF_FF), bf16),
            jax.ShapeDtypeStruct((FF, 512), bf16),
            jax.ShapeDtypeStruct((SEQ_ROWS, HEAD_DIM), jnp.float32),
            jax.ShapeDtypeStruct((SEQ_ROWS, HEAD_DIM), jnp.float32),
        ),
        in_specs=[any_spec] * 9 + [pl.BlockSpec(memory_space=pltpu.VMEM)],
        out_specs=[any_spec] * 6 + [pl.BlockSpec(memory_space=pltpu.VMEM)] * 2,
        scratch_shapes=[
            pltpu.SemaphoreType.DMA((copies,)),
            pltpu.SemaphoreType.DMA((copies,)),
            pltpu.SemaphoreType.DMA((9,)),
            pltpu.SemaphoreType.DMA((9,)),
            pltpu.VMEM((32, 512), bf16),
            pltpu.VMEM((32, 256), bf16),
            pltpu.VMEM((32, 256), bf16),
            pltpu.VMEM((64, 256), bf16),
            pltpu.VMEM((8, 128), jnp.float32),
            pltpu.VMEM((32, HALF_FF), bf16),
            pltpu.VMEM((32, HALF_FF), bf16),
            pltpu.VMEM((96, 512), bf16),
            pltpu.VMEM((ROWS, MODEL_DIM), bf16),
        ],
        compiler_params=pltpu.CompilerParams(
            collective_id=0, has_side_effects=True, vmem_limit_bytes=VMEM_LIMIT
        ),
        name="front_gather",
    )(tok, wq, wk, wv, wo, gn, wg, wu, wd, inverse)


def line_peers(p, l, c):
    return [
        {"p": (p + a) % 2, "l": (l + b) % 2, "c": (c + d) % 2}
        for a in range(2)
        for b in range(2)
        for d in range(2)
        if a + b + d > 0
    ]


class Return:
    def __init__(self, where, src, dst, send_sem, recv_sem):
        self.where = where[2:]
        self.src, self.dst, self.send_sem, self.recv_sem = src, dst, send_sem, recv_sem

    def stays(self, index):
        p, l, c = self.where
        return (p == c) & (index == c)

    def local(self, c0):
        p, l, c = self.where
        return pltpu.make_async_copy(self.src.at[pl.ds(c0 * ROWS, ROWS)], self.dst.at[p], self.send_sem.at[c0])

    def remote(self, c0):
        p, l, c = self.where
        return pltpu.make_async_remote_copy(
            src_ref=self.src.at[pl.ds(c0 * ROWS, ROWS)],
            dst_ref=self.dst.at[p],
            send_sem=self.send_sem.at[c0],
            recv_sem=self.recv_sem.at[p],
            device_id={"p": c, "l": (p + l + c) % 2, "c": c0},
            device_id_type=MESH,
        )

    def start_one(self, c0):
        here = self.stays(c0)

        @pl.when(here)
        def _():
            self.local(c0).start()

        @pl.when(jnp.logical_not(here))
        def _():
            self.remote(c0).start()

    def start(self):
        for c0 in range(2):
            self.start_one(c0)

    def wait(self):
        p, l, c = self.where
        for c0 in range(2):
            here = self.stays(c0)

            @pl.when(here)
            def _():
                self.local(c0).wait()

            @pl.when(jnp.logical_not(here))
            def _():
                self.remote(c0).wait_send()

        for seq in range(2):

            @pl.when(jnp.logical_not(self.stays(seq)))
            def _():
                pltpu.make_async_remote_copy(
                    src_ref=self.src.at[pl.ds(0, ROWS)],
                    dst_ref=self.dst.at[seq],
                    send_sem=self.send_sem.at[0],
                    recv_sem=self.recv_sem.at[seq],
                    device_id={"p": 1 - p},
                    device_id_type=MESH,
                ).wait_recv()


class Spread:
    def __init__(self, where, src, dst, send_sem, recv_sem):
        self.where = where[2:]
        self.src, self.dst, self.send_sem, self.recv_sem = src, dst, send_sem, recv_sem

    def here(self, index):
        p, l, c = self.where
        return (p == c) & (index == c)

    def local(self, seq):
        p, l, c = self.where
        return pltpu.make_async_copy(self.src.at[seq], self.dst.at[p, c], self.send_sem.at[seq])

    def remote(self, seq):
        p, l, c = self.where
        return pltpu.make_async_remote_copy(
            src_ref=self.src.at[seq],
            dst_ref=self.dst.at[p, c],
            send_sem=self.send_sem.at[seq],
            recv_sem=self.recv_sem.at[c],
            device_id={"p": seq, "l": (seq + l + p) % 2, "c": p},
            device_id_type=MESH,
        )

    def start(self):
        for seq in range(2):

            @pl.when(self.here(seq))
            def _():
                self.local(seq).start()

            @pl.when(jnp.logical_not(self.here(seq)))
            def _():
                self.remote(seq).start()

    def wait(self):
        p, l, c = self.where
        for seq in range(2):

            @pl.when(self.here(seq))
            def _():
                self.local(seq).wait()

            @pl.when(jnp.logical_not(self.here(seq)))
            def _():
                self.remote(seq).wait_send()

        for block in range(2):

            @pl.when(jnp.logical_not(self.here(block)))
            def _():
                pltpu.make_async_remote_copy(
                    src_ref=self.src.at[0],
                    dst_ref=self.dst.at[c, block],
                    send_sem=self.send_sem.at[0],
                    recv_sem=self.recv_sem.at[block],
                    device_id={"p": 1 - p},
                    device_id_type=MESH,
                ).wait_recv()


def turn(value):
    return pltpu.roll(value, HEAD_DIM // 2, 1)


def block_mask(key_dim, flags, index):
    shape = (BLK, BLK)
    key = lax.broadcasted_iota(jnp.int32, shape, key_dim)
    query = lax.broadcasted_iota(jnp.int32, shape, 1 - key_dim)
    upper = query // PIECE
    piece = jnp.where(upper == 0, flags[2 * index], flags[2 * index + 1])
    return (key <= query) | ((key // PIECE == upper) & (piece > 0))


PROJECT = 4
TALL = SEQ_ROWS // PROJECT


def attend_kernel(
    flags, x_ref, w_ref, ga_ref, gq_ref, gk_ref, cos_ref, sin_ref, woq, wgu_in, wdn_in,
    n_ref, q_ref, k_ref, v_ref, qr_ref, kr_ref, o_ref, lse_ref, wo, wgu, wdn,
    stage, send_sem, recv_sem, local_sem,
):
    y, x, p, l, c = place()
    peer = peers_of(x, y, p, l, c)
    t = 2 * l + c
    net = Plan(send_sem, recv_sem)

    def chip(yy, xx, pp, ll):
        slot = (yy * 2 + xx) * 4 + 2 * pp + ll
        return in_place(wgu.at[:, rows_at(slot, 64)], wdn.at[rows_at(slot, 192)])

    def rows_of(q):
        return woq.at[rows_at(q, 512)], wo.at[:, rows_at(t, 256)]

    go_mlp_y = net.add(peer["y"], chip(y, x, p, l) + chip(y, 1 - x, p, l))
    go_mlp_x = net.add(peer["x"], chip(y, x, p, 1 - l) + chip(1 - y, x, p, 1 - l))
    go_far = [net.add(peer["p"], [pair]) for pair in chip(y, x, p, l)]
    go_far_l = [net.add(peer["l"], [pair]) for pair in chip(y, x, 1 - p, l)]
    go_near_y = net.add(peer["y"], chip(y, x, p, 1 - l))
    go_wo_l = net.add(peer["l"], [rows_of(2 * (1 - l) + c)])
    go_wo_d = net.add(peer["d"], [rows_of(2 * (1 - l) + 1 - c)])
    go_wo_c = net.add(peer["c"], [rows_of(2 * l + 1 - c)])
    step = pl.program_id(0)

    @pl.when(step == 0)
    def _():
        greet(list(peer.values()))
        net.start(go_near_y, *go_far, go_wo_l, go_wo_d, go_wo_c)
        copy = pltpu.make_async_copy(rows_of(t)[0], stage, local_sem.at[0])
        copy.start()
        copy.wait()
        pltpu.make_async_copy(stage, rows_of(t)[1], local_sem.at[1]).start()

    @pl.when(step < PROJECT)
    def _():
        value = x_ref[...].astype(jnp.float32)
        r = lax.rsqrt(jnp.mean(value * value, axis=-1, keepdims=True) + EPS)
        normed = (value * r * ga_ref[...]).astype(jnp.bfloat16)
        n_ref[...] = normed
        full = dot(normed, w_ref[...])
        cosine, sine = cos_ref[...], sin_ref[...]
        rows = rows_at(jnp.minimum(step, PROJECT - 1), TALL)
        for h in range(QH + KH):
            u = full[:, h * HEAD_DIM : (h + 1) * HEAD_DIM]
            raw_ref, out_ref, g_ref, at = (qr_ref, q_ref, gq_ref, h) if h < QH else (kr_ref, k_ref, gk_ref, h - QH)
            raw_ref[at] = u
            n = u * lax.rsqrt(jnp.mean(u * u, axis=-1, keepdims=True) + EPS) * g_ref[...]
            out_ref[at, rows, :] = (n * cosine + turn(n) * sine).astype(jnp.bfloat16)
        for h in range(KH):
            at = (QH + KH + h) * HEAD_DIM
            v_ref[h, rows, :] = full[:, at : at + HEAD_DIM].astype(jnp.bfloat16)

    @pl.when(step == PROJECT)
    def _():
        net.arrived(go_near_y)
        net.start(go_mlp_x, go_mlp_y)

    for k, at in enumerate((PROJECT + 3, PROJECT + 5)):

        @pl.when(step == at)
        def _():
            net.arrived(go_far[k])
            net.start(go_far_l[k])

    @pl.when(step >= PROJECT)
    def _():
        order = jnp.maximum(step - PROJECT, 0)
        g, i = order // NBLK, order % NBLK
        ones = jnp.ones((BLK, HEAD_DIM), jnp.bfloat16)
        mask = block_mask(1, flags, i)

        def values(j):
            return jnp.concatenate([v_ref[g, rows_at(j, BLK), :], ones], axis=1)

        queries = [q_ref[2 * g + h, rows_at(i, BLK), :] for h in range(2)]

        def part(j, masked):
            keys, both = k_ref[g, rows_at(j, BLK), :], values(j)
            found = []
            for q in queries:
                probs = jnp.exp2(dot(q, keys, NT) * (SCALE * LOG2E))
                if masked:
                    probs = jnp.where(mask, probs, 0.0)
                found.append(dot(probs.astype(jnp.bfloat16), both))
            return found

        def one(j, accs):
            return tuple(acc + more for acc, more in zip(accs, part(j, False)))

        accs = lax.fori_loop(0, i, one, tuple(part(i, True)))
        for h, acc in enumerate(accs):
            total = acc[:, HEAD_DIM:]
            o_ref[:, h * HEAD_DIM : (h + 1) * HEAD_DIM] = (acc[:, :HEAD_DIM] / total).astype(jnp.bfloat16)
            lse_ref[h] = jnp.log2(total).T[0:8, :]

    @pl.when(step == PROJECT + 2 * NBLK - 1)
    def _():
        pltpu.make_async_copy(stage, rows_of(t)[1], local_sem.at[1]).wait()
        net.arrived(go_mlp_y, go_mlp_x, *go_far_l, go_wo_l, go_wo_d, go_wo_c)
        net.sent()


def attend(flags, x, w, ga, gq, gk, cosine, sine, woq, wgu, wdn):
    bf16, f32 = jnp.bfloat16, jnp.float32

    def early(s):
        return jnp.minimum(s, PROJECT - 1)

    def late(s):
        return jnp.maximum(s - PROJECT, 0)

    def row(width):
        return pl.BlockSpec((TALL, width), lambda s, f: (early(s), 0))

    def whole(shape):
        return pl.BlockSpec(shape, lambda s, f: (0,) * len(shape))

    def heads(n):
        return pl.BlockSpec((n, TALL, HEAD_DIM), lambda s, f: (0, early(s), 0))

    def shape(n, dtype):
        return jax.ShapeDtypeStruct((n, SEQ_ROWS, HEAD_DIM), dtype)

    any_spec = pl.BlockSpec(memory_space=pl.ANY)
    copies = 20
    return pl.pallas_call(
        attend_kernel,
        out_shape=(
            jax.ShapeDtypeStruct((SEQ_ROWS, MODEL_DIM), bf16),
            shape(QH, bf16),
            shape(KH, bf16),
            shape(KH, bf16),
            shape(QH, f32),
            shape(KH, f32),
            jax.ShapeDtypeStruct((SEQ_ROWS, QH * HEAD_DIM), bf16),
            jax.ShapeDtypeStruct((QH, 8, SEQ_ROWS), f32),
            jax.ShapeDtypeStruct((512, MODEL_DIM), bf16),
            jax.ShapeDtypeStruct(wgu.shape, bf16),
            jax.ShapeDtypeStruct(wdn.shape, bf16),
        ),
        grid_spec=pltpu.PrefetchScalarGridSpec(
            num_scalar_prefetch=1,
            grid=(PROJECT + KH * NBLK,),
            in_specs=[row(MODEL_DIM), whole(w.shape), whole(ga.shape), whole(gq.shape), whole(gk.shape), row(HEAD_DIM), row(HEAD_DIM)]
            + [any_spec] * 3,
            out_specs=[
                row(MODEL_DIM),
                whole((QH, SEQ_ROWS, HEAD_DIM)),
                whole((KH, SEQ_ROWS, HEAD_DIM)),
                whole((KH, SEQ_ROWS, HEAD_DIM)),
                heads(QH),
                heads(KH),
                pl.BlockSpec((BLK, 2 * HEAD_DIM), lambda s, f: (late(s) % NBLK, late(s) // NBLK)),
                pl.BlockSpec((2, 8, BLK), lambda s, f: (late(s) // NBLK, 0, late(s) % NBLK)),
            ]
            + [any_spec] * 3,
            scratch_shapes=[pltpu.VMEM((512, 256), bf16)]
            + [pltpu.SemaphoreType.DMA((copies,))] * 2
            + [pltpu.SemaphoreType.DMA((2,))],
        ),
        input_output_aliases={9: 9, 10: 10},
        compiler_params=pltpu.CompilerParams(
            collective_id=2, has_side_effects=True, vmem_limit_bytes=VMEM_LIMIT
        ),
        cost_estimate=pl.CostEstimate(
            flops=4 * QH * SEQ_ROWS * SEQ_ROWS * HEAD_DIM, bytes_accessed=24 << 20, transcendentals=QH * SEQ_ROWS * SEQ_ROWS
        ),
        name="attend",
    )(flags, x, w, ga, gq, gk, cosine, sine, woq, wgu, wdn)


def resid_kernel(
    attn, wo, g_mlp, xs, cot, wgu_in, wdn_in,
    resid, mlp_in, wgu, wdn, wdx, dy,
    send_c, recv_c, send_l, recv_l, keep, x_own, send_sem, recv_sem, local_sem, dy_send, dy_recv,
):
    where = place()
    y, x, p, l, c = where
    peer = peers_of(x, y, p, l, c)
    net = Plan(send_sem, recv_sem)

    def chip(yy, xx, pp, ll):
        slot = (yy * 2 + xx) * 4 + 2 * pp + ll
        return in_place(wgu.at[:, rows_at(slot, 64)], wdn.at[rows_at(slot, 192)])

    def down(pp, ll):
        found = []
        for xx in range(2):
            slot = xx * 4 + 2 * pp + ll
            found.append((wdn.at[rows_at((1 - c) * 8 + slot, 192)], wdx.at[rows_at(slot, 192)]))
        return found

    def hop(name, *chips):
        found = [chip(*one) for one in chips]
        return [net.add(peer[name], [pairs[k] for pairs in found]) for k in range(2)]

    go_far_x = hop("x", (y, x, 1 - p, l))
    go_far_y = hop("y", (y, x, 1 - p, l), (y, 1 - x, 1 - p, l))
    go_fal_y = hop("y", (y, x, 1 - p, 1 - l))
    go_fal_x = hop("x", (y, x, 1 - p, 1 - l), (1 - y, x, 1 - p, 1 - l))
    go_down_me = net.add(peer["c"], down(p, l))
    go_down_near = net.add(peer["c"], down(p, 1 - l))
    go_down_far = net.add(peer["c"], down(1 - p, l))
    go_down_fal = net.add(peer["c"], down(1 - p, 1 - l))
    halves = [pl.ds(n * ROWS, ROWS) for n in range(2)]
    go_give_0 = [net.add(peer["c"], [(send_c.at[0, half], recv_c.at[0, half])]) for half in halves]
    go_give_1 = net.add(peer["c"], [(send_c.at[1], recv_c.at[1])])
    go_cross = [net.add(peer["l"], [(send_l.at[half], recv_l.at[half])]) for half in halves]
    go_share = [net.add(peer["c"], in_place(mlp_in.at[c, half])) for half in halves]
    go_dy_c = net.add(peer["c"], in_place(dy.at[c]))
    spread = Spread(where, cot, dy, dy_send, dy_recv)
    greet(line_peers(p, l, c) + [peer["x"], peer["y"]])
    spread.start()
    net.start(go_far_x[1], go_fal_y[1], go_far_x[0], go_fal_y[0], go_down_me, go_down_near)
    fetch = pltpu.make_async_copy(xs.at[rows_at(owned(p, l, c), OWN)], x_own, local_sem.at[0])
    fetch.start()

    def project(ll, cc, write, first=0, count=OWN):
        part = attn[pl.ds(pl.multiple_of(owned(p, ll, cc) * OWN + first, ROWS), count), :]

        def chunk(n, carry):
            cols = rows_at(n, 256)
            write(pl.ds(first, count), cols, dot(part, wo[:, cols]))
            return carry

        lax.fori_loop(0, 4, chunk, 0)

    def give(n):
        def write(rows, cols, value):
            send_c[n, rows, cols] = value.astype(jnp.bfloat16)

        return write

    def hold(n):
        def write(rows, cols, value):
            keep[n, rows, cols] = value

        return write

    def relay_hop(k):
        net.arrived(go_far_x[k])
        net.start(go_far_y[k])
        net.arrived(go_fal_y[k])
        net.start(go_fal_x[k])

    for n, half in enumerate(halves):
        project(1 - l, 1 - c, give(0), n * ROWS, ROWS)
        net.start(go_give_0[n])
        project(1 - l, c, hold(0), n * ROWS, ROWS)
        net.arrived(go_give_0[n])
        send_l[half, :] = (keep[0, half, :] + recv_c[0, half, :].astype(jnp.float32)).astype(jnp.bfloat16)
        net.start(go_cross[n])
    relay_hop(1)
    project(l, 1 - c, give(1))
    net.start(go_give_1)
    project(l, c, hold(1))
    fetch.wait()
    relay_hop(0)
    net.arrived(go_give_1)
    keep[1] += recv_c[1].astype(jnp.float32) + x_own[...].astype(jnp.float32)
    for n, half in enumerate(halves):
        net.arrived(go_cross[n])
        total = keep[1, half, :] + recv_l[half, :].astype(jnp.float32)
        resid[half, :] = total
        r = lax.rsqrt(jnp.mean(total * total, axis=-1, keepdims=True) + EPS)
        mlp_in[c, half, :] = (total * r * g_mlp[...]).astype(jnp.bfloat16)
        net.start(go_share[n])
    net.arrived(go_far_y[1])
    net.start(go_down_far)
    spread.wait()
    net.start(go_dy_c)
    net.arrived(go_fal_x[1])
    net.start(go_down_fal)
    net.arrived(go_far_y[0], go_fal_x[0])
    net.arrived(go_down_me, go_down_near, go_down_far, go_down_fal, *go_share, go_dy_c)
    net.sent()


def finish_resid(attn, wo, g_mlp, xs, cot, wgu, wdn):
    bf16, f32 = jnp.bfloat16, jnp.float32
    any_spec = pl.BlockSpec(memory_space=pl.ANY)
    vmem = pl.BlockSpec(memory_space=pltpu.VMEM)
    copies = 32
    return pl.pallas_call(
        resid_kernel,
        out_shape=(
            jax.ShapeDtypeStruct((OWN, MODEL_DIM), f32),
            jax.ShapeDtypeStruct((2, OWN, MODEL_DIM), bf16),
            jax.ShapeDtypeStruct(wgu.shape, bf16),
            jax.ShapeDtypeStruct(wdn.shape, bf16),
            jax.ShapeDtypeStruct((HALF_FF, 512), bf16),
            jax.ShapeDtypeStruct((2, 2, ROWS, MODEL_DIM), bf16),
        ),
        in_specs=[vmem] * 3 + [any_spec] * 4,
        out_specs=[vmem] * 2 + [any_spec] * 4,
        scratch_shapes=[
            pltpu.VMEM((2, OWN, MODEL_DIM), bf16),
            pltpu.VMEM((2, OWN, MODEL_DIM), bf16),
            pltpu.VMEM((OWN, MODEL_DIM), bf16),
            pltpu.VMEM((OWN, MODEL_DIM), bf16),
            pltpu.VMEM((2, OWN, MODEL_DIM), f32),
            pltpu.VMEM((OWN, MODEL_DIM), bf16),
            pltpu.SemaphoreType.DMA((copies,)),
            pltpu.SemaphoreType.DMA((copies,)),
            pltpu.SemaphoreType.DMA((1,)),
            pltpu.SemaphoreType.DMA((2,)),
            pltpu.SemaphoreType.DMA((2,)),
        ],
        input_output_aliases={5: 2, 6: 3},
        compiler_params=pltpu.CompilerParams(
            collective_id=3, has_side_effects=True, vmem_limit_bytes=VMEM_LIMIT
        ),
        name="residual",
    )(attn, wo, g_mlp, xs, cot, wgu, wdn)


CHUNK = 512
EARLY = 1024


def forward_kernel(
    m_ref, dy_ref, w_ref, wdn, wx_ref, resid, g_mlp,
    ggu, gdb, rb, d_resid, db, res, dg,
    mt, hid, dgt, dup, d_in, down, give, take, all_down, ggv, gdv, send_sem, recv_sem, load_sem, out_sem,
):
    where = place()
    y, x, p, l, c = where
    peer = peers_of(x, y, p, l, c)
    red = Reduction(where)
    net = Plan(send_sem, recv_sem)
    go_d_in = net.add(peer["c"], [(give.at[0], take.at[0])])
    go_down = net.add(peer["c"], [(give.at[1], take.at[1])])
    go_gd, go_wide, outs = [], [], []
    for f in range(HALF_FF // CHUNK):
        part_f = pl.ds(f * CHUNK, CHUNK)
        go_gd.append(net.add(peer["c"], [(gdv.at[part_f, rows_at(1 - c, 512)], gdb.at[c, part_f])]))
        outs.append(
            [
                pltpu.make_async_copy(ggv.at[:, :, part_f], ggu.at[:, :, part_f], out_sem.at[2 * f]),
                pltpu.make_async_copy(gdv.at[part_f, rows_at(c, 512)], gdb.at[c, part_f], out_sem.at[2 * f + 1]),
            ]
        )
        go_wide.append([])
        if f * CHUNK < EARLY:
            for n, kind in enumerate(KINDS):
                pairs = []
                for k in range(2):
                    slot = chip_slot(*red.place(kind, k, True), *red.z[kind])
                    pairs.append((ggv.at[:, rows_at(slot, 64), part_f], rb.at[n, k, :, :, part_f]))
                go_wide[f].append(net.add(peer[red.first_peer(kind)], pairs))
    step = pl.program_id(0)
    fetch = pltpu.make_async_copy(wdn.at[rows_at(c, HALF_FF)], all_down, load_sem.at[0])

    @pl.when(step == 0)
    def _():
        fetch.start()
        greet([peer["c"], peer["x"], peer["y"]])

        def flip(k, carry):
            rows = rows_at(k, 256)
            mt[:, rows] = m_ref[rows, :].T
            return carry

        lax.fori_loop(0, 4, flip, 0)
        d_in[...] = jnp.zeros_like(d_in)
        down[...] = jnp.zeros_like(down)
        fetch.wait()

    wo_ref = all_down.at[rows_at(step, CHUNK)]
    own_cols, other_cols = rows_at(c, 512), rows_at(1 - c, 512)

    def part(r, carry):
        rows = rows_at(r, 512)
        value, grad = m_ref[rows, :], dy_ref
        gate, up = dot(value, w_ref[0]), dot(value, w_ref[1])
        d_hidden = dot(grad[rows, own_cols], wo_ref[...], NT) + dot(grad[rows, other_cols], wx_ref[...], NT)
        s = 1.0 / (1.0 + jnp.exp(-gate))
        silu = gate * s
        hidden = (silu * up).astype(jnp.bfloat16)
        d_up = (d_hidden * silu).astype(jnp.bfloat16)
        d_gate = (d_hidden * up * (s * (1.0 + gate * (1.0 - s)))).astype(jnp.bfloat16)
        hid[rows, :] = hidden
        dup[rows, :] = d_up
        dgt[rows, :] = d_gate
        d_in[rows, :] += dot(d_gate, w_ref[0], NT) + dot(d_up, w_ref[1], NT)
        down[rows, own_cols] += dot(hidden, wo_ref[...])
        down[rows, other_cols] += dot(hidden, wx_ref[...])
        return carry

    lax.fori_loop(0, 2, part, 0)

    @pl.when(step == pl.num_programs(0) - 1)
    def _():
        give[0] = d_in[rows_at(1 - c, OWN), :].astype(jnp.bfloat16)
        give[1] = down[rows_at(1 - c, OWN), :].astype(jnp.bfloat16)
        net.start(go_d_in, go_down)

    now = rows_at(step, CHUNK)

    def weights(k, carry):
        rows = rows_at(k, 1024)
        ggv[0, rows, now] = dot(mt[rows, :], dgt[...]).astype(jnp.bfloat16)
        ggv[1, rows, now] = dot(mt[rows, :], dup[...]).astype(jnp.bfloat16)
        gdv[now, rows] = dot(hid[...], dy_ref[:, rows], TN).astype(jnp.bfloat16)
        return carry

    lax.fori_loop(0, 1, weights, 0)
    for f in range(HALF_FF // CHUNK):

        @pl.when(step == f)
        def _():
            net.start(*go_wide[f], go_gd[f])
            for copy in outs[f]:
                copy.start()

    @pl.when(step == pl.num_programs(0) - 1)
    def _():
        net.arrived(go_d_in, go_down)
        dg[...] = jnp.zeros_like(dg)

        def finish(k, carry):
            rows = rows_at(k, 64)
            here = pl.ds(pl.multiple_of(c * OWN + k * 64, 64), 64)
            value = resid[rows, :]
            grad = d_in[here, :] + take[0, rows, :].astype(jnp.float32)
            r = lax.rsqrt(jnp.mean(value * value, axis=-1, keepdims=True) + EPS)
            scaled = value * r
            gained = grad * g_mlp[...]
            total = dy_ref[here, :].astype(jnp.float32) + r * (gained - scaled * jnp.mean(scaled * gained, axis=-1, keepdims=True))
            d_resid[rows, :] = total
            db[rows, :] = total.astype(jnp.bfloat16)
            dg[...] += jnp.sum((grad * scaled).reshape(-1, 8, MODEL_DIM), axis=0)
            res[rows, :] = (value + down[here, :] + take[1, rows, :].astype(jnp.float32)).astype(jnp.bfloat16)
            return carry

        lax.fori_loop(0, 8, finish, 0)
        for f in range(HALF_FF // CHUNK):
            net.arrived(*go_wide[f], go_gd[f])
            for copy in outs[f]:
                copy.wait()
        net.sent()


def feed_forward(mlp_in, dy, wgu, wdn, wdx, resid, g_mlp):
    bf16, f32 = jnp.bfloat16, jnp.float32

    def whole(shape):
        return pl.BlockSpec(shape, lambda f: (0,) * len(shape), pipeline_mode=pl.Buffered(1))

    down = pl.BlockSpec((CHUNK, 512), lambda f: (f, 0))
    copies = 24
    rows = (1024, MODEL_DIM)
    own = (OWN, MODEL_DIM)
    return pl.pallas_call(
        forward_kernel,
        grid=(HALF_FF // CHUNK,),
        out_shape=(
            jax.ShapeDtypeStruct((2, MODEL_DIM, HALF_FF), bf16),
            jax.ShapeDtypeStruct((2, HALF_FF, 512), bf16),
            jax.ShapeDtypeStruct((4, 2, 2, 64, EARLY), bf16),
            jax.ShapeDtypeStruct(own, f32),
            jax.ShapeDtypeStruct(own, bf16),
            jax.ShapeDtypeStruct(own, bf16),
            jax.ShapeDtypeStruct((8, MODEL_DIM), f32),
        ),
        in_specs=[whole(rows), whole(rows), pl.BlockSpec((2, MODEL_DIM, CHUNK), lambda f: (0, 0, f))]
        + [pl.BlockSpec(memory_space=pl.ANY), down]
        + [whole(own), whole((1, MODEL_DIM))],
        out_specs=[pl.BlockSpec(memory_space=pl.ANY)] * 3
        + [whole(own), whole(own), whole(own), whole((8, MODEL_DIM))],
        scratch_shapes=[
            pltpu.VMEM(rows, bf16),
            pltpu.VMEM((1024, CHUNK), bf16),
            pltpu.VMEM((1024, CHUNK), bf16),
            pltpu.VMEM((1024, CHUNK), bf16),
            pltpu.VMEM(rows, f32),
            pltpu.VMEM(rows, f32),
            pltpu.VMEM((2,) + own, bf16),
            pltpu.VMEM((2,) + own, bf16),
            pltpu.VMEM((HALF_FF, 512), bf16),
            pltpu.VMEM((2, MODEL_DIM, HALF_FF), bf16),
            pltpu.VMEM((HALF_FF, MODEL_DIM), bf16),
            pltpu.SemaphoreType.DMA((copies,)),
            pltpu.SemaphoreType.DMA((copies,)),
            pltpu.SemaphoreType.DMA((1,)),
            pltpu.SemaphoreType.DMA((6,)),
        ],
        compiler_params=pltpu.CompilerParams(
            collective_id=6, has_side_effects=True, vmem_limit_bytes=VMEM_LIMIT
        ),
        name="feed_forward",
    )(mlp_in, dy, wgu, wdn, wdx, resid, g_mlp)


KINDS = ME, NEAR, FAR, FAL = range(4)


def chip_slot(yy, xx, pp, ll):
    return (yy * 2 + xx) * 4 + 2 * pp + ll


class Reduction:
    def __init__(self, where):
        y, x, p, l, c = where
        self.z = ((p, l), (p, 1 - l), (1 - p, l), (1 - p, 1 - l))
        self.y, self.x = y, x

    def y_first(self, kind):
        return kind in (ME, FAR)

    def first_peer(self, kind):
        return "y" if self.y_first(kind) else "x"

    def second_peer(self, kind):
        return "x" if self.y_first(kind) else "y"

    def place(self, kind, index, given):
        if self.y_first(kind):
            return (1 - self.y if given else self.y), index
        return index, (1 - self.x if given else self.x)

    def kept(self, kind):
        return self.x if self.y_first(kind) else self.y


def attend_back_kernel(
    flags, q_in, k_in, v_in, o_in, db_in, wo_in, lse_in, qr_in, kr_in, cos_in, sin_in, ggu, gdb, rb_in, res, gq_ref, gk_ref,
    d_out, goq, og_out, od_out, fw_out, fd_out, out, dg_ref,
    q_ref, k_ref, v_ref, o_ref, dall, wo, lse_ref, qr_ref, kr_ref, cos_ref, sin_ref,
    da, delta, dbuf, dq_acc, dk_acc, dv_acc, og, od, rb, rbd, rc, rcd, rz, rzd, go,
    send_sem, recv_sem, load_sem, own_sem, out_sem, back_send, back_recv,
):
    where = place()
    y, x, p, l, c = where
    peer = peers_of(x, y, p, l, c)
    red = Reduction(where)
    net = Plan(send_sem, recv_sem)
    t = 2 * l + c

    def block(index):
        return dall.at[rows_at(index, OWN)]

    mine = owned(p, l, c)
    go_db_l = net.add(peer["l"], [(db_in, block(mine))])
    go_db_c = net.add(peer["c"], [(db_in, block(mine))])
    go_db_r = net.add(peer["c"], in_place(block(owned(p, 1 - l, c))))
    early, late = pl.ds(0, EARLY), pl.ds(EARLY, HALF_FF - EARLY)
    first_of, second_a, second_b = {}, {}, {}
    for n, kind in enumerate(KINDS):
        pairs = []
        for k in range(2):
            yy, xx = red.place(kind, k, True)
            slot = chip_slot(yy, xx, *red.z[kind])
            pairs.append((ggu.at[:, rows_at(slot, 64), late], rb.at[n, k, :, :, late]))
            pairs.append((gdb.at[yy, rows_at(xx * 4 + 2 * red.z[kind][0] + red.z[kind][1], 192)], rbd.at[n, k]))
        first_of[kind] = net.add(peer[red.first_peer(kind)], pairs)
        if n >= 2:
            away, link = 1 - red.kept(kind), peer[red.second_peer(kind)]
            second_a[kind] = net.add(link, [(og.at[n, away, :, :, early], rc.at[n - 2, :, :, early])])
            second_b[kind] = net.add(link, [(og.at[n, away, :, :, late], rc.at[n - 2, :, :, late]), (od.at[n, away], rcd.at[n - 2])])
    u_far, u_fal = red.kept(FAR), red.kept(FAL)
    go_fal_a = net.add(peer["l"], [(og.at[FAL, u_fal, :, :, early], rz.at[:, :, early])])
    go_fal_b = net.add(peer["l"], [(og.at[FAL, u_fal, :, :, late], rz.at[:, :, late]), (od.at[FAL, u_fal], rzd)])
    go_far_a = net.add(peer["p"], [(og.at[FAR, u_far, :, :, early], fw_out.at[:, :, early])])
    go_far_b = net.add(peer["p"], [(og.at[FAR, u_far, :, :, late], fw_out.at[:, :, late]), (od.at[FAR, u_far], fd_out)])
    home = Return(where, res, out, back_send, back_recv)

    def columns(q):
        return [(go.at[:, rows_at(q, 256)], goq.at[rows_at(t, 512)])]

    go_go_l = net.add(peer["l"], columns(2 * (1 - l) + c))
    go_go_d = net.add(peer["d"], columns(2 * (1 - l) + 1 - c))
    go_go_c = net.add(peer["c"], columns(2 * l + 1 - c))
    own_go = pltpu.make_async_copy(*columns(t)[0], out_sem.at[1])
    loads = [
        pltpu.make_async_copy(src, dst, load_sem.at[k])
        for k, (src, dst) in enumerate(
            [
                (db_in, block(mine)), (wo_in, wo), (o_in, o_ref), (q_in, q_ref), (k_in, k_ref), (v_in, v_ref), (lse_in, lse_ref),
                (cos_in, cos_ref), (sin_in, sin_ref), (qr_in, qr_ref), (kr_in, kr_ref),
            ]
        )
    ]
    own = [pltpu.make_async_copy(rb_in, rb.at[:, :, :, :, early], own_sem.at[0])]
    for n, kind in enumerate(KINDS):
        for k in range(2):
            yy, xx = red.place(kind, k, False)
            slot = chip_slot(yy, xx, *red.z[kind])
            own.append(pltpu.make_async_copy(ggu.at[:, rows_at(slot, 64)], og.at[n, k], own_sem.at[len(own)]))
            rows = rows_at(xx * 4 + 2 * red.z[kind][0] + red.z[kind][1], 192)
            own.append(pltpu.make_async_copy(gdb.at[yy, rows], od.at[n, k], own_sem.at[len(own)]))

    def plus(target, other):
        target[...] = (target[...].astype(jnp.float32) + other[...].astype(jnp.float32)).astype(jnp.bfloat16)

    def wide_sum(n, cols):
        def wide(r, carry):
            k, m, rows = r // 4, (r // 2) % 2, rows_at(r % 2, 32)
            plus(og.at[n, k, m, rows, cols], rb.at[n, k, m, rows, cols])
            return carry

        lax.fori_loop(0, 8, wide, 0)

    def deep_sum(n):
        def deep(r, carry):
            k, rows = r // 3, rows_at(r % 3, 64)
            plus(od.at[n, k, rows, :], rbd.at[n, k, rows, :])
            return carry

        lax.fori_loop(0, 6, deep, 0)

    def branch(index):
        rows = rows_at(index, OWN)
        value = dot(dall[rows, :], wo[...], NT).astype(jnp.bfloat16)
        da[rows, :] = value
        for h in range(QH):
            cols = slice(h * HEAD_DIM, (h + 1) * HEAD_DIM)
            prod = value[:, cols].astype(jnp.float32) * o_ref[rows, cols].astype(jnp.float32)
            delta[h, :, rows] = jnp.broadcast_to(jnp.sum(prod.T, axis=0, keepdims=True), (8, BLK))

    def unrope(grad, u, gain, rows):
        grad = grad * SCALE
        e = grad * cos_ref[rows, :] + turn(grad * sin_ref[rows, :])
        r = lax.rsqrt(jnp.mean(u * u, axis=-1, keepdims=True) + EPS)
        ur = u * r
        ge = e * gain
        d = r * (ge - ur * jnp.mean(ur * ge, axis=-1, keepdims=True))
        return d.astype(jnp.bfloat16), jnp.sum((e * ur).reshape(-1, 8, HEAD_DIM), axis=0)

    step = pl.program_id(0)
    b, g = step // KH, step % KH
    i = owned(p, (l + b // 2) % 2, b % 2)

    @pl.when(step == 0)
    def _():
        for copy in loads[:3]:
            copy.start()
        for copy in own:
            copy.start()
        for copy in loads[3:]:
            copy.start()
        greet(line_peers(p, l, c) + [peer["x"], peer["y"]])
        net.start(go_db_l, go_db_c, first_of[FAR], first_of[FAL])
        dk_acc[...] = jnp.zeros_like(dk_acc)
        dv_acc[...] = jnp.zeros_like(dv_acc)
        dg_ref[...] = jnp.zeros_like(dg_ref)
        for copy in own:
            copy.wait()
        for kind in (FAR, FAL):
            wide_sum(kind, early)
            net.start(second_a[kind])
        for copy in loads[:3]:
            copy.wait()
        branch(mine)
        net.arrived(go_db_c)
        branch(owned(p, l, 1 - c))
        for copy in loads[3:]:
            copy.wait()

    @pl.when(step == 2)
    def _():
        net.arrived(second_a[FAL])
        plus(og.at[FAL, u_fal, :, :, early], rc.at[1, :, :, early])
        net.start(go_fal_a)
        net.arrived(second_a[FAR])
        plus(og.at[FAR, u_far, :, :, early], rc.at[0, :, :, early])

    @pl.when(step == 0)
    def _():
        home.start()

    @pl.when(step == 3)
    def _():
        for kind in (FAR, FAL):
            net.arrived(first_of[kind])
            wide_sum(kind, late)
            deep_sum(kind)
            net.start(second_b[kind])
        net.start(first_of[ME], first_of[NEAR])

    @pl.when(step == 2 * KH)
    def _():
        net.arrived(go_db_l)
        net.start(go_db_r)
        branch(owned(p, 1 - l, c))
        net.arrived(go_db_r)
        branch(owned(p, 1 - l, 1 - c))

    @pl.when(step == 4)
    def _():
        net.arrived(go_fal_a)
        plus(og.at[FAR, u_far, :, :, early], rz.at[:, :, early])
        net.start(go_far_a)

    @pl.when(step == 5)
    def _():
        net.arrived(second_b[FAL])
        plus(og.at[FAL, u_fal, :, :, late], rc.at[1, :, :, late])
        plus(od.at[FAL, u_fal], rcd.at[1])
        net.start(go_fal_b)
        net.arrived(second_b[FAR])
        plus(og.at[FAR, u_far, :, :, late], rc.at[0, :, :, late])
        plus(od.at[FAR, u_far], rcd.at[0])

    @pl.when(step == 7)
    def _():
        net.arrived(go_fal_b)
        plus(og.at[FAR, u_far, :, :, late], rz.at[:, :, late])
        plus(od.at[FAR, u_far], rzd)
        net.start(go_far_b)

    @pl.when(step == 5)
    def _():
        def grad_out(k, carry):
            cols = rows_at(k, 256)
            go[cols, :] = dot(o_ref[:, cols], dall[...], TN).astype(jnp.bfloat16)
            return carry

        lax.fori_loop(0, 2, grad_out, 0)
        net.start(go_go_l, go_go_d, go_go_c)
        own_go.start()

    dq_acc[...] = jnp.zeros_like(dq_acc)
    rows = rows_at(i, BLK)
    heads = [2 * g + n for n in range(2)]
    spans = [rows_at(h, HEAD_DIM) for h in heads]
    queries = [q_ref[h, rows, :] for h in heads]
    grads = [da[rows, span] for span in spans]

    def tile(j, mask=None):
        keys = rows_at(j, BLK)
        k, v = k_ref[g, keys, :], v_ref[g, keys, :]
        turned = k.T
        dv, dk = None, None
        for n, h in enumerate(heads):
            probs = jnp.exp2(dot(k, queries[n], NT) * (SCALE * LOG2E) - lse_ref[h, 0:1, rows])
            if mask is not None:
                probs = jnp.where(mask, probs, 0.0)
            d_scores = (probs * (dot(v, grads[n], NT) - delta[h, 0:1, rows])).astype(jnp.bfloat16)
            dv_more, dk_more = dot(probs.astype(jnp.bfloat16), grads[n]), dot(d_scores, queries[n])
            dv, dk = (dv_more, dk_more) if dv is None else (dv + dv_more, dk + dk_more)
            dq_acc[n] += dot(turned, d_scores)
        dv_acc[g, keys, :] += dv
        dk_acc[g, keys, :] += dk

    def loop(j, carry):
        tile(j)
        return carry

    tile(i, block_mask(0, flags, i))
    lax.fori_loop(0, i, loop, 0)
    for n, h in enumerate(heads):
        low, total = unrope(dq_acc[n].T, qr_ref[h, rows, :], gq_ref[...], rows)
        dbuf[rows, spans[n]] = low
        dg_ref[0] += total

    @pl.when(step == 4 * KH - 1)
    def _():
        for gg_at in range(KH):

            def finish(r, carry):
                rows = rows_at(r, 256)
                low, total = unrope(dk_acc[gg_at, rows, :], kr_ref[gg_at, rows, :], gk_ref[...], rows)
                dbuf[rows, pl.ds((QH + gg_at) * HEAD_DIM, HEAD_DIM)] = low
                dbuf[rows, pl.ds((QH + KH + gg_at) * HEAD_DIM, HEAD_DIM)] = dv_acc[gg_at, rows, :].astype(jnp.bfloat16)
                dg_ref[1] += total
                return carry

            lax.fori_loop(0, 8, finish, 0)
        outs = [pltpu.make_async_copy(dbuf, d_out, out_sem.at[0])]
        outs[0].start()
        for kind in (ME, NEAR):
            wide_sum(kind, early)
            net.arrived(first_of[kind])
            wide_sum(kind, late)
            deep_sum(kind)
        outs += [
            pltpu.make_async_copy(og.at[pl.ds(0, 2)], og_out, out_sem.at[2]),
            pltpu.make_async_copy(od.at[pl.ds(0, 2)], od_out, out_sem.at[3]),
        ]
        for copy in outs[1:]:
            copy.start()
        net.arrived(go_go_l, go_go_d, go_go_c, go_far_a, go_far_b)
        own_go.wait()
        net.sent()
        home.wait()
        for copy in outs:
            copy.wait()


def attend_back(flags, q, k, v, o, db, wo, lse, qr, kr, cosine, sine, ggu, gdb, rb, res, gq, gk):
    bf16, f32 = jnp.bfloat16, jnp.float32
    any_spec = pl.BlockSpec(memory_space=pl.ANY)
    gain = pl.BlockSpec((1, HEAD_DIM), lambda s, f: (0, 0))
    copies = 40

    def vm(a):
        return pltpu.VMEM(a.shape, a.dtype)

    return pl.pallas_call(
        attend_back_kernel,
        out_shape=(
            jax.ShapeDtypeStruct((SEQ_ROWS, 1024), bf16),
            jax.ShapeDtypeStruct((2048, 256), bf16),
            jax.ShapeDtypeStruct((2, 2, 2, 64, HALF_FF), bf16),
            jax.ShapeDtypeStruct((2, 2, 192, 512), bf16),
            jax.ShapeDtypeStruct((2, 64, HALF_FF), bf16),
            jax.ShapeDtypeStruct((192, 512), bf16),
            jax.ShapeDtypeStruct((2, ROWS, MODEL_DIM), bf16),
            jax.ShapeDtypeStruct((2, 8, HEAD_DIM), f32),
        ),
        grid_spec=pltpu.PrefetchScalarGridSpec(
            num_scalar_prefetch=1,
            grid=(4 * KH,),
            in_specs=[any_spec] * 15 + [gain] * 2,
            out_specs=[any_spec] * 7 + [pl.BlockSpec((2, 8, HEAD_DIM), lambda s, f: (0, 0, 0))],
            scratch_shapes=[vm(q), vm(k), vm(v), vm(o), pltpu.VMEM((SEQ_ROWS, MODEL_DIM), bf16), vm(wo), vm(lse), vm(qr), vm(kr)]
            + [vm(cosine), vm(sine)]
            + [
                pltpu.VMEM((SEQ_ROWS, QH * HEAD_DIM), bf16),
                pltpu.VMEM((QH, 8, SEQ_ROWS), f32),
                pltpu.VMEM((SEQ_ROWS, 1024), bf16),
                pltpu.VMEM((2, HEAD_DIM, BLK), f32),
                pltpu.VMEM((KH, SEQ_ROWS, HEAD_DIM), f32),
                pltpu.VMEM((KH, SEQ_ROWS, HEAD_DIM), f32),
                pltpu.VMEM((4, 2, 2, 64, HALF_FF), bf16),
                pltpu.VMEM((4, 2, 192, 512), bf16),
                pltpu.VMEM((4, 2, 2, 64, HALF_FF), bf16),
                pltpu.VMEM((4, 2, 192, 512), bf16),
                pltpu.VMEM((2, 2, 64, HALF_FF), bf16),
                pltpu.VMEM((2, 192, 512), bf16),
                pltpu.VMEM((2, 64, HALF_FF), bf16),
                pltpu.VMEM((192, 512), bf16),
                pltpu.VMEM((512, MODEL_DIM), bf16),
                pltpu.SemaphoreType.DMA((copies,)),
                pltpu.SemaphoreType.DMA((copies,)),
                pltpu.SemaphoreType.DMA((11,)),
                pltpu.SemaphoreType.DMA((17,)),
                pltpu.SemaphoreType.DMA((4,)),
                pltpu.SemaphoreType.DMA((2,)),
                pltpu.SemaphoreType.DMA((2,)),
            ],
        ),
        compiler_params=pltpu.CompilerParams(
            collective_id=4, has_side_effects=True, vmem_limit_bytes=VMEM_LIMIT
        ),
        cost_estimate=pl.CostEstimate(
            flops=10 * QH * SEQ_ROWS * SEQ_ROWS * HEAD_DIM, bytes_accessed=40 << 20, transcendentals=QH * SEQ_ROWS * SEQ_ROWS
        ),
        name="attend_back",
    )(flags, q, k, v, o, db, wo, lse, qr, kr, cosine, sine, ggu, gdb, rb, res, gq, gk)


def tail_kernel(
    d_in, w_in, n_in, xs, og_in, od_in, fw_in, fd_in, goq_in, dr_ref, ga_ref, dgm_ref, dgh_ref,
    rq, rqo, fw, fd, gout, landed,
    d_ref, w_ref, n_ref, x_ref, goq, send_c, recv_c, send_l, recv_l, keep, gt,
    og, od, rx, rxd, rz, rzd, total_w, total_d,
    pq, work, wgo, ry, ryo, ox, oxo, rs, rso, gs, gr,
    send_sem, recv_sem, load_sem, back_send, back_recv,
):
    where = place()
    y, x, p, l, c = where
    peer = peers_of(x, y, p, l, c)
    red = Reduction(where)
    net = Plan(send_sem, recv_sem)
    second_of = {}
    t = 2 * l + c
    for n, kind in enumerate(KINDS[:2]):
        away = 1 - red.kept(kind)
        second_of[kind] = net.add(peer[red.second_peer(kind)], [(og_in.at[n, away], rx.at[n]), (od_in.at[n, away], rxd.at[n])])
    u_me, u_near = red.kept(ME), red.kept(NEAR)
    go_near = net.add(peer["l"], [(og.at[1], rz.at[1]), (od.at[1], rzd.at[1])])
    go_halves = net.add(peer["c"], [(total_w.at[1 - c], fw.at[c]), (total_d.at[1 - c], fd.at[c])])
    go_give_0 = net.add(peer["c"], [(send_c.at[0], recv_c.at[0])])
    go_give_1 = net.add(peer["c"], [(send_c.at[1], recv_c.at[1])])
    halves = [pl.ds(k * ROWS, ROWS) for k in range(2)]
    go_cross = [net.add(peer["l"], [(send_l.at[half], recv_l.at[half])]) for half in halves]

    def group(yy, xx, pp):
        return (yy * 2 + xx) * 2 + pp

    def moved(sources, groups, targets, at=0):
        return [(src.at[one], dst.at[at + k]) for k, one in enumerate(groups) for src, dst in zip(sources, targets)]

    source, working, small = (pq, goq), (work, wgo), (rs, rso)
    base, across = group(y, x, p), group(y, x, 1 - p)
    give_y = (group(1 - y, 0, p), group(1 - y, 1, p))
    give_x = (group(0, 1 - x, 1 - p), group(1, 1 - x, 1 - p))
    go_own_y = [[net.add(peer["y"], moved((a,), give_y[k : k + 1], (b,), k)) for k in range(2)] for a, b in ((pq, ry), (goq_in, ryo))]
    go_other_x = [[net.add(peer["x"], moved((a,), give_x[k : k + 1], (b,), k)) for k in range(2)] for a, b in ((pq, ox), (goq_in, oxo))]
    go_own_x = [net.add(peer["x"], moved(working[k : k + 1], (group(y, 1 - x, p),), small[k : k + 1], 0)) for k in range(2)]
    go_other_y = [net.add(peer["y"], moved(working[k : k + 1], (group(1 - y, x, 1 - p),), small[k : k + 1], 1)) for k in range(2)]
    go_across = [net.add(peer["p"], moved(working[k : k + 1], (across,), small[k : k + 1], 2)) for k in range(2)]

    def parts(q):
        return [(work.at[base, rows_at(q, 32)], rq.at[t]), (wgo.at[base, rows_at(q, 64)], rqo.at[t])]

    go_last_l = net.add(peer["l"], parts(2 * (1 - l) + c))
    go_last_d = net.add(peer["d"], parts(2 * (1 - l) + 1 - c))
    go_last_c = net.add(peer["c"], parts(2 * l + 1 - c))
    go_gain = [net.add(peer[name], [(gs.at[k], gr.at[k])]) for k, name in enumerate(("c", "x", "y", "p", "l"))]
    home = Return(where, gt, landed, back_send, back_recv)

    def gain_hop(k):
        net.arrived(go_gain[k])
        gs[k + 1] = gs[k] + gr[k]
        if k + 1 < len(AXES):
            net.start(go_gain[k + 1])

    loads = [
        pltpu.make_async_copy(src, dst, load_sem.at[k])
        for k, (src, dst) in enumerate(
            [
                (d_in, d_ref), (w_in, w_ref), (n_in, n_ref), (goq_in, goq), (xs.at[rows_at(owned(p, l, c), OWN)], x_ref),
                (og_in.at[0, u_me], og.at[0]), (og_in.at[1, u_near], og.at[1]),
                (od_in.at[0, u_me], od.at[0]), (od_in.at[1, u_near], od.at[1]),
                (fw_in, rz.at[0]), (fd_in, rzd.at[0]),
            ]
        )
    ]
    for copy in loads:
        copy.start()
    greet(line_peers(p, l, c) + [peer["x"], peer["y"]])
    net.start(second_of[NEAR], second_of[ME], *go_own_y[1], *go_other_x[1])

    def project(ll, cc, write):
        part = d_ref[rows_at(owned(p, ll, cc), OWN), :]

        def chunk(k, carry):
            cols = rows_at(k, 256)
            write(cols, dot(part, w_ref[cols, :], NT))
            return carry

        lax.fori_loop(0, 4, chunk, 0)

    def give(k):
        def write(cols, value):
            send_c[k, :, cols] = value.astype(jnp.bfloat16)

        return write

    def hold(k):
        def write(cols, value):
            keep[k, :, cols] = value

        return write

    def add(k, at, left, right, place_at):
        total = left[at].astype(jnp.float32) + right[place_at].astype(jnp.float32)
        working[k][at] = total.astype(jnp.bfloat16)

    def first_sums(k):
        net.arrived(*go_other_x[k])
        for yy in (0, 1):
            add(k, group(yy, x, 1 - p), source[k], (ox, oxo)[k], yy)
        net.start(go_other_y[k])
        net.arrived(*go_own_y[k])
        for xx in (0, 1):
            add(k, group(y, xx, p), source[k], (ry, ryo)[k], xx)
        net.start(go_own_x[k])

    def second_sums(k):
        net.arrived(go_other_y[k])
        add(k, across, working[k], small[k], 1)
        net.start(go_across[k])
        net.arrived(go_own_x[k])
        add(k, base, working[k], small[k], 0)

    loads[0].wait()
    loads[1].wait()
    project(1 - l, 1 - c, give(0))
    net.start(go_give_0)
    project(1 - l, c, hold(0))
    net.arrived(go_give_0)
    send_l[...] = (keep[0] + recv_c[0].astype(jnp.float32)).astype(jnp.bfloat16)
    net.start(*go_cross)
    project(l, 1 - c, give(1))
    net.start(go_give_1)
    project(l, c, hold(1))
    for copy in loads[2:]:
        copy.wait()

    def grad_qkv(yy, xx):
        k = yy * 2 + xx
        value = dot(n_ref[:, rows_at(k, 256)], d_ref[...], TN).astype(jnp.bfloat16)
        pq[2 * k] = value[:128]
        pq[2 * k + 1] = value[128:]

    def start_if(index, groups):
        for k in range(2):

            @pl.when(index == k)
            def _():
                net.start(groups[k])

    def one_chunk(k, carry):
        yy, xx = jnp.where(k % 2 == 0, 1 - y, y), jnp.where(k < 2, 1 - x, x)
        grad_qkv(yy, xx)

        @pl.when(k < 2)
        def _():
            start_if(yy, go_other_x[0])

        @pl.when(k % 2 == 0)
        def _():
            start_if(xx, go_own_y[0])

        return carry

    gs[0] = jnp.zeros_like(gs[0])

    def rows_back(k, total):
        rows = rows_at(k, 64)
        value = x_ref[rows, :].astype(jnp.float32)
        grad = keep[1, rows, :] + recv_c[1, rows, :].astype(jnp.float32) + recv_l[rows, :].astype(jnp.float32)
        r = lax.rsqrt(jnp.mean(value * value, axis=-1, keepdims=True) + EPS)
        scaled = value * r
        gained = grad * ga_ref[...]
        back = r * (gained - scaled * jnp.mean(scaled * gained, axis=-1, keepdims=True))
        gt[rows, :] = (dr_ref[rows, :] + back).astype(jnp.bfloat16)
        return total + jnp.sum(grad * scaled, axis=0, keepdims=True)

    lax.fori_loop(0, 2, one_chunk, 0)
    net.arrived(go_give_1, go_cross[0])
    d_attn = lax.fori_loop(0, 4, rows_back, jnp.zeros((1, MODEL_DIM), jnp.float32))
    home.start_one(0)
    lax.fori_loop(2, 4, one_chunk, 0)
    first_sums(1)
    net.arrived(go_cross[1])
    d_attn = lax.fori_loop(4, 8, rows_back, d_attn)
    home.start_one(1)
    net.arrived(second_of[NEAR])
    og[1] = (og[1].astype(jnp.float32) + rx[1].astype(jnp.float32)).astype(jnp.bfloat16)
    od[1] = (od[1].astype(jnp.float32) + rxd[1].astype(jnp.float32)).astype(jnp.bfloat16)
    net.start(go_near)
    first_sums(0)
    second_sums(1)
    d_mlp = jnp.sum(dgm_ref[...], axis=0, keepdims=True)
    for k in range(8):
        lanes = slice(k * 128, (k + 1) * 128)
        gs[0, k : k + 1, :] = d_attn[:, lanes]
        gs[0, 8 + k : 9 + k, :] = d_mlp[:, lanes]
    for k in range(2):
        gs[0, 16 + k : 17 + k, :] = jnp.sum(dgh_ref[k], axis=0, keepdims=True)
    net.start(go_gain[0])
    second_sums(0)
    gain_hop(0)
    net.arrived(second_of[ME])
    gain_hop(1)
    net.arrived(go_near)
    for cc in range(2):
        rows = pl.ds(32 * cc, 32)
        total_w[cc] = (
            og[0, :, rows, :].astype(jnp.float32) + rx[0, :, rows, :].astype(jnp.float32)
            + rz[0, :, rows, :].astype(jnp.float32) + rz[1, :, rows, :].astype(jnp.float32)
        )
        rows = pl.ds(96 * cc, 96)
        total_d[cc] = (
            od[0, rows, :].astype(jnp.float32) + rxd[0, rows, :].astype(jnp.float32)
            + rzd[0, rows, :].astype(jnp.float32) + rzd[1, rows, :].astype(jnp.float32)
        )
    net.start(go_halves)
    fw[c] = total_w[c]
    fd[c] = total_d[c]
    gain_hop(2)
    net.arrived(go_halves)
    for k in (1, 0):
        net.arrived(go_across[k])
        add(k, base, working[k], small[k], 2)
    net.start(go_last_l, go_last_d, go_last_c)
    rq[t] = work[base, rows_at(t, 32), :]
    rqo[t] = wgo[base, rows_at(t, 64), :]
    gain_hop(3)
    home.wait()
    gain_hop(4)
    gout[...] = gs[len(AXES)]
    net.arrived(go_last_l, go_last_d, go_last_c)
    net.sent()


def finish_kernel(
    rq, rqo, fw, fd, landed, result,
    output, tokens, out_query, out_key, out_value, out_out, out_gate, out_up, out_down,
):
    output[...] = result[...]
    tokens[...] = landed[...].astype(jnp.float32)
    for half in range(2):
        cols = slice(half * HALF_FF, (half + 1) * HALF_FF)
        out_gate[:, cols] = fw[half, 0]
        out_up[:, cols] = fw[half, 1]
        out_down[:, half * 512 : (half + 1) * 512] = fd[half]
    for q in range(4):
        value = rq[q].astype(jnp.float32)
        out_query[:, 512 * q : 512 * (q + 1)] = value[:, :512]
        out_key[:, 256 * q : 256 * (q + 1)] = value[:, 512:768]
        out_value[:, 256 * q : 256 * (q + 1)] = value[:, 768:]
        out_out[:, 256 * q : 256 * (q + 1)] = rqo[q].astype(jnp.float32)


def finish(rq, rqo, fw, fd, landed, result):
    f32 = jnp.float32
    vmem = pl.BlockSpec(memory_space=pltpu.VMEM)
    return pl.pallas_call(
        finish_kernel,
        out_shape=(
            jax.ShapeDtypeStruct((2, ROWS, MODEL_DIM), jnp.bfloat16),
            jax.ShapeDtypeStruct((2, ROWS, MODEL_DIM), f32),
            jax.ShapeDtypeStruct((32, 2048), f32),
            jax.ShapeDtypeStruct((32, 1024), f32),
            jax.ShapeDtypeStruct((32, 1024), f32),
            jax.ShapeDtypeStruct((64, 1024), f32),
            jax.ShapeDtypeStruct((32, FF), f32),
            jax.ShapeDtypeStruct((32, FF), f32),
            jax.ShapeDtypeStruct((96, 1024), f32),
        ),
        in_specs=[vmem] * 6,
        out_specs=[vmem] * 9,
        compiler_params=pltpu.CompilerParams(vmem_limit_bytes=VMEM_LIMIT),
        name="finish",
    )(rq, rqo, fw, fd, landed, result)


def tail(d, w, normed, xs, og, od, fw, fd, goq, d_resid, g_attn, d_g_mlp, d_g_heads):
    bf16, f32 = jnp.bfloat16, jnp.float32
    any_spec = pl.BlockSpec(memory_space=pl.ANY)
    vmem = pl.BlockSpec(memory_space=pltpu.VMEM)
    copies = 48
    wide, deep = (2, 64, HALF_FF), (192, 512)
    own = (OWN, MODEL_DIM)
    big, tall = (128, 1024), (256, 256)

    def vm(a):
        return pltpu.VMEM(a.shape, a.dtype)

    def low(*shape):
        return pltpu.VMEM(shape, bf16)

    goq = goq.reshape(8, 256, 256)
    return pl.pallas_call(
        tail_kernel,
        out_shape=(
            jax.ShapeDtypeStruct((4, 32, 1024), bf16),
            jax.ShapeDtypeStruct((4, 64, 256), bf16),
            jax.ShapeDtypeStruct((2, 2, 32, HALF_FF), f32),
            jax.ShapeDtypeStruct((2, 96, 512), f32),
            jax.ShapeDtypeStruct((24, 128), f32),
            jax.ShapeDtypeStruct((2, ROWS, MODEL_DIM), bf16),
        ),
        in_specs=[any_spec] * 9 + [vmem] * 4,
        out_specs=[vmem] * 6,
        scratch_shapes=[
            vm(d), vm(w), vm(normed), low(*own), vm(goq),
            low(2, *own), low(2, *own), low(*own), low(*own),
            pltpu.VMEM((2,) + own, f32),
            low(*own),
            low(2, *wide), low(2, *deep),
            low(2, *wide), low(2, *deep), low(2, *wide), low(2, *deep),
            pltpu.VMEM((2, 2, 32, HALF_FF), f32), pltpu.VMEM((2, 96, 512), f32),
            low(8, *big), low(8, *big), low(8, *tall),
            low(2, *big), low(2, *tall), low(2, *big), low(2, *tall), low(3, *big), low(3, *tall),
            pltpu.VMEM((6, 24, 128), f32), pltpu.VMEM((5, 24, 128), f32),
            pltpu.SemaphoreType.DMA((copies,)),
            pltpu.SemaphoreType.DMA((copies,)),
            pltpu.SemaphoreType.DMA((11,)),
            pltpu.SemaphoreType.DMA((2,)),
            pltpu.SemaphoreType.DMA((2,)),
        ],
        compiler_params=pltpu.CompilerParams(
            collective_id=5, has_side_effects=True, vmem_limit_bytes=VMEM_LIMIT
        ),
        name="tail_reduce",
    )(d, w, normed, xs, og, od, fw, fd, goq, d_resid, g_attn, d_g_mlp, d_g_heads)


def pick(value, index):
    return lax.dynamic_index_in_dim(value, index, 0, keepdims=False)


def fast_device(tokens, cotangent, starts, w_query, key_matrix, value_matrix, w_out, w_gate, w_up, w_down, gains):
    p = lax.axis_index("p")
    gn = jnp.pad(gains.astype(jnp.float32), (0, 952)).reshape(8, 128)
    half_steps = jnp.arange(HEAD_DIM // 2, dtype=jnp.float32)
    inverse = THETA ** (-2.0 * half_steps / HEAD_DIM)
    inverse = jnp.broadcast_to(jnp.concatenate([inverse, inverse])[None], (8, HEAD_DIM))
    own_starts = pick(starts, p)
    block_at = jnp.arange(SEQ_ROWS // PIECE, dtype=jnp.int32) * PIECE
    flags = jnp.any(own_starts[None, :] == block_at[:, None], axis=1).astype(jnp.int32)
    xs, w_qkv, woq, gf, wgu, wdn, cosine, sine = front(
        tokens, w_query, key_matrix, value_matrix, w_out, gn, w_gate, w_up, w_down, inverse
    )
    xs = xs.reshape(SEQ_ROWS, MODEL_DIM)
    gain_all = gf.reshape(32, 1024)[:, :72].reshape(2304)
    g_attn = gain_all[None, :1024]
    g_mlp = gain_all[None, 1024:2048]
    g_q = gain_all[None, 2048:2176]
    g_k = gain_all[None, 2176:]
    normed, q, k, v, q_raw, k_raw, attn, lse, wo, wgu, wdn = attend(
        flags, xs, w_qkv, g_attn, g_q, g_k, cosine, sine, woq, wgu, wdn
    )
    resid, mlp_in, wgu, wdn, wdx, dy = finish_resid(attn, wo, g_mlp, xs, cotangent, wgu, wdn)
    ggu, gdb, rb, d_resid, d_branch, result, d_g_mlp = feed_forward(
        mlp_in.reshape(1024, MODEL_DIM), dy.reshape(1024, MODEL_DIM), wgu, wdn, wdx, resid, g_mlp
    )
    d_qkv, goq, og, od, fw, fd, output, d_g_heads = attend_back(
        flags, q, k, v, attn, d_branch, wo, lse, q_raw, k_raw, cosine, sine, ggu, gdb, rb, result, g_q, g_k
    )
    rq, rqo, wide, deep, gains_sum, landed = tail(
        d_qkv, w_qkv, normed, xs, og, od, fw, fd, goq, d_resid, g_attn, d_g_mlp, d_g_heads
    )
    device = lax.axis_index(AXES)
    out_gains = lax.dynamic_slice(gains_sum.reshape(3072), (device * 72,), (72,))
    return (*finish(rq, rqo, wide, deep, landed, output), out_gains)


def fast_solution(mesh):
    wide = Mesh(mesh.devices.reshape(2, 2, 2, 2, 2), AXES)
    rows = ("y", "x")
    places = ("p", "l", "c")
    weight = P(AXES, None)
    return jax.shard_map(
        fast_device,
        mesh=wide,
        in_specs=(P(rows, places, None), P(rows, places, None), P(rows, None)) + (weight,) * 7 + (P(AXES),),
        out_specs=(P(rows, places, None), P(rows, places, None)) + (weight,) * 7 + (P(AXES),),
        check_vma=False,
    )


def solution(mesh):
    if dict(mesh.shape) == {"dp": 4, "ctx": 8}:
        return fast_solution(mesh)
    return generic_solution(mesh)
```
